32 devices in a mesh: seq: 8 (over z, x), rep: 4 (over y, core).
Axes of the slice: x: 2, y: 2, z: 4, core: 2. Of those that a mesh axis runs over, the one named last changes fastest.
Arguments:
- layer_in: bfloat16 [2, 16384, 768], P(None, ('seq', 'rep')), may hold values from -6 to 6
- qkv_weight: bfloat16 [768, 2304], replicated, may hold values from -0.21875 to 0.21875
- out_weight: bfloat16 [768, 768], replicated, may hold values from -0.21875 to 0.21875
- up_weight: bfloat16 [768, 3072], replicated, may hold values from -0.21875 to 0.21875
- down_weight: bfloat16 [3072, 768], replicated, may hold values from -0.109375 to 0.109375
- input_gain: float32 [768], replicated, may hold values from 0.5 to 1.5
- input_bias: float32 [768], replicated, may hold values from -3 to 3
- mixer_gain: float32 [768], replicated, may hold values from 0.5 to 1.5
- mixer_bias: float32 [768], replicated, may hold values from -3 to 3
- block_gain: float32 [768], replicated, may hold values from 0.5 to 1.5
- block_bias: float32 [768], replicated, may hold values from -3 to 3
- hidden_gain: float32 [3072], replicated, may hold values from 0.5 to 1.5
- hidden_bias: float32 [3072], replicated, may hold values from -3 to 3
- output_grad: bfloat16 [2, 16384, 768], P(None, ('seq', 'rep')), may hold values from -6 to 6
- seq_lengths: int32 [2, 4], replicated, may hold values from 1024 to 13312, as said below
Outputs:
- layer_out: bfloat16 [2, 16384, 768], P(None, ('seq', 'rep'))
- input_grad: bfloat16 [2, 16384, 768], P(None, ('seq', 'rep'))
- grad_qkv: float32 [768, 2304], P('seq')
- grad_proj: float32 [768, 768], P('seq')
- grad_up: float32 [768, 3072], P('seq')
- grad_down: float32 [3072, 768], P('seq')
- grad_norms: float32 [768, 6], P('seq')
- grad_hidden_norm: float32 [3072, 2], P('seq')
The draws below stay inside these ranges and needn't reach their ends.
Inputs may be any that keep to these rules, and one draw needn't show every extreme that they name: `seq_lengths`: each row holds 4 positive multiples of 1024 that add up to 16384; the first row holds 3 sequences of 1024 and one of the largest length.
All inputs are finite; a program needn't handle non-finite values.
Results may differ from the reference program's by a relative error of at most 0.024.
Values may be sent and summed in bfloat16 or wider, within the bound.
A program may use at most 512 MiB of HBM per device.

```python
import math
from functools import reduce
import jax
import jax.numpy as jnp
from jax import lax

D = 768
HEADS = 12
FF = 3072
HD = 64
W0 = 2048
PATTERNS = 3
MICRO = 2
SEQS = 4
TOKENS = 16384


def draw_seq_lengths(key, part):
    length_rows = []
    for micro_index in range(MICRO):
        micro_key = jax.random.fold_in(key, micro_index + 11)
        if micro_index == 0:
            cut_points = jnp.arange(1, SEQS, dtype=jnp.int32)
        else:
            cut_points = jnp.sort(jax.random.permutation(micro_key, 15)[:SEQS - 1] + 1).astype(jnp.int32)
        edge_list = jnp.concatenate([jnp.zeros((1,), jnp.int32), cut_points, jnp.full((1,), 16, jnp.int32)])
        units = (edge_list[1:] - edge_list[:-1]).astype(jnp.int32)
        if micro_index == 0:
            shift_by = jax.random.randint(micro_key, (), 0, SEQS, dtype=jnp.int32)
            units = jnp.roll(units, shift_by)
        length_rows.append(units * (TOKENS // 16))
    return jnp.stack(length_rows).astype(jnp.int32)


def shard_levels(stream_key, shape, shards, least, top_value):
    factor_of = 1.0
    for axis_at, shards_of in shards:
        draws = jax.random.uniform(jax.random.fold_in(jax.random.fold_in(stream_key, 6), axis_at), (shards_of,), jnp.float32, least / len(shards), top_value / len(shards))
        factor_of = factor_of * jnp.repeat(jnp.exp(draws), shape[axis_at] // shards_of).reshape((-1,) + (1,) * (len(shape) - 1 - axis_at))
    return factor_of


def gaussian(stream_key, shape, scale, bound, cuts=(), kind=jnp.bfloat16):
    entries = jax.random.normal(stream_key, shape, jnp.float32) * scale
    if len(cuts) > 0:
        entries = shard_levels(stream_key, shape, cuts, -0.22, 0.18) * entries
    return jnp.clip(entries, min=-bound, max=bound).astype(kind)


def setup_inputs(seed: int = 0) -> dict:
    key_of = jax.random.split(jax.random.key(seed), 16)
    return {
        "layer_in": gaussian(key_of[0], (MICRO, TOKENS, D), 1.0, 6.0, ((1, 32),)),
        "qkv_weight": gaussian(key_of[1], (D, 3 * D), D ** -0.5, 0.21875),
        "out_weight": gaussian(key_of[2], (D, D), D ** -0.5, 0.21875),
        "up_weight": gaussian(key_of[3], (D, FF), D ** -0.5, 0.21875),
        "down_weight": gaussian(key_of[4], (FF, D), FF ** -0.5, 0.109375),
        "input_gain": jnp.clip(1.0 + 0.1 * jax.random.normal(key_of[5], (D,), jnp.float32), 0.5, 1.5),
        "input_bias": gaussian(key_of[6], (D,), 0.5, 3.0, (), jnp.float32),
        "mixer_gain": jnp.clip(1.0 + 0.1 * jax.random.normal(key_of[7], (D,), jnp.float32), 0.5, 1.5),
        "mixer_bias": gaussian(key_of[8], (D,), 0.5, 3.0, (), jnp.float32),
        "block_gain": jnp.clip(1.0 + 0.1 * jax.random.normal(key_of[9], (D,), jnp.float32), 0.5, 1.5),
        "block_bias": gaussian(key_of[10], (D,), 0.5, 3.0, (), jnp.float32),
        "hidden_gain": jnp.clip(1.0 + 0.1 * jax.random.normal(key_of[11], (FF,), jnp.float32), 0.5, 1.5),
        "hidden_bias": gaussian(key_of[12], (FF,), 0.5, 3.0, (), jnp.float32),
        "output_grad": gaussian(key_of[13], (MICRO, TOKENS, D), 1.0, 6.0, ((1, 32),)),
        "seq_lengths": draw_seq_lengths(jax.random.fold_in(key_of[15], 71), 0),
    }


@jax.custom_vjp
def low(v):
    return lax.optimization_barrier(v.astype(jnp.bfloat16)).astype(jnp.float32)

@jax.custom_vjp
def low_back(v):
    return v

def low_keep(v):
    return (low(v), None)

def low_pass(kept, grad):
    return (grad,)

def back_keep(v):
    return (v, None)

def back_low(kept, grad):
    return (low(grad),)
low.defvjp(low_keep, low_pass)
low_back.defvjp(back_keep, back_low)
norm_eps = 1e-05
neg_large = -1e+30
exact_mode = lax.Precision.HIGHEST

def layer_norm(values, norm_gain, norm_bias):
    centred = values - lax.optimization_barrier(jnp.mean(values, axis=-1, keepdims=True))
    spread = lax.optimization_barrier(jnp.mean(centred * centred, axis=-1, keepdims=True))
    return centred * lax.rsqrt(spread + norm_eps) * norm_gain + norm_bias

def matmul_exact(left_side, right_side):
    return jnp.dot(left_side, right_side, precision=exact_mode, preferred_element_type=jnp.float32)

def solve_problem(problem):
    query_rows, key_rows, value_rows, positions, doc_ids = problem
    scale = 1.0 / math.sqrt(HD)
    scores = low_back(scale * jnp.einsum('qd,kd->qk', query_rows, key_rows, precision=exact_mode))
    allowed = (positions[None, :] <= positions[:, None]) & (doc_ids[None, :] == doc_ids[:, None])
    scores = jnp.where(allowed, scores, neg_large)
    top_score = lax.optimization_barrier(jnp.max(scores, axis=1, keepdims=True))
    log_total = top_score + jnp.log(lax.optimization_barrier(jnp.sum(jnp.exp(scores - top_score), axis=1, keepdims=True)))
    weights = low(jnp.exp(scores - log_total))
    outputs = low_back(jnp.einsum('qk,kd->qd', weights, value_rows, precision=exact_mode))
    return (outputs, log_total[:, 0])

def pattern_attend(qkv_heads, doc_of, pattern):
    dilation = 2 ** pattern
    span = W0 * dilation
    block_count = TOKENS // span
    head_ids = jnp.arange(HEADS, dtype=jnp.int32)
    phases = head_ids % dilation
    reshaped_block = qkv_heads.reshape(block_count, W0, dilation, 3, HEADS, HD)
    picked = reshaped_block[:, :, phases, :, head_ids, :]
    block_ids = jnp.arange(block_count, dtype=jnp.int32)
    row_ids = jnp.arange(W0, dtype=jnp.int32)
    positions = block_ids[None, :, None] * span + row_ids[None, None, :] * dilation + phases[:, None, None]
    doc_ids = doc_of[positions]
    problem_count = HEADS * block_count
    flat = picked.reshape(problem_count, W0, 3, HD)
    outputs, log_sums = lax.map(jax.checkpoint(solve_problem), (flat[:, :, 0], flat[:, :, 1], flat[:, :, 2], positions.reshape(problem_count, W0), doc_ids.reshape(problem_count, W0)))
    outputs = outputs.reshape(HEADS, block_count, W0, HD).transpose(1, 2, 0, 3)
    log_sums = log_sums.reshape(HEADS, block_count, W0).transpose(1, 2, 0)
    full_out = jnp.zeros((block_count, W0, dilation, HEADS, HD), jnp.float32).at[:, :, phases, head_ids, :].set(outputs)
    full_lse = jnp.zeros((block_count, W0, dilation, HEADS), jnp.float32).at[:, :, phases, head_ids].set(log_sums)
    chosen = jnp.arange(dilation, dtype=jnp.int32)[:, None] == phases[None, :]
    chosen = jnp.broadcast_to(chosen[None, None], (block_count, W0, dilation, HEADS)).reshape(TOKENS, HEADS)
    return (full_out.reshape(TOKENS, HEADS, HD), full_lse.reshape(TOKENS, HEADS), chosen)

def forward_micro(sheet_line, length_row, qkv_weight, out_weight, up_weight, down_weight, input_gain, input_bias, mixer_gain, mixer_bias, block_gain, block_bias, hidden_gain, hidden_bias):
    bounds = jnp.cumsum(length_row).astype(jnp.int32)
    doc_of = lax.optimization_barrier(jnp.sum((jnp.arange(TOKENS, dtype=jnp.int32)[:, None] >= bounds[None, :]).astype(jnp.int32), axis=1))
    normed_in = low(layer_norm(sheet_line, input_gain, input_bias))
    qkv = low(low_back(matmul_exact(normed_in, qkv_weight)))
    qkv_heads = qkv.reshape(TOKENS, 3, HEADS, HD)
    results = [pattern_attend(qkv_heads, doc_of, pattern) for pattern in range(PATTERNS)]
    masked = [jnp.where(entry[2], entry[1], neg_large) for entry in results]
    top_lse = reduce(jnp.maximum, masked)
    mix_total = top_lse + jnp.log(sum((jnp.exp(item_lse - top_lse) for item_lse in masked)))
    mixed = sum((jnp.exp(item_lse - mix_total)[:, :, None] * entry[0] for item_lse, entry in zip(masked, results)))
    attended = low(low_back(mixed)).reshape(TOKENS, D)
    mixer_normed = low(layer_norm(attended, mixer_gain, mixer_bias))
    after_mixer = sheet_line + low_back(matmul_exact(mixer_normed, out_weight))
    block_normed = low(layer_norm(after_mixer, block_gain, block_bias))
    upward = low_back(matmul_exact(block_normed, up_weight))
    hidden = low(layer_norm(jax.nn.gelu(upward, approximate=False), hidden_gain, hidden_bias))
    return after_mixer + matmul_exact(hidden, down_weight)

def reference(layer_in, qkv_weight, out_weight, up_weight, down_weight, input_gain, input_bias, mixer_gain, mixer_bias, block_gain, block_bias, hidden_gain, hidden_bias, output_grad, seq_lengths):
    params = tuple((one_param.astype(jnp.float32) for one_param in (qkv_weight, out_weight, up_weight, down_weight, input_gain, input_bias, mixer_gain, mixer_bias, block_gain, block_bias, hidden_gain, hidden_bias)))

    def forward_all(layer_all, *weights_all):
        return jnp.stack([forward_micro(layer_all[micro_index], seq_lengths[micro_index], *weights_all) for micro_index in range(MICRO)])
    result, pullback = jax.vjp(forward_all, layer_in.astype(jnp.float32), *params)
    grad_list = pullback(output_grad.astype(jnp.float32))
    return (result.astype(jnp.bfloat16), grad_list[0].astype(jnp.bfloat16), grad_list[1], grad_list[2], grad_list[3], grad_list[4], jnp.stack(grad_list[5:11], axis=1), jnp.stack(grad_list[11:13], axis=1))
```

```python
import functools
import math

import jax
import jax.numpy as jnp
from jax import lax
from jax.experimental import pallas as pl
from jax.experimental.pallas import tpu as pltpu
from jax.sharding import PartitionSpec as P

HEADS = 12
HD = 64
HPAD = 80
CLASS_SLOT = (0, 2, 1, 3)
LOG2E = 1.4426950408889634
NEG = -1e30
EPS = 1e-05
VMEM = 56 << 20

f32 = jnp.float32
bf16 = jnp.bfloat16


def dot_nn(a, b):
    return lax.dot_general(a, b, (((1,), (0,)), ((), ())), preferred_element_type=f32)


def dot_nt(a, b):
    return lax.dot_general(a, b, (((1,), (1,)), ((), ())), preferred_element_type=f32)


def dot_tn(a, b):
    return lax.dot_general(a, b, (((0,), (0,)), ((), ())), preferred_element_type=f32)


def class_slot(cls):
    return jnp.where(cls == 1, 2, jnp.where(cls == 2, 1, cls))


def rel_pos(shape, dim, offset, pattern):
    i = lax.broadcasted_iota(jnp.int32, shape, dim) + offset
    if pattern == 0:
        return (i % 128) * 4 + class_slot((i // 128) % 4)
    if pattern == 1:
        return (i // 256) * 512 + (i % 128) * 4 + ((i // 128) % 2) * 2
    return i


def doc_rows(len_ref, micro, start, dilation, count):
    pos = lax.broadcasted_iota(jnp.int32, (1, count), 1) * dilation + start
    edge = len_ref[micro, 0]
    doc = (pos >= edge).astype(jnp.int32)
    for n in range(1, len_ref.shape[1] - 1):
        edge = edge + len_ref[micro, n]
        doc = doc + (pos >= edge).astype(jnp.int32)
    return doc


def segment_start(pattern, span):
    team = 2**pattern
    return (lax.axis_index("seq") // team) * (team * span)


def split3(x):
    hi = x.astype(bf16).astype(f32)
    mid = (x - hi).astype(bf16).astype(f32)
    return hi, mid, x - hi - mid


def stat_rows(rows, count):
    r = lax.broadcasted_iota(jnp.int32, (HPAD - HD, count), 0)
    out = jnp.zeros((HPAD - HD, count), f32)
    for n, row in enumerate(rows):
        out = jnp.where(r == n, row, out)
    return out.astype(bf16)


def attn_fwd_body(x_ref, len_ref, o_ref, ks, qs, *, pattern, micro, span):
    groups, _, _, lanes = x_ref.shape
    count = groups * lanes
    doc = doc_rows(len_ref, micro, segment_start(pattern, span), 2**pattern, count)

    def block(c, start, size):
        return x_ref[start // lanes, c, :, start % lanes : start % lanes + size]

    kb = min(512, lanes)
    for s in range(0, count, kb):
        sl = slice(s, s + kb)
        r = lax.broadcasted_iota(jnp.int32, (HD, kb), 0)
        same = doc[:, sl] == r
        aux_k = jnp.where(same, 1.0, 0.0).astype(bf16)
        aux_q = jnp.where(same | (r >= 4), 0.0, NEG).astype(bf16)
        q = (block(0, s, kb).astype(f32) * 0.125).astype(bf16)
        qs[:, sl] = jnp.concatenate([q, aux_q], 0)
        ks[sl, :] = jnp.concatenate([block(1, s, kb), aux_k], 0).T

    qb = 256
    grain = 512 if pattern == 0 else 256

    def tiles(i):
        low = (i * qb) // grain * grain
        out = [(s, min(512, low - s), False) for s in range(0, low, 512)]
        return out + [(low, grain, True)]

    def scores(i):
        out = []
        for s, size, diagonal in tiles(i):
            t = dot_nn(ks[s : s + size, :], qs[:, i * qb : (i + 1) * qb])
            if diagonal:
                keep = rel_pos((size, qb), 0, s % 512, pattern) <= rel_pos(
                    (size, qb), 1, (i * qb) % 512, pattern
                )
                t = jnp.where(keep, t, NEG)
            out.append(t)
        return out

    following = scores(0)
    for i in range(count // qb):
        current = following
        if (i + 1) * qb < count:
            following = scores(i + 1)
        top = functools.reduce(jnp.maximum, [jnp.max(t, 0, keepdims=True) for t in current])
        top2 = top * LOG2E
        acc, total = None, None
        for t, (s, size, _) in zip(current, tiles(i)):
            p = jnp.exp2(t * LOG2E - top2)
            part = jnp.sum(p, 0, keepdims=True)
            out = dot_nn(block(2, s, size), p.astype(bf16))
            acc = out if acc is None else acc + out
            total = part if total is None else total + part
        lse = top + jnp.log(total)
        g, at = (i * qb) // lanes, (i * qb) % lanes
        o_ref[g, :HD, at : at + qb] = (acc / total).astype(bf16)
        o_ref[g, HD:, at : at + qb] = stat_rows(split3(lse), qb)


def attn_bwd_body(
    x_ref, g_ref, len_ref, o_ref, ks, vs, qs, qr, gs, gr, dq, *, pattern, micro, span
):
    groups, _, _, lanes = x_ref.shape
    count = groups * lanes
    doc = doc_rows(len_ref, micro, segment_start(pattern, span), 2**pattern, count)
    bs = min(512, lanes)

    def block(c, start, size):
        return x_ref[start // lanes, c, :, start % lanes : start % lanes + size]

    zeros = jnp.zeros((HD, bs), bf16)
    r = lax.broadcasted_iota(jnp.int32, (HD, bs), 0)
    fill = jnp.zeros((HD - 32, bs), bf16)
    for s in range(0, count, bs):
        sl = slice(s, s + bs)
        same = doc[:, sl] == r
        aux_k = jnp.where(same | ((r >= 16) & (r < 19)), 1.0, 0.0).astype(bf16)
        aux_q = jnp.where(same | (r >= 4), 0.0, NEG).astype(bf16)
        aux_v = jnp.where((r >= 19) & (r < 21), 1.0, 0.0).astype(bf16)
        q = (block(0, s, bs).astype(f32) * 0.125).astype(bf16)
        k = block(1, s, bs)
        v = block(2, s, bs)
        at = s % lanes
        g = g_ref[s // lanes, :HD, at : at + bs]
        stats = g_ref[s // lanes, HD:, at : at + bs]
        qs[:, sl] = jnp.concatenate([q, aux_q[:16], stats, fill], 0)
        gs[:, sl] = jnp.concatenate([g, zeros[:16], stats, fill], 0)
        qr[sl, :] = jnp.concatenate([q, zeros], 0).T
        gr[sl, :] = jnp.concatenate([g, zeros], 0).T
        ks[sl, :] = jnp.concatenate([k, aux_k], 0).T
        vs[sl, :] = jnp.concatenate([v, aux_v], 0).T

    keep = rel_pos((bs, bs), 0, 0, pattern) <= rel_pos((bs, bs), 1, 0, pattern)
    for j in range(count // bs):
        jl = slice(j * bs, (j + 1) * bs)
        dva, dka = None, None
        for i in range(j, count // bs):
            il = slice(i * bs, (i + 1) * bs)
            p = jnp.exp2(dot_nn(ks[jl, :], qs[:, il]) * LOG2E)
            if i == j:
                p = jnp.where(keep, p, 0.0)
            dp = dot_nn(vs[jl, :], gs[:, il])
            ds = (p * dp).astype(bf16)
            dvi = dot_nn(p.astype(bf16), gr[il, :])
            dki = dot_nn(ds, qr[il, :])
            dva = dvi if dva is None else dva + dvi
            dka = dki if dka is None else dka + dki
            dqi = dot_nn(block(1, j * bs, bs), ds) * 0.125
            if j == 0:
                dq[:, il] = dqi
            else:
                dq[:, il] += dqi
        g, at = (j * bs) // lanes, (j * bs) % lanes
        o_ref[g, 1, :, at : at + bs] = dka.T[:HD].astype(bf16)
        o_ref[g, 2, :, at : at + bs] = dva.T[:HD].astype(bf16)
        o_ref[g, 0, :, at : at + bs] = dq[:, jl].astype(bf16)


def specs_of(pattern, span, reps):
    if pattern == 0:
        return (
            3,
            pl.BlockSpec((reps, 3, HD, span // reps), lambda n: (0, 0, n, 0)),
            pl.BlockSpec((reps, None, HPAD, span // reps), lambda n: (0, n, 0, 0)),
            (reps, 3, HPAD, span // reps),
            (reps, 3, 3 * HD, span // reps),
        )
    if pattern == 1:
        return (
            2,
            pl.BlockSpec((2, None, 3, HD, span // 2), lambda n: (0, n, 0, 0, 0)),
            pl.BlockSpec((2, None, HPAD, span // 2), lambda n: (0, n, 0, 0)),
            (2, 2, HPAD, span // 2),
            (2, 2, 3, HD, span // 2),
        )
    return (
        1,
        pl.BlockSpec((4, 3, HD, span // 4), lambda n: (0, 0, 0, 0)),
        pl.BlockSpec((4, HPAD, span // 4), lambda n: (0, 0, 0)),
        (4, HPAD, span // 4),
        (4, 3, HD, span // 4),
    )


def smem_spec():
    return pl.BlockSpec(memory_space=pltpu.SMEM)


def attn_fwd(x, lengths, pattern, micro, span, reps):
    n, x_spec, o_spec, o_shape, _ = specs_of(pattern, span, reps)
    return pl.pallas_call(
        functools.partial(attn_fwd_body, pattern=pattern, micro=micro, span=span),
        grid=(n,),
        in_specs=[x_spec, smem_spec()],
        out_specs=o_spec,
        out_shape=jax.ShapeDtypeStruct(o_shape, bf16),
        scratch_shapes=[pltpu.VMEM((span, 128), bf16), pltpu.VMEM((128, span), bf16)],
        compiler_params=pltpu.CompilerParams(vmem_limit_bytes=VMEM),
        cost_estimate=pl.CostEstimate(
            flops=n * 5_000_000_000, bytes_accessed=n * 1_200_000, transcendentals=n * 2_600_000
        ),
        name=f"attn_fwd_{pattern}_{micro}",
    )(x, lengths)


def attn_bwd(x, g, lengths, pattern, micro, span, reps):
    n, x_spec, g_spec, _, d_shape = specs_of(pattern, span, reps)
    wide = pltpu.VMEM((128, span), bf16)
    tall = pltpu.VMEM((span, 128), bf16)
    return pl.pallas_call(
        functools.partial(attn_bwd_body, pattern=pattern, micro=micro, span=span),
        grid=(n,),
        in_specs=[x_spec, g_spec, smem_spec()],
        out_specs=x_spec,
        out_shape=jax.ShapeDtypeStruct(d_shape, bf16),
        scratch_shapes=[tall, tall, wide, tall, wide, tall, pltpu.VMEM((HD, span), f32)],
        compiler_params=pltpu.CompilerParams(vmem_limit_bytes=VMEM),
        cost_estimate=pl.CostEstimate(
            flops=n * 8_000_000_000, bytes_accessed=n * 2_000_000, transcendentals=n * 2_600_000
        ),
        name=f"attn_bwd_{pattern}_{micro}",
    )(x, g, lengths)


OWNER1 = {(0, 0): 0, (0, 1): 2, (1, 0): 1}
PLACE1 = {0: (0, 0), 1: (1, 0), 2: (0, 1)}


def half_of(j):
    return (3 * lax.axis_index("rep") + j) % 2


def quarter_of(j):
    return class_slot((3 * lax.axis_index("rep") + j) % 4)


def lane_slice(start, size):
    return pl.ds(pl.multiple_of(start, size), size)


def pack_qkv_body(r_ref, p1_ref, p2_ref):
    reps = r_ref.shape[0]
    for e in range(2):
        for s in range(2):
            j = OWNER1.get((e, s), 1)
            for b in range(reps):
                p1_ref[e, s, :, :, b * 256 : (b + 1) * 256] = r_ref[
                    b, :, j * HD : (j + 1) * HD, lane_slice(half_of(j) * 256, 256)
                ]
    for g in range(4):
        j = min(g, 2)
        for b in range(reps):
            p2_ref[g, :, :, b * 128 : (b + 1) * 128] = r_ref[
                b, :, j * HD : (j + 1) * HD, lane_slice(quarter_of(j) * 128, 128)
            ]


def vmem_spec():
    return pl.BlockSpec(memory_space=pltpu.VMEM)


def small_call(body, outs, args, name, nbytes, scratch=(), smem=()):
    return pl.pallas_call(
        body,
        in_specs=[smem_spec() if n in smem else vmem_spec() for n in range(len(args))],
        out_specs=[vmem_spec() for _ in outs],
        out_shape=[jax.ShapeDtypeStruct(s, d) for s, d in outs],
        scratch_shapes=list(scratch),
        compiler_params=pltpu.CompilerParams(vmem_limit_bytes=VMEM),
        cost_estimate=pl.CostEstimate(flops=1_000_000, bytes_accessed=nbytes, transcendentals=0),
        name=name,
    )(*args)


def pack_qkv(r, span, reps, micro):
    return small_call(
        pack_qkv_body,
        [((2, 2, 3, HD, span // 2), bf16), ((4, 3, HD, span // 4), bf16)],
        (r,),
        f"pack_qkv_{micro}",
        5_000_000,
    )


def mix_body(o0_ref, o1_ref, o2_ref, att_ref, mix_ref):
    reps = o0_ref.shape[0]

    def stat(tile):
        t = tile[HD:, :].astype(f32)
        return t[0:1] + t[1:2] + t[2:3]

    mix_ref[...] = jnp.zeros_like(mix_ref)
    for j in range(3):
        half, quarter = half_of(j), quarter_of(j)
        e, s = PLACE1[j]
        for b in range(reps):
            for a in range(4):
                la = slice(a * 128, (a + 1) * 128)
                t0 = o0_ref[b, j, :, la]
                lb = b * 256 + (a % 2) * 128
                t1 = o1_ref[e, s, :, lb : lb + 128]
                t2 = o2_ref[j, :, b * 128 : (b + 1) * 128]
                l0 = stat(t0)
                l1 = jnp.where(half == a // 2, stat(t1), NEG)
                l2 = jnp.where(quarter == a, stat(t2), NEG)
                top = jnp.maximum(jnp.maximum(l0, l1), l2)
                e0, e1, e2 = jnp.exp(l0 - top), jnp.exp(l1 - top), jnp.exp(l2 - top)
                total = e0 + e1 + e2
                inv = 1.0 / total
                mixed = (
                    t0[:HD].astype(f32) * (e0 * inv)
                    + t1[:HD].astype(f32) * (e1 * inv)
                    + t2[:HD].astype(f32) * (e2 * inv)
                )
                att_ref[b, j * HD : (j + 1) * HD, la] = mixed.astype(bf16)
                col = b * 512 + a * 128
                mix_ref[j : j + 1, col : col + 128] = top + jnp.log(total)


def mix(o0, o1, o2, span, reps, micro):
    return small_call(
        mix_body,
        [((reps, 3 * HD, span // reps), bf16), ((8, span), f32)],
        (o0, o1, o2),
        f"mix_{micro}",
        4_000_000,
    )


def pack_grad_body(g_ref, att_ref, mix_ref, g0_ref, p1_ref, p2_ref):
    reps, _, tok = g_ref.shape
    for j in range(3):
        rows = slice(j * HD, (j + 1) * HD)
        for b in range(reps):
            g = g_ref[b, rows, :]
            inner = jnp.sum(g.astype(f32) * att_ref[b, rows, :].astype(f32), 0, keepdims=True)
            total = mix_ref[j : j + 1, b * tok : (b + 1) * tok]
            h, m, l = split3(-total)
            ih, im, _ = split3(-inner)
            g0_ref[b, j, :HD, :] = g
            g0_ref[b, j, HD:, :] = stat_rows((h, m, l, ih, im), tok)
    for e in range(2):
        for s in range(2):
            j = OWNER1.get((e, s), 1)
            for b in range(reps):
                p1_ref[e, s, :, b * 256 : (b + 1) * 256] = g0_ref[
                    b, j, :, lane_slice(half_of(j) * 256, 256)
                ]
    for g in range(4):
        j = min(g, 2)
        for b in range(reps):
            p2_ref[g, :, b * 128 : (b + 1) * 128] = g0_ref[
                b, j, :, lane_slice(quarter_of(j) * 128, 128)
            ]


def pack_grad(g, att, mixed, span, reps, micro):
    return small_call(
        pack_grad_body,
        [
            ((reps, 3, HPAD, span // reps), bf16),
            ((2, 2, HPAD, span // 2), bf16),
            ((4, HPAD, span // 4), bf16),
        ],
        (g, att, mixed),
        f"pack_grad_{micro}",
        5_000_000,
    )


def sum_grad_body(d0_ref, d1_ref, d2_ref, out_ref):
    reps = d0_ref.shape[0]
    for j in range(3):
        rows = slice(j * HD, (j + 1) * HD)
        half, quarter = half_of(j), quarter_of(j)
        e, s = PLACE1[j]
        for b in range(reps):
            for a in range(4):
                la = slice(a * 128, (a + 1) * 128)
                lb = b * 256 + (a % 2) * 128
                t0 = d0_ref[b, :, rows, la].astype(f32)
                t1 = d1_ref[e, s, :, :, lb : lb + 128].astype(f32)
                t2 = d2_ref[j, :, :, b * 128 : (b + 1) * 128].astype(f32)
                t = t0 + jnp.where(half == a // 2, t1, 0.0) + jnp.where(quarter == a, t2, 0.0)
                out_ref[b, :, rows, la] = t.astype(bf16)


def sum_grad(d0, d1, d2, span, reps, micro):
    return small_call(
        sum_grad_body,
        [((reps, 3, 3 * HD, span // reps), bf16)],
        (d0, d1, d2),
        f"sum_grad_{micro}",
        7_000_000,
    )[0]


def onehot_rows(tok):
    i = lax.broadcasted_iota(jnp.int32, (tok, tok), 0)
    t = lax.broadcasted_iota(jnp.int32, (tok, tok), 1)
    return ((i % 128) * 4 + class_slot(i // 128) == t).astype(bf16)


def onehot_cols(tok):
    t = lax.broadcasted_iota(jnp.int32, (tok, tok), 0)
    i = lax.broadcasted_iota(jnp.int32, (tok, tok), 1)
    return ((i % 128) * 4 + class_slot(i // 128) == t).astype(bf16)


def normalize(x):
    c = x - jnp.mean(x, axis=-1, keepdims=True)
    rstd = lax.rsqrt(jnp.mean(c * c, axis=-1, keepdims=True) + EPS)
    return c * rstd, rstd


def norm_back(grad, gain, xhat, rstd):
    dn = grad * gain
    low = jnp.mean(dn, axis=-1, keepdims=True)
    along = jnp.mean(dn * xhat, axis=-1, keepdims=True)
    dx = rstd * (dn - low - xhat * along)
    return dx, jnp.sum(grad * xhat, 0, keepdims=True), jnp.sum(grad, 0, keepdims=True)


def qkv_body(x_ref, w_ref, gain_ref, bias_ref, out_ref, xp_ref, nt_ref, n_scr):
    tok, width = x_ref.shape

    @pl.when(pl.program_id(0) == 0)
    def _():
        xp = dot_nn(onehot_rows(tok), x_ref[...])
        xp_ref[...] = xp.astype(bf16)
        xhat, _ = normalize(xp)
        n = (xhat * gain_ref[...] + bias_ref[...]).astype(bf16)
        n_scr[...] = n
        nt_ref[...] = n.T

    t = dot_nn(n_scr[...], w_ref[...]).astype(bf16).T
    reps, _, cols, _ = out_ref.shape
    for r in range(reps):
        out_ref[r, 0] = t[r * cols : (r + 1) * cols]


def qkv_call(layer_in, weight, gain, bias, m, reps):
    _, tok, width = layer_in.shape
    cols = width // reps
    return pl.pallas_call(
        qkv_body,
        grid=(3,),
        in_specs=[
            pl.BlockSpec((None, tok, width), lambda c: (m, 0, 0)),
            pl.BlockSpec((width, width), lambda c: (0, c)),
            pl.BlockSpec((1, width), lambda c: (0, 0)),
            pl.BlockSpec((1, width), lambda c: (0, 0)),
        ],
        out_specs=[
            pl.BlockSpec((reps, 1, cols, tok), lambda c: (0, c, 0, 0)),
            pl.BlockSpec((tok, width), lambda c: (0, 0)),
            pl.BlockSpec((width, tok), lambda c: (0, 0)),
        ],
        out_shape=[
            jax.ShapeDtypeStruct((reps, 3, cols, tok), bf16),
            jax.ShapeDtypeStruct((tok, width), bf16),
            jax.ShapeDtypeStruct((width, tok), bf16),
        ],
        scratch_shapes=[pltpu.VMEM((tok, width), bf16)],
        compiler_params=pltpu.CompilerParams(vmem_limit_bytes=VMEM),
        cost_estimate=pl.CostEstimate(
            flops=6 * tok * width * width, bytes_accessed=9_000_000, transcendentals=0
        ),
        name=f"qkv_{m}",
    )(layer_in, weight, gain, bias)


CHUNK = 512
SQRT_HALF = 0.7071067811865476
INV_SQRT_2PI = 0.3989422804014327


def ffn_body(
    att_ref,
    xp_ref,
    cot_ref,
    wo_hbm,
    wu_hbm,
    wd_hbm,
    mg_ref,
    mb_ref,
    bg_ref,
    bb_ref,
    hg_ref,
    hb_ref,
    out_ref,
    branch_ref,
    da_ref,
    mix_ref,
    low_ref,
    hid_ref,
    dup_ref,
    brl_ref,
    cotp_ref,
    ng_ref,
    nh_ref,
    wo,
    wu,
    wd,
    g_scr,
    dg_scr,
    dn_scr,
    am_scr,
    acc_scr,
    sems,
):
    tok, width = xp_ref.shape
    hidden = hid_ref.shape[1]
    chunks = hidden // CHUNK
    reps, cols, _ = att_ref.shape
    copies = [
        pltpu.make_async_copy(a, b, sems.at[n])
        for n, (a, b) in enumerate(((wo_hbm, wo), (wu_hbm, wu), (wd_hbm, wd)))
    ]
    for c in copies:
        c.start()
    cotp = dot_nn(onehot_rows(tok), cot_ref[...])
    cotp_ref[...] = cotp.astype(bf16)
    att = att_ref[...].reshape(width, tok).T.astype(f32)
    ahat, _ = normalize(att)
    mix_ref[...] = (ahat * mg_ref[...] + mb_ref[...]).astype(bf16)
    copies[0].wait()
    am = xp_ref[...].astype(f32) + dot_nn(mix_ref[...], wo[...])
    am_scr[...] = am
    bhat, _ = normalize(am)
    low_ref[...] = (bhat * bg_ref[...] + bb_ref[...]).astype(bf16)
    copies[1].wait()

    def lanes(n):
        return pl.ds(pl.multiple_of(n * CHUNK, CHUNK), CHUNK)

    def upward(n, total):
        u = dot_nn(low_ref[...], wu[:, lanes(n)])
        cdf = 0.5 + 0.5 * lax.erf(u * SQRT_HALF)
        g = u * cdf
        g_scr[:, lanes(n)] = g
        dg_scr[:, lanes(n)] = cdf + u * (jnp.exp(u * u * -0.5) * INV_SQRT_2PI)
        return total + jnp.sum(g, 1, keepdims=True)

    mean = lax.fori_loop(0, chunks, upward, jnp.zeros((tok, 1), f32)) / hidden

    def spread(n, total):
        c = g_scr[:, lanes(n)] - mean
        return total + jnp.sum(c * c, 1, keepdims=True)

    var = lax.fori_loop(0, chunks, spread, jnp.zeros((tok, 1), f32)) / hidden
    rstd = lax.rsqrt(var + EPS)
    copies[2].wait()
    acc_scr[...] = jnp.zeros_like(acc_scr)

    def downward(n, sums):
        first, second = sums
        ghat = (g_scr[:, lanes(n)] - mean) * rstd
        g_scr[:, lanes(n)] = ghat
        gain = hg_ref[:, lanes(n)]
        h = (ghat * gain + hb_ref[:, lanes(n)]).astype(bf16)
        hid_ref[:, lanes(n)] = h
        acc_scr[...] += dot_nn(h, wd[lanes(n), :])
        back = dot_nt(cotp_ref[...], wd[lanes(n), :])
        nh_ref[0:1, lanes(n)] = jnp.sum(back * ghat, 0, keepdims=True)
        nh_ref[1:2, lanes(n)] = jnp.sum(back, 0, keepdims=True)
        dn = back * gain
        dn_scr[:, lanes(n)] = dn
        return (
            first + jnp.sum(dn, 1, keepdims=True),
            second + jnp.sum(dn * ghat, 1, keepdims=True),
        )

    zero = jnp.zeros((tok, 1), f32)
    first, second = lax.fori_loop(0, chunks, downward, (zero, zero))
    first, second = first / hidden, second / hidden
    out_ref[...] = dot_nn(onehot_cols(tok), (am_scr[...] + acc_scr[...]).astype(bf16)).astype(bf16)
    acc_scr[...] = jnp.zeros_like(acc_scr)

    def backward(n, carry):
        d = rstd * (dn_scr[:, lanes(n)] - first - g_scr[:, lanes(n)] * second)
        dup = (d * dg_scr[:, lanes(n)]).astype(bf16)
        dup_ref[:, lanes(n)] = dup
        acc_scr[...] += dot_nt(dup, wu[:, lanes(n)])
        return carry

    lax.fori_loop(0, chunks, backward, 0)
    bhat, brstd = normalize(am_scr[...])
    middle, gain_b, bias_b = norm_back(acc_scr[...], bg_ref[...], bhat, brstd)
    branch = cotp_ref[...].astype(f32) + middle
    branch_ref[...] = branch
    brl_ref[...] = branch.astype(bf16)
    att = att_ref[...].reshape(width, tok).T.astype(f32)
    ahat, arstd = normalize(att)
    da, gain_m, bias_m = norm_back(dot_nt(brl_ref[...], wo[...]), mg_ref[...], ahat, arstd)
    da_ref[...] = da.astype(bf16).T.reshape(reps, cols, tok)
    ng_ref[0:1] = gain_m
    ng_ref[1:2] = bias_m
    ng_ref[2:3] = gain_b
    ng_ref[3:4] = bias_b


def ffn_call(att, xp, output_grad, weights, gains, m):
    reps, cols, tok = att.shape
    width = xp.shape[1]
    hidden = weights[1].shape[1]
    vec = vmem_spec()
    shapes = [
        ((tok, width), bf16),
        ((tok, width), f32),
        ((reps, cols, tok), bf16),
        ((tok, width), bf16),
        ((tok, width), bf16),
        ((tok, hidden), bf16),
        ((tok, hidden), bf16),
        ((tok, width), bf16),
        ((tok, width), bf16),
        ((4, width), f32),
        ((2, hidden), f32),
    ]
    return pl.pallas_call(
        ffn_body,
        grid=(1,),
        in_specs=[
            pl.BlockSpec((reps, cols, tok), lambda n: (0, 0, 0)),
            pl.BlockSpec((tok, width), lambda n: (0, 0)),
            pl.BlockSpec((None, tok, width), lambda n: (m, 0, 0)),
        ]
        + [pl.BlockSpec(memory_space=pl.ANY)] * 3
        + [pl.BlockSpec(g.shape, lambda n: (0, 0)) for g in gains],
        out_specs=[pl.BlockSpec(s, lambda n, k=len(s): (0,) * k) for s, _ in shapes],
        out_shape=[jax.ShapeDtypeStruct(s, d) for s, d in shapes],
        scratch_shapes=[pltpu.VMEM(w.shape, bf16) for w in weights]
        + [pltpu.VMEM((tok, hidden), f32)] * 3
        + [pltpu.VMEM((tok, width), f32)] * 2
        + [pltpu.SemaphoreType.DMA((3,))],
        compiler_params=pltpu.CompilerParams(vmem_limit_bytes=VMEM),
        cost_estimate=pl.CostEstimate(
            flops=4 * tok * width * (2 * hidden + width),
            bytes_accessed=25_000_000,
            transcendentals=2 * tok * hidden,
        ),
        name=f"ffn_{m}",
    )(att, xp, output_grad, *weights, *gains)


def weight_grad_body(*refs):
    micros = (len(refs) - 6) // 6
    groups = [refs[6 * k : 6 * k + 6] for k in range(micros)]
    down_ref, up_ref, proj_ref, lt, _, _ = refs[6 * micros :]

    @pl.when(pl.program_id(0) == 0)
    def _():
        total = None
        for k, (low, dup, hid, cot, mix, brl) in enumerate(groups):
            lt[k] = low[...].T
            part = dot_tn(mix[...], brl[...])
            total = part if total is None else total + part
        proj_ref[...] = total.astype(bf16)

    up = down = None
    for k, (low, dup, hid, cot, mix, brl) in enumerate(groups):
        u = dot_nn(lt[k], dup[...])
        d = dot_tn(hid[...], cot[...])
        up = u if up is None else up + u
        down = d if down is None else down + d
    up_ref[...] = up.astype(bf16)
    down_ref[...] = down.astype(bf16)


def weight_grads(groups, tok, width, hidden):
    full = pl.BlockSpec((tok, width), lambda n: (0, 0))
    part = pl.BlockSpec((tok, CHUNK), lambda n: (0, n))
    micros = len(groups)
    return pl.pallas_call(
        weight_grad_body,
        grid=(hidden // CHUNK,),
        in_specs=[full, part, part, full, full, full] * micros,
        out_specs=[
            pl.BlockSpec((CHUNK, width), lambda n: (n, 0)),
            pl.BlockSpec((width, CHUNK), lambda n: (0, n)),
            pl.BlockSpec((width, width), lambda n: (0, 0)),
        ],
        out_shape=[
            jax.ShapeDtypeStruct((hidden, width), bf16),
            jax.ShapeDtypeStruct((width, hidden), bf16),
            jax.ShapeDtypeStruct((width, width), bf16),
        ],
        scratch_shapes=[pltpu.VMEM((micros, width, tok), bf16)]
        + [pltpu.VMEM((8, 128), f32)] * 2,
        compiler_params=pltpu.CompilerParams(vmem_limit_bytes=VMEM),
        cost_estimate=pl.CostEstimate(
            flops=2 * micros * tok * width * (2 * hidden + width),
            bytes_accessed=30_000_000,
            transcendentals=0,
        ),
        name="weight_grads",
    )(*[a for g in groups for a in g])


def join_heads(tg_ref, c):
    reps = tg_ref.shape[0]
    return jnp.concatenate([tg_ref[r, c] for r in range(reps)], 0)


def qkv_grad_body(*refs):
    micros = (len(refs) - 1) // 2
    out_ref = refs[-1]
    total = None
    for k in range(micros):
        nt, tg = refs[2 * k], refs[2 * k + 1]
        part = dot_nt(nt[...], join_heads(tg, 0))
        total = part if total is None else total + part
    out_ref[...] = total.astype(bf16)


def qkv_grad_call(pairs, tok, width, reps):
    cols = width // reps
    return pl.pallas_call(
        qkv_grad_body,
        grid=(3,),
        in_specs=[
            pl.BlockSpec((width, tok), lambda c: (0, 0)),
            pl.BlockSpec((reps, 1, cols, tok), lambda c: (0, c, 0, 0)),
        ]
        * len(pairs),
        out_specs=pl.BlockSpec((width, width), lambda c: (0, c)),
        out_shape=jax.ShapeDtypeStruct((width, 3 * width), bf16),
        compiler_params=pltpu.CompilerParams(vmem_limit_bytes=VMEM),
        cost_estimate=pl.CostEstimate(
            flops=6 * len(pairs) * tok * width * width, bytes_accessed=10_000_000, transcendentals=0
        ),
        name="qkv_grad",
    )(*[a for p in pairs for a in p])


def input_grad_body(tg_ref, w_ref, xp_ref, branch_ref, gain_ref, out_ref, ng_ref, acc):
    tok, width = xp_ref.shape
    c = pl.program_id(0)
    part = dot_nn(w_ref[...], join_heads(tg_ref, 0))

    @pl.when(c == 0)
    def _():
        acc[...] = part

    @pl.when(c > 0)
    def _():
        acc[...] += part

    @pl.when(c == 2)
    def _():
        xhat, rstd = normalize(xp_ref[...].astype(f32))
        dx, gain_i, bias_i = norm_back(acc[...].T, gain_ref[...], xhat, rstd)
        ng_ref[0:1] = gain_i
        ng_ref[1:2] = bias_i
        total = (branch_ref[...] + dx).astype(bf16)
        out_ref[...] = dot_nn(onehot_cols(tok), total).astype(bf16)


def input_grad_call(tg, weight, xp, branch, gain, m):
    reps, _, cols, tok = tg.shape
    width = reps * cols
    return pl.pallas_call(
        input_grad_body,
        grid=(3,),
        in_specs=[
            pl.BlockSpec((reps, 1, cols, tok), lambda c: (0, c, 0, 0)),
            pl.BlockSpec((width, width), lambda c: (0, c)),
            pl.BlockSpec((tok, width), lambda c: (0, 0)),
            pl.BlockSpec((tok, width), lambda c: (0, 0)),
            pl.BlockSpec((1, width), lambda c: (0, 0)),
        ],
        out_specs=[
            pl.BlockSpec((tok, width), lambda c: (0, 0)),
            pl.BlockSpec((2, width), lambda c: (0, 0)),
        ],
        out_shape=[
            jax.ShapeDtypeStruct((tok, width), bf16),
            jax.ShapeDtypeStruct((2, width), f32),
        ],
        scratch_shapes=[pltpu.VMEM((width, tok), f32)],
        compiler_params=pltpu.CompilerParams(vmem_limit_bytes=VMEM),
        cost_estimate=pl.CostEstimate(
            flops=6 * tok * width * width, bytes_accessed=10_000_000, transcendentals=0
        ),
        name=f"input_grad_{m}",
    )(tg, weight, xp, branch, gain)


def swap(block, axis, bit):
    count = lax.axis_size(axis)
    return lax.ppermute(block, axis, [(n, n ^ (1 << bit)) for n in range(count)])


def bits_of(count):
    return count.bit_length() - 1


def reduce_rows(x, order):
    seqs, reps = lax.axis_size("seq"), lax.axis_size("rep")
    rows, cols = x.shape
    sb, rb = bits_of(seqs), bits_of(reps)
    y = x.reshape((2,) * (sb + rb) + (rows // (seqs * reps), cols))
    names = [("seq", b) for b in reversed(range(sb))] + [("rep", b) for b in reversed(range(rb))]
    for step in order(sb, rb):
        at = names.index(step)
        axis, bit = step
        mine = (lax.axis_index(axis) >> bit) & 1
        send = lax.dynamic_index_in_dim(y, 1 - mine, at, keepdims=False)
        keep = lax.dynamic_index_in_dim(y, mine, at, keepdims=False)
        got = swap(send.astype(x.dtype), axis, bit)
        y = (keep.astype(f32) + got.astype(f32)).astype(x.dtype)
        names.pop(at)
    for bit in range(rb):
        other = swap(y, "rep", bit)
        mine = (lax.axis_index("rep") >> bit) & 1
        y = jnp.where(mine == 0, jnp.stack([y, other]), jnp.stack([other, y]))
        y = y.reshape((-1,) + y.shape[2:])
    return y.astype(f32)


def order_yxz(sb, rb):
    return [("rep", b) for b in range(rb)] + [("seq", b) for b in range(sb)]


def order_xzy(sb, rb):
    return [("rep", 0)] + [("seq", b) for b in range(sb)] + [("rep", b) for b in range(1, rb)]


def on_device(
    layer_in,
    qkv_weight,
    out_weight,
    up_weight,
    down_weight,
    input_gain,
    input_bias,
    mixer_gain,
    mixer_bias,
    block_gain,
    block_bias,
    hidden_gain,
    hidden_bias,
    output_grad,
    seq_lengths,
):
    micro_count, tok, width = layer_in.shape
    reps = lax.axis_size("rep")
    seqs = lax.axis_size("seq")
    span = tok * reps
    heads_dev = HEADS // reps
    cols = heads_dev * HD
    pairs = [[2 * n, 2 * n + 1] for n in range(seqs // 2)]
    fours = [[4 * n + k for k in range(4)] for n in range(seqs // 4)]

    def to_reps(x):
        return lax.all_to_all(x, "rep", 0, 0, tiled=True)

    def to_pair(x):
        return lax.all_to_all(x, "seq", 0, 0, tiled=True, axis_index_groups=pairs)

    def to_four(x):
        return lax.all_to_all(x, "seq", 0, 0, tiled=True, axis_index_groups=fours)

    def row(v):
        return v.reshape(1, -1)

    micros = range(micro_count)
    residual, normed, got_qkv = [], [], []
    for m in micros:
        sent, xp, nt = qkv_call(layer_in, qkv_weight, row(input_gain), row(input_bias), m, reps)
        residual.append(xp)
        normed.append(nt)
        got_qkv.append(to_reps(sent))

    pieces, attended, own_att, totals = [], [], [], []
    for m in micros:
        p1, p2 = pack_qkv(got_qkv[m], span, reps, m)
        p1, p2 = to_pair(p1), to_four(p2)
        pieces.append((got_qkv[m], p1, p2))
        o0 = attn_fwd(got_qkv[m], seq_lengths, 0, m, span, reps)
        o1 = to_pair(attn_fwd(p1, seq_lengths, 1, m, span, reps))
        o2 = to_four(attn_fwd(p2, seq_lengths, 2, m, span, reps))
        att, total = mix(o0, o1, o2, span, reps, m)
        own_att.append(att)
        totals.append(total)
        attended.append(to_reps(att))

    outputs, branch_grads, head_grads, groups, norm_terms, hidden_terms = [], [], [], [], [], []
    weights = (out_weight, up_weight, down_weight)
    gains = tuple(
        row(v) for v in (mixer_gain, mixer_bias, block_gain, block_bias, hidden_gain, hidden_bias)
    )
    for m in micros:
        out, branch, da, mixl, low, hid, dup, brl, cotp, ng, nh = ffn_call(
            attended[m], residual[m], output_grad, weights, gains, m
        )
        outputs.append(out)
        branch_grads.append(branch)
        head_grads.append(to_reps(da))
        groups.append((low, dup, hid, cotp, mixl, brl))
        norm_terms.append(ng)
        hidden_terms.append(nh)
    grad_down, grad_up, grad_proj = weight_grads(groups, tok, width, up_weight.shape[1])

    down_total = reduce_rows(grad_down, order_yxz)
    up_total = reduce_rows(grad_up, order_xzy)
    proj_total = reduce_rows(grad_proj, order_xzy)

    input_grads, input_terms, token_grads = [], [], []
    for m in micros:
        g0, g1, g2 = pack_grad(head_grads[m], own_att[m], totals[m], span, reps, m)
        g1, g2 = to_pair(g1), to_four(g2)
        x0, x1, x2 = pieces[m]
        d0 = attn_bwd(x0, g0, seq_lengths, 0, m, span, reps)
        d1 = to_pair(attn_bwd(x1, g1, seq_lengths, 1, m, span, reps))
        d2 = to_four(attn_bwd(x2, g2, seq_lengths, 2, m, span, reps))
        token_grads.append(to_reps(sum_grad(d0, d1, d2, span, reps, m)))
    grad_qkv = qkv_grad_call(list(zip(normed, token_grads)), tok, width, reps)
    for m in micros:
        grad, terms = input_grad_call(
            token_grads[m], qkv_weight, residual[m], branch_grads[m], row(input_gain), m
        )
        input_grads.append(grad)
        input_terms.append(terms)

    qkv_total = reduce_rows(grad_qkv, order_yxz)
    model = jnp.concatenate([sum(input_terms), sum(norm_terms)], 0)
    norm_total = reduce_rows(model.T, order_yxz)
    hidden_total = reduce_rows(sum(hidden_terms).T, order_yxz)
    return (
        jnp.stack(outputs),
        jnp.stack(input_grads),
        qkv_total,
        proj_total,
        up_total,
        down_total,
        norm_total,
        hidden_total,
    )


def solution(mesh):
    tokens = P(None, ("seq", "rep"), None)
    rows = P("seq", None)
    return jax.shard_map(
        on_device,
        mesh=mesh,
        in_specs=(tokens,) + (P(),) * 12 + (tokens, P()),
        out_specs=(tokens, tokens) + (rows,) * 6,
        check_vma=False,
    )
```

```python
import functools
import math

import jax
import jax.numpy as jnp
from jax import lax
from jax.experimental import pallas as pl
from jax.experimental.pallas import tpu as pltpu
from jax.sharding import PartitionSpec as P

HEADS = 12
HD = 64
HPAD = 80
CLASS_SLOT = (0, 2, 1, 3)
LOG2E = 1.4426950408889634
NEG = -1e30
EPS = 1e-05
VMEM = 56 << 20

f32 = jnp.float32
bf16 = jnp.bfloat16


def dot_nn(a, b):
    return lax.dot_general(a, b, (((1,), (0,)), ((), ())), preferred_element_type=f32)


def dot_nt(a, b):
    return lax.dot_general(a, b, (((1,), (1,)), ((), ())), preferred_element_type=f32)


def dot_tn(a, b):
    return lax.dot_general(a, b, (((0,), (0,)), ((), ())), preferred_element_type=f32)


def class_slot(cls):
    return jnp.where(cls == 1, 2, jnp.where(cls == 2, 1, cls))


def rel_pos(shape, dim, offset, pattern):
    i = lax.broadcasted_iota(jnp.int32, shape, dim) + offset
    if pattern == 0:
        return (i % 128) * 4 + class_slot((i // 128) % 4)
    if pattern == 1:
        return (i // 256) * 512 + (i % 128) * 4 + ((i // 128) % 2) * 2
    return i


def doc_rows(len_ref, micro, start, dilation, count):
    pos = lax.broadcasted_iota(jnp.int32, (1, count), 1) * dilation + start
    edge = len_ref[micro, 0]
    doc = (pos >= edge).astype(jnp.int32)
    for n in range(1, len_ref.shape[1] - 1):
        edge = edge + len_ref[micro, n]
        doc = doc + (pos >= edge).astype(jnp.int32)
    return doc


def segment_start(pattern, span):
    team = 2**pattern
    return (lax.axis_index("seq") // team) * (team * span)


def split3(x):
    hi = x.astype(bf16).astype(f32)
    mid = (x - hi).astype(bf16).astype(f32)
    return hi, mid, x - hi - mid


def stat_rows(rows, count):
    r = lax.broadcasted_iota(jnp.int32, (HPAD - HD, count), 0)
    out = jnp.zeros((HPAD - HD, count), f32)
    for n, row in enumerate(rows):
        out = jnp.where(r == n, row, out)
    return out.astype(bf16)


def attn_fwd_body(x_ref, len_ref, o_ref, ks, qs, *, pattern, micro, span):
    groups, _, _, lanes = x_ref.shape
    count = groups * lanes
    doc = doc_rows(len_ref, micro, segment_start(pattern, span), 2**pattern, count)

    def block(c, start, size):
        return x_ref[start // lanes, c, :, start % lanes : start % lanes + size]

    kb = min(512, lanes)
    for s in range(0, count, kb):
        sl = slice(s, s + kb)
        r = lax.broadcasted_iota(jnp.int32, (HD, kb), 0)
        same = doc[:, sl] == r
        aux_k = jnp.where(same, 1.0, 0.0).astype(bf16)
        aux_q = jnp.where(same | (r >= 4), 0.0, NEG).astype(bf16)
        q = (block(0, s, kb).astype(f32) * 0.125).astype(bf16)
        qs[:, sl] = jnp.concatenate([q, aux_q], 0)
        ks[sl, :] = jnp.concatenate([block(1, s, kb), aux_k], 0).T

    qb = 256
    grain = 512 if pattern == 0 else 256

    def tiles(i):
        low = (i * qb) // grain * grain
        out = [(s, min(512, low - s), False) for s in range(0, low, 512)]
        return out + [(low, grain, True)]

    def scores(i):
        out = []
        for s, size, diagonal in tiles(i):
            t = dot_nn(ks[s : s + size, :], qs[:, i * qb : (i + 1) * qb])
            if diagonal:
                keep = rel_pos((size, qb), 0, s % 512, pattern) <= rel_pos(
                    (size, qb), 1, (i * qb) % 512, pattern
                )
                t = jnp.where(keep, t, NEG)
            out.append(t)
        return out

    following = scores(0)
    for i in range(count // qb):
        current = following
        if (i + 1) * qb < count:
            following = scores(i + 1)
        top = functools.reduce(jnp.maximum, [jnp.max(t, 0, keepdims=True) for t in current])
        top2 = top * LOG2E
        acc, total = None, None
        for t, (s, size, _) in zip(current, tiles(i)):
            p = jnp.exp2(t * LOG2E - top2)
            part = jnp.sum(p, 0, keepdims=True)
            out = dot_nn(block(2, s, size), p.astype(bf16))
            acc = out if acc is None else acc + out
            total = part if total is None else total + part
        lse = top + jnp.log(total)
        g, at = (i * qb) // lanes, (i * qb) % lanes
        o_ref[g, :HD, at : at + qb] = (acc / total).astype(bf16)
        o_ref[g, HD:, at : at + qb] = stat_rows(split3(lse), qb)


def attn_bwd_body(
    x_ref, g_ref, len_ref, o_ref, ks, vs, qs, qr, gs, gr, dq, *, pattern, micro, span
):
    groups, _, _, lanes = x_ref.shape
    count = groups * lanes
    doc = doc_rows(len_ref, micro, segment_start(pattern, span), 2**pattern, count)
    bs = min(512, lanes)

    def block(c, start, size):
        return x_ref[start // lanes, c, :, start % lanes : start % lanes + size]

    zeros = jnp.zeros((HD, bs), bf16)
    r = lax.broadcasted_iota(jnp.int32, (HD, bs), 0)
    fill = jnp.zeros((HD - 32, bs), bf16)
    for s in range(0, count, bs):
        sl = slice(s, s + bs)
        same = doc[:, sl] == r
        aux_k = jnp.where(same | ((r >= 16) & (r < 19)), 1.0, 0.0).astype(bf16)
        aux_q = jnp.where(same | (r >= 4), 0.0, NEG).astype(bf16)
        aux_v = jnp.where((r >= 19) & (r < 21), 1.0, 0.0).astype(bf16)
        q = (block(0, s, bs).astype(f32) * 0.125).astype(bf16)
        k = block(1, s, bs)
        v = block(2, s, bs)
        at = s % lanes
        g = g_ref[s // lanes, :HD, at : at + bs]
        stats = g_ref[s // lanes, HD:, at : at + bs]
        qs[:, sl] = jnp.concatenate([q, aux_q[:16], stats, fill], 0)
        gs[:, sl] = jnp.concatenate([g, zeros[:16], stats, fill], 0)
        qr[sl, :] = jnp.concatenate([q, zeros], 0).T
        gr[sl, :] = jnp.concatenate([g, zeros], 0).T
        ks[sl, :] = jnp.concatenate([k, aux_k], 0).T
        vs[sl, :] = jnp.concatenate([v, aux_v], 0).T

    keep = rel_pos((bs, bs), 0, 0, pattern) <= rel_pos((bs, bs), 1, 0, pattern)
    for j in range(count // bs):
        jl = slice(j * bs, (j + 1) * bs)
        dva, dka = None, None
        for i in range(j, count // bs):
            il = slice(i * bs, (i + 1) * bs)
            p = jnp.exp2(dot_nn(ks[jl, :], qs[:, il]) * LOG2E)
            if i == j:
                p = jnp.where(keep, p, 0.0)
            dp = dot_nn(vs[jl, :], gs[:, il])
            ds = (p * dp).astype(bf16)
            dvi = dot_nn(p.astype(bf16), gr[il, :])
            dki = dot_nn(ds, qr[il, :])
            dva = dvi if dva is None else dva + dvi
            dka = dki if dka is None else dka + dki
            dqi = dot_nn(block(1, j * bs, bs), ds) * 0.125
            if j == 0:
                dq[:, il] = dqi
            else:
                dq[:, il] += dqi
        g, at = (j * bs) // lanes, (j * bs) % lanes
        o_ref[g, 1, :, at : at + bs] = dka.T[:HD].astype(bf16)
        o_ref[g, 2, :, at : at + bs] = dva.T[:HD].astype(bf16)
        o_ref[g, 0, :, at : at + bs] = dq[:, jl].astype(bf16)


def specs_of(pattern, span, reps):
    if pattern == 0:
        return (
            3,
            pl.BlockSpec((reps, 3, HD, span // reps), lambda n: (0, 0, n, 0)),
            pl.BlockSpec((reps, None, HPAD, span // reps), lambda n: (0, n, 0, 0)),
            (reps, 3, HPAD, span // reps),
            (reps, 3, 3 * HD, span // reps),
        )
    if pattern == 1:
        return (
            2,
            pl.BlockSpec((2, None, 3, HD, span // 2), lambda n: (0, n, 0, 0, 0)),
            pl.BlockSpec((2, None, HPAD, span // 2), lambda n: (0, n, 0, 0)),
            (2, 2, HPAD, span // 2),
            (2, 2, 3, HD, span // 2),
        )
    return (
        1,
        pl.BlockSpec((4, 3, HD, span // 4), lambda n: (0, 0, 0, 0)),
        pl.BlockSpec((4, HPAD, span // 4), lambda n: (0, 0, 0)),
        (4, HPAD, span // 4),
        (4, 3, HD, span // 4),
    )


def smem_spec():
    return pl.BlockSpec(memory_space=pltpu.SMEM)


def attn_fwd(x, lengths, pattern, micro, span, reps):
    n, x_spec, o_spec, o_shape, _ = specs_of(pattern, span, reps)
    return pl.pallas_call(
        functools.partial(attn_fwd_body, pattern=pattern, micro=micro, span=span),
        grid=(n,),
        in_specs=[x_spec, smem_spec()],
        out_specs=o_spec,
        out_shape=jax.ShapeDtypeStruct(o_shape, bf16),
        scratch_shapes=[pltpu.VMEM((span, 128), bf16), pltpu.VMEM((128, span), bf16)],
        compiler_params=pltpu.CompilerParams(vmem_limit_bytes=VMEM),
        cost_estimate=pl.CostEstimate(
            flops=n * 5_000_000_000, bytes_accessed=n * 1_200_000, transcendentals=n * 2_600_000
        ),
        name=f"attn_fwd_{pattern}_{micro}",
    )(x, lengths)


def attn_bwd(x, g, lengths, pattern, micro, span, reps):
    n, x_spec, g_spec, _, d_shape = specs_of(pattern, span, reps)
    wide = pltpu.VMEM((128, span), bf16)
    tall = pltpu.VMEM((span, 128), bf16)
    return pl.pallas_call(
        functools.partial(attn_bwd_body, pattern=pattern, micro=micro, span=span),
        grid=(n,),
        in_specs=[x_spec, g_spec, smem_spec()],
        out_specs=x_spec,
        out_shape=jax.ShapeDtypeStruct(d_shape, bf16),
        scratch_shapes=[tall, tall, wide, tall, wide, tall, pltpu.VMEM((HD, span), f32)],
        compiler_params=pltpu.CompilerParams(vmem_limit_bytes=VMEM),
        cost_estimate=pl.CostEstimate(
            flops=n * 8_000_000_000, bytes_accessed=n * 2_000_000, transcendentals=n * 2_600_000
        ),
        name=f"attn_bwd_{pattern}_{micro}",
    )(x, g, lengths)


OWNER1 = {(0, 0): 0, (0, 1): 2, (1, 0): 1}
PLACE1 = {0: (0, 0), 1: (1, 0), 2: (0, 1)}


def half_of(j):
    return (3 * lax.axis_index("rep") + j) % 2


def quarter_of(j):
    return class_slot((3 * lax.axis_index("rep") + j) % 4)


def lane_slice(start, size):
    return pl.ds(pl.multiple_of(start, size), size)


def pack_qkv_body(r_ref, p1_ref, p2_ref):
    reps = r_ref.shape[0]
    for e in range(2):
        for s in range(2):
            j = OWNER1.get((e, s), 1)
            for b in range(reps):
                p1_ref[e, s, :, :, b * 256 : (b + 1) * 256] = r_ref[
                    b, :, j * HD : (j + 1) * HD, lane_slice(half_of(j) * 256, 256)
                ]
    for g in range(4):
        j = min(g, 2)
        for b in range(reps):
            p2_ref[g, :, :, b * 128 : (b + 1) * 128] = r_ref[
                b, :, j * HD : (j + 1) * HD, lane_slice(quarter_of(j) * 128, 128)
            ]


def vmem_spec():
    return pl.BlockSpec(memory_space=pltpu.VMEM)


def small_call(body, outs, args, name, nbytes, scratch=(), smem=()):
    return pl.pallas_call(
        body,
        in_specs=[smem_spec() if n in smem else vmem_spec() for n in range(len(args))],
        out_specs=[vmem_spec() for _ in outs],
        out_shape=[jax.ShapeDtypeStruct(s, d) for s, d in outs],
        scratch_shapes=list(scratch),
        compiler_params=pltpu.CompilerParams(vmem_limit_bytes=VMEM),
        cost_estimate=pl.CostEstimate(flops=1_000_000, bytes_accessed=nbytes, transcendentals=0),
        name=name,
    )(*args)


def pack_qkv(r, span, reps, micro):
    return small_call(
        pack_qkv_body,
        [((2, 2, 3, HD, span // 2), bf16), ((4, 3, HD, span // 4), bf16)],
        (r,),
        f"pack_qkv_{micro}",
        5_000_000,
    )


def mix_body(o0_ref, o1_ref, o2_ref, att_ref, mix_ref):
    reps = o0_ref.shape[0]

    def stat(tile):
        t = tile[HD:, :].astype(f32)
        return t[0:1] + t[1:2] + t[2:3]

    mix_ref[...] = jnp.zeros_like(mix_ref)
    for j in range(3):
        half, quarter = half_of(j), quarter_of(j)
        e, s = PLACE1[j]
        for b in range(reps):
            for a in range(4):
                la = slice(a * 128, (a + 1) * 128)
                t0 = o0_ref[b, j, :, la]
                lb = b * 256 + (a % 2) * 128
                t1 = o1_ref[e, s, :, lb : lb + 128]
                t2 = o2_ref[j, :, b * 128 : (b + 1) * 128]
                l0 = stat(t0)
                l1 = jnp.where(half == a // 2, stat(t1), NEG)
                l2 = jnp.where(quarter == a, stat(t2), NEG)
                top = jnp.maximum(jnp.maximum(l0, l1), l2)
                e0, e1, e2 = jnp.exp(l0 - top), jnp.exp(l1 - top), jnp.exp(l2 - top)
                total = e0 + e1 + e2
                inv = 1.0 / total
                mixed = (
                    t0[:HD].astype(f32) * (e0 * inv)
                    + t1[:HD].astype(f32) * (e1 * inv)
                    + t2[:HD].astype(f32) * (e2 * inv)
                )
                att_ref[b, j * HD : (j + 1) * HD, la] = mixed.astype(bf16)
                col = b * 512 + a * 128
                mix_ref[j : j + 1, col : col + 128] = top + jnp.log(total)


def mix(o0, o1, o2, span, reps, micro):
    return small_call(
        mix_body,
        [((reps, 3 * HD, span // reps), bf16), ((8, span), f32)],
        (o0, o1, o2),
        f"mix_{micro}",
        4_000_000,
    )


def pack_grad_body(g_ref, att_ref, mix_ref, g0_ref, p1_ref, p2_ref):
    reps, _, tok = g_ref.shape
    for j in range(3):
        rows = slice(j * HD, (j + 1) * HD)
        for b in range(reps):
            g = g_ref[b, rows, :]
            inner = jnp.sum(g.astype(f32) * att_ref[b, rows, :].astype(f32), 0, keepdims=True)
            total = mix_ref[j : j + 1, b * tok : (b + 1) * tok]
            h, m, l = split3(-total)
            ih, im, _ = split3(-inner)
            g0_ref[b, j, :HD, :] = g
            g0_ref[b, j, HD:, :] = stat_rows((h, m, l, ih, im), tok)
    for e in range(2):
        for s in range(2):
            j = OWNER1.get((e, s), 1)
            for b in range(reps):
                p1_ref[e, s, :, b * 256 : (b + 1) * 256] = g0_ref[
                    b, j, :, lane_slice(half_of(j) * 256, 256)
                ]
    for g in range(4):
        j = min(g, 2)
        for b in range(reps):
            p2_ref[g, :, b * 128 : (b + 1) * 128] = g0_ref[
                b, j, :, lane_slice(quarter_of(j) * 128, 128)
            ]


def pack_grad(g, att, mixed, span, reps, micro):
    return small_call(
        pack_grad_body,
        [
            ((reps, 3, HPAD, span // reps), bf16),
            ((2, 2, HPAD, span // 2), bf16),
            ((4, HPAD, span // 4), bf16),
        ],
        (g, att, mixed),
        f"pack_grad_{micro}",
        5_000_000,
    )


def sum_grad_body(d0_ref, d1_ref, d2_ref, out_ref):
    reps = d0_ref.shape[0]
    for j in range(3):
        rows = slice(j * HD, (j + 1) * HD)
        half, quarter = half_of(j), quarter_of(j)
        e, s = PLACE1[j]
        for b in range(reps):
            for a in range(4):
                la = slice(a * 128, (a + 1) * 128)
                lb = b * 256 + (a % 2) * 128
                t0 = d0_ref[b, :, rows, la].astype(f32)
                t1 = d1_ref[e, s, :, :, lb : lb + 128].astype(f32)
                t2 = d2_ref[j, :, :, b * 128 : (b + 1) * 128].astype(f32)
                t = t0 + jnp.where(half == a // 2, t1, 0.0) + jnp.where(quarter == a, t2, 0.0)
                out_ref[b, :, rows, la] = t.astype(bf16)


def sum_grad(d0, d1, d2, span, reps, micro):
    return small_call(
        sum_grad_body,
        [((reps, 3, 3 * HD, span // reps), bf16)],
        (d0, d1, d2),
        f"sum_grad_{micro}",
        7_000_000,
    )[0]


def onehot_rows(tok):
    i = lax.broadcasted_iota(jnp.int32, (tok, tok), 0)
    t = lax.broadcasted_iota(jnp.int32, (tok, tok), 1)
    return ((i % 128) * 4 + class_slot(i // 128) == t).astype(bf16)


def onehot_cols(tok):
    t = lax.broadcasted_iota(jnp.int32, (tok, tok), 0)
    i = lax.broadcasted_iota(jnp.int32, (tok, tok), 1)
    return ((i % 128) * 4 + class_slot(i // 128) == t).astype(bf16)


def normalize(x):
    c = x - jnp.mean(x, axis=-1, keepdims=True)
    rstd = lax.rsqrt(jnp.mean(c * c, axis=-1, keepdims=True) + EPS)
    return c * rstd, rstd


def norm_back(grad, gain, xhat, rstd):
    dn = grad * gain
    low = jnp.mean(dn, axis=-1, keepdims=True)
    along = jnp.mean(dn * xhat, axis=-1, keepdims=True)
    dx = rstd * (dn - low - xhat * along)
    return dx, jnp.sum(grad * xhat, 0, keepdims=True), jnp.sum(grad, 0, keepdims=True)


def qkv_body(x_ref, w_ref, gain_ref, bias_ref, out_ref, xp_ref, nt_ref, n_scr):
    tok, width = x_ref.shape

    @pl.when(pl.program_id(0) == 0)
    def _():
        xp = dot_nn(onehot_rows(tok), x_ref[...])
        xp_ref[...] = xp.astype(bf16)
        xhat, _ = normalize(xp)
        n = (xhat * gain_ref[...] + bias_ref[...]).astype(bf16)
        n_scr[...] = n
        nt_ref[...] = n.T

    t = dot_nn(n_scr[...], w_ref[...]).astype(bf16).T
    reps, _, cols, _ = out_ref.shape
    for r in range(reps):
        out_ref[r, 0] = t[r * cols : (r + 1) * cols]


def qkv_call(layer_in, weight, gain, bias, m, reps):
    _, tok, width = layer_in.shape
    cols = width // reps
    return pl.pallas_call(
        qkv_body,
        grid=(3,),
        in_specs=[
            pl.BlockSpec((None, tok, width), lambda c: (m, 0, 0)),
            pl.BlockSpec((width, width), lambda c: (0, c)),
            pl.BlockSpec((1, width), lambda c: (0, 0)),
            pl.BlockSpec((1, width), lambda c: (0, 0)),
        ],
        out_specs=[
            pl.BlockSpec((reps, 1, cols, tok), lambda c: (0, c, 0, 0)),
            pl.BlockSpec((tok, width), lambda c: (0, 0)),
            pl.BlockSpec((width, tok), lambda c: (0, 0)),
        ],
        out_shape=[
            jax.ShapeDtypeStruct((reps, 3, cols, tok), bf16),
            jax.ShapeDtypeStruct((tok, width), bf16),
            jax.ShapeDtypeStruct((width, tok), bf16),
        ],
        scratch_shapes=[pltpu.VMEM((tok, width), bf16)],
        compiler_params=pltpu.CompilerParams(vmem_limit_bytes=VMEM),
        cost_estimate=pl.CostEstimate(
            flops=6 * tok * width * width, bytes_accessed=9_000_000, transcendentals=0
        ),
        name=f"qkv_{m}",
    )(layer_in, weight, gain, bias)


CHUNK = 512
SQRT_HALF = 0.7071067811865476
INV_SQRT_2PI = 0.3989422804014327


def ffn_body(
    att_ref,
    xp_ref,
    cot_ref,
    wo_hbm,
    wu_hbm,
    wd_hbm,
    mg_ref,
    mb_ref,
    bg_ref,
    bb_ref,
    hg_ref,
    hb_ref,
    out_ref,
    branch_ref,
    da_ref,
    mix_ref,
    low_ref,
    hid_ref,
    dup_ref,
    brl_ref,
    cotp_ref,
    ng_ref,
    nh_ref,
    wo,
    wu,
    wd,
    g_scr,
    dg_scr,
    dn_scr,
    am_scr,
    acc_scr,
    sems,
):
    tok, width = xp_ref.shape
    hidden = hid_ref.shape[1]
    chunks = hidden // CHUNK
    reps, cols, _ = att_ref.shape
    copies = [
        pltpu.make_async_copy(a, b, sems.at[n])
        for n, (a, b) in enumerate(((wo_hbm, wo), (wu_hbm, wu), (wd_hbm, wd)))
    ]
    for c in copies:
        c.start()
    cotp = dot_nn(onehot_rows(tok), cot_ref[...])
    cotp_ref[...] = cotp.astype(bf16)
    att = att_ref[...].reshape(width, tok).T.astype(f32)
    ahat, _ = normalize(att)
    mix_ref[...] = (ahat * mg_ref[...] + mb_ref[...]).astype(bf16)
    copies[0].wait()
    am = xp_ref[...].astype(f32) + dot_nn(mix_ref[...], wo[...])
    am_scr[...] = am
    bhat, _ = normalize(am)
    low_ref[...] = (bhat * bg_ref[...] + bb_ref[...]).astype(bf16)
    copies[1].wait()

    def lanes(n):
        return pl.ds(pl.multiple_of(n * CHUNK, CHUNK), CHUNK)

    def upward(n, total):
        u = dot_nn(low_ref[...], wu[:, lanes(n)])
        cdf = 0.5 + 0.5 * lax.erf(u * SQRT_HALF)
        g = u * cdf
        g_scr[:, lanes(n)] = g
        dg_scr[:, lanes(n)] = cdf + u * (jnp.exp(u * u * -0.5) * INV_SQRT_2PI)
        return total + jnp.sum(g, 1, keepdims=True)

    mean = lax.fori_loop(0, chunks, upward, jnp.zeros((tok, 1), f32)) / hidden

    def spread(n, total):
        c = g_scr[:, lanes(n)] - mean
        return total + jnp.sum(c * c, 1, keepdims=True)

    var = lax.fori_loop(0, chunks, spread, jnp.zeros((tok, 1), f32)) / hidden
    rstd = lax.rsqrt(var + EPS)
    copies[2].wait()
    acc_scr[...] = jnp.zeros_like(acc_scr)

    def downward(n, sums):
        first, second = sums
        ghat = (g_scr[:, lanes(n)] - mean) * rstd
        g_scr[:, lanes(n)] = ghat
        gain = hg_ref[:, lanes(n)]
        h = (ghat * gain + hb_ref[:, lanes(n)]).astype(bf16)
        hid_ref[:, lanes(n)] = h
        acc_scr[...] += dot_nn(h, wd[lanes(n), :])
        back = dot_nt(cotp_ref[...], wd[lanes(n), :])
        nh_ref[0:1, lanes(n)] = jnp.sum(back * ghat, 0, keepdims=True)
        nh_ref[1:2, lanes(n)] = jnp.sum(back, 0, keepdims=True)
        dn = back * gain
        dn_scr[:, lanes(n)] = dn
        return (
            first + jnp.sum(dn, 1, keepdims=True),
            second + jnp.sum(dn * ghat, 1, keepdims=True),
        )

    zero = jnp.zeros((tok, 1), f32)
    first, second = lax.fori_loop(0, chunks, downward, (zero, zero))
    first, second = first / hidden, second / hidden
    out_ref[...] = dot_nn(onehot_cols(tok), (am_scr[...] + acc_scr[...]).astype(bf16)).astype(bf16)
    acc_scr[...] = jnp.zeros_like(acc_scr)

    def backward(n, carry):
        d = rstd * (dn_scr[:, lanes(n)] - first - g_scr[:, lanes(n)] * second)
        dup = (d * dg_scr[:, lanes(n)]).astype(bf16)
        dup_ref[:, lanes(n)] = dup
        acc_scr[...] += dot_nt(dup, wu[:, lanes(n)])
        return carry

    lax.fori_loop(0, chunks, backward, 0)
    bhat, brstd = normalize(am_scr[...])
    middle, gain_b, bias_b = norm_back(acc_scr[...], bg_ref[...], bhat, brstd)
    branch = cotp_ref[...].astype(f32) + middle
    branch_ref[...] = branch
    brl_ref[...] = branch.astype(bf16)
    att = att_ref[...].reshape(width, tok).T.astype(f32)
    ahat, arstd = normalize(att)
    da, gain_m, bias_m = norm_back(dot_nt(brl_ref[...], wo[...]), mg_ref[...], ahat, arstd)
    da_ref[...] = da.astype(bf16).T.reshape(reps, cols, tok)
    ng_ref[0:1] = gain_m
    ng_ref[1:2] = bias_m
    ng_ref[2:3] = gain_b
    ng_ref[3:4] = bias_b


def ffn_call(att, xp, output_grad, weights, gains, m):
    reps, cols, tok = att.shape
    width = xp.shape[1]
    hidden = weights[1].shape[1]
    vec = vmem_spec()
    shapes = [
        ((tok, width), bf16),
        ((tok, width), f32),
        ((reps, cols, tok), bf16),
        ((tok, width), bf16),
        ((tok, width), bf16),
        ((tok, hidden), bf16),
        ((tok, hidden), bf16),
        ((tok, width), bf16),
        ((tok, width), bf16),
        ((4, width), f32),
        ((2, hidden), f32),
    ]
    return pl.pallas_call(
        ffn_body,
        grid=(1,),
        in_specs=[
            pl.BlockSpec((reps, cols, tok), lambda n: (0, 0, 0)),
            pl.BlockSpec((tok, width), lambda n: (0, 0)),
            pl.BlockSpec((None, tok, width), lambda n: (m, 0, 0)),
        ]
        + [pl.BlockSpec(memory_space=pl.ANY)] * 3
        + [pl.BlockSpec(g.shape, lambda n: (0, 0)) for g in gains],
        out_specs=[pl.BlockSpec(s, lambda n, k=len(s): (0,) * k) for s, _ in shapes],
        out_shape=[jax.ShapeDtypeStruct(s, d) for s, d in shapes],
        scratch_shapes=[pltpu.VMEM(w.shape, bf16) for w in weights]
        + [pltpu.VMEM((tok, hidden), f32)] * 3
        + [pltpu.VMEM((tok, width), f32)] * 2
        + [pltpu.SemaphoreType.DMA((3,))],
        compiler_params=pltpu.CompilerParams(vmem_limit_bytes=VMEM),
        cost_estimate=pl.CostEstimate(
            flops=4 * tok * width * (2 * hidden + width),
            bytes_accessed=25_000_000,
            transcendentals=2 * tok * hidden,
        ),
        name=f"ffn_{m}",
    )(att, xp, output_grad, *weights, *gains)


def weight_grad_body(*refs):
    micros = (len(refs) - 6) // 6
    groups = [refs[6 * k : 6 * k + 6] for k in range(micros)]
    down_ref, up_ref, proj_ref, lt, _, _ = refs[6 * micros :]

    @pl.when(pl.program_id(0) == 0)
    def _():
        total = None
        for k, (low, dup, hid, cot, mix, brl) in enumerate(groups):
            lt[k] = low[...].T
            part = dot_tn(mix[...], brl[...])
            total = part if total is None else total + part
        proj_ref[...] = total.astype(bf16)

    up = down = None
    for k, (low, dup, hid, cot, mix, brl) in enumerate(groups):
        u = dot_nn(lt[k], dup[...])
        d = dot_tn(hid[...], cot[...])
        up = u if up is None else up + u
        down = d if down is None else down + d
    up_ref[...] = up.astype(bf16)
    down_ref[...] = down.astype(bf16)


def weight_grads(groups, tok, width, hidden):
    full = pl.BlockSpec((tok, width), lambda n: (0, 0))
    part = pl.BlockSpec((tok, CHUNK), lambda n: (0, n))
    micros = len(groups)
    return pl.pallas_call(
        weight_grad_body,
        grid=(hidden // CHUNK,),
        in_specs=[full, part, part, full, full, full] * micros,
        out_specs=[
            pl.BlockSpec((CHUNK, width), lambda n: (n, 0)),
            pl.BlockSpec((width, CHUNK), lambda n: (0, n)),
            pl.BlockSpec((width, width), lambda n: (0, 0)),
        ],
        out_shape=[
            jax.ShapeDtypeStruct((hidden, width), bf16),
            jax.ShapeDtypeStruct((width, hidden), bf16),
            jax.ShapeDtypeStruct((width, width), bf16),
        ],
        scratch_shapes=[pltpu.VMEM((micros, width, tok), bf16)]
        + [pltpu.VMEM((8, 128), f32)] * 2,
        compiler_params=pltpu.CompilerParams(vmem_limit_bytes=VMEM),
        cost_estimate=pl.CostEstimate(
            flops=2 * micros * tok * width * (2 * hidden + width),
            bytes_accessed=30_000_000,
            transcendentals=0,
        ),
        name="weight_grads",
    )(*[a for g in groups for a in g])


def join_heads(tg_ref, c):
    reps = tg_ref.shape[0]
    return jnp.concatenate([tg_ref[r, c] for r in range(reps)], 0)


def qkv_grad_body(*refs):
    micros = (len(refs) - 1) // 2
    out_ref = refs[-1]
    total = None
    for k in range(micros):
        nt, tg = refs[2 * k], refs[2 * k + 1]
        part = dot_nt(nt[...], join_heads(tg, 0))
        total = part if total is None else total + part
    out_ref[...] = total.astype(bf16)


def qkv_grad_call(pairs, tok, width, reps):
    cols = width // reps
    return pl.pallas_call(
        qkv_grad_body,
        grid=(3,),
        in_specs=[
            pl.BlockSpec((width, tok), lambda c: (0, 0)),
            pl.BlockSpec((reps, 1, cols, tok), lambda c: (0, c, 0, 0)),
        ]
        * len(pairs),
        out_specs=pl.BlockSpec((width, width), lambda c: (0, c)),
        out_shape=jax.ShapeDtypeStruct((width, 3 * width), bf16),
        compiler_params=pltpu.CompilerParams(vmem_limit_bytes=VMEM),
        cost_estimate=pl.CostEstimate(
            flops=6 * len(pairs) * tok * width * width, bytes_accessed=10_000_000, transcendentals=0
        ),
        name="qkv_grad",
    )(*[a for p in pairs for a in p])


def input_grad_body(tg_ref, w_ref, xp_ref, branch_ref, gain_ref, out_ref, ng_ref, acc):
    tok, width = xp_ref.shape
    c = pl.program_id(0)
    part = dot_nn(w_ref[...], join_heads(tg_ref, 0))

    @pl.when(c == 0)
    def _():
        acc[...] = part

    @pl.when(c > 0)
    def _():
        acc[...] += part

    @pl.when(c == 2)
    def _():
        xhat, rstd = normalize(xp_ref[...].astype(f32))
        dx, gain_i, bias_i = norm_back(acc[...].T, gain_ref[...], xhat, rstd)
        ng_ref[0:1] = gain_i
        ng_ref[1:2] = bias_i
        total = (branch_ref[...] + dx).astype(bf16)
        out_ref[...] = dot_nn(onehot_cols(tok), total).astype(bf16)


def input_grad_call(tg, weight, xp, branch, gain, m):
    reps, _, cols, tok = tg.shape
    width = reps * cols
    return pl.pallas_call(
        input_grad_body,
        grid=(3,),
        in_specs=[
            pl.BlockSpec((reps, 1, cols, tok), lambda c: (0, c, 0, 0)),
            pl.BlockSpec((width, width), lambda c: (0, c)),
            pl.BlockSpec((tok, width), lambda c: (0, 0)),
            pl.BlockSpec((tok, width), lambda c: (0, 0)),
            pl.BlockSpec((1, width), lambda c: (0, 0)),
        ],
        out_specs=[
            pl.BlockSpec((tok, width), lambda c: (0, 0)),
            pl.BlockSpec((2, width), lambda c: (0, 0)),
        ],
        out_shape=[
            jax.ShapeDtypeStruct((tok, width), bf16),
            jax.ShapeDtypeStruct((2, width), f32),
        ],
        scratch_shapes=[pltpu.VMEM((width, tok), f32)],
        compiler_params=pltpu.CompilerParams(vmem_limit_bytes=VMEM),
        cost_estimate=pl.CostEstimate(
            flops=6 * tok * width * width, bytes_accessed=10_000_000, transcendentals=0
        ),
        name=f"input_grad_{m}",
    )(tg, weight, xp, branch, gain)


def rep_peer(k):
    count = lax.axis_size("rep")
    return (lax.axis_index("rep") + k) % count


def team_place():
    return lax.axis_index("seq") % 4


def team_member(k):
    s = lax.axis_index("seq")
    return s // 4 * 4 + (s + k) % 4


def pair_partner():
    s = lax.axis_index("seq")
    return s + 1 - 2 * (s % 2)


def remote(src, dst, send_sem, recv_sem, axis, peer):
    return pltpu.make_async_remote_copy(
        src_ref=src,
        dst_ref=dst,
        send_sem=send_sem,
        recv_sem=recv_sem,
        device_id={axis: peer},
        device_id_type=pl.DeviceIdType.MESH,
    )


def meet_peers():
    barrier = pltpu.get_barrier_semaphore()
    for k in range(1, 4):
        for axis, peer in (("rep", rep_peer(k)), ("seq", team_member(k))):
            pl.semaphore_signal(
                barrier, inc=1, device_id={axis: peer}, device_id_type=pl.DeviceIdType.MESH
            )
    pl.semaphore_wait(barrier, 6)


def head_rows(j):
    return pl.ds(pl.multiple_of(j * HD, HD), HD)


def attend(block, doc, put, ks, qs, pattern, count, lanes):
    kb = min(512, lanes)
    for s in range(0, count, kb):
        sl = slice(s, s + kb)
        r = lax.broadcasted_iota(jnp.int32, (HD, kb), 0)
        same = doc[:, sl] == r
        aux_k = jnp.where(same, 1.0, 0.0).astype(bf16)
        aux_q = jnp.where(same | (r >= 4), 0.0, NEG).astype(bf16)
        q = (block(0, s, kb).astype(f32) * 0.125).astype(bf16)
        qs[:, sl] = jnp.concatenate([q, aux_q], 0)
        ks[sl, :] = jnp.concatenate([block(1, s, kb), aux_k], 0).T

    qb = 256
    grain = 512 if pattern == 0 else 256

    def tiles(i):
        low = (i * qb) // grain * grain
        out = [(s, min(512, low - s), False) for s in range(0, low, 512)]
        return out + [(low, grain, True)]

    def scores(i):
        out = []
        for s, size, diagonal in tiles(i):
            t = dot_nn(ks[s : s + size, :], qs[:, i * qb : (i + 1) * qb])
            if diagonal:
                keep = rel_pos((size, qb), 0, s % 512, pattern) <= rel_pos(
                    (size, qb), 1, (i * qb) % 512, pattern
                )
                t = jnp.where(keep, t, NEG)
            out.append(t)
        return out

    following = scores(0)
    for i in range(count // qb):
        current = following
        if (i + 1) * qb < count:
            following = scores(i + 1)
        top = functools.reduce(jnp.maximum, [jnp.max(t, 0, keepdims=True) for t in current])
        top2 = top * LOG2E
        acc, total = None, None
        for t, (s, size, _) in zip(current, tiles(i)):
            p = jnp.exp2(t * LOG2E - top2)
            part = jnp.sum(p, 0, keepdims=True)
            out = dot_nn(block(2, s, size), p.astype(bf16))
            acc = out if acc is None else acc + out
            total = part if total is None else total + part
        lse = top + jnp.log(total)
        put(i * qb, qb, (acc / total).astype(bf16), stat_rows(split3(lse), qb))


def forward_body(
    x_ref,
    w_ref,
    gain_ref,
    bias_ref,
    len_ref,
    xp_ref,
    nt_ref,
    r_out,
    p1_out,
    p2_out,
    att_ref,
    got_ref,
    mix_ref,
    sent,
    r,
    stage1,
    stage2,
    p1,
    p2,
    o0,
    o1,
    o2,
    b1,
    b2,
    ks,
    qs,
    qkv_sems,
    p1_sems,
    p2_sems,
    b1_sems,
    b2_sems,
    att_sems,
    out_sems,
):
    micros, tok, width = x_ref.shape
    reps = r.shape[1]
    span = tok * reps
    cols = width // reps
    me = lax.axis_index("rep")
    place = team_place()
    side = place % 2
    meet_peers()

    def qkv_copy(m, j, k, source):
        return remote(
            sent.at[m, rep_peer(k), :, head_rows(j)],
            r.at[m, source, :, head_rows(j)],
            qkv_sems.at[0, m, j, k - 1],
            qkv_sems.at[1, m, j, k - 1],
            "rep",
            rep_peer(k),
        )

    def p1_copy(m, s, source):
        return remote(
            stage1.at[m, s],
            p1.at[m, source, s],
            p1_sems.at[0, m, s],
            p1_sems.at[1, m, s],
            "seq",
            pair_partner(),
        )

    def p2_copy(m, k, source):
        return remote(
            stage2.at[m, (place + k) % 4],
            p2.at[m, source],
            p2_sems.at[0, m, k - 1],
            p2_sems.at[1, m, k - 1],
            "seq",
            team_member(k),
        )

    def b1_copy(m, s, source):
        return remote(
            o1.at[m, s, 1 - side],
            b1.at[m, source, s],
            b1_sems.at[0, m, s],
            b1_sems.at[1, m, s],
            "seq",
            pair_partner(),
        )

    def b2_copy(m, k, source):
        return remote(
            o2.at[m, (place + k) % 4],
            b2.at[m, source],
            b2_sems.at[0, m, k - 1],
            b2_sems.at[1, m, k - 1],
            "seq",
            team_member(k),
        )

    def att_copy(k, source):
        return remote(
            att_ref.at[0, rep_peer(k)],
            got_ref.at[source],
            att_sems.at[0, k - 1],
            att_sems.at[1, k - 1],
            "rep",
            rep_peer(k),
        )

    def out_copies(m):
        return (
            pltpu.make_async_copy(r.at[m], r_out.at[m], out_sems.at[m, 0]),
            pltpu.make_async_copy(p1.at[m], p1_out.at[m], out_sems.at[m, 1]),
            pltpu.make_async_copy(p2.at[m], p2_out.at[m], out_sems.at[m, 2]),
        )

    def project(m, carry):
        xp = dot_nn(onehot_rows(tok), x_ref[m])
        xp_ref[m] = xp.astype(bf16)
        xhat, _ = normalize(xp)
        n = (xhat * gain_ref[...] + bias_ref[...]).astype(bf16)
        nt_ref[m] = n.T
        for c in range(3):
            t = dot_nn(n, w_ref[:, c * width : (c + 1) * width]).astype(bf16).T
            for d in range(reps):
                sent[m, d, c] = t[d * cols : (d + 1) * cols]
        for j in range(3):
            for k in range(1, 4):
                qkv_copy(m, j, k, me).start()
        r[m, me] = sent[m, me]
        return carry

    lax.fori_loop(0, micros, project, 0)

    def half(j):
        return pl.ds(pl.multiple_of(((3 * me + j) % 2) * 256, 256), 256)

    def quarter_at(j):
        c = (3 * me + j) % 4
        return c % 2 * 2 + c // 2

    def quarter(j):
        return pl.ds(pl.multiple_of(quarter_at(j) * 128, 128), 128)

    def send_first(m):
        for b in range(reps):
            bl = slice(b * 256, (b + 1) * 256)
            stage1[m, 0, :, :, bl] = r[m, b, :, head_rows(1 - side), half(1 - side)]
            p1[m, side, 0, :, :, bl] = r[m, b, :, head_rows(side), half(side)]
        p1_copy(m, 0, side).start()

    def send_second(m):
        for b in range(reps):
            bl = slice(b * 256, (b + 1) * 256)
            piece = r[m, b, :, head_rows(2), half(2)]
            stage1[m, 1, :, :, bl] = piece
            p1[m, side, 1, :, :, bl] = piece
        p1_copy(m, 1, side).start()
        for g in range(4):
            j = min(g, 2)
            for b in range(reps):
                stage2[m, g, :, :, b * 128 : (b + 1) * 128] = r[m, b, :, head_rows(j), quarter(j)]
        p2[m, place] = stage2[m, place]
        for k in range(1, 4):
            p2_copy(m, k, place).start()

    def mix_all(m):
        for s in range(2):
            b1_copy(m, s, 1 - side).wait_recv()
        for k in range(1, 4):
            b2_copy(m, k, (place + 4 - k) % 4).wait_recv()

        def stat(tile):
            t = tile[HD:, :].astype(f32)
            return t[0:1] + t[1:2] + t[2:3]

        mix_ref[m] = jnp.zeros(mix_ref.shape[1:], f32)
        for j in range(3):
            e, s = PLACE1[j]
            for b in range(reps):
                for a in range(4):
                    la = slice(a * 128, (a + 1) * 128)
                    lb = b * 256 + (a % 2) * 128
                    t0 = o0[m, j, b, :, la]
                    t1 = b1[m, e, s, :, lb : lb + 128]
                    t2 = b2[m, j, :, b * 128 : (b + 1) * 128]
                    l0 = stat(t0)
                    l1 = jnp.where((3 * me + j) % 2 == a // 2, stat(t1), NEG)
                    l2 = jnp.where(quarter_at(j) == a, stat(t2), NEG)
                    top = jnp.maximum(jnp.maximum(l0, l1), l2)
                    e0, e1, e2 = jnp.exp(l0 - top), jnp.exp(l1 - top), jnp.exp(l2 - top)
                    total = e0 + e1 + e2
                    inv = 1.0 / total
                    mixed = (
                        t0[:HD].astype(f32) * (e0 * inv)
                        + t1[:HD].astype(f32) * (e1 * inv)
                        + t2[:HD].astype(f32) * (e2 * inv)
                    )
                    att_ref[m, b, j * HD : (j + 1) * HD, la] = mixed.astype(bf16)
                    col = b * tok + a * 128
                    mix_ref[m, j : j + 1, col : col + 128] = top + jnp.log(total)

    docs_of = lambda m, pattern: doc_rows(
        len_ref, m, segment_start(pattern, span), 2**pattern, span
    )

    def micro(m, carry):
        def local(j, inner):
            for k in range(1, 4):
                qkv_copy(m, j, k, (me + reps - k) % reps).wait_recv()

            @pl.when(j == 1)
            def _():
                send_first(m)

            @pl.when(j == 2)
            def _():
                send_second(m)

            def block(c, start, size):
                at = start % tok
                return r[m, start // tok, c, head_rows(j), at : at + size]

            def put(start, size, out, stats):
                at = start % tok
                o0[m, j, start // tok, :HD, at : at + size] = out
                o0[m, j, start // tok, HD:, at : at + size] = stats

            attend(block, docs_of(m, 0), put, ks, qs, 0, span, tok)
            return inner

        lax.fori_loop(0, 3, local, 0)

        @pl.when(m == 1)
        def _():
            mix_all(0)
            for k in range(1, 4):
                att_copy(k, me).start()
            got_ref[me] = att_ref[0, me]

        def paired(s, inner):
            p1_copy(m, s, 1 - side).wait_recv()
            wide = span // 2

            def block(c, start, size):
                at = start % wide
                return p1[m, start // wide, s, c, :, at : at + size]

            def put(start, size, out, stats):
                at = start % wide
                o1[m, s, start // wide, :HD, at : at + size] = out
                o1[m, s, start // wide, HD:, at : at + size] = stats

            attend(block, docs_of(m, 1), put, ks, qs, 1, span, wide)
            b1[m, side, s] = o1[m, s, side]
            b1_copy(m, s, side).start()
            return inner

        lax.fori_loop(0, 2, paired, 0)
        for k in range(1, 4):
            p2_copy(m, k, (place + 4 - k) % 4).wait_recv()

        def block(c, start, size):
            at = start % tok
            return p2[m, start // tok, c, :, at : at + size]

        def put(start, size, out, stats):
            at = start % tok
            o2[m, start // tok, :HD, at : at + size] = out
            o2[m, start // tok, HD:, at : at + size] = stats

        attend(block, docs_of(m, 2), put, ks, qs, 2, span, tok)
        b2[m, place] = o2[m, place]
        for k in range(1, 4):
            b2_copy(m, k, place).start()
        for c in out_copies(m):
            c.start()
        return carry

    lax.fori_loop(0, micros, micro, 0)
    mix_all(1)
    for k in range(1, 4):
        att_copy(k, (me + reps - k) % reps).wait_recv()
        att_copy(k, me).wait_send()

    def finish(m, carry):
        for c in out_copies(m):
            c.wait()
        for k in range(1, 4):
            for j in range(3):
                qkv_copy(m, j, k, me).wait_send()
            p2_copy(m, k, place).wait_send()
            b2_copy(m, k, place).wait_send()
        for s in range(2):
            p1_copy(m, s, side).wait_send()
            b1_copy(m, s, side).wait_send()
        return carry

    lax.fori_loop(0, micros, finish, 0)


def forward_call(layer_in, weight, gain, bias, lengths, reps):
    micros, tok, width = layer_in.shape
    span, cols = tok * reps, width // reps
    any_spec = pl.BlockSpec(memory_space=pl.ANY)
    outs = [
        ((micros, tok, width), bf16, vmem_spec()),
        ((micros, width, tok), bf16, vmem_spec()),
        ((micros, reps, 3, cols, tok), bf16, any_spec),
        ((micros, 2, 2, 3, HD, span // 2), bf16, any_spec),
        ((micros, 4, 3, HD, span // 4), bf16, any_spec),
        ((micros, reps, cols, tok), bf16, vmem_spec()),
        ((reps, cols, tok), bf16, vmem_spec()),
        ((micros, 8, span), f32, vmem_spec()),
    ]

    def vm(*shape):
        return pltpu.VMEM(shape, bf16)

    dma = pltpu.SemaphoreType.DMA
    return pl.pallas_call(
        forward_body,
        in_specs=[vmem_spec()] * 4 + [smem_spec()],
        out_specs=[o[2] for o in outs],
        out_shape=[jax.ShapeDtypeStruct(o[0], o[1]) for o in outs],
        scratch_shapes=[
            vm(micros, reps, 3, cols, tok),
            vm(micros, reps, 3, cols, tok),
            vm(micros, 2, 3, HD, span // 2),
            vm(micros, 4, 3, HD, span // 4),
            vm(micros, 2, 2, 3, HD, span // 2),
            vm(micros, 4, 3, HD, span // 4),
            vm(micros, 3, reps, HPAD, tok),
            vm(micros, 2, 2, HPAD, span // 2),
            vm(micros, 4, HPAD, span // 4),
            vm(micros, 2, 2, HPAD, span // 2),
            vm(micros, 4, HPAD, span // 4),
            vm(span, 128),
            vm(128, span),
            dma((2, micros, 3, 3)),
            dma((2, micros, 2)),
            dma((2, micros, 3)),
            dma((2, micros, 2)),
            dma((2, micros, 3)),
            dma((2, 3)),
            dma((micros, 3)),
        ],
        compiler_params=pltpu.CompilerParams(
            vmem_limit_bytes=VMEM, collective_id=1, has_side_effects=True
        ),
        cost_estimate=pl.CostEstimate(
            flops=60_000_000_000, bytes_accessed=30_000_000, transcendentals=30_000_000
        ),
        name="forward",
    )(layer_in, weight, gain, bias, lengths)


def swap(block, axis, bit):
    count = lax.axis_size(axis)
    return lax.ppermute(block, axis, [(n, n ^ (1 << bit)) for n in range(count)])


def bits_of(count):
    return count.bit_length() - 1


def reduce_rows(x, order):
    seqs, reps = lax.axis_size("seq"), lax.axis_size("rep")
    rows, cols = x.shape
    sb, rb = bits_of(seqs), bits_of(reps)
    y = x.reshape((2,) * (sb + rb) + (rows // (seqs * reps), cols))
    names = [("seq", b) for b in reversed(range(sb))] + [("rep", b) for b in reversed(range(rb))]
    for step in order(sb, rb):
        at = names.index(step)
        axis, bit = step
        mine = (lax.axis_index(axis) >> bit) & 1
        send = lax.dynamic_index_in_dim(y, 1 - mine, at, keepdims=False)
        keep = lax.dynamic_index_in_dim(y, mine, at, keepdims=False)
        got = swap(send.astype(x.dtype), axis, bit)
        y = (keep.astype(f32) + got.astype(f32)).astype(x.dtype)
        names.pop(at)
    for bit in range(rb):
        other = swap(y, "rep", bit)
        mine = (lax.axis_index("rep") >> bit) & 1
        y = jnp.where(mine == 0, jnp.stack([y, other]), jnp.stack([other, y]))
        y = y.reshape((-1,) + y.shape[2:])
    return y.astype(f32)


def order_yxz(sb, rb):
    return [("rep", b) for b in range(rb)] + [("seq", b) for b in range(sb)]


def order_xzy(sb, rb):
    return [("rep", 0)] + [("seq", b) for b in range(sb)] + [("rep", b) for b in range(1, rb)]


def on_device(
    layer_in,
    qkv_weight,
    out_weight,
    up_weight,
    down_weight,
    input_gain,
    input_bias,
    mixer_gain,
    mixer_bias,
    block_gain,
    block_bias,
    hidden_gain,
    hidden_bias,
    output_grad,
    seq_lengths,
):
    micro_count, tok, width = layer_in.shape
    reps = lax.axis_size("rep")
    seqs = lax.axis_size("seq")
    span = tok * reps
    heads_dev = HEADS // reps
    cols = heads_dev * HD
    pairs = [[2 * n, 2 * n + 1] for n in range(seqs // 2)]
    fours = [[4 * n + k for k in range(4)] for n in range(seqs // 4)]

    def to_reps(x):
        return lax.all_to_all(x, "rep", 0, 0, tiled=True)

    def to_pair(x):
        return lax.all_to_all(x, "seq", 0, 0, tiled=True, axis_index_groups=pairs)

    def to_four(x):
        return lax.all_to_all(x, "seq", 0, 0, tiled=True, axis_index_groups=fours)

    def row(v):
        return v.reshape(1, -1)

    micros = range(micro_count)
    xp, nt, got_qkv, got_pair, got_four, own_att, got_att, totals = forward_call(
        layer_in, qkv_weight, row(input_gain), row(input_bias), seq_lengths, reps
    )
    residual = [xp[m] for m in micros]
    normed = [nt[m] for m in micros]
    pieces = [(got_qkv[m], got_pair[m], got_four[m]) for m in micros]
    attended = [got_att, to_reps(own_att[1])]

    outputs, branch_grads, head_grads, groups, norm_terms, hidden_terms = [], [], [], [], [], []
    weights = (out_weight, up_weight, down_weight)
    gains = tuple(
        row(v) for v in (mixer_gain, mixer_bias, block_gain, block_bias, hidden_gain, hidden_bias)
    )
    for m in micros:
        out, branch, da, mixl, low, hid, dup, brl, cotp, ng, nh = ffn_call(
            attended[m], residual[m], output_grad, weights, gains, m
        )
        outputs.append(out)
        branch_grads.append(branch)
        head_grads.append(to_reps(da))
        groups.append((low, dup, hid, cotp, mixl, brl))
        norm_terms.append(ng)
        hidden_terms.append(nh)
    grad_down, grad_up, grad_proj = weight_grads(groups, tok, width, up_weight.shape[1])

    down_total = reduce_rows(grad_down, order_yxz)
    up_total = reduce_rows(grad_up, order_xzy)
    proj_total = reduce_rows(grad_proj, order_xzy)

    input_grads, input_terms, token_grads = [], [], []
    for m in micros:
        g0, g1, g2 = pack_grad(head_grads[m], own_att[m], totals[m], span, reps, m)
        g1, g2 = to_pair(g1), to_four(g2)
        x0, x1, x2 = pieces[m]
        d0 = attn_bwd(x0, g0, seq_lengths, 0, m, span, reps)
        d1 = to_pair(attn_bwd(x1, g1, seq_lengths, 1, m, span, reps))
        d2 = to_four(attn_bwd(x2, g2, seq_lengths, 2, m, span, reps))
        token_grads.append(to_reps(sum_grad(d0, d1, d2, span, reps, m)))
    grad_qkv = qkv_grad_call(list(zip(normed, token_grads)), tok, width, reps)
    for m in micros:
        grad, terms = input_grad_call(
            token_grads[m], qkv_weight, residual[m], branch_grads[m], row(input_gain), m
        )
        input_grads.append(grad)
        input_terms.append(terms)

    qkv_total = reduce_rows(grad_qkv, order_yxz)
    model = jnp.concatenate([sum(input_terms), sum(norm_terms)], 0)
    norm_total = reduce_rows(model.T, order_yxz)
    hidden_total = reduce_rows(sum(hidden_terms).T, order_yxz)
    return (
        jnp.stack(outputs),
        jnp.stack(input_grads),
        qkv_total,
        proj_total,
        up_total,
        down_total,
        norm_total,
        hidden_total,
    )


def solution(mesh):
    tokens = P(None, ("seq", "rep"), None)
    rows = P("seq", None)
    return jax.shard_map(
        on_device,
        mesh=mesh,
        in_specs=(tokens,) + (P(),) * 12 + (tokens, P()),
        out_specs=(tokens, tokens) + (rows,) * 6,
        check_vma=False,
    )
```

```python
import functools
import math

import jax
import jax.numpy as jnp
from jax import lax
from jax.experimental import pallas as pl
from jax.experimental.pallas import tpu as pltpu
from jax.sharding import PartitionSpec as P

HEADS = 12
HD = 64
HPAD = 80
CLASS_SLOT = (0, 2, 1, 3)
LOG2E = 1.4426950408889634
NEG = -1e30
EPS = 1e-05
VMEM = 56 << 20

f32 = jnp.float32
bf16 = jnp.bfloat16


def dot_nn(a, b):
    return lax.dot_general(a, b, (((1,), (0,)), ((), ())), preferred_element_type=f32)


def dot_nt(a, b):
    return lax.dot_general(a, b, (((1,), (1,)), ((), ())), preferred_element_type=f32)


def dot_tn(a, b):
    return lax.dot_general(a, b, (((0,), (0,)), ((), ())), preferred_element_type=f32)


def class_slot(cls):
    return jnp.where(cls == 1, 2, jnp.where(cls == 2, 1, cls))


def rel_pos(shape, dim, offset, pattern):
    i = lax.broadcasted_iota(jnp.int32, shape, dim) + offset
    if pattern == 0:
        return (i % 128) * 4 + class_slot((i // 128) % 4)
    if pattern == 1:
        return (i // 256) * 512 + (i % 128) * 4 + ((i // 128) % 2) * 2
    return i


def doc_rows(len_ref, micro, start, dilation, count):
    pos = lax.broadcasted_iota(jnp.int32, (1, count), 1) * dilation + start
    edge = len_ref[micro, 0]
    doc = (pos >= edge).astype(jnp.int32)
    for n in range(1, len_ref.shape[1] - 1):
        edge = edge + len_ref[micro, n]
        doc = doc + (pos >= edge).astype(jnp.int32)
    return doc


def segment_start(pattern, span):
    team = 2**pattern
    return (lax.axis_index("seq") // team) * (team * span)


def split3(x):
    hi = x.astype(bf16).astype(f32)
    mid = (x - hi).astype(bf16).astype(f32)
    return hi, mid, x - hi - mid


def stat_rows(rows, count):
    r = lax.broadcasted_iota(jnp.int32, (HPAD - HD, count), 0)
    out = jnp.zeros((HPAD - HD, count), f32)
    for n, row in enumerate(rows):
        out = jnp.where(r == n, row, out)
    return out.astype(bf16)


def attn_fwd_body(x_ref, len_ref, o_ref, ks, qs, *, pattern, micro, span):
    groups, _, _, lanes = x_ref.shape
    count = groups * lanes
    doc = doc_rows(len_ref, micro, segment_start(pattern, span), 2**pattern, count)

    def block(c, start, size):
        return x_ref[start // lanes, c, :, start % lanes : start % lanes + size]

    kb = min(512, lanes)
    for s in range(0, count, kb):
        sl = slice(s, s + kb)
        r = lax.broadcasted_iota(jnp.int32, (HD, kb), 0)
        same = doc[:, sl] == r
        aux_k = jnp.where(same, 1.0, 0.0).astype(bf16)
        aux_q = jnp.where(same | (r >= 4), 0.0, NEG).astype(bf16)
        q = (block(0, s, kb).astype(f32) * 0.125).astype(bf16)
        qs[:, sl] = jnp.concatenate([q, aux_q], 0)
        ks[sl, :] = jnp.concatenate([block(1, s, kb), aux_k], 0).T

    qb = 256
    grain = 512 if pattern == 0 else 256

    def tiles(i):
        low = (i * qb) // grain * grain
        out = [(s, min(512, low - s), False) for s in range(0, low, 512)]
        return out + [(low, grain, True)]

    def scores(i):
        out = []
        for s, size, diagonal in tiles(i):
            t = dot_nn(ks[s : s + size, :], qs[:, i * qb : (i + 1) * qb])
            if diagonal:
                keep = rel_pos((size, qb), 0, s % 512, pattern) <= rel_pos(
                    (size, qb), 1, (i * qb) % 512, pattern
                )
                t = jnp.where(keep, t, NEG)
            out.append(t)
        return out

    following = scores(0)
    for i in range(count // qb):
        current = following
        if (i + 1) * qb < count:
            following = scores(i + 1)
        top = functools.reduce(jnp.maximum, [jnp.max(t, 0, keepdims=True) for t in current])
        top2 = top * LOG2E
        acc, total = None, None
        for t, (s, size, _) in zip(current, tiles(i)):
            p = jnp.exp2(t * LOG2E - top2)
            part = jnp.sum(p, 0, keepdims=True)
            out = dot_nn(block(2, s, size), p.astype(bf16))
            acc = out if acc is None else acc + out
            total = part if total is None else total + part
        lse = top + jnp.log(total)
        g, at = (i * qb) // lanes, (i * qb) % lanes
        o_ref[g, :HD, at : at + qb] = (acc / total).astype(bf16)
        o_ref[g, HD:, at : at + qb] = stat_rows(split3(lse), qb)


def attn_bwd_body(
    x_ref, g_ref, len_ref, o_ref, ks, vs, qs, qr, gs, gr, dq, *, pattern, micro, span
):
    groups, _, _, lanes = x_ref.shape
    count = groups * lanes
    doc = doc_rows(len_ref, micro, segment_start(pattern, span), 2**pattern, count)
    bs = min(512, lanes)

    def block(c, start, size):
        return x_ref[start // lanes, c, :, start % lanes : start % lanes + size]

    zeros = jnp.zeros((HD, bs), bf16)
    r = lax.broadcasted_iota(jnp.int32, (HD, bs), 0)
    fill = jnp.zeros((HD - 32, bs), bf16)
    for s in range(0, count, bs):
        sl = slice(s, s + bs)
        same = doc[:, sl] == r
        aux_k = jnp.where(same | ((r >= 16) & (r < 19)), 1.0, 0.0).astype(bf16)
        aux_q = jnp.where(same | (r >= 4), 0.0, NEG).astype(bf16)
        aux_v = jnp.where((r >= 19) & (r < 21), 1.0, 0.0).astype(bf16)
        q = (block(0, s, bs).astype(f32) * 0.125).astype(bf16)
        k = block(1, s, bs)
        v = block(2, s, bs)
        at = s % lanes
        g = g_ref[s // lanes, :HD, at : at + bs]
        stats = g_ref[s // lanes, HD:, at : at + bs]
        qs[:, sl] = jnp.concatenate([q, aux_q[:16], stats, fill], 0)
        gs[:, sl] = jnp.concatenate([g, zeros[:16], stats, fill], 0)
        qr[sl, :] = jnp.concatenate([q, zeros], 0).T
        gr[sl, :] = jnp.concatenate([g, zeros], 0).T
        ks[sl, :] = jnp.concatenate([k, aux_k], 0).T
        vs[sl, :] = jnp.concatenate([v, aux_v], 0).T

    keep = rel_pos((bs, bs), 0, 0, pattern) <= rel_pos((bs, bs), 1, 0, pattern)
    for j in range(count // bs):
        jl = slice(j * bs, (j + 1) * bs)
        dva, dka = None, None
        for i in range(j, count // bs):
            il = slice(i * bs, (i + 1) * bs)
            p = jnp.exp2(dot_nn(ks[jl, :], qs[:, il]) * LOG2E)
            if i == j:
                p = jnp.where(keep, p, 0.0)
            dp = dot_nn(vs[jl, :], gs[:, il])
            ds = (p * dp).astype(bf16)
            dvi = dot_nn(p.astype(bf16), gr[il, :])
            dki = dot_nn(ds, qr[il, :])
            dva = dvi if dva is None else dva + dvi
            dka = dki if dka is None else dka + dki
            dqi = dot_nn(block(1, j * bs, bs), ds) * 0.125
            if j == 0:
                dq[:, il] = dqi
            else:
                dq[:, il] += dqi
        g, at = (j * bs) // lanes, (j * bs) % lanes
        o_ref[g, 1, :, at : at + bs] = dka.T[:HD].astype(bf16)
        o_ref[g, 2, :, at : at + bs] = dva.T[:HD].astype(bf16)
        o_ref[g, 0, :, at : at + bs] = dq[:, jl].astype(bf16)


def specs_of(pattern, span, reps):
    if pattern == 0:
        return (
            3,
            pl.BlockSpec((reps, 3, HD, span // reps), lambda n: (0, 0, n, 0)),
            pl.BlockSpec((reps, None, HPAD, span // reps), lambda n: (0, n, 0, 0)),
            (reps, 3, HPAD, span // reps),
            (reps, 3, 3 * HD, span // reps),
        )
    if pattern == 1:
        return (
            2,
            pl.BlockSpec((2, None, 3, HD, span // 2), lambda n: (0, n, 0, 0, 0)),
            pl.BlockSpec((2, None, HPAD, span // 2), lambda n: (0, n, 0, 0)),
            (2, 2, HPAD, span // 2),
            (2, 2, 3, HD, span // 2),
        )
    return (
        1,
        pl.BlockSpec((4, 3, HD, span // 4), lambda n: (0, 0, 0, 0)),
        pl.BlockSpec((4, HPAD, span // 4), lambda n: (0, 0, 0)),
        (4, HPAD, span // 4),
        (4, 3, HD, span // 4),
    )


def smem_spec():
    return pl.BlockSpec(memory_space=pltpu.SMEM)


def attn_fwd(x, lengths, pattern, micro, span, reps):
    n, x_spec, o_spec, o_shape, _ = specs_of(pattern, span, reps)
    return pl.pallas_call(
        functools.partial(attn_fwd_body, pattern=pattern, micro=micro, span=span),
        grid=(n,),
        in_specs=[x_spec, smem_spec()],
        out_specs=o_spec,
        out_shape=jax.ShapeDtypeStruct(o_shape, bf16),
        scratch_shapes=[pltpu.VMEM((span, 128), bf16), pltpu.VMEM((128, span), bf16)],
        compiler_params=pltpu.CompilerParams(vmem_limit_bytes=VMEM),
        cost_estimate=pl.CostEstimate(
            flops=n * 5_000_000_000, bytes_accessed=n * 1_200_000, transcendentals=n * 2_600_000
        ),
        name=f"attn_fwd_{pattern}_{micro}",
    )(x, lengths)


def attn_bwd(x, g, lengths, pattern, micro, span, reps):
    n, x_spec, g_spec, _, d_shape = specs_of(pattern, span, reps)
    wide = pltpu.VMEM((128, span), bf16)
    tall = pltpu.VMEM((span, 128), bf16)
    return pl.pallas_call(
        functools.partial(attn_bwd_body, pattern=pattern, micro=micro, span=span),
        grid=(n,),
        in_specs=[x_spec, g_spec, smem_spec()],
        out_specs=x_spec,
        out_shape=jax.ShapeDtypeStruct(d_shape, bf16),
        scratch_shapes=[tall, tall, wide, tall, wide, tall, pltpu.VMEM((HD, span), f32)],
        compiler_params=pltpu.CompilerParams(vmem_limit_bytes=VMEM),
        cost_estimate=pl.CostEstimate(
            flops=n * 8_000_000_000, bytes_accessed=n * 2_000_000, transcendentals=n * 2_600_000
        ),
        name=f"attn_bwd_{pattern}_{micro}",
    )(x, g, lengths)


OWNER1 = {(0, 0): 0, (0, 1): 2, (1, 0): 1}
PLACE1 = {0: (0, 0), 1: (1, 0), 2: (0, 1)}


def half_of(j):
    return (3 * lax.axis_index("rep") + j) % 2


def quarter_of(j):
    return class_slot((3 * lax.axis_index("rep") + j) % 4)


def lane_slice(start, size):
    return pl.ds(pl.multiple_of(start, size), size)


def pack_qkv_body(r_ref, p1_ref, p2_ref):
    reps = r_ref.shape[0]
    for e in range(2):
        for s in range(2):
            j = OWNER1.get((e, s), 1)
            for b in range(reps):
                p1_ref[e, s, :, :, b * 256 : (b + 1) * 256] = r_ref[
                    b, :, j * HD : (j + 1) * HD, lane_slice(half_of(j) * 256, 256)
                ]
    for g in range(4):
        j = min(g, 2)
        for b in range(reps):
            p2_ref[g, :, :, b * 128 : (b + 1) * 128] = r_ref[
                b, :, j * HD : (j + 1) * HD, lane_slice(quarter_of(j) * 128, 128)
            ]


def vmem_spec():
    return pl.BlockSpec(memory_space=pltpu.VMEM)


def small_call(body, outs, args, name, nbytes, scratch=(), smem=()):
    return pl.pallas_call(
        body,
        in_specs=[smem_spec() if n in smem else vmem_spec() for n in range(len(args))],
        out_specs=[vmem_spec() for _ in outs],
        out_shape=[jax.ShapeDtypeStruct(s, d) for s, d in outs],
        scratch_shapes=list(scratch),
        compiler_params=pltpu.CompilerParams(vmem_limit_bytes=VMEM),
        cost_estimate=pl.CostEstimate(flops=1_000_000, bytes_accessed=nbytes, transcendentals=0),
        name=name,
    )(*args)


def pack_qkv(r, span, reps, micro):
    return small_call(
        pack_qkv_body,
        [((2, 2, 3, HD, span // 2), bf16), ((4, 3, HD, span // 4), bf16)],
        (r,),
        f"pack_qkv_{micro}",
        5_000_000,
    )


def mix_body(o0_ref, o1_ref, o2_ref, att_ref, mix_ref):
    reps = o0_ref.shape[0]

    def stat(tile):
        t = tile[HD:, :].astype(f32)
        return t[0:1] + t[1:2] + t[2:3]

    mix_ref[...] = jnp.zeros_like(mix_ref)
    for j in range(3):
        half, quarter = half_of(j), quarter_of(j)
        e, s = PLACE1[j]
        for b in range(reps):
            for a in range(4):
                la = slice(a * 128, (a + 1) * 128)
                t0 = o0_ref[b, j, :, la]
                lb = b * 256 + (a % 2) * 128
                t1 = o1_ref[e, s, :, lb : lb + 128]
                t2 = o2_ref[j, :, b * 128 : (b + 1) * 128]
                l0 = stat(t0)
                l1 = jnp.where(half == a // 2, stat(t1), NEG)
                l2 = jnp.where(quarter == a, stat(t2), NEG)
                top = jnp.maximum(jnp.maximum(l0, l1), l2)
                e0, e1, e2 = jnp.exp(l0 - top), jnp.exp(l1 - top), jnp.exp(l2 - top)
                total = e0 + e1 + e2
                inv = 1.0 / total
                mixed = (
                    t0[:HD].astype(f32) * (e0 * inv)
                    + t1[:HD].astype(f32) * (e1 * inv)
                    + t2[:HD].astype(f32) * (e2 * inv)
                )
                att_ref[b, j * HD : (j + 1) * HD, la] = mixed.astype(bf16)
                col = b * 512 + a * 128
                mix_ref[j : j + 1, col : col + 128] = top + jnp.log(total)


def mix(o0, o1, o2, span, reps, micro):
    return small_call(
        mix_body,
        [((reps, 3 * HD, span // reps), bf16), ((8, span), f32)],
        (o0, o1, o2),
        f"mix_{micro}",
        4_000_000,
    )


def pack_grad_body(g_ref, att_ref, mix_ref, g0_ref, p1_ref, p2_ref):
    reps, _, tok = g_ref.shape
    for j in range(3):
        rows = slice(j * HD, (j + 1) * HD)
        for b in range(reps):
            g = g_ref[b, rows, :]
            inner = jnp.sum(g.astype(f32) * att_ref[b, rows, :].astype(f32), 0, keepdims=True)
            total = mix_ref[j : j + 1, b * tok : (b + 1) * tok]
            h, m, l = split3(-total)
            ih, im, _ = split3(-inner)
            g0_ref[b, j, :HD, :] = g
            g0_ref[b, j, HD:, :] = stat_rows((h, m, l, ih, im), tok)
    for e in range(2):
        for s in range(2):
            j = OWNER1.get((e, s), 1)
            for b in range(reps):
                p1_ref[e, s, :, b * 256 : (b + 1) * 256] = g0_ref[
                    b, j, :, lane_slice(half_of(j) * 256, 256)
                ]
    for g in range(4):
        j = min(g, 2)
        for b in range(reps):
            p2_ref[g, :, b * 128 : (b + 1) * 128] = g0_ref[
                b, j, :, lane_slice(quarter_of(j) * 128, 128)
            ]


def pack_grad(g, att, mixed, span, reps, micro):
    return small_call(
        pack_grad_body,
        [
            ((reps, 3, HPAD, span // reps), bf16),
            ((2, 2, HPAD, span // 2), bf16),
            ((4, HPAD, span // 4), bf16),
        ],
        (g, att, mixed),
        f"pack_grad_{micro}",
        5_000_000,
    )


def sum_grad_body(d0_ref, d1_ref, d2_ref, out_ref):
    reps = d0_ref.shape[0]
    for j in range(3):
        rows = slice(j * HD, (j + 1) * HD)
        half, quarter = half_of(j), quarter_of(j)
        e, s = PLACE1[j]
        for b in range(reps):
            for a in range(4):
                la = slice(a * 128, (a + 1) * 128)
                lb = b * 256 + (a % 2) * 128
                t0 = d0_ref[b, :, rows, la].astype(f32)
                t1 = d1_ref[e, s, :, :, lb : lb + 128].astype(f32)
                t2 = d2_ref[j, :, :, b * 128 : (b + 1) * 128].astype(f32)
                t = t0 + jnp.where(half == a // 2, t1, 0.0) + jnp.where(quarter == a, t2, 0.0)
                out_ref[b, :, rows, la] = t.astype(bf16)


def sum_grad(d0, d1, d2, span, reps, micro):
    return small_call(
        sum_grad_body,
        [((reps, 3, 3 * HD, span // reps), bf16)],
        (d0, d1, d2),
        f"sum_grad_{micro}",
        7_000_000,
    )[0]


def onehot_rows(tok):
    i = lax.broadcasted_iota(jnp.int32, (tok, tok), 0)
    t = lax.broadcasted_iota(jnp.int32, (tok, tok), 1)
    return ((i % 128) * 4 + class_slot(i // 128) == t).astype(bf16)


def onehot_cols(tok):
    t = lax.broadcasted_iota(jnp.int32, (tok, tok), 0)
    i = lax.broadcasted_iota(jnp.int32, (tok, tok), 1)
    return ((i % 128) * 4 + class_slot(i // 128) == t).astype(bf16)


def normalize(x):
    c = x - jnp.mean(x, axis=-1, keepdims=True)
    rstd = lax.rsqrt(jnp.mean(c * c, axis=-1, keepdims=True) + EPS)
    return c * rstd, rstd


def norm_back(grad, gain, xhat, rstd):
    dn = grad * gain
    low = jnp.mean(dn, axis=-1, keepdims=True)
    along = jnp.mean(dn * xhat, axis=-1, keepdims=True)
    dx = rstd * (dn - low - xhat * along)
    return dx, jnp.sum(grad * xhat, 0, keepdims=True), jnp.sum(grad, 0, keepdims=True)


def qkv_body(x_ref, w_ref, gain_ref, bias_ref, out_ref, xp_ref, nt_ref, n_scr):
    tok, width = x_ref.shape

    @pl.when(pl.program_id(0) == 0)
    def _():
        xp = dot_nn(onehot_rows(tok), x_ref[...])
        xp_ref[...] = xp.astype(bf16)
        xhat, _ = normalize(xp)
        n = (xhat * gain_ref[...] + bias_ref[...]).astype(bf16)
        n_scr[...] = n
        nt_ref[...] = n.T

    t = dot_nn(n_scr[...], w_ref[...]).astype(bf16).T
    reps, _, cols, _ = out_ref.shape
    for r in range(reps):
        out_ref[r, 0] = t[r * cols : (r + 1) * cols]


def qkv_call(layer_in, weight, gain, bias, m, reps):
    _, tok, width = layer_in.shape
    cols = width // reps
    return pl.pallas_call(
        qkv_body,
        grid=(3,),
        in_specs=[
            pl.BlockSpec((None, tok, width), lambda c: (m, 0, 0)),
            pl.BlockSpec((width, width), lambda c: (0, c)),
            pl.BlockSpec((1, width), lambda c: (0, 0)),
            pl.BlockSpec((1, width), lambda c: (0, 0)),
        ],
        out_specs=[
            pl.BlockSpec((reps, 1, cols, tok), lambda c: (0, c, 0, 0)),
            pl.BlockSpec((tok, width), lambda c: (0, 0)),
            pl.BlockSpec((width, tok), lambda c: (0, 0)),
        ],
        out_shape=[
            jax.ShapeDtypeStruct((reps, 3, cols, tok), bf16),
            jax.ShapeDtypeStruct((tok, width), bf16),
            jax.ShapeDtypeStruct((width, tok), bf16),
        ],
        scratch_shapes=[pltpu.VMEM((tok, width), bf16)],
        compiler_params=pltpu.CompilerParams(vmem_limit_bytes=VMEM),
        cost_estimate=pl.CostEstimate(
            flops=6 * tok * width * width, bytes_accessed=9_000_000, transcendentals=0
        ),
        name=f"qkv_{m}",
    )(layer_in, weight, gain, bias)


CHUNK = 512
SQRT_HALF = 0.7071067811865476
INV_SQRT_2PI = 0.3989422804014327


def ffn_body(
    att_ref,
    xp_ref,
    cot_ref,
    wo_hbm,
    wu_hbm,
    wd_hbm,
    mg_ref,
    mb_ref,
    bg_ref,
    bb_ref,
    hg_ref,
    hb_ref,
    out_ref,
    branch_ref,
    da_ref,
    mix_ref,
    low_ref,
    hid_ref,
    dup_ref,
    brl_ref,
    cotp_ref,
    ng_ref,
    nh_ref,
    wo,
    wu,
    wd,
    g_scr,
    dg_scr,
    dn_scr,
    am_scr,
    acc_scr,
    sems,
):
    tok, width = xp_ref.shape
    hidden = hid_ref.shape[1]
    chunks = hidden // CHUNK
    reps, cols, _ = att_ref.shape
    copies = [
        pltpu.make_async_copy(a, b, sems.at[n])
        for n, (a, b) in enumerate(((wo_hbm, wo), (wu_hbm, wu), (wd_hbm, wd)))
    ]
    for c in copies:
        c.start()
    cotp = dot_nn(onehot_rows(tok), cot_ref[...])
    cotp_ref[...] = cotp.astype(bf16)
    att = att_ref[...].reshape(width, tok).T.astype(f32)
    ahat, _ = normalize(att)
    mix_ref[...] = (ahat * mg_ref[...] + mb_ref[...]).astype(bf16)
    copies[0].wait()
    am = xp_ref[...].astype(f32) + dot_nn(mix_ref[...], wo[...])
    am_scr[...] = am
    bhat, _ = normalize(am)
    low_ref[...] = (bhat * bg_ref[...] + bb_ref[...]).astype(bf16)
    copies[1].wait()

    def lanes(n):
        return pl.ds(pl.multiple_of(n * CHUNK, CHUNK), CHUNK)

    def upward(n, total):
        u = dot_nn(low_ref[...], wu[:, lanes(n)])
        cdf = 0.5 + 0.5 * lax.erf(u * SQRT_HALF)
        g = u * cdf
        g_scr[:, lanes(n)] = g
        dg_scr[:, lanes(n)] = cdf + u * (jnp.exp(u * u * -0.5) * INV_SQRT_2PI)
        return total + jnp.sum(g, 1, keepdims=True)

    mean = lax.fori_loop(0, chunks, upward, jnp.zeros((tok, 1), f32)) / hidden

    def spread(n, total):
        c = g_scr[:, lanes(n)] - mean
        return total + jnp.sum(c * c, 1, keepdims=True)

    var = lax.fori_loop(0, chunks, spread, jnp.zeros((tok, 1), f32)) / hidden
    rstd = lax.rsqrt(var + EPS)
    copies[2].wait()
    acc_scr[...] = jnp.zeros_like(acc_scr)

    def downward(n, sums):
        first, second = sums
        ghat = (g_scr[:, lanes(n)] - mean) * rstd
        g_scr[:, lanes(n)] = ghat
        gain = hg_ref[:, lanes(n)]
        h = (ghat * gain + hb_ref[:, lanes(n)]).astype(bf16)
        hid_ref[:, lanes(n)] = h
        acc_scr[...] += dot_nn(h, wd[lanes(n), :])
        back = dot_nt(cotp_ref[...], wd[lanes(n), :])
        nh_ref[0:1, lanes(n)] = jnp.sum(back * ghat, 0, keepdims=True)
        nh_ref[1:2, lanes(n)] = jnp.sum(back, 0, keepdims=True)
        dn = back * gain
        dn_scr[:, lanes(n)] = dn
        return (
            first + jnp.sum(dn, 1, keepdims=True),
            second + jnp.sum(dn * ghat, 1, keepdims=True),
        )

    zero = jnp.zeros((tok, 1), f32)
    first, second = lax.fori_loop(0, chunks, downward, (zero, zero))
    first, second = first / hidden, second / hidden
    out_ref[...] = dot_nn(onehot_cols(tok), (am_scr[...] + acc_scr[...]).astype(bf16)).astype(bf16)
    acc_scr[...] = jnp.zeros_like(acc_scr)

    def backward(n, carry):
        d = rstd * (dn_scr[:, lanes(n)] - first - g_scr[:, lanes(n)] * second)
        dup = (d * dg_scr[:, lanes(n)]).astype(bf16)
        dup_ref[:, lanes(n)] = dup
        acc_scr[...] += dot_nt(dup, wu[:, lanes(n)])
        return carry

    lax.fori_loop(0, chunks, backward, 0)
    bhat, brstd = normalize(am_scr[...])
    middle, gain_b, bias_b = norm_back(acc_scr[...], bg_ref[...], bhat, brstd)
    branch = cotp_ref[...].astype(f32) + middle
    branch_ref[...] = branch
    brl_ref[...] = branch.astype(bf16)
    att = att_ref[...].reshape(width, tok).T.astype(f32)
    ahat, arstd = normalize(att)
    da, gain_m, bias_m = norm_back(dot_nt(brl_ref[...], wo[...]), mg_ref[...], ahat, arstd)
    da_ref[...] = da.astype(bf16).T.reshape(reps, cols, tok)
    ng_ref[0:1] = gain_m
    ng_ref[1:2] = bias_m
    ng_ref[2:3] = gain_b
    ng_ref[3:4] = bias_b


def ffn_call(att, xp, output_grad, weights, gains, m):
    reps, cols, tok = att.shape
    width = xp.shape[1]
    hidden = weights[1].shape[1]
    vec = vmem_spec()
    shapes = [
        ((tok, width), bf16),
        ((tok, width), f32),
        ((reps, cols, tok), bf16),
        ((tok, width), bf16),
        ((tok, width), bf16),
        ((tok, hidden), bf16),
        ((tok, hidden), bf16),
        ((tok, width), bf16),
        ((tok, width), bf16),
        ((4, width), f32),
        ((2, hidden), f32),
    ]
    return pl.pallas_call(
        ffn_body,
        grid=(1,),
        in_specs=[
            pl.BlockSpec((reps, cols, tok), lambda n: (0, 0, 0)),
            pl.BlockSpec((tok, width), lambda n: (0, 0)),
            pl.BlockSpec((None, tok, width), lambda n: (m, 0, 0)),
        ]
        + [pl.BlockSpec(memory_space=pl.ANY)] * 3
        + [pl.BlockSpec(g.shape, lambda n: (0, 0)) for g in gains],
        out_specs=[pl.BlockSpec(s, lambda n, k=len(s): (0,) * k) for s, _ in shapes],
        out_shape=[jax.ShapeDtypeStruct(s, d) for s, d in shapes],
        scratch_shapes=[pltpu.VMEM(w.shape, bf16) for w in weights]
        + [pltpu.VMEM((tok, hidden), f32)] * 3
        + [pltpu.VMEM((tok, width), f32)] * 2
        + [pltpu.SemaphoreType.DMA((3,))],
        compiler_params=pltpu.CompilerParams(vmem_limit_bytes=VMEM),
        cost_estimate=pl.CostEstimate(
            flops=4 * tok * width * (2 * hidden + width),
            bytes_accessed=25_000_000,
            transcendentals=2 * tok * hidden,
        ),
        name=f"ffn_{m}",
    )(att, xp, output_grad, *weights, *gains)


def join_heads(tg_ref, c):
    reps = tg_ref.shape[0]
    return jnp.concatenate([tg_ref[r, c] for r in range(reps)], 0)


def qkv_grad_body(*refs):
    micros = (len(refs) - 1) // 2
    out_ref = refs[-1]
    total = None
    for k in range(micros):
        nt, tg = refs[2 * k], refs[2 * k + 1]
        part = dot_nt(nt[...], join_heads(tg, 0))
        total = part if total is None else total + part
    out_ref[...] = total.astype(bf16)


def qkv_grad_call(pairs, tok, width, reps):
    cols = width // reps
    return pl.pallas_call(
        qkv_grad_body,
        grid=(3,),
        in_specs=[
            pl.BlockSpec((width, tok), lambda c: (0, 0)),
            pl.BlockSpec((reps, 1, cols, tok), lambda c: (0, c, 0, 0)),
        ]
        * len(pairs),
        out_specs=pl.BlockSpec((width, width), lambda c: (0, c)),
        out_shape=jax.ShapeDtypeStruct((width, 3 * width), bf16),
        compiler_params=pltpu.CompilerParams(vmem_limit_bytes=VMEM),
        cost_estimate=pl.CostEstimate(
            flops=6 * len(pairs) * tok * width * width, bytes_accessed=10_000_000, transcendentals=0
        ),
        name="qkv_grad",
    )(*[a for p in pairs for a in p])


def input_grad_body(tg_ref, w_ref, xp_ref, branch_ref, gain_ref, out_ref, ng_ref, acc):
    tok, width = xp_ref.shape
    c = pl.program_id(0)
    part = dot_nn(w_ref[...], join_heads(tg_ref, 0))

    @pl.when(c == 0)
    def _():
        acc[...] = part

    @pl.when(c > 0)
    def _():
        acc[...] += part

    @pl.when(c == 2)
    def _():
        xhat, rstd = normalize(xp_ref[...].astype(f32))
        dx, gain_i, bias_i = norm_back(acc[...].T, gain_ref[...], xhat, rstd)
        ng_ref[0:1] = gain_i
        ng_ref[1:2] = bias_i
        total = (branch_ref[...] + dx).astype(bf16)
        out_ref[...] = dot_nn(onehot_cols(tok), total).astype(bf16)


def input_grad_call(tg, weight, xp, branch, gain, m):
    reps, _, cols, tok = tg.shape
    width = reps * cols
    return pl.pallas_call(
        input_grad_body,
        grid=(3,),
        in_specs=[
            pl.BlockSpec((reps, 1, cols, tok), lambda c: (0, c, 0, 0)),
            pl.BlockSpec((width, width), lambda c: (0, c)),
            pl.BlockSpec((tok, width), lambda c: (0, 0)),
            pl.BlockSpec((tok, width), lambda c: (0, 0)),
            pl.BlockSpec((1, width), lambda c: (0, 0)),
        ],
        out_specs=[
            pl.BlockSpec((tok, width), lambda c: (0, 0)),
            pl.BlockSpec((2, width), lambda c: (0, 0)),
        ],
        out_shape=[
            jax.ShapeDtypeStruct((tok, width), bf16),
            jax.ShapeDtypeStruct((2, width), f32),
        ],
        scratch_shapes=[pltpu.VMEM((width, tok), f32)],
        compiler_params=pltpu.CompilerParams(vmem_limit_bytes=VMEM),
        cost_estimate=pl.CostEstimate(
            flops=6 * tok * width * width, bytes_accessed=10_000_000, transcendentals=0
        ),
        name=f"input_grad_{m}",
    )(tg, weight, xp, branch, gain)


def rep_peer(k):
    count = lax.axis_size("rep")
    return (lax.axis_index("rep") + k) % count


def team_place():
    return lax.axis_index("seq") % 4


def team_member(k):
    s = lax.axis_index("seq")
    return s // 4 * 4 + (s + k) % 4


def pair_partner():
    s = lax.axis_index("seq")
    return s + 1 - 2 * (s % 2)


def remote(src, dst, send_sem, recv_sem, axis, peer):
    return pltpu.make_async_remote_copy(
        src_ref=src,
        dst_ref=dst,
        send_sem=send_sem,
        recv_sem=recv_sem,
        device_id={axis: peer},
        device_id_type=pl.DeviceIdType.MESH,
    )


def meet_peers():
    barrier = pltpu.get_barrier_semaphore()
    for k in range(1, 4):
        for axis, peer in (("rep", rep_peer(k)), ("seq", team_member(k))):
            pl.semaphore_signal(
                barrier, inc=1, device_id={axis: peer}, device_id_type=pl.DeviceIdType.MESH
            )
    pl.semaphore_wait(barrier, 6)


def head_rows(j):
    return pl.ds(pl.multiple_of(j * HD, HD), HD)


def attend(block, doc, put, ks, qs, pattern, count, lanes):
    kb = min(512, lanes)
    for s in range(0, count, kb):
        sl = slice(s, s + kb)
        r = lax.broadcasted_iota(jnp.int32, (HD, kb), 0)
        same = doc[:, sl] == r
        aux_k = jnp.where(same, 1.0, 0.0).astype(bf16)
        aux_q = jnp.where(same | (r >= 4), 0.0, NEG).astype(bf16)
        q = (block(0, s, kb).astype(f32) * 0.125).astype(bf16)
        qs[:, sl] = jnp.concatenate([q, aux_q], 0)
        ks[sl, :] = jnp.concatenate([block(1, s, kb), aux_k], 0).T

    qb = 256
    grain = 512 if pattern == 0 else 256

    def tiles(i):
        low = (i * qb) // grain * grain
        out = [(s, min(512, low - s), False) for s in range(0, low, 512)]
        return out + [(low, grain, True)]

    def scores(i):
        out = []
        for s, size, diagonal in tiles(i):
            t = dot_nn(ks[s : s + size, :], qs[:, i * qb : (i + 1) * qb])
            if diagonal:
                keep = rel_pos((size, qb), 0, s % 512, pattern) <= rel_pos(
                    (size, qb), 1, (i * qb) % 512, pattern
                )
                t = jnp.where(keep, t, NEG)
            out.append(t)
        return out

    following = scores(0)
    for i in range(count // qb):
        current = following
        if (i + 1) * qb < count:
            following = scores(i + 1)
        top = functools.reduce(jnp.maximum, [jnp.max(t, 0, keepdims=True) for t in current])
        top2 = top * LOG2E
        acc, total = None, None
        for t, (s, size, _) in zip(current, tiles(i)):
            p = jnp.exp2(t * LOG2E - top2)
            part = jnp.sum(p, 0, keepdims=True)
            out = dot_nn(block(2, s, size), p.astype(bf16))
            acc = out if acc is None else acc + out
            total = part if total is None else total + part
        lse = top + jnp.log(total)
        put(i * qb, qb, (acc / total).astype(bf16), stat_rows(split3(lse), qb))


def forward_body(
    x_ref,
    w_ref,
    gain_ref,
    bias_ref,
    len_ref,
    xp_ref,
    nt_ref,
    r_out,
    p1_out,
    p2_out,
    att_ref,
    got_ref,
    mix_ref,
    sent,
    r,
    stage1,
    stage2,
    p1,
    p2,
    o0,
    o1,
    o2,
    b1,
    b2,
    ks,
    qs,
    qkv_sems,
    p1_sems,
    p2_sems,
    b1_sems,
    b2_sems,
    att_sems,
    out_sems,
):
    micros, tok, width = x_ref.shape
    reps = r.shape[1]
    span = tok * reps
    cols = width // reps
    me = lax.axis_index("rep")
    place = team_place()
    side = place % 2
    meet_peers()

    def qkv_copy(m, j, k, source):
        return remote(
            sent.at[m, rep_peer(k), :, head_rows(j)],
            r.at[m, source, :, head_rows(j)],
            qkv_sems.at[0, m, j, k - 1],
            qkv_sems.at[1, m, j, k - 1],
            "rep",
            rep_peer(k),
        )

    def p1_copy(m, s, source):
        return remote(
            stage1.at[m, s],
            p1.at[m, source, s],
            p1_sems.at[0, m, s],
            p1_sems.at[1, m, s],
            "seq",
            pair_partner(),
        )

    def p2_copy(m, k, source):
        return remote(
            stage2.at[m, (place + k) % 4],
            p2.at[m, source],
            p2_sems.at[0, m, k - 1],
            p2_sems.at[1, m, k - 1],
            "seq",
            team_member(k),
        )

    def b1_copy(m, s, source):
        return remote(
            o1.at[m, s, 1 - side],
            b1.at[m, source, s],
            b1_sems.at[0, m, s],
            b1_sems.at[1, m, s],
            "seq",
            pair_partner(),
        )

    def b2_copy(m, k, source):
        return remote(
            o2.at[m, (place + k) % 4],
            b2.at[m, source],
            b2_sems.at[0, m, k - 1],
            b2_sems.at[1, m, k - 1],
            "seq",
            team_member(k),
        )

    def att_copy(k, source):
        return remote(
            att_ref.at[0, rep_peer(k)],
            got_ref.at[source],
            att_sems.at[0, k - 1],
            att_sems.at[1, k - 1],
            "rep",
            rep_peer(k),
        )

    def out_copies(m):
        return (
            pltpu.make_async_copy(r.at[m], r_out.at[m], out_sems.at[m, 0]),
            pltpu.make_async_copy(p1.at[m], p1_out.at[m], out_sems.at[m, 1]),
            pltpu.make_async_copy(p2.at[m], p2_out.at[m], out_sems.at[m, 2]),
        )

    def project(m, carry):
        xp = dot_nn(onehot_rows(tok), x_ref[m])
        xp_ref[m] = xp.astype(bf16)
        xhat, _ = normalize(xp)
        n = (xhat * gain_ref[...] + bias_ref[...]).astype(bf16)
        nt_ref[m] = n.T
        for c in range(3):
            t = dot_nn(n, w_ref[:, c * width : (c + 1) * width]).astype(bf16).T
            for d in range(reps):
                sent[m, d, c] = t[d * cols : (d + 1) * cols]
        for j in range(3):
            for k in range(1, 4):
                qkv_copy(m, j, k, me).start()
        r[m, me] = sent[m, me]
        return carry

    lax.fori_loop(0, micros, project, 0)

    def half(j):
        return pl.ds(pl.multiple_of(((3 * me + j) % 2) * 256, 256), 256)

    def quarter_at(j):
        c = (3 * me + j) % 4
        return c % 2 * 2 + c // 2

    def quarter(j):
        return pl.ds(pl.multiple_of(quarter_at(j) * 128, 128), 128)

    def send_first(m):
        for b in range(reps):
            bl = slice(b * 256, (b + 1) * 256)
            stage1[m, 0, :, :, bl] = r[m, b, :, head_rows(1 - side), half(1 - side)]
            p1[m, side, 0, :, :, bl] = r[m, b, :, head_rows(side), half(side)]
        p1_copy(m, 0, side).start()

    def send_second(m):
        for b in range(reps):
            bl = slice(b * 256, (b + 1) * 256)
            piece = r[m, b, :, head_rows(2), half(2)]
            stage1[m, 1, :, :, bl] = piece
            p1[m, side, 1, :, :, bl] = piece
        p1_copy(m, 1, side).start()
        for g in range(4):
            j = min(g, 2)
            for b in range(reps):
                stage2[m, g, :, :, b * 128 : (b + 1) * 128] = r[m, b, :, head_rows(j), quarter(j)]
        p2[m, place] = stage2[m, place]
        for k in range(1, 4):
            p2_copy(m, k, place).start()

    def mix_all(m):
        for s in range(2):
            b1_copy(m, s, 1 - side).wait_recv()
        for k in range(1, 4):
            b2_copy(m, k, (place + 4 - k) % 4).wait_recv()

        def stat(tile):
            t = tile[HD:, :].astype(f32)
            return t[0:1] + t[1:2] + t[2:3]

        mix_ref[m] = jnp.zeros(mix_ref.shape[1:], f32)
        for j in range(3):
            e, s = PLACE1[j]
            for b in range(reps):
                for a in range(4):
                    la = slice(a * 128, (a + 1) * 128)
                    lb = b * 256 + (a % 2) * 128
                    t0 = o0[m, j, b, :, la]
                    t1 = b1[m, e, s, :, lb : lb + 128]
                    t2 = b2[m, j, :, b * 128 : (b + 1) * 128]
                    l0 = stat(t0)
                    l1 = jnp.where((3 * me + j) % 2 == a // 2, stat(t1), NEG)
                    l2 = jnp.where(quarter_at(j) == a, stat(t2), NEG)
                    top = jnp.maximum(jnp.maximum(l0, l1), l2)
                    e0, e1, e2 = jnp.exp(l0 - top), jnp.exp(l1 - top), jnp.exp(l2 - top)
                    total = e0 + e1 + e2
                    inv = 1.0 / total
                    mixed = (
                        t0[:HD].astype(f32) * (e0 * inv)
                        + t1[:HD].astype(f32) * (e1 * inv)
                        + t2[:HD].astype(f32) * (e2 * inv)
                    )
                    att_ref[m, b, j * HD : (j + 1) * HD, la] = mixed.astype(bf16)
                    col = b * tok + a * 128
                    mix_ref[m, j : j + 1, col : col + 128] = top + jnp.log(total)

    docs_of = lambda m, pattern: doc_rows(
        len_ref, m, segment_start(pattern, span), 2**pattern, span
    )

    def micro(m, carry):
        def local(j, inner):
            for k in range(1, 4):
                qkv_copy(m, j, k, (me + reps - k) % reps).wait_recv()

            @pl.when(j == 1)
            def _():
                send_first(m)

            @pl.when(j == 2)
            def _():
                send_second(m)

            def block(c, start, size):
                at = start % tok
                return r[m, start // tok, c, head_rows(j), at : at + size]

            def put(start, size, out, stats):
                at = start % tok
                o0[m, j, start // tok, :HD, at : at + size] = out
                o0[m, j, start // tok, HD:, at : at + size] = stats

            attend(block, docs_of(m, 0), put, ks, qs, 0, span, tok)
            return inner

        lax.fori_loop(0, 3, local, 0)

        @pl.when(m == 1)
        def _():
            mix_all(0)
            for k in range(1, 4):
                att_copy(k, me).start()
            got_ref[me] = att_ref[0, me]

        def paired(s, inner):
            p1_copy(m, s, 1 - side).wait_recv()
            wide = span // 2

            def block(c, start, size):
                at = start % wide
                return p1[m, start // wide, s, c, :, at : at + size]

            def put(start, size, out, stats):
                at = start % wide
                o1[m, s, start // wide, :HD, at : at + size] = out
                o1[m, s, start // wide, HD:, at : at + size] = stats

            attend(block, docs_of(m, 1), put, ks, qs, 1, span, wide)
            b1[m, side, s] = o1[m, s, side]
            b1_copy(m, s, side).start()
            return inner

        lax.fori_loop(0, 2, paired, 0)
        for k in range(1, 4):
            p2_copy(m, k, (place + 4 - k) % 4).wait_recv()

        def block(c, start, size):
            at = start % tok
            return p2[m, start // tok, c, :, at : at + size]

        def put(start, size, out, stats):
            at = start % tok
            o2[m, start // tok, :HD, at : at + size] = out
            o2[m, start // tok, HD:, at : at + size] = stats

        attend(block, docs_of(m, 2), put, ks, qs, 2, span, tok)
        b2[m, place] = o2[m, place]
        for k in range(1, 4):
            b2_copy(m, k, place).start()
        for c in out_copies(m):
            c.start()
        return carry

    lax.fori_loop(0, micros, micro, 0)
    mix_all(1)
    for k in range(1, 4):
        att_copy(k, (me + reps - k) % reps).wait_recv()
        att_copy(k, me).wait_send()

    def finish(m, carry):
        for c in out_copies(m):
            c.wait()
        for k in range(1, 4):
            for j in range(3):
                qkv_copy(m, j, k, me).wait_send()
            p2_copy(m, k, place).wait_send()
            b2_copy(m, k, place).wait_send()
        for s in range(2):
            p1_copy(m, s, side).wait_send()
            b1_copy(m, s, side).wait_send()
        return carry

    lax.fori_loop(0, micros, finish, 0)


def forward_call(layer_in, weight, gain, bias, lengths, reps):
    micros, tok, width = layer_in.shape
    span, cols = tok * reps, width // reps
    any_spec = pl.BlockSpec(memory_space=pl.ANY)
    outs = [
        ((micros, tok, width), bf16, vmem_spec()),
        ((micros, width, tok), bf16, vmem_spec()),
        ((micros, reps, 3, cols, tok), bf16, any_spec),
        ((micros, 2, 2, 3, HD, span // 2), bf16, any_spec),
        ((micros, 4, 3, HD, span // 4), bf16, any_spec),
        ((micros, reps, cols, tok), bf16, vmem_spec()),
        ((reps, cols, tok), bf16, vmem_spec()),
        ((micros, 8, span), f32, vmem_spec()),
    ]

    def vm(*shape):
        return pltpu.VMEM(shape, bf16)

    dma = pltpu.SemaphoreType.DMA
    return pl.pallas_call(
        forward_body,
        in_specs=[vmem_spec()] * 4 + [smem_spec()],
        out_specs=[o[2] for o in outs],
        out_shape=[jax.ShapeDtypeStruct(o[0], o[1]) for o in outs],
        scratch_shapes=[
            vm(micros, reps, 3, cols, tok),
            vm(micros, reps, 3, cols, tok),
            vm(micros, 2, 3, HD, span // 2),
            vm(micros, 4, 3, HD, span // 4),
            vm(micros, 2, 2, 3, HD, span // 2),
            vm(micros, 4, 3, HD, span // 4),
            vm(micros, 3, reps, HPAD, tok),
            vm(micros, 2, 2, HPAD, span // 2),
            vm(micros, 4, HPAD, span // 4),
            vm(micros, 2, 2, HPAD, span // 2),
            vm(micros, 4, HPAD, span // 4),
            vm(span, 128),
            vm(128, span),
            dma((2, micros, 3, 3)),
            dma((2, micros, 2)),
            dma((2, micros, 3)),
            dma((2, micros, 2)),
            dma((2, micros, 3)),
            dma((2, 3)),
            dma((micros, 3)),
        ],
        compiler_params=pltpu.CompilerParams(
            vmem_limit_bytes=VMEM, collective_id=1, has_side_effects=True
        ),
        cost_estimate=pl.CostEstimate(
            flops=60_000_000_000, bytes_accessed=30_000_000, transcendentals=30_000_000
        ),
        name="forward",
    )(layer_in, weight, gain, bias, lengths)


def bit_of(axis, bit):
    return lax.axis_index(axis) // (1 << bit) % 2


def bit_peer(axis, bit):
    return lax.axis_index(axis) + (1 << bit) * (1 - 2 * bit_of(axis, bit))


def attend_back(block, gblock, doc, put, scr, pattern, count, lanes):
    ks, vs, qs, qr, gs, gr, dq = scr
    bs = min(512, lanes)
    zeros = jnp.zeros((HD, bs), bf16)
    r = lax.broadcasted_iota(jnp.int32, (HD, bs), 0)
    fill = jnp.zeros((HD - 32, bs), bf16)
    for s in range(0, count, bs):
        sl = slice(s, s + bs)
        same = doc[:, sl] == r
        aux_k = jnp.where(same | ((r >= 16) & (r < 19)), 1.0, 0.0).astype(bf16)
        aux_q = jnp.where(same | (r >= 4), 0.0, NEG).astype(bf16)
        aux_v = jnp.where((r >= 19) & (r < 21), 1.0, 0.0).astype(bf16)
        q = (block(0, s, bs).astype(f32) * 0.125).astype(bf16)
        tile = gblock(s, bs)
        g, stats = tile[:HD], tile[HD:]
        qs[:, sl] = jnp.concatenate([q, aux_q[:16], stats, fill], 0)
        gs[:, sl] = jnp.concatenate([g, zeros[:16], stats, fill], 0)
        qr[sl, :] = jnp.concatenate([q, zeros], 0).T
        gr[sl, :] = jnp.concatenate([g, zeros], 0).T
        ks[sl, :] = jnp.concatenate([block(1, s, bs), aux_k], 0).T
        vs[sl, :] = jnp.concatenate([block(2, s, bs), aux_v], 0).T

    keep = rel_pos((bs, bs), 0, 0, pattern) <= rel_pos((bs, bs), 1, 0, pattern)
    for j in range(count // bs):
        jl = slice(j * bs, (j + 1) * bs)
        dva, dka = None, None
        for i in range(j, count // bs):
            il = slice(i * bs, (i + 1) * bs)
            p = jnp.exp2(dot_nn(ks[jl, :], qs[:, il]) * LOG2E)
            if i == j:
                p = jnp.where(keep, p, 0.0)
            dp = dot_nn(vs[jl, :], gs[:, il])
            ds = (p * dp).astype(bf16)
            dvi = dot_nn(p.astype(bf16), gr[il, :])
            dki = dot_nn(ds, qr[il, :])
            dva = dvi if dva is None else dva + dvi
            dka = dki if dka is None else dka + dki
            dqi = dot_nn(block(1, j * bs, bs), ds) * 0.125
            if j == 0:
                dq[:, il] = dqi
            else:
                dq[:, il] += dqi
        put(1, j * bs, bs, dka.T[:HD].astype(bf16))
        put(2, j * bs, bs, dva.T[:HD].astype(bf16))
        put(0, j * bs, bs, dq[:, jl].astype(bf16))


class Halving:
    def __init__(self, source, steps, buffers, gathered, out, sems):
        self.source, self.steps, self.buffers = source, steps, buffers
        self.gathered, self.out, self.sems = gathered, out, sems
        self.names = ["high", "x", "y"]
        self.at = 0
        self.pending = None

    def pick(self, ref, axis, name, index):
        lead = (slice(None),) * axis
        if name == "high":
            half = ref.shape[axis] // 2
            return lead + (pl.ds(index * half, half),)
        return lead + (index,)

    def start(self):
        if self.at < len(self.steps):
            name, axis_name, bit = self.steps[self.at]
            axis = self.names.index(name)
            mine = bit_of(axis_name, bit)
            target = self.buffers[self.at]
            copy = remote(
                self.source.at[self.pick(self.source, axis, name, 1 - mine)],
                target,
                self.sems.at[0, self.at],
                self.sems.at[1, self.at],
                axis_name,
                bit_peer(axis_name, bit),
            )
            copy.start()
            self.pending = ("sum", copy, target, self.pick(self.source, axis, name, mine))
            if name != "high":
                self.names.pop(axis)
            return
        stage = self.at - len(self.steps)
        y, c = bit_of("rep", 1), bit_of("rep", 0)
        if stage == 0:
            self.gathered[y, c] = self.source[0]
            part, landing, bit = (y, c), (1 - y, c), 1
        elif stage == 1:
            part, landing, bit = (slice(None), c), (slice(None), 1 - c), 0
        else:
            self.pending = None
            return
        copy = lambda place: remote(
            self.gathered.at[part],
            self.gathered.at[place],
            self.sems.at[0, self.at],
            self.sems.at[1, self.at],
            "rep",
            bit_peer("rep", bit),
        )
        copy(part).start()
        self.pending = ("gather", copy(part), copy(landing), None)

    def finish(self):
        kind, first, second, mine = self.pending
        if kind == "sum":
            first.wait()
            rows = second.shape[0]

            def add(n, carry):
                at = (n,) if mine[0] == slice(None) else None
                if at is None:
                    head = mine[0]
                    base = head.start if isinstance(head, pl.Slice) else None
                    value = self.source[(base + n,) + mine[1:]]
                else:
                    value = self.source[at + mine[1:]]
                second[n] = (second[n].astype(f32) + value.astype(f32)).astype(bf16)
                return carry

            lax.fori_loop(0, rows, add, 0)
            self.source = second
        else:
            first.wait_send()
            second.wait_recv()
        self.at += 1

    def pump(self):
        if self.pending is not None:
            self.finish()
            self.start()

    def drain(self):
        while self.pending is not None:
            self.pump()
        for y in range(2):
            for c in range(2):
                self.out[y, c] = self.gathered[y, c].astype(f32)


def reduce_steps(order, seq_bits):
    steps = []
    for name in order:
        if name == "y":
            steps.append(("y", "rep", 1))
        elif name == "x":
            steps.append(("x", "seq", 0))
        else:
            steps += [("high", "seq", b) for b in range(seq_bits - 1, 0, -1)]
    return steps


def reduce_buffers(shape, steps):
    high, rows, cols = shape[0], shape[3], shape[4]
    rest = ["x", "y"]
    out = []
    for name, _, _ in steps:
        if name == "high":
            high //= 2
        else:
            rest.remove(name)
        out.append((high,) + (2,) * len(rest) + (rows, cols))
    return out


REDUCE_ORDERS = ("yxz", "xyz", "yxz")


def backward_body(
    r_hbm,
    p1_hbm,
    p2_hbm,
    da0_ref,
    da1_ref,
    att_ref,
    mix_ref,
    len_ref,
    w0_ref,
    w1_ref,
    w2_ref,
    tg_ref,
    t0_ref,
    t1_ref,
    t2_ref,
    *scratch,
    seq_bits,
):
    (r, p1, p2, g0, g1s, g2s, g1, g2, d1, d2, e1, e2, sums, ks, vs, qs, qr, gs, gr, dq) = scratch[:20]
    load_sems, g1_sems, g2_sems, d1_sems, d2_sems, tg_sems, tg1_sems, own_sems = scratch[20:28]
    rest = list(scratch[28:])
    halvings = []
    for order, source, out in zip(
        REDUCE_ORDERS, (w0_ref, w1_ref, w2_ref), (t0_ref, t1_ref, t2_ref)
    ):
        steps = reduce_steps(order, seq_bits)
        buffers = [rest.pop(0) for _ in steps]
        gathered, sems = rest.pop(0), rest.pop(0)
        halvings.append(Halving(source, steps, buffers, gathered, out, sems))
    reps, cols, tok = da0_ref.shape
    micros = att_ref.shape[0]
    span = tok * reps
    wide = span // 2
    me = lax.axis_index("rep")
    place = team_place()
    side = place % 2
    scr = (ks, vs, qs, qr, gs, gr, dq)

    barrier = pltpu.get_barrier_semaphore()
    peers = [("rep", rep_peer(k)) for k in range(1, 4)]
    peers += [("seq", team_member(k)) for k in range(1, 4)]
    peers += [("seq", bit_peer("seq", b)) for b in range(2, seq_bits)]
    for axis, peer in peers:
        pl.semaphore_signal(
            barrier, inc=1, device_id={axis: peer}, device_id_type=pl.DeviceIdType.MESH
        )
    load_r = lambda m: pltpu.make_async_copy(r_hbm.at[m], r, load_sems.at[0])
    load_1 = lambda m: pltpu.make_async_copy(p1_hbm.at[m], p1, load_sems.at[1])
    load_2 = lambda m: pltpu.make_async_copy(p2_hbm.at[m], p2, load_sems.at[2])
    load_r(0).start()
    load_1(0).start()
    load_2(0).start()
    pl.semaphore_wait(barrier, len(peers))
    for h in halvings:
        h.start()

    def pump():
        for h in halvings:
            h.pump()

    def g1_copy(m, s, source):
        return remote(
            g1s.at[m, s],
            g1.at[m, source, s],
            g1_sems.at[0, m, s],
            g1_sems.at[1, m, s],
            "seq",
            pair_partner(),
        )

    def g2_copy(m, k, source):
        return remote(
            g2s.at[m, (place + k) % 4],
            g2.at[m, source],
            g2_sems.at[0, m, k - 1],
            g2_sems.at[1, m, k - 1],
            "seq",
            team_member(k),
        )

    def d1_copy(m, s, source):
        return remote(
            d1.at[m, s, 1 - side],
            e1.at[m, source, s],
            d1_sems.at[0, m, s],
            d1_sems.at[1, m, s],
            "seq",
            pair_partner(),
        )

    def d2_copy(m, k, source):
        return remote(
            d2.at[m, (place + k) % 4],
            e2.at[m, source],
            d2_sems.at[0, m, k - 1],
            d2_sems.at[1, m, k - 1],
            "seq",
            team_member(k),
        )

    def tg0_copy(k, source):
        return remote(
            sums.at[0, rep_peer(k)],
            tg_ref.at[0, source],
            tg_sems.at[0, k - 1],
            tg_sems.at[1, k - 1],
            "rep",
            rep_peer(k),
        )

    def tg1_copy(j, k, source):
        return remote(
            sums.at[1, rep_peer(k), :, head_rows(j)],
            tg_ref.at[1, source, :, head_rows(j)],
            tg1_sems.at[0, j, k - 1],
            tg1_sems.at[1, j, k - 1],
            "rep",
            rep_peer(k),
        )

    own_copy = lambda m: pltpu.make_async_copy(sums.at[m, me], tg_ref.at[m, me], own_sems.at[m])

    def half(j):
        return pl.ds(pl.multiple_of(((3 * me + j) % 2) * 256, 256), 256)

    def quarter_at(j):
        c = (3 * me + j) % 4
        return c % 2 * 2 + c // 2

    def quarter(j):
        return pl.ds(pl.multiple_of(quarter_at(j) * 128, 128), 128)

    for m, da_ref in enumerate((da0_ref, da1_ref)):
        for j in range(3):
            rows = slice(j * HD, (j + 1) * HD)
            for b in range(reps):
                g = da_ref[b, rows, :]
                inner = jnp.sum(
                    g.astype(f32) * att_ref[m, b, rows, :].astype(f32), 0, keepdims=True
                )
                total = mix_ref[m, j : j + 1, b * tok : (b + 1) * tok]
                high, mid, low = split3(-total)
                inner_high, inner_mid, _ = split3(-inner)
                g0[m, j, b, :HD, :] = g
                g0[m, j, b, HD:, :] = stat_rows((high, mid, low, inner_high, inner_mid), tok)
        for b in range(reps):
            bl = slice(b * 256, (b + 1) * 256)
            g1s[m, 0, :, bl] = g0[m, 1 - side, b, :, half(1 - side)]
            g1[m, side, 0, :, bl] = g0[m, side, b, :, half(side)]
            piece = g0[m, 2, b, :, half(2)]
            g1s[m, 1, :, bl] = piece
            g1[m, side, 1, :, bl] = piece
            for g in range(4):
                j = min(g, 2)
                g2s[m, g, :, b * 128 : (b + 1) * 128] = g0[m, j, b, :, quarter(j)]
        g2[m, place] = g2s[m, place]
        for s in range(2):
            g1_copy(m, s, side).start()
        for k in range(1, 4):
            g2_copy(m, k, place).start()

    def docs(m, pattern):
        return doc_rows(len_ref, m, segment_start(pattern, span), 2**pattern, span)

    def own_head(m, j):
        def block(c, start, size):
            at = start % tok
            return r[start // tok, c, head_rows(j), at : at + size]

        def gblock(start, size):
            at = start % tok
            return g0[m, j, start // tok, :, at : at + size]

        def put(c, start, size, value):
            at = start % tok
            sums[m, start // tok, c, head_rows(j), at : at + size] = value

        attend_back(block, gblock, docs(m, 0), put, scr, 0, span, tok)

    def add_others(m, j):
        e, s = PLACE1[j]
        for b in range(reps):
            bl = slice(b * 256, (b + 1) * 256)
            t = sums[m, b, :, j * HD : (j + 1) * HD, half(j)].astype(f32)
            t = t + e1[m, e, s, :, :, bl].astype(f32)
            sums[m, b, :, j * HD : (j + 1) * HD, half(j)] = t.astype(bf16)
            t = sums[m, b, :, j * HD : (j + 1) * HD, quarter(j)].astype(f32)
            t = t + e2[m, j, :, :, b * 128 : (b + 1) * 128].astype(f32)
            sums[m, b, :, j * HD : (j + 1) * HD, quarter(j)] = t.astype(bf16)

    def wait_others(m):
        for s in range(2):
            d1_copy(m, s, 1 - side).wait_recv()
        for k in range(1, 4):
            d2_copy(m, k, (place + 4 - k) % 4).wait_recv()

    load_r(0).wait()

    def first_heads(j, carry):
        own_head(0, j)
        return carry

    lax.fori_loop(0, 3, first_heads, 0)
    load_r(1).start()

    def others(m):
        def paired(s, inner):
            g1_copy(m, s, 1 - side).wait_recv()

            def block(c, start, size):
                at = start % wide
                return p1[start // wide, s, c, :, at : at + size]

            def gblock(start, size):
                at = start % wide
                return g1[m, start // wide, s, :, at : at + size]

            def put(c, start, size, value):
                at = start % wide
                d1[m, s, start // wide, c, :, at : at + size] = value

            attend_back(block, gblock, docs(m, 1), put, scr, 1, span, wide)
            e1[m, side, s] = d1[m, s, side]
            d1_copy(m, s, side).start()
            return inner

        load_1(m).wait()
        lax.fori_loop(0, 2, paired, 0)
        if m + 1 < micros:
            load_1(m + 1).start()
        pump()
        if m == 1:
            wait_others(0)
            for j in range(3):
                add_others(0, j)
            for k in range(1, 4):
                tg0_copy(k, me).start()
            own_copy(0).start()
        for k in range(1, 4):
            g2_copy(m, k, (place + 4 - k) % 4).wait_recv()
        load_2(m).wait()

        def block(c, start, size):
            at = start % tok
            return p2[start // tok, c, :, at : at + size]

        def gblock(start, size):
            at = start % tok
            return g2[m, start // tok, :, at : at + size]

        def put(c, start, size, value):
            at = start % tok
            d2[m, start // tok, c, :, at : at + size] = value

        attend_back(block, gblock, docs(m, 2), put, scr, 2, span, tok)
        e2[m, place] = d2[m, place]
        for k in range(1, 4):
            d2_copy(m, k, place).start()
        if m + 1 < micros:
            load_2(m + 1).start()

    others(0)
    others(1)
    load_r(1).wait()
    for j in range(3):
        own_head(1, j)
        if j == 0:
            wait_others(1)
        add_others(1, j)
        for k in range(1, 4):
            tg1_copy(j, k, me).start()
        pump()
    own_copy(1).start()
    for h in halvings:
        h.drain()
    for m in range(micros):
        own_copy(m).wait()
        for s in range(2):
            g1_copy(m, s, side).wait_send()
            d1_copy(m, s, side).wait_send()
        for k in range(1, 4):
            g2_copy(m, k, place).wait_send()
            d2_copy(m, k, place).wait_send()
    for k in range(1, 4):
        source = (me + reps - k) % reps
        tg0_copy(k, source).wait_recv()
        tg0_copy(k, me).wait_send()
        for j in range(3):
            tg1_copy(j, k, source).wait_recv()
            tg1_copy(j, k, me).wait_send()


def backward_call(pieces, da, att, totals, lengths, grads, seq_bits):
    micros, reps, cols, tok = att.shape
    span = tok * reps
    any_spec = pl.BlockSpec(memory_space=pl.ANY)

    def vm(*shape):
        return pltpu.VMEM(shape, bf16)

    dma = pltpu.SemaphoreType.DMA
    halving = []
    for order, g in zip(REDUCE_ORDERS, grads):
        steps = reduce_steps(order, seq_bits)
        halving += [vm(*b) for b in reduce_buffers(g.shape, steps)]
        halving += [vm(2, 2, *g.shape[3:]), dma((2, len(steps) + 2))]
    tall, flat = vm(span, 128), vm(128, span)
    outs = [((micros, reps, 3, cols, tok), bf16, any_spec)]
    outs += [((2, 2) + g.shape[3:], f32, vmem_spec()) for g in grads]
    return pl.pallas_call(
        functools.partial(backward_body, seq_bits=seq_bits),
        in_specs=[any_spec] * 3 + [vmem_spec()] * 4 + [smem_spec()] + [vmem_spec()] * 3,
        out_specs=[o[2] for o in outs],
        out_shape=[jax.ShapeDtypeStruct(o[0], o[1]) for o in outs],
        scratch_shapes=[
            vm(reps, 3, cols, tok),
            vm(2, 2, 3, HD, span // 2),
            vm(4, 3, HD, span // 4),
            vm(micros, 3, reps, HPAD, tok),
            vm(micros, 2, HPAD, span // 2),
            vm(micros, 4, HPAD, span // 4),
            vm(micros, 2, 2, HPAD, span // 2),
            vm(micros, 4, HPAD, span // 4),
            vm(micros, 2, 2, 3, HD, span // 2),
            vm(micros, 4, 3, HD, span // 4),
            vm(micros, 2, 2, 3, HD, span // 2),
            vm(micros, 4, 3, HD, span // 4),
            vm(micros, reps, 3, cols, tok),
            tall,
            tall,
            flat,
            tall,
            flat,
            tall,
            pltpu.VMEM((HD, span), f32),
            dma((3,)),
            dma((2, micros, 2)),
            dma((2, micros, 3)),
            dma((2, micros, 2)),
            dma((2, micros, 3)),
            dma((2, 3)),
            dma((2, 3, 3)),
            dma((micros,)),
            *halving,
        ],
        compiler_params=pltpu.CompilerParams(
            vmem_limit_bytes=60 << 20, collective_id=2, has_side_effects=True
        ),
        cost_estimate=pl.CostEstimate(
            flops=100_000_000_000, bytes_accessed=40_000_000, transcendentals=30_000_000
        ),
        name="backward",
    )(*pieces, *da, att, totals, lengths, *grads)


def split_rows(value, parts, rows):
    mine, other = [], []
    first = bit_of("rep", 0) == 0
    for n in range(parts):
        a = value[(2 * n) * rows : (2 * n + 1) * rows]
        b = value[(2 * n + 1) * rows : (2 * n + 2) * rows]
        mine.append(jnp.where(first, a, b))
        other.append(jnp.where(first, b, a))
    return mine, other


def weight_grad_body(*refs, chunks):
    ins, refs = refs[:12], refs[12:]
    down_ref, up_ref, proj_ref, lt = refs[:4]
    keeps, sends, gets, sems = refs[4:7], refs[7:10], refs[10:13], refs[13:16]
    groups = [ins[:6], ins[6:]]
    n = pl.program_id(0)

    def copy(t, slot):
        return remote(
            sends[t].at[slot],
            gets[t].at[slot],
            sems[t].at[0, slot],
            sems[t].at[1, slot],
            "rep",
            bit_peer("rep", 0),
        )

    def spread(t, slot, value):
        keep = keeps[t]
        parts, rows = keep.shape[1], keep.shape[2]
        mine, other = split_rows(value, parts, rows)
        for k in range(parts):
            keep[slot, k] = mine[k].astype(bf16)
            sends[t][slot, k] = other[k].astype(bf16)
        copy(t, slot).start()

    @pl.when(n == 0)
    def _():
        barrier = pltpu.get_barrier_semaphore()
        pl.semaphore_signal(
            barrier,
            inc=1,
            device_id={"rep": bit_peer("rep", 0)},
            device_id_type=pl.DeviceIdType.MESH,
        )
        pl.semaphore_wait(barrier, 1)
        total = None
        for k, (low, dup, hid, cot, mix, brl) in enumerate(groups):
            lt[k] = low[...].T
            part = dot_tn(mix[...], brl[...])
            total = part if total is None else total + part
        spread(2, 0, total)

    @pl.when(n < chunks)
    def _():
        up = down = None
        for k, (low, dup, hid, cot, mix, brl) in enumerate(groups):
            u = dot_nn(lt[k], dup[...])
            d = dot_tn(hid[...], cot[...])
            up = u if up is None else up + u
            down = d if down is None else down + d
        spread(0, n, down)
        spread(1, n, up)

    def merged(t, slot, out_ref):
        copy(t, slot).wait()
        keep, got = keeps[t], gets[t]
        for k in range(keep.shape[1]):
            out_ref[k] = (keep[slot, k].astype(f32) + got[slot, k].astype(f32)).astype(bf16)

    @pl.when(n > 0)
    def _():
        merged(0, n - 1, down_ref)
        merged(1, n - 1, up_ref)

    @pl.when(n == chunks)
    def _():
        merged(2, 0, proj_ref)


def weight_grads(groups, tok, width, hidden, seqs, reps):
    chunk = 768
    chunks = hidden // chunk
    last = chunks - 1
    full = pl.BlockSpec((tok, width), lambda n: (0, 0))
    part = pl.BlockSpec((tok, chunk), lambda n: (0, jnp.minimum(n, last)))
    down_rows, up_rows = hidden // seqs // reps, width // seqs // reps
    per = chunk // down_rows // 2
    blocks = seqs * reps // 2
    shapes = [(chunks, per, down_rows, width), (chunks, blocks, up_rows, chunk), (1, blocks, up_rows, width)]
    boxes = [pltpu.VMEM(s, bf16) for s in shapes]
    return pl.pallas_call(
        functools.partial(weight_grad_body, chunks=chunks),
        grid=(chunks + 1,),
        in_specs=[full, part, part, full, full, full] * 2,
        out_specs=[
            pl.BlockSpec((per, down_rows, width), lambda n: (jnp.maximum(n - 1, 0), 0, 0)),
            pl.BlockSpec((blocks, up_rows, chunk), lambda n: (0, 0, jnp.maximum(n - 1, 0))),
            pl.BlockSpec((blocks, up_rows, width), lambda n: (0, 0, 0)),
        ],
        out_shape=[
            jax.ShapeDtypeStruct((blocks, down_rows, width), bf16),
            jax.ShapeDtypeStruct((blocks, up_rows, hidden), bf16),
            jax.ShapeDtypeStruct((blocks, up_rows, width), bf16),
        ],
        scratch_shapes=[pltpu.VMEM((2, width, tok), bf16)]
        + boxes
        + boxes
        + boxes
        + [pltpu.SemaphoreType.DMA((2, s[0])) for s in shapes],
        compiler_params=pltpu.CompilerParams(
            vmem_limit_bytes=VMEM, collective_id=3, has_side_effects=True
        ),
        cost_estimate=pl.CostEstimate(
            flops=4 * tok * width * (2 * hidden + width),
            bytes_accessed=30_000_000,
            transcendentals=0,
        ),
        name="weight_grads",
    )(*[a for g in groups for a in g])


def swap(block, axis, bit):
    count = lax.axis_size(axis)
    return lax.ppermute(block, axis, [(n, n ^ (1 << bit)) for n in range(count)])


def bits_of(count):
    return count.bit_length() - 1


def reduce_rows(x, order):
    seqs, reps = lax.axis_size("seq"), lax.axis_size("rep")
    rows, cols = x.shape
    sb, rb = bits_of(seqs), bits_of(reps)
    y = x.reshape((2,) * (sb + rb) + (rows // (seqs * reps), cols))
    names = [("seq", b) for b in reversed(range(sb))] + [("rep", b) for b in reversed(range(rb))]
    for step in order(sb, rb):
        at = names.index(step)
        axis, bit = step
        mine = (lax.axis_index(axis) >> bit) & 1
        send = lax.dynamic_index_in_dim(y, 1 - mine, at, keepdims=False)
        keep = lax.dynamic_index_in_dim(y, mine, at, keepdims=False)
        got = swap(send.astype(x.dtype), axis, bit)
        y = (keep.astype(f32) + got.astype(f32)).astype(x.dtype)
        names.pop(at)
    for bit in range(rb):
        other = swap(y, "rep", bit)
        mine = (lax.axis_index("rep") >> bit) & 1
        y = jnp.where(mine == 0, jnp.stack([y, other]), jnp.stack([other, y]))
        y = y.reshape((-1,) + y.shape[2:])
    return y.astype(f32)


def order_yxz(sb, rb):
    return [("rep", b) for b in range(rb)] + [("seq", b) for b in range(sb)]


def order_xzy(sb, rb):
    return [("rep", 0)] + [("seq", b) for b in range(sb)] + [("rep", b) for b in range(1, rb)]


def on_device(
    layer_in,
    qkv_weight,
    out_weight,
    up_weight,
    down_weight,
    input_gain,
    input_bias,
    mixer_gain,
    mixer_bias,
    block_gain,
    block_bias,
    hidden_gain,
    hidden_bias,
    output_grad,
    seq_lengths,
):
    micro_count, tok, width = layer_in.shape
    reps = lax.axis_size("rep")
    seqs = lax.axis_size("seq")
    span = tok * reps
    heads_dev = HEADS // reps
    cols = heads_dev * HD
    pairs = [[2 * n, 2 * n + 1] for n in range(seqs // 2)]
    fours = [[4 * n + k for k in range(4)] for n in range(seqs // 4)]

    def to_reps(x):
        return lax.all_to_all(x, "rep", 0, 0, tiled=True)

    def to_pair(x):
        return lax.all_to_all(x, "seq", 0, 0, tiled=True, axis_index_groups=pairs)

    def to_four(x):
        return lax.all_to_all(x, "seq", 0, 0, tiled=True, axis_index_groups=fours)

    def row(v):
        return v.reshape(1, -1)

    micros = range(micro_count)
    xp, nt, got_qkv, got_pair, got_four, own_att, got_att, totals = forward_call(
        layer_in, qkv_weight, row(input_gain), row(input_bias), seq_lengths, reps
    )
    residual = [xp[m] for m in micros]
    normed = [nt[m] for m in micros]
    attended = [got_att, to_reps(own_att[1])]

    outputs, branch_grads, head_grads, groups, norm_terms, hidden_terms = [], [], [], [], [], []
    weights = (out_weight, up_weight, down_weight)
    gains = tuple(
        row(v) for v in (mixer_gain, mixer_bias, block_gain, block_bias, hidden_gain, hidden_bias)
    )
    for m in micros:
        out, branch, da, mixl, low, hid, dup, brl, cotp, ng, nh = ffn_call(
            attended[m], residual[m], output_grad, weights, gains, m
        )
        outputs.append(out)
        branch_grads.append(branch)
        head_grads.append(to_reps(da))
        groups.append((low, dup, hid, cotp, mixl, brl))
        norm_terms.append(ng)
        hidden_terms.append(nh)
    seq_bits = bits_of(seqs)
    grads = [
        g.reshape((seqs // 2, 2, reps // 2) + g.shape[1:])
        for g in weight_grads(groups, tok, width, up_weight.shape[1], seqs, reps)
    ]
    token_grad, down_total, up_total, proj_total = backward_call(
        (got_qkv, got_pair, got_four), head_grads, own_att, totals, seq_lengths, grads, seq_bits
    )
    down_total, up_total, proj_total = (
        t.reshape(-1, t.shape[-1]) for t in (down_total, up_total, proj_total)
    )
    token_grads = [token_grad[m] for m in micros]
    input_grads, input_terms = [], []
    grad_qkv = qkv_grad_call(list(zip(normed, token_grads)), tok, width, reps)
    for m in micros:
        grad, terms = input_grad_call(
            token_grads[m], qkv_weight, residual[m], branch_grads[m], row(input_gain), m
        )
        input_grads.append(grad)
        input_terms.append(terms)

    qkv_total = reduce_rows(grad_qkv, order_yxz)
    model = jnp.concatenate([sum(input_terms), sum(norm_terms)], 0)
    norm_total = reduce_rows(model.T, order_yxz)
    hidden_total = reduce_rows(sum(hidden_terms).T, order_yxz)
    return (
        jnp.stack(outputs),
        jnp.stack(input_grads),
        qkv_total,
        proj_total,
        up_total,
        down_total,
        norm_total,
        hidden_total,
    )


def solution(mesh):
    tokens = P(None, ("seq", "rep"), None)
    rows = P("seq", None)
    return jax.shard_map(
        on_device,
        mesh=mesh,
        in_specs=(tokens,) + (P(),) * 12 + (tokens, P()),
        out_specs=(tokens, tokens) + (rows,) * 6,
        check_vma=False,
    )
```

```python
import functools
import math

import jax
import jax.numpy as jnp
from jax import lax
from jax.experimental import pallas as pl
from jax.experimental.pallas import tpu as pltpu
from jax.sharding import PartitionSpec as P

HEADS = 12
HD = 64
HPAD = 80
CLASS_SLOT = (0, 2, 1, 3)
LOG2E = 1.4426950408889634
NEG = -1e30
EPS = 1e-05
VMEM = 56 << 20

f32 = jnp.float32
bf16 = jnp.bfloat16


def dot_nn(a, b):
    return lax.dot_general(a, b, (((1,), (0,)), ((), ())), preferred_element_type=f32)


def dot_nt(a, b):
    return lax.dot_general(a, b, (((1,), (1,)), ((), ())), preferred_element_type=f32)


def dot_tn(a, b):
    return lax.dot_general(a, b, (((0,), (0,)), ((), ())), preferred_element_type=f32)


def class_slot(cls):
    return jnp.where(cls == 1, 2, jnp.where(cls == 2, 1, cls))


def rel_pos(shape, dim, offset, pattern):
    i = lax.broadcasted_iota(jnp.int32, shape, dim) + offset
    if pattern == 0:
        return (i % 128) * 4 + class_slot((i // 128) % 4)
    if pattern == 1:
        return (i // 256) * 512 + (i % 128) * 4 + ((i // 128) % 2) * 2
    return i


def doc_rows(len_ref, micro, start, dilation, count):
    pos = lax.broadcasted_iota(jnp.int32, (1, count), 1) * dilation + start
    edge = len_ref[micro, 0]
    doc = (pos >= edge).astype(jnp.int32)
    for n in range(1, len_ref.shape[1] - 1):
        edge = edge + len_ref[micro, n]
        doc = doc + (pos >= edge).astype(jnp.int32)
    return doc


def segment_start(pattern, span):
    team = 2**pattern
    return (lax.axis_index("seq") // team) * (team * span)


def split3(x):
    hi = x.astype(bf16).astype(f32)
    mid = (x - hi).astype(bf16).astype(f32)
    return hi, mid, x - hi - mid


def stat_rows(rows, count):
    r = lax.broadcasted_iota(jnp.int32, (HPAD - HD, count), 0)
    out = jnp.zeros((HPAD - HD, count), f32)
    for n, row in enumerate(rows):
        out = jnp.where(r == n, row, out)
    return out.astype(bf16)


def shift():
    return lax.axis_index("rep") % 2


def taker():
    return shift()


def owner_of(j):
    return (j + shift()) % 4


def slot_of(place):
    return (place + 4 - shift()) % 4


def clamp_slot(j):
    return j - j // 3


def place1(j):
    return (taker(), 1) if j == 2 else (j, 0)


def smem_spec():
    return pl.BlockSpec(memory_space=pltpu.SMEM)


def vmem_spec():
    return pl.BlockSpec(memory_space=pltpu.VMEM)


def onehot_rows(tok):
    i = lax.broadcasted_iota(jnp.int32, (tok, tok), 0)
    t = lax.broadcasted_iota(jnp.int32, (tok, tok), 1)
    return ((i % 128) * 4 + class_slot(i // 128) == t).astype(bf16)


def onehot_cols(tok):
    t = lax.broadcasted_iota(jnp.int32, (tok, tok), 0)
    i = lax.broadcasted_iota(jnp.int32, (tok, tok), 1)
    return ((i % 128) * 4 + class_slot(i // 128) == t).astype(bf16)


def normalize(x):
    c = x - jnp.mean(x, axis=-1, keepdims=True)
    rstd = lax.rsqrt(jnp.mean(c * c, axis=-1, keepdims=True) + EPS)
    return c * rstd, rstd


def norm_back(grad, gain, xhat, rstd):
    dn = grad * gain
    low = jnp.mean(dn, axis=-1, keepdims=True)
    along = jnp.mean(dn * xhat, axis=-1, keepdims=True)
    dx = rstd * (dn - low - xhat * along)
    return dx, jnp.sum(grad * xhat, 0, keepdims=True), jnp.sum(grad, 0, keepdims=True)


CHUNK = 512
SQRT_HALF = 0.7071067811865476
INV_SQRT_2PI = 0.3989422804014327


def ffn_body(
    att_ref,
    xp_ref,
    cot_ref,
    wo_hbm,
    wu_hbm,
    wd_hbm,
    mg_ref,
    mb_ref,
    bg_ref,
    bb_ref,
    hg_ref,
    hb_ref,
    out_ref,
    branch_ref,
    da_ref,
    mix_ref,
    low_ref,
    hid_ref,
    dup_ref,
    brl_ref,
    cotp_ref,
    ng_ref,
    nh_ref,
    wo,
    wu,
    wd,
    g_scr,
    dg_scr,
    dn_scr,
    am_scr,
    acc_scr,
    sems,
):
    tok, width = xp_ref.shape
    hidden = hid_ref.shape[1]
    chunks = hidden // CHUNK
    reps, cols, _ = att_ref.shape
    copies = [
        pltpu.make_async_copy(a, b, sems.at[n])
        for n, (a, b) in enumerate(((wo_hbm, wo), (wu_hbm, wu), (wd_hbm, wd)))
    ]
    for c in copies:
        c.start()
    cotp = dot_nn(onehot_rows(tok), cot_ref[...])
    cotp_ref[...] = cotp.astype(bf16)
    att = att_ref[...].reshape(width, tok).T.astype(f32)
    ahat, _ = normalize(att)
    mix_ref[...] = (ahat * mg_ref[...] + mb_ref[...]).astype(bf16)
    copies[0].wait()
    am = xp_ref[...].astype(f32) + dot_nn(mix_ref[...], wo[...])
    am_scr[...] = am
    bhat, _ = normalize(am)
    low_ref[...] = (bhat * bg_ref[...] + bb_ref[...]).astype(bf16)
    copies[1].wait()

    def lanes(n):
        return pl.ds(pl.multiple_of(n * CHUNK, CHUNK), CHUNK)

    def upward(n, total):
        u = dot_nn(low_ref[...], wu[:, lanes(n)])
        cdf = 0.5 + 0.5 * lax.erf(u * SQRT_HALF)
        g = u * cdf
        g_scr[:, lanes(n)] = g
        dg_scr[:, lanes(n)] = cdf + u * (jnp.exp(u * u * -0.5) * INV_SQRT_2PI)
        return total + jnp.sum(g, 1, keepdims=True)

    mean = lax.fori_loop(0, chunks, upward, jnp.zeros((tok, 1), f32)) / hidden

    def spread(n, total):
        c = g_scr[:, lanes(n)] - mean
        return total + jnp.sum(c * c, 1, keepdims=True)

    var = lax.fori_loop(0, chunks, spread, jnp.zeros((tok, 1), f32)) / hidden
    rstd = lax.rsqrt(var + EPS)
    copies[2].wait()
    acc_scr[...] = jnp.zeros_like(acc_scr)

    def downward(n, sums):
        first, second = sums
        ghat = (g_scr[:, lanes(n)] - mean) * rstd
        g_scr[:, lanes(n)] = ghat
        gain = hg_ref[:, lanes(n)]
        h = (ghat * gain + hb_ref[:, lanes(n)]).astype(bf16)
        hid_ref[:, lanes(n)] = h
        acc_scr[...] += dot_nn(h, wd[lanes(n), :])
        back = dot_nt(cotp_ref[...], wd[lanes(n), :])
        nh_ref[0:1, lanes(n)] = jnp.sum(back * ghat, 0, keepdims=True)
        nh_ref[1:2, lanes(n)] = jnp.sum(back, 0, keepdims=True)
        dn = back * gain
        dn_scr[:, lanes(n)] = dn
        return (
            first + jnp.sum(dn, 1, keepdims=True),
            second + jnp.sum(dn * ghat, 1, keepdims=True),
        )

    zero = jnp.zeros((tok, 1), f32)
    first, second = lax.fori_loop(0, chunks, downward, (zero, zero))
    first, second = first / hidden, second / hidden
    out_ref[...] = dot_nn(onehot_cols(tok), (am_scr[...] + acc_scr[...]).astype(bf16)).astype(bf16)
    acc_scr[...] = jnp.zeros_like(acc_scr)

    def backward(n, carry):
        d = rstd * (dn_scr[:, lanes(n)] - first - g_scr[:, lanes(n)] * second)
        dup = (d * dg_scr[:, lanes(n)]).astype(bf16)
        dup_ref[:, lanes(n)] = dup
        acc_scr[...] += dot_nt(dup, wu[:, lanes(n)])
        return carry

    lax.fori_loop(0, chunks, backward, 0)
    bhat, brstd = normalize(am_scr[...])
    middle, gain_b, bias_b = norm_back(acc_scr[...], bg_ref[...], bhat, brstd)
    branch = cotp_ref[...].astype(f32) + middle
    branch_ref[...] = branch
    brl_ref[...] = branch.astype(bf16)
    att = att_ref[...].reshape(width, tok).T.astype(f32)
    ahat, arstd = normalize(att)
    da, gain_m, bias_m = norm_back(dot_nt(brl_ref[...], wo[...]), mg_ref[...], ahat, arstd)
    da_ref[...] = da.astype(bf16).T.reshape(reps, cols, tok)
    ng_ref[0:1] = gain_m
    ng_ref[1:2] = bias_m
    ng_ref[2:3] = gain_b
    ng_ref[3:4] = bias_b


def ffn_call(att, xp, output_grad, weights, gains, m):
    reps, cols, tok = att.shape
    width = xp.shape[2]
    hidden = weights[1].shape[1]
    vec = vmem_spec()
    shapes = [
        ((tok, width), bf16),
        ((tok, width), f32),
        ((reps, cols, tok), bf16),
        ((tok, width), bf16),
        ((tok, width), bf16),
        ((tok, hidden), bf16),
        ((tok, hidden), bf16),
        ((tok, width), bf16),
        ((tok, width), bf16),
        ((4, width), f32),
        ((2, hidden), f32),
    ]
    return pl.pallas_call(
        ffn_body,
        grid=(1,),
        in_specs=[
            pl.BlockSpec((reps, cols, tok), lambda n: (0, 0, 0)),
            pl.BlockSpec((None, tok, width), lambda n: (m, 0, 0)),
            pl.BlockSpec((None, tok, width), lambda n: (m, 0, 0)),
        ]
        + [pl.BlockSpec(memory_space=pl.ANY)] * 3
        + [pl.BlockSpec(g.shape, lambda n: (0, 0)) for g in gains],
        out_specs=[pl.BlockSpec(s, lambda n, k=len(s): (0,) * k) for s, _ in shapes],
        out_shape=[jax.ShapeDtypeStruct(s, d) for s, d in shapes],
        scratch_shapes=[pltpu.VMEM(w.shape, bf16) for w in weights]
        + [pltpu.VMEM((tok, hidden), f32)] * 3
        + [pltpu.VMEM((tok, width), f32)] * 2
        + [pltpu.SemaphoreType.DMA((3,))],
        compiler_params=pltpu.CompilerParams(vmem_limit_bytes=VMEM),
        cost_estimate=pl.CostEstimate(
            flops=4 * tok * width * (2 * hidden + width),
            bytes_accessed=25_000_000,
            transcendentals=2 * tok * hidden,
        ),
        name=f"ffn_{m}",
    )(att, xp, output_grad, *weights, *gains)


def rep_peer(k):
    count = lax.axis_size("rep")
    return (lax.axis_index("rep") + k) % count


def team_place():
    return lax.axis_index("seq") % 4


def team_member(k):
    s = lax.axis_index("seq")
    return s // 4 * 4 + (s + k) % 4


def pair_partner():
    s = lax.axis_index("seq")
    return s + 1 - 2 * (s % 2)


def remote(src, dst, send_sem, recv_sem, axis, peer):
    return pltpu.make_async_remote_copy(
        src_ref=src,
        dst_ref=dst,
        send_sem=send_sem,
        recv_sem=recv_sem,
        device_id={axis: peer},
        device_id_type=pl.DeviceIdType.MESH,
    )


def meet_peers():
    barrier = pltpu.get_barrier_semaphore()
    for k in range(1, 4):
        for axis, peer in (("rep", rep_peer(k)), ("seq", team_member(k))):
            pl.semaphore_signal(
                barrier, inc=1, device_id={axis: peer}, device_id_type=pl.DeviceIdType.MESH
            )
    pl.semaphore_wait(barrier, 6)


def head_rows(j):
    return pl.ds(pl.multiple_of(j * HD, HD), HD)


def attend(block, doc, put, ks, qs, pattern, count, lanes):
    kb = min(512, lanes)
    for s in range(0, count, kb):
        sl = slice(s, s + kb)
        r = lax.broadcasted_iota(jnp.int32, (HD, kb), 0)
        same = doc[:, sl] == r
        aux_k = jnp.where(same, 1.0, 0.0).astype(bf16)
        aux_q = jnp.where(same | (r >= 4), 0.0, NEG).astype(bf16)
        q = (block(0, s, kb).astype(f32) * 0.125).astype(bf16)
        qs[:, sl] = jnp.concatenate([q, aux_q], 0)
        ks[sl, :] = jnp.concatenate([block(1, s, kb), aux_k], 0).T

    qb = 256
    grain = 512 if pattern == 0 else 256

    def tiles(i):
        low = (i * qb) // grain * grain
        out = [(s, min(512, low - s), False) for s in range(0, low, 512)]
        return out + [(low, grain, True)]

    def scores(i):
        out = []
        for s, size, diagonal in tiles(i):
            t = dot_nn(ks[s : s + size, :], qs[:, i * qb : (i + 1) * qb])
            if diagonal:
                keep = rel_pos((size, qb), 0, s % 512, pattern) <= rel_pos(
                    (size, qb), 1, (i * qb) % 512, pattern
                )
                t = jnp.where(keep, t, NEG)
            out.append(t)
        return out

    following = scores(0)
    for i in range(count // qb):
        current = following
        if (i + 1) * qb < count:
            following = scores(i + 1)
        top = functools.reduce(jnp.maximum, [jnp.max(t, 0, keepdims=True) for t in current])
        top2 = top * LOG2E
        acc, total = None, None
        for t, (s, size, _) in zip(current, tiles(i)):
            p = jnp.exp2(t * LOG2E - top2)
            part = jnp.sum(p, 0, keepdims=True)
            out = dot_nn(block(2, s, size), p.astype(bf16))
            acc = out if acc is None else acc + out
            total = part if total is None else total + part
        lse = top + jnp.log(total)
        put(i * qb, qb, (acc / total).astype(bf16), stat_rows(split3(lse), qb))


def forward_body(
    x_ref,
    w_ref,
    gain_ref,
    bias_ref,
    len_ref,
    xp_ref,
    nt_ref,
    r_out,
    p1_out,
    p2_out,
    att_ref,
    got_ref,
    mix_ref,
    sent,
    r,
    stage1,
    stage2,
    p1,
    p2,
    o0,
    o1,
    o2,
    b1,
    b2,
    ks,
    qs,
    qkv_sems,
    p1_sems,
    p2_sems,
    b1_sems,
    b2_sems,
    att_sems,
    out_sems,
):
    micros, tok, width = x_ref.shape
    reps = r.shape[1]
    span = tok * reps
    cols = width // reps
    me = lax.axis_index("rep")
    place = team_place()
    side = place % 2
    meet_peers()

    def qkv_copy(m, j, k, source):
        return remote(
            sent.at[m, rep_peer(k), :, head_rows(j)],
            r.at[m, source, :, head_rows(j)],
            qkv_sems.at[0, m, j, k - 1],
            qkv_sems.at[1, m, j, k - 1],
            "rep",
            rep_peer(k),
        )

    def p1_copy(m, s, source):
        return remote(
            stage1.at[m, s],
            p1.at[m, source, s],
            p1_sems.at[0, m, s],
            p1_sems.at[1, m, s],
            "seq",
            pair_partner(),
        )

    def p2_copy(m, k, source):
        return remote(
            stage2.at[m, (place + k) % 4],
            p2.at[m, source],
            p2_sems.at[0, m, k - 1],
            p2_sems.at[1, m, k - 1],
            "seq",
            team_member(k),
        )

    def b1_copy(m, s, source):
        return remote(
            o1.at[m, s, 1 - side],
            b1.at[m, source, s],
            b1_sems.at[0, m, s],
            b1_sems.at[1, m, s],
            "seq",
            pair_partner(),
        )

    def b2_copy(m, k, source):
        return remote(
            o2.at[m, (place + k) % 4],
            b2.at[m, source],
            b2_sems.at[0, m, k - 1],
            b2_sems.at[1, m, k - 1],
            "seq",
            team_member(k),
        )

    def att_copy(k, source):
        return remote(
            att_ref.at[0, rep_peer(k)],
            got_ref.at[source],
            att_sems.at[0, k - 1],
            att_sems.at[1, k - 1],
            "rep",
            rep_peer(k),
        )

    def out_copies(m):
        return (
            pltpu.make_async_copy(r.at[m], r_out.at[m], out_sems.at[m, 0]),
            pltpu.make_async_copy(p1.at[m], p1_out.at[m], out_sems.at[m, 1]),
            pltpu.make_async_copy(p2.at[m], p2_out.at[m], out_sems.at[m, 2]),
        )

    def project(m, carry):
        xp = dot_nn(onehot_rows(tok), x_ref[m])
        xp_ref[m] = xp.astype(bf16)
        xhat, _ = normalize(xp)
        n = (xhat * gain_ref[...] + bias_ref[...]).astype(bf16)
        nt_ref[m] = n.T
        for c in range(3):
            t = dot_nn(n, w_ref[:, c * width : (c + 1) * width]).astype(bf16).T
            for d in range(reps):
                sent[m, d, c] = t[d * cols : (d + 1) * cols]
        for j in range(3):
            for k in range(1, 4):
                qkv_copy(m, j, k, me).start()
        r[m, me] = sent[m, me]
        return carry

    lax.fori_loop(0, micros, project, 0)

    def half(j):
        return pl.ds(pl.multiple_of(((3 * me + j) % 2) * 256, 256), 256)

    def quarter_at(j):
        c = (3 * me + j) % 4
        return c % 2 * 2 + c // 2

    def quarter(j):
        return pl.ds(pl.multiple_of(quarter_at(j) * 128, 128), 128)

    def send_first(m):
        for b in range(reps):
            bl = slice(b * 256, (b + 1) * 256)
            stage1[m, 0, :, :, bl] = r[m, b, :, head_rows(1 - side), half(1 - side)]
            p1[m, side, 0, :, :, bl] = r[m, b, :, head_rows(side), half(side)]
        p1_copy(m, 0, side).start()

    def send_second(m):
        for b in range(reps):
            bl = slice(b * 256, (b + 1) * 256)
            piece = r[m, b, :, head_rows(2), half(2)]
            stage1[m, 1, :, :, bl] = piece
            p1[m, side, 1, :, :, bl] = piece

        @pl.when(side != taker())
        def _():
            p1_copy(m, 1, side).start()

        for g in range(4):
            j = clamp_slot(slot_of(g))
            for b in range(reps):
                stage2[m, g, :, :, b * 128 : (b + 1) * 128] = r[m, b, :, head_rows(j), quarter(j)]
        p2[m, place] = stage2[m, place]
        for k in range(1, 4):

            @pl.when(slot_of(place + k) < 3)
            def _():
                p2_copy(m, k, place).start()

    def mix_all(m):
        b1_copy(m, 0, 1 - side).wait_recv()

        @pl.when(side != taker())
        def _():
            b1_copy(m, 1, 1 - side).wait_recv()

        for k in range(1, 4):

            @pl.when(slot_of(place + 4 - k) < 3)
            def _():
                b2_copy(m, k, (place + 4 - k) % 4).wait_recv()

        def stat(tile):
            t = tile[HD:, :].astype(f32)
            return t[0:1] + t[1:2] + t[2:3]

        mix_ref[m] = jnp.zeros(mix_ref.shape[1:], f32)
        for j in range(3):
            e, s = place1(j)
            for b in range(reps):
                for a in range(4):
                    la = slice(a * 128, (a + 1) * 128)
                    lb = b * 256 + (a % 2) * 128
                    t0 = o0[m, j, b, :, la]
                    t1 = b1[m, e, s, :, lb : lb + 128]
                    t2 = b2[m, owner_of(j), :, b * 128 : (b + 1) * 128]
                    l0 = stat(t0)
                    l1 = jnp.where((3 * me + j) % 2 == a // 2, stat(t1), NEG)
                    l2 = jnp.where(quarter_at(j) == a, stat(t2), NEG)
                    top = jnp.maximum(jnp.maximum(l0, l1), l2)
                    e0, e1, e2 = jnp.exp(l0 - top), jnp.exp(l1 - top), jnp.exp(l2 - top)
                    total = e0 + e1 + e2
                    inv = 1.0 / total
                    mixed = (
                        t0[:HD].astype(f32) * (e0 * inv)
                        + t1[:HD].astype(f32) * (e1 * inv)
                        + t2[:HD].astype(f32) * (e2 * inv)
                    )
                    att_ref[m, b, j * HD : (j + 1) * HD, la] = mixed.astype(bf16)
                    col = b * tok + a * 128
                    mix_ref[m, j : j + 1, col : col + 128] = top + jnp.log(total)

    docs_of = lambda m, pattern: doc_rows(
        len_ref, m, segment_start(pattern, span), 2**pattern, span
    )

    def micro(m, carry):
        def local(j, inner):
            for k in range(1, 4):
                qkv_copy(m, j, k, (me + reps - k) % reps).wait_recv()

            @pl.when(j == 1)
            def _():
                send_first(m)

            @pl.when(j == 2)
            def _():
                send_second(m)

            def block(c, start, size):
                at = start % tok
                return r[m, start // tok, c, head_rows(j), at : at + size]

            def put(start, size, out, stats):
                at = start % tok
                o0[m, j, start // tok, :HD, at : at + size] = out
                o0[m, j, start // tok, HD:, at : at + size] = stats

            attend(block, docs_of(m, 0), put, ks, qs, 0, span, tok)
            return inner

        lax.fori_loop(0, 3, local, 0)

        @pl.when(m == 1)
        def _():
            mix_all(0)
            for k in range(1, 4):
                att_copy(k, me).start()
            got_ref[me] = att_ref[0, me]

        wide = span // 2

        def paired(s):
            p1_copy(m, s, 1 - side).wait_recv()

            def block(c, start, size):
                at = start % wide
                return p1[m, start // wide, s, c, :, at : at + size]

            def put(start, size, out, stats):
                at = start % wide
                o1[m, s, start // wide, :HD, at : at + size] = out
                o1[m, s, start // wide, HD:, at : at + size] = stats

            attend(block, docs_of(m, 1), put, ks, qs, 1, span, wide)
            b1[m, side, s] = o1[m, s, side]
            b1_copy(m, s, side).start()

        def each_pair(s, inner):
            @pl.when((s == 0) | (side == taker()))
            def _():
                paired(s)

            return inner

        lax.fori_loop(0, 2, each_pair, 0)

        def block(c, start, size):
            at = start % tok
            return p2[m, start // tok, c, :, at : at + size]

        def put(start, size, out, stats):
            at = start % tok
            o2[m, start // tok, :HD, at : at + size] = out
            o2[m, start // tok, HD:, at : at + size] = stats

        @pl.when(slot_of(place) < 3)
        def _():
            for k in range(1, 4):
                p2_copy(m, k, (place + 4 - k) % 4).wait_recv()
            attend(block, docs_of(m, 2), put, ks, qs, 2, span, tok)
            b2[m, place] = o2[m, place]
            for k in range(1, 4):
                b2_copy(m, k, place).start()

        for c in out_copies(m):
            c.start()
        return carry

    lax.fori_loop(0, micros, micro, 0)
    mix_all(1)
    for k in range(1, 4):
        att_copy(k, (me + reps - k) % reps).wait_recv()
        att_copy(k, me).wait_send()

    def finish(m, carry):
        for c in out_copies(m):
            c.wait()
        for k in range(1, 4):
            for j in range(3):
                qkv_copy(m, j, k, me).wait_send()

            @pl.when(slot_of(place + k) < 3)
            def _():
                p2_copy(m, k, place).wait_send()

            @pl.when(slot_of(place) < 3)
            def _():
                b2_copy(m, k, place).wait_send()

        p1_copy(m, 0, side).wait_send()
        b1_copy(m, 0, side).wait_send()

        @pl.when(side != taker())
        def _():
            p1_copy(m, 1, side).wait_send()

        @pl.when(side == taker())
        def _():
            b1_copy(m, 1, side).wait_send()

        return carry

    lax.fori_loop(0, micros, finish, 0)


def forward_call(layer_in, weight, gain, bias, lengths, reps):
    micros, tok, width = layer_in.shape
    span, cols = tok * reps, width // reps
    any_spec = pl.BlockSpec(memory_space=pl.ANY)
    outs = [
        ((micros, tok, width), bf16, vmem_spec()),
        ((micros, width, tok), bf16, vmem_spec()),
        ((micros, reps, 3, cols, tok), bf16, any_spec),
        ((micros, 2, 2, 3, HD, span // 2), bf16, any_spec),
        ((micros, 4, 3, HD, span // 4), bf16, any_spec),
        ((micros, reps, cols, tok), bf16, vmem_spec()),
        ((reps, cols, tok), bf16, vmem_spec()),
        ((micros, 8, span), f32, vmem_spec()),
    ]

    def vm(*shape):
        return pltpu.VMEM(shape, bf16)

    dma = pltpu.SemaphoreType.DMA
    return pl.pallas_call(
        forward_body,
        in_specs=[vmem_spec()] * 4 + [smem_spec()],
        out_specs=[o[2] for o in outs],
        out_shape=[jax.ShapeDtypeStruct(o[0], o[1]) for o in outs],
        scratch_shapes=[
            vm(micros, reps, 3, cols, tok),
            vm(micros, reps, 3, cols, tok),
            vm(micros, 2, 3, HD, span // 2),
            vm(micros, 4, 3, HD, span // 4),
            vm(micros, 2, 2, 3, HD, span // 2),
            vm(micros, 4, 3, HD, span // 4),
            vm(micros, 3, reps, HPAD, tok),
            vm(micros, 2, 2, HPAD, span // 2),
            vm(micros, 4, HPAD, span // 4),
            vm(micros, 2, 2, HPAD, span // 2),
            vm(micros, 4, HPAD, span // 4),
            vm(span, 128),
            vm(128, span),
            dma((2, micros, 3, 3)),
            dma((2, micros, 2)),
            dma((2, micros, 3)),
            dma((2, micros, 2)),
            dma((2, micros, 3)),
            dma((2, 3)),
            dma((micros, 3)),
        ],
        compiler_params=pltpu.CompilerParams(
            vmem_limit_bytes=VMEM, collective_id=1, has_side_effects=True
        ),
        cost_estimate=pl.CostEstimate(
            flops=60_000_000_000, bytes_accessed=30_000_000, transcendentals=30_000_000
        ),
        name="forward",
    )(layer_in, weight, gain, bias, lengths)


def bit_of(axis, bit):
    return lax.axis_index(axis) // (1 << bit) % 2


def bit_peer(axis, bit):
    return lax.axis_index(axis) + (1 << bit) * (1 - 2 * bit_of(axis, bit))


def attend_back(block, gblock, doc, put, scr, pattern, count, lanes):
    ks, vs, qs, qr, gs, gr, dq = scr
    bs = min(512, lanes)
    zeros = jnp.zeros((HD, bs), bf16)
    r = lax.broadcasted_iota(jnp.int32, (HD, bs), 0)
    fill = jnp.zeros((HD - 32, bs), bf16)
    for s in range(0, count, bs):
        sl = slice(s, s + bs)
        same = doc[:, sl] == r
        aux_k = jnp.where(same | ((r >= 16) & (r < 19)), 1.0, 0.0).astype(bf16)
        aux_q = jnp.where(same | (r >= 4), 0.0, NEG).astype(bf16)
        aux_v = jnp.where((r >= 19) & (r < 21), 1.0, 0.0).astype(bf16)
        q = (block(0, s, bs).astype(f32) * 0.125).astype(bf16)
        tile = gblock(s, bs)
        g, stats = tile[:HD], tile[HD:]
        qs[:, sl] = jnp.concatenate([q, aux_q[:16], stats, fill], 0)
        gs[:, sl] = jnp.concatenate([g, zeros[:16], stats, fill], 0)
        qr[sl, :] = jnp.concatenate([q, zeros], 0).T
        gr[sl, :] = jnp.concatenate([g, zeros], 0).T
        ks[sl, :] = jnp.concatenate([block(1, s, bs), aux_k], 0).T
        vs[sl, :] = jnp.concatenate([block(2, s, bs), aux_v], 0).T

    keep = rel_pos((bs, bs), 0, 0, pattern) <= rel_pos((bs, bs), 1, 0, pattern)
    for j in range(count // bs):
        jl = slice(j * bs, (j + 1) * bs)
        dva, dka = None, None
        for i in range(j, count // bs):
            il = slice(i * bs, (i + 1) * bs)
            p = jnp.exp2(dot_nn(ks[jl, :], qs[:, il]) * LOG2E)
            if i == j:
                p = jnp.where(keep, p, 0.0)
            dp = dot_nn(vs[jl, :], gs[:, il])
            ds = (p * dp).astype(bf16)
            dvi = dot_nn(p.astype(bf16), gr[il, :])
            dki = dot_nn(ds, qr[il, :])
            dva = dvi if dva is None else dva + dvi
            dka = dki if dka is None else dka + dki
            dqi = dot_nn(block(1, j * bs, bs), ds) * 0.125
            if j == 0:
                dq[:, il] = dqi
            else:
                dq[:, il] += dqi
        put(1, j * bs, bs, dka.T[:HD].astype(bf16))
        put(2, j * bs, bs, dva.T[:HD].astype(bf16))
        put(0, j * bs, bs, dq[:, jl].astype(bf16))


class Halving:
    def __init__(self, source, steps, buffers, gathered, out, sems):
        self.source, self.steps, self.buffers = source, steps, buffers
        self.gathered, self.out, self.sems = gathered, out, sems
        self.names = ["high", "z", "x", "y"]
        self.at = 0
        self.pending = None

    def pick(self, ref, axis, name, index):
        lead = (slice(None),) * axis
        if name == "high":
            half = ref.shape[axis] // 2
            return lead + (pl.ds(index * half, half),)
        return lead + (index,)

    def start(self):
        if self.at < len(self.steps):
            name, axis_name, bit = self.steps[self.at]
            axis = self.names.index(name)
            mine = bit_of(axis_name, bit)
            target = self.buffers[self.at]
            copy = remote(
                self.source.at[self.pick(self.source, axis, name, 1 - mine)],
                target,
                self.sems.at[0, self.at],
                self.sems.at[1, self.at],
                axis_name,
                bit_peer(axis_name, bit),
            )
            copy.start()
            self.pending = ("sum", copy, target, self.pick(self.source, axis, name, mine))
            if name != "high":
                self.names.pop(axis)
            return
        stage = self.at - len(self.steps)
        y, c = bit_of("rep", 1), bit_of("rep", 0)
        if stage == 0:
            self.gathered[y, c] = self.source[0]
            part, landing, bit = (y, c), (1 - y, c), 1
        elif stage == 1:
            part, landing, bit = (slice(None), c), (slice(None), 1 - c), 0
        else:
            self.pending = None
            return
        copy = lambda place: remote(
            self.gathered.at[part],
            self.gathered.at[place],
            self.sems.at[0, self.at],
            self.sems.at[1, self.at],
            "rep",
            bit_peer("rep", bit),
        )
        copy(part).start()
        self.pending = ("gather", copy(part), copy(landing), None)

    def finish(self):
        kind, first, second, mine = self.pending
        if kind == "sum":
            first.wait()
            rows = second.shape[0]

            def add(n, carry):
                at = (n,) if mine[0] == slice(None) else None
                if at is None:
                    head = mine[0]
                    base = head.start if isinstance(head, pl.Slice) else None
                    value = self.source[(base + n,) + mine[1:]]
                else:
                    value = self.source[at + mine[1:]]
                second[n] = (second[n].astype(f32) + value.astype(f32)).astype(bf16)
                return carry

            lax.fori_loop(0, rows, add, 0)
            self.source = second
        else:
            first.wait_send()
            second.wait_recv()
        self.at += 1

    def pump(self):
        if self.pending is not None:
            self.finish()
            self.start()

    def drain(self):
        while self.pending is not None:
            self.pump()
        self.out[...] = self.gathered[...]


def reduce_steps(order, seq_bits):
    steps = []
    for name in order:
        if name == "y":
            steps.append(("y", "rep", 1))
        elif name == "x":
            steps.append(("x", "seq", 0))
        elif name == "z":
            steps.append(("z", "seq", 1))
        else:
            steps += [("high", "seq", b) for b in range(seq_bits - 1, 1, -1)]
    return steps


def reduce_buffers(shape, steps):
    high, rows, cols = shape[0], shape[4], shape[5]
    left = 3
    out = []
    for name, _, _ in steps:
        if name == "high":
            high //= 2
        else:
            left -= 1
        out.append((high,) + (2,) * left + (rows, cols))
    return out


def grad_parts(width, hidden):
    return (
        (0, slice(0, width), "yzhx"),
        (1, slice(0, hidden // 2), "zhyx"),
        (1, slice(hidden // 2, hidden), "xyzh"),
        (2, slice(0, width), "xyzh"),
    )


def backward_body(
    r_hbm,
    p1_hbm,
    p2_hbm,
    da0_ref,
    da1_ref,
    att_ref,
    mix_ref,
    len_ref,
    w0_ref,
    w1_ref,
    w2_ref,
    tg_ref,
    t0_ref,
    t1_ref,
    t2_ref,
    *scratch,
    seq_bits,
):
    (r, p1, p2, g0, g1s, g2s, g1, g2, d1, d2, e1, e2, sums, ks, vs, qs, qr, gs, gr, dq) = scratch[:20]
    load_sems, g1_sems, g2_sems, d1_sems, d2_sems, tg_sems, tg1_sems, own_sems = scratch[20:28]
    rest = list(scratch[28:])
    halvings = []
    sources, outs = (w0_ref, w1_ref, w2_ref), (t0_ref, t1_ref, t2_ref)
    for n, lanes, order in grad_parts(w0_ref.shape[-1], w1_ref.shape[-1]):
        steps = reduce_steps(order, seq_bits)
        buffers = [rest.pop(0) for _ in steps]
        gathered, sems = rest.pop(0), rest.pop(0)
        source = sources[n].at[:, :, :, :, :, lanes]
        out = outs[n].at[:, :, :, lanes]
        halvings.append(Halving(source, steps, buffers, gathered, out, sems))
    reps, cols, tok = da0_ref.shape
    micros = att_ref.shape[0]
    span = tok * reps
    wide = span // 2
    me = lax.axis_index("rep")
    place = team_place()
    side = place % 2
    scr = (ks, vs, qs, qr, gs, gr, dq)

    barrier = pltpu.get_barrier_semaphore()
    peers = [("rep", rep_peer(k)) for k in range(1, 4)]
    peers += [("seq", team_member(k)) for k in range(1, 4)]
    peers += [("seq", bit_peer("seq", b)) for b in range(2, seq_bits)]
    for axis, peer in peers:
        pl.semaphore_signal(
            barrier, inc=1, device_id={axis: peer}, device_id_type=pl.DeviceIdType.MESH
        )
    load_r = lambda m: pltpu.make_async_copy(r_hbm.at[m], r, load_sems.at[0])
    load_1 = lambda m: pltpu.make_async_copy(p1_hbm.at[m], p1, load_sems.at[1])
    load_2 = lambda m: pltpu.make_async_copy(p2_hbm.at[m], p2, load_sems.at[2])
    load_r(0).start()
    load_1(0).start()
    load_2(0).start()
    pl.semaphore_wait(barrier, len(peers))
    for h in halvings:
        h.start()

    def pump():
        for h in halvings:
            h.pump()

    def g1_copy(m, s, source):
        return remote(
            g1s.at[m, s],
            g1.at[m, source, s],
            g1_sems.at[0, m, s],
            g1_sems.at[1, m, s],
            "seq",
            pair_partner(),
        )

    def g2_copy(m, k, source):
        return remote(
            g2s.at[m, (place + k) % 4],
            g2.at[m, source],
            g2_sems.at[0, m, k - 1],
            g2_sems.at[1, m, k - 1],
            "seq",
            team_member(k),
        )

    def d1_copy(m, s, source):
        return remote(
            d1.at[m, s, 1 - side],
            e1.at[m, source, s],
            d1_sems.at[0, m, s],
            d1_sems.at[1, m, s],
            "seq",
            pair_partner(),
        )

    def d2_copy(m, k, source):
        return remote(
            d2.at[m, (place + k) % 4],
            e2.at[m, source],
            d2_sems.at[0, m, k - 1],
            d2_sems.at[1, m, k - 1],
            "seq",
            team_member(k),
        )

    def tg0_copy(k, source):
        return remote(
            sums.at[0, rep_peer(k)],
            tg_ref.at[0, source],
            tg_sems.at[0, k - 1],
            tg_sems.at[1, k - 1],
            "rep",
            rep_peer(k),
        )

    def tg1_copy(j, k, source):
        return remote(
            sums.at[1, rep_peer(k), :, head_rows(j)],
            tg_ref.at[1, source, :, head_rows(j)],
            tg1_sems.at[0, j, k - 1],
            tg1_sems.at[1, j, k - 1],
            "rep",
            rep_peer(k),
        )

    own_copy = lambda m: pltpu.make_async_copy(sums.at[m, me], tg_ref.at[m, me], own_sems.at[m])

    def half(j):
        return pl.ds(pl.multiple_of(((3 * me + j) % 2) * 256, 256), 256)

    def quarter_at(j):
        c = (3 * me + j) % 4
        return c % 2 * 2 + c // 2

    def quarter(j):
        return pl.ds(pl.multiple_of(quarter_at(j) * 128, 128), 128)

    for m, da_ref in enumerate((da0_ref, da1_ref)):
        for j in range(3):
            rows = slice(j * HD, (j + 1) * HD)
            for b in range(reps):
                g = da_ref[b, rows, :]
                inner = jnp.sum(
                    g.astype(f32) * att_ref[m, b, rows, :].astype(f32), 0, keepdims=True
                )
                total = mix_ref[m, j : j + 1, b * tok : (b + 1) * tok]
                high, mid, low = split3(-total)
                inner_high, inner_mid, _ = split3(-inner)
                g0[m, j, b, :HD, :] = g
                g0[m, j, b, HD:, :] = stat_rows((high, mid, low, inner_high, inner_mid), tok)
        for b in range(reps):
            bl = slice(b * 256, (b + 1) * 256)
            g1s[m, 0, :, bl] = g0[m, 1 - side, b, :, half(1 - side)]
            g1[m, side, 0, :, bl] = g0[m, side, b, :, half(side)]
            piece = g0[m, 2, b, :, half(2)]
            g1s[m, 1, :, bl] = piece
            g1[m, side, 1, :, bl] = piece
            for g in range(4):
                j = clamp_slot(slot_of(g))
                g2s[m, g, :, b * 128 : (b + 1) * 128] = g0[m, j, b, :, quarter(j)]
        g2[m, place] = g2s[m, place]
        g1_copy(m, 0, side).start()

        @pl.when(side != taker())
        def _():
            g1_copy(m, 1, side).start()

        for k in range(1, 4):

            @pl.when(slot_of(place + k) < 3)
            def _():
                g2_copy(m, k, place).start()

    def docs(m, pattern):
        return doc_rows(len_ref, m, segment_start(pattern, span), 2**pattern, span)

    def own_head(m, j):
        def block(c, start, size):
            at = start % tok
            return r[start // tok, c, head_rows(j), at : at + size]

        def gblock(start, size):
            at = start % tok
            return g0[m, j, start // tok, :, at : at + size]

        def put(c, start, size, value):
            at = start % tok
            sums[m, start // tok, c, head_rows(j), at : at + size] = value

        attend_back(block, gblock, docs(m, 0), put, scr, 0, span, tok)

    def add_others(m, j):
        e, s = place1(j)
        for b in range(reps):
            bl = slice(b * 256, (b + 1) * 256)
            t = sums[m, b, :, j * HD : (j + 1) * HD, half(j)].astype(f32)
            t = t + e1[m, e, s, :, :, bl].astype(f32)
            sums[m, b, :, j * HD : (j + 1) * HD, half(j)] = t.astype(bf16)
            t = sums[m, b, :, j * HD : (j + 1) * HD, quarter(j)].astype(f32)
            t = t + e2[m, owner_of(j), :, :, b * 128 : (b + 1) * 128].astype(f32)
            sums[m, b, :, j * HD : (j + 1) * HD, quarter(j)] = t.astype(bf16)

    def wait_others(m):
        d1_copy(m, 0, 1 - side).wait_recv()

        @pl.when(side != taker())
        def _():
            d1_copy(m, 1, 1 - side).wait_recv()

        for k in range(1, 4):

            @pl.when(slot_of(place + 4 - k) < 3)
            def _():
                d2_copy(m, k, (place + 4 - k) % 4).wait_recv()

    load_r(0).wait()

    def first_heads(j, carry):
        own_head(0, j)
        return carry

    lax.fori_loop(0, 3, first_heads, 0)
    load_r(1).start()

    def others(m):
        def paired(s):
            g1_copy(m, s, 1 - side).wait_recv()

            def block(c, start, size):
                at = start % wide
                return p1[start // wide, s, c, :, at : at + size]

            def gblock(start, size):
                at = start % wide
                return g1[m, start // wide, s, :, at : at + size]

            def put(c, start, size, value):
                at = start % wide
                d1[m, s, start // wide, c, :, at : at + size] = value

            attend_back(block, gblock, docs(m, 1), put, scr, 1, span, wide)
            e1[m, side, s] = d1[m, s, side]
            d1_copy(m, s, side).start()

        def each_pair(s, inner):
            @pl.when((s == 0) | (side == taker()))
            def _():
                paired(s)

            return inner

        load_1(m).wait()
        lax.fori_loop(0, 2, each_pair, 0)
        if m + 1 < micros:
            load_1(m + 1).start()
        pump()
        if m == 1:
            wait_others(0)
            for j in range(3):
                add_others(0, j)
            for k in range(1, 4):
                tg0_copy(k, me).start()
            own_copy(0).start()
        load_2(m).wait()

        def block(c, start, size):
            at = start % tok
            return p2[start // tok, c, :, at : at + size]

        def gblock(start, size):
            at = start % tok
            return g2[m, start // tok, :, at : at + size]

        def put(c, start, size, value):
            at = start % tok
            d2[m, start // tok, c, :, at : at + size] = value

        @pl.when(slot_of(place) < 3)
        def _():
            for k in range(1, 4):
                g2_copy(m, k, (place + 4 - k) % 4).wait_recv()
            attend_back(block, gblock, docs(m, 2), put, scr, 2, span, tok)
            e2[m, place] = d2[m, place]
            for k in range(1, 4):
                d2_copy(m, k, place).start()

        if m + 1 < micros:
            load_2(m + 1).start()

    others(0)
    others(1)
    load_r(1).wait()
    for j in range(3):
        own_head(1, j)
        if j == 0:
            wait_others(1)
        add_others(1, j)
        for k in range(1, 4):
            tg1_copy(j, k, me).start()
        pump()
    own_copy(1).start()
    for h in halvings:
        h.drain()
    for m in range(micros):
        own_copy(m).wait()
        g1_copy(m, 0, side).wait_send()
        d1_copy(m, 0, side).wait_send()

        @pl.when(side != taker())
        def _():
            g1_copy(m, 1, side).wait_send()

        @pl.when(side == taker())
        def _():
            d1_copy(m, 1, side).wait_send()

        for k in range(1, 4):

            @pl.when(slot_of(place + k) < 3)
            def _():
                g2_copy(m, k, place).wait_send()

            @pl.when(slot_of(place) < 3)
            def _():
                d2_copy(m, k, place).wait_send()

    for k in range(1, 4):
        source = (me + reps - k) % reps
        tg0_copy(k, source).wait_recv()
        tg0_copy(k, me).wait_send()
        for j in range(3):
            tg1_copy(j, k, source).wait_recv()
            tg1_copy(j, k, me).wait_send()


def backward_call(pieces, da, att, totals, lengths, grads, seq_bits):
    micros, reps, cols, tok = att.shape
    span = tok * reps
    any_spec = pl.BlockSpec(memory_space=pl.ANY)

    def vm(*shape):
        return pltpu.VMEM(shape, bf16)

    dma = pltpu.SemaphoreType.DMA
    halving = []
    for n, lanes, order in grad_parts(grads[0].shape[-1], grads[1].shape[-1]):
        steps = reduce_steps(order, seq_bits)
        shape = grads[n].shape[:5] + (lanes.stop - lanes.start,)
        halving += [vm(*b) for b in reduce_buffers(shape, steps)]
        halving += [vm(2, 2, *shape[4:]), dma((2, len(steps) + 2))]
    tall, flat = vm(span, 128), vm(128, span)
    outs = [((micros, reps, 3, cols, tok), bf16, any_spec)]
    outs += [((2, 2) + g.shape[4:], bf16, vmem_spec()) for g in grads]
    return pl.pallas_call(
        functools.partial(backward_body, seq_bits=seq_bits),
        in_specs=[any_spec] * 3 + [vmem_spec()] * 4 + [smem_spec()] + [vmem_spec()] * 3,
        out_specs=[o[2] for o in outs],
        out_shape=[jax.ShapeDtypeStruct(o[0], o[1]) for o in outs],
        scratch_shapes=[
            vm(reps, 3, cols, tok),
            vm(2, 2, 3, HD, span // 2),
            vm(4, 3, HD, span // 4),
            vm(micros, 3, reps, HPAD, tok),
            vm(micros, 2, HPAD, span // 2),
            vm(micros, 4, HPAD, span // 4),
            vm(micros, 2, 2, HPAD, span // 2),
            vm(micros, 4, HPAD, span // 4),
            vm(micros, 2, 2, 3, HD, span // 2),
            vm(micros, 4, 3, HD, span // 4),
            vm(micros, 2, 2, 3, HD, span // 2),
            vm(micros, 4, 3, HD, span // 4),
            vm(micros, reps, 3, cols, tok),
            tall,
            tall,
            flat,
            tall,
            flat,
            tall,
            pltpu.VMEM((HD, span), f32),
            dma((3,)),
            dma((2, micros, 2)),
            dma((2, micros, 3)),
            dma((2, micros, 2)),
            dma((2, micros, 3)),
            dma((2, 3)),
            dma((2, 3, 3)),
            dma((micros,)),
            *halving,
        ],
        compiler_params=pltpu.CompilerParams(
            vmem_limit_bytes=60 << 20, collective_id=2, has_side_effects=True
        ),
        cost_estimate=pl.CostEstimate(
            flops=100_000_000_000, bytes_accessed=40_000_000, transcendentals=30_000_000
        ),
        name="backward",
    )(*pieces, *da, att, totals, lengths, *grads)


def split_rows(value, parts, rows):
    mine, other = [], []
    first = bit_of("rep", 0) == 0
    for n in range(parts):
        a = value[(2 * n) * rows : (2 * n + 1) * rows]
        b = value[(2 * n + 1) * rows : (2 * n + 2) * rows]
        mine.append(jnp.where(first, a, b))
        other.append(jnp.where(first, b, a))
    return mine, other


def weight_grad_body(*refs, chunks):
    ins, refs = refs[:12], refs[12:]
    down_ref, up_ref, proj_ref, lt = refs[:4]
    keeps, sends, gets, sems = refs[4:7], refs[7:10], refs[10:13], refs[13:16]
    groups = [ins[:6], ins[6:]]
    n = pl.program_id(0)

    def copy(t, slot):
        return remote(
            sends[t].at[slot],
            gets[t].at[slot],
            sems[t].at[0, slot],
            sems[t].at[1, slot],
            "rep",
            bit_peer("rep", 0),
        )

    def spread(t, slot, value):
        keep = keeps[t]
        parts, rows = keep.shape[1], keep.shape[2]
        mine, other = split_rows(value, parts, rows)
        for k in range(parts):
            keep[slot, k] = mine[k].astype(bf16)
            sends[t][slot, k] = other[k].astype(bf16)
        copy(t, slot).start()

    @pl.when(n == 0)
    def _():
        barrier = pltpu.get_barrier_semaphore()
        pl.semaphore_signal(
            barrier,
            inc=1,
            device_id={"rep": bit_peer("rep", 0)},
            device_id_type=pl.DeviceIdType.MESH,
        )
        pl.semaphore_wait(barrier, 1)
        total = None
        for k, (low, dup, hid, cot, mix, brl) in enumerate(groups):
            lt[k] = low[...].T
            part = dot_tn(mix[...], brl[...])
            total = part if total is None else total + part
        spread(2, 0, total)

    @pl.when(n < chunks)
    def _():
        up = down = None
        for k, (low, dup, hid, cot, mix, brl) in enumerate(groups):
            u = dot_nn(lt[k], dup[...])
            d = dot_tn(hid[...], cot[...])
            up = u if up is None else up + u
            down = d if down is None else down + d
        spread(0, n, down)
        spread(1, n, up)

    def merged(t, slot, out_ref):
        copy(t, slot).wait()
        keep, got = keeps[t], gets[t]
        for k in range(keep.shape[1]):
            out_ref[k] = (keep[slot, k].astype(f32) + got[slot, k].astype(f32)).astype(bf16)

    @pl.when(n > 0)
    def _():
        merged(0, n - 1, down_ref)
        merged(1, n - 1, up_ref)

    @pl.when(n == chunks)
    def _():
        merged(2, 0, proj_ref)


def weight_grads(groups, tok, width, hidden, seqs, reps):
    chunk = 768
    chunks = hidden // chunk
    last = chunks - 1
    full = pl.BlockSpec((tok, width), lambda n: (0, 0))
    part = pl.BlockSpec((tok, chunk), lambda n: (0, jnp.minimum(n, last)))
    down_rows, up_rows = hidden // seqs // reps, width // seqs // reps
    per = chunk // down_rows // 2
    blocks = seqs * reps // 2
    shapes = [(chunks, per, down_rows, width), (chunks, blocks, up_rows, chunk), (1, blocks, up_rows, width)]
    boxes = [pltpu.VMEM(s, bf16) for s in shapes]
    return pl.pallas_call(
        functools.partial(weight_grad_body, chunks=chunks),
        grid=(chunks + 1,),
        in_specs=[full, part, part, full, full, full] * 2,
        out_specs=[
            pl.BlockSpec((per, down_rows, width), lambda n: (jnp.maximum(n - 1, 0), 0, 0)),
            pl.BlockSpec((blocks, up_rows, chunk), lambda n: (0, 0, jnp.maximum(n - 1, 0))),
            pl.BlockSpec((blocks, up_rows, width), lambda n: (0, 0, 0)),
        ],
        out_shape=[
            jax.ShapeDtypeStruct((blocks, down_rows, width), bf16),
            jax.ShapeDtypeStruct((blocks, up_rows, hidden), bf16),
            jax.ShapeDtypeStruct((blocks, up_rows, width), bf16),
        ],
        scratch_shapes=[pltpu.VMEM((2, width, tok), bf16)]
        + boxes
        + boxes
        + boxes
        + [pltpu.SemaphoreType.DMA((2, s[0])) for s in shapes],
        compiler_params=pltpu.CompilerParams(
            vmem_limit_bytes=VMEM, collective_id=3, has_side_effects=True
        ),
        cost_estimate=pl.CostEstimate(
            flops=4 * tok * width * (2 * hidden + width),
            bytes_accessed=30_000_000,
            transcendentals=0,
        ),
        name="weight_grads",
    )(*[a for g in groups for a in g])


TAIL_ORDERS = ("yxzh", "xzhy", "zhyx")


def tail_body(
    tg_hbm,
    w_hbm,
    branch0_hbm,
    branch1_hbm,
    xp_ref,
    nt_ref,
    gain_ref,
    ng0_ref,
    ng1_ref,
    nh0_ref,
    nh1_ref,
    out_ref,
    total_ref,
    norm_ref,
    hidden_ref,
    *scratch,
    seq_bits,
):
    tg, w, branch, acc, keep, send, get, vec, vec_get, load_sems, core_sems, vec_sems = scratch[:12]
    rest = list(scratch[12:])
    micros, tok, width = xp_ref.shape
    reps = tg.shape[2]
    parts, rows = keep.shape[1], keep.shape[2]

    barrier = pltpu.get_barrier_semaphore()
    bits = [("rep", 0), ("rep", 1)] + [("seq", b) for b in range(seq_bits)]
    for axis, bit in bits:
        pl.semaphore_signal(
            barrier,
            inc=1,
            device_id={axis: bit_peer(axis, bit)},
            device_id_type=pl.DeviceIdType.MESH,
        )
    loads = [
        pltpu.make_async_copy(tg_hbm.at[m, :, c], tg.at[m, c], load_sems.at[m * 3 + c])
        for c in range(3)
        for m in range(micros)
    ]
    loads += [pltpu.make_async_copy(w_hbm, w, load_sems.at[6])]
    loads += [
        pltpu.make_async_copy(b, branch.at[m], load_sems.at[7 + m])
        for m, b in enumerate((branch0_hbm, branch1_hbm))
    ]
    for c in loads:
        c.start()
    pl.semaphore_wait(barrier, len(bits))

    def core_copy(c):
        return remote(
            send.at[c],
            get.at[c],
            core_sems.at[0, c],
            core_sems.at[1, c],
            "rep",
            bit_peer("rep", 0),
        )

    def piece(m, c):
        return jnp.concatenate([tg[m, c, r] for r in range(reps)], 0)

    for c in range(3):
        total = None
        for m in range(micros):
            loads[c * micros + m].wait()
            part = dot_nt(nt_ref[m], piece(m, c))
            total = part if total is None else total + part
        mine, other = split_rows(total, parts, rows)
        for k in range(parts):
            keep[c, k] = mine[k].astype(bf16)
            send[c, k] = other[k].astype(bf16)
        core_copy(c).start()

    halvings = []
    for c, order in enumerate(TAIL_ORDERS):
        steps = reduce_steps(order, seq_bits)
        summed = rest.pop(0)
        buffers = [rest.pop(0) for _ in steps]
        gathered, sems = rest.pop(0), rest.pop(0)
        out = total_ref.at[:, :, :, c * width : (c + 1) * width]
        halvings.append(Halving(summed, steps, buffers, gathered, out, sems))

    def core_sum(c):
        core_copy(c).wait()
        summed = halvings[c].source

        def add(z, carry):
            for n in range(8):
                k = z * 8 + n
                total = keep[c, k].astype(f32) + get[c, k].astype(f32)
                summed[z, n // 4, n // 2 % 2, n % 2] = total.astype(bf16)
            return carry

        lax.fori_loop(0, parts // 8, add, 0)
        halvings[c].start()

    loads[6].wait()

    def grad_part(m, c):
        part = dot_nn(w[:, c * width : (c + 1) * width], piece(m, c))
        if c == 0:
            acc[...] = part
        else:
            acc[...] += part

    def grad_end(m):
        xhat, rstd = normalize(xp_ref[m].astype(f32))
        dx, gain_i, bias_i = norm_back(acc[...].T, gain_ref[...], xhat, rstd)
        loads[7 + m].wait()
        total = (branch[m] + dx).astype(bf16)
        out_ref[m] = dot_nn(onehot_cols(tok), total).astype(bf16)
        return gain_i, bias_i

    core_sum(0)
    grad_part(0, 0)
    core_sum(1)
    grad_part(0, 1)
    core_sum(2)
    grad_part(0, 2)
    gain0, bias0 = grad_end(0)

    def pump():
        for h in halvings:
            h.pump()

    pump()
    grad_part(1, 0)
    grad_part(1, 1)
    pump()
    grad_part(1, 2)
    gain1, bias1 = grad_end(1)
    vec[0] = jnp.zeros(vec.shape[1:], f32)
    vec[0, 0:1] = gain0 + gain1
    vec[0, 1:2] = bias0 + bias1
    vec[0, 2:6] = ng0_ref[...] + ng1_ref[...]
    fold = nh0_ref.shape[1] // width
    for n in range(2):
        for k in range(fold):
            cl = slice(k * width, (k + 1) * width)
            row = 8 + n * fold + k
            vec[0, row : row + 1] = nh0_ref[n : n + 1, cl] + nh1_ref[n : n + 1, cl]
    for n, (axis, bit) in enumerate(bits):
        copy = remote(
            vec.at[n],
            vec_get.at[n],
            vec_sems.at[0, n],
            vec_sems.at[1, n],
            axis,
            bit_peer(axis, bit),
        )
        copy.start()
        pump()
        copy.wait()
        vec[n + 1] = vec[n] + vec_get[n]
    s = lax.axis_index("seq")
    last = len(bits)
    seqs = 1 << seq_bits
    cols = vec[last].T
    acc[:, : cols.shape[1]] = cols


    def rows_at(block, size):
        if size % 8 == 0:
            return acc[pl.ds(pl.multiple_of(block * size, 8), size), :16]
        out = cols[:size]
        for n in range(1, width // size):
            out = jnp.where(block == n, cols[n * size : (n + 1) * size], out)
        return out

    norm_ref[...] = rows_at(s, norm_ref.shape[0])[:, :6]
    own = hidden_ref.shape[0]
    per = width // own
    picked = rows_at(s % per, own)
    out = jnp.zeros((own, 2), f32)
    for k in range(fold):
        pair = jnp.concatenate(
            [picked[:, 8 + k : 9 + k], picked[:, 8 + fold + k : 9 + fold + k]], 1
        )
        out = jnp.where(s // per == k, pair, out)
    hidden_ref[...] = out
    for h in halvings:
        h.drain()


def tail_call(tg, weight, branch, xp, nt, gain, ng, nh, seq_bits):
    micros, tok, width = xp.shape
    reps, _, cols = tg.shape[1:4]
    hidden = nh[0].shape[1]
    seqs = 1 << seq_bits
    rows = width // seqs // reps
    parts = seqs * reps // 2
    any_spec = pl.BlockSpec(memory_space=pl.ANY)

    def vm(*shape):
        return pltpu.VMEM(shape, bf16)

    dma = pltpu.SemaphoreType.DMA
    shape = (seqs // 4, 2, 2, reps // 2, rows, width)
    halving = []
    for order in TAIL_ORDERS:
        steps = reduce_steps(order, seq_bits)
        halving += [vm(*shape)] + [vm(*b) for b in reduce_buffers(shape, steps)]
        halving += [vm(2, 2, rows, width), dma((2, len(steps) + 2))]
    outs = [
        ((micros, tok, width), bf16),
        ((2, 2, rows, 3 * width), bf16),
        ((width // seqs, 6), f32),
        ((hidden // seqs, 2), f32),
    ]
    return pl.pallas_call(
        functools.partial(tail_body, seq_bits=seq_bits),
        in_specs=[any_spec] * 4 + [vmem_spec()] * 7,
        out_specs=[vmem_spec()] * 4,
        out_shape=[jax.ShapeDtypeStruct(s, d) for s, d in outs],
        scratch_shapes=[
            vm(micros, 3, reps, cols, tok),
            vm(width, 3 * width),
            pltpu.VMEM((micros, tok, width), f32),
            pltpu.VMEM((width, tok), f32),
            vm(3, parts, rows, width),
            vm(3, parts, rows, width),
            vm(3, parts, rows, width),
            pltpu.VMEM((seq_bits + 3, 16, width), f32),
            pltpu.VMEM((seq_bits + 2, 16, width), f32),
            dma((9,)),
            dma((2, 3)),
            dma((2, seq_bits + 2)),
            *halving,
        ],
        compiler_params=pltpu.CompilerParams(
            vmem_limit_bytes=VMEM, collective_id=4, has_side_effects=True
        ),
        cost_estimate=pl.CostEstimate(
            flops=24 * tok * width * width, bytes_accessed=20_000_000, transcendentals=0
        ),
        name="tail",
    )(tg, weight, *branch, xp, nt, gain, *ng, *nh)


def bits_of(count):
    return count.bit_length() - 1


def on_device(
    layer_in,
    qkv_weight,
    out_weight,
    up_weight,
    down_weight,
    input_gain,
    input_bias,
    mixer_gain,
    mixer_bias,
    block_gain,
    block_bias,
    hidden_gain,
    hidden_bias,
    output_grad,
    seq_lengths,
):
    micro_count, tok, width = layer_in.shape
    reps = lax.axis_size("rep")
    seqs = lax.axis_size("seq")
    span = tok * reps
    heads_dev = HEADS // reps
    cols = heads_dev * HD
    pairs = [[2 * n, 2 * n + 1] for n in range(seqs // 2)]
    fours = [[4 * n + k for k in range(4)] for n in range(seqs // 4)]

    def to_reps(x):
        return lax.all_to_all(x, "rep", 0, 0, tiled=True)

    def to_pair(x):
        return lax.all_to_all(x, "seq", 0, 0, tiled=True, axis_index_groups=pairs)

    def to_four(x):
        return lax.all_to_all(x, "seq", 0, 0, tiled=True, axis_index_groups=fours)

    def row(v):
        return v.reshape(1, -1)

    micros = range(micro_count)
    xp, nt, got_qkv, got_pair, got_four, own_att, got_att, totals = forward_call(
        layer_in, qkv_weight, row(input_gain), row(input_bias), seq_lengths, reps
    )
    attended = [got_att, to_reps(own_att[1])]

    outputs, branch_grads, head_grads, groups, norm_terms, hidden_terms = [], [], [], [], [], []
    weights = (out_weight, up_weight, down_weight)
    gains = tuple(
        row(v) for v in (mixer_gain, mixer_bias, block_gain, block_bias, hidden_gain, hidden_bias)
    )
    for m in micros:
        out, branch, da, mixl, low, hid, dup, brl, cotp, ng, nh = ffn_call(
            attended[m], xp, output_grad, weights, gains, m
        )
        outputs.append(out)
        branch_grads.append(branch)
        head_grads.append(to_reps(da))
        groups.append((low, dup, hid, cotp, mixl, brl))
        norm_terms.append(ng)
        hidden_terms.append(nh)
    seq_bits = bits_of(seqs)
    grads = [
        g.reshape((seqs // 4, 2, 2, reps // 2) + g.shape[1:])
        for g in weight_grads(groups, tok, width, up_weight.shape[1], seqs, reps)
    ]
    token_grad, down_total, up_total, proj_total = backward_call(
        (got_qkv, got_pair, got_four), head_grads, own_att, totals, seq_lengths, grads, seq_bits
    )
    down_total, up_total, proj_total = (
        t.reshape(-1, t.shape[-1]).astype(f32) for t in (down_total, up_total, proj_total)
    )
    input_grad, qkv_total, norm_total, hidden_total = tail_call(
        token_grad,
        qkv_weight,
        branch_grads,
        xp,
        nt,
        row(input_gain),
        norm_terms,
        hidden_terms,
        seq_bits,
    )
    qkv_total = qkv_total.reshape(-1, qkv_total.shape[-1]).astype(f32)
    return (
        jnp.stack(outputs),
        input_grad,
        qkv_total,
        proj_total,
        up_total,
        down_total,
        norm_total,
        hidden_total,
    )


def solution(mesh):
    tokens = P(None, ("seq", "rep"), None)
    rows = P("seq", None)
    return jax.shard_map(
        on_device,
        mesh=mesh,
        in_specs=(tokens,) + (P(),) * 12 + (tokens, P()),
        out_specs=(tokens, tokens) + (rows,) * 6,
        check_vma=False,
    )
```

```python
import functools
import math

import jax
import jax.numpy as jnp
from jax import lax
from jax.experimental import pallas as pl
from jax.experimental.pallas import tpu as pltpu
from jax.sharding import PartitionSpec as P

HEADS = 12
HD = 64
HPAD = 80
CLASS_SLOT = (0, 2, 1, 3)
LOG2E = 1.4426950408889634
NEG = -1e30
EPS = 1e-05
VMEM = 56 << 20

f32 = jnp.float32
bf16 = jnp.bfloat16


def dot_nn(a, b):
    return lax.dot_general(a, b, (((1,), (0,)), ((), ())), preferred_element_type=f32)


def dot_nt(a, b):
    return lax.dot_general(a, b, (((1,), (1,)), ((), ())), preferred_element_type=f32)


def dot_tn(a, b):
    return lax.dot_general(a, b, (((0,), (0,)), ((), ())), preferred_element_type=f32)


def class_slot(cls):
    return jnp.where(cls == 1, 2, jnp.where(cls == 2, 1, cls))


def rel_pos(shape, dim, offset, pattern):
    i = lax.broadcasted_iota(jnp.int32, shape, dim) + offset
    if pattern == 0:
        return (i % 128) * 4 + class_slot((i // 128) % 4)
    if pattern == 1:
        return (i // 256) * 512 + (i % 128) * 4 + ((i // 128) % 2) * 2
    return i


def doc_rows(len_ref, micro, start, dilation, count):
    pos = lax.broadcasted_iota(jnp.int32, (1, count), 1) * dilation + start
    edge = len_ref[micro, 0]
    doc = (pos >= edge).astype(jnp.int32)
    for n in range(1, len_ref.shape[1] - 1):
        edge = edge + len_ref[micro, n]
        doc = doc + (pos >= edge).astype(jnp.int32)
    return doc


def segment_start(pattern, span):
    team = 2**pattern
    return (lax.axis_index("seq") // team) * (team * span)


def split3(x):
    hi = x.astype(bf16).astype(f32)
    mid = (x - hi).astype(bf16).astype(f32)
    return hi, mid, x - hi - mid


def stat_rows(rows, count):
    r = lax.broadcasted_iota(jnp.int32, (HPAD - HD, count), 0)
    out = jnp.zeros((HPAD - HD, count), f32)
    for n, row in enumerate(rows):
        out = jnp.where(r == n, row, out)
    return out.astype(bf16)


def shift():
    return lax.axis_index("rep") % 2


def taker():
    return shift()


def owner_of(j):
    return (j + shift()) % 4


def slot_of(place):
    return (place + 4 - shift()) % 4


def clamp_slot(j):
    return j - j // 3


def place1(j):
    return (taker(), 1) if j == 2 else (j, 0)


def smem_spec():
    return pl.BlockSpec(memory_space=pltpu.SMEM)


def vmem_spec():
    return pl.BlockSpec(memory_space=pltpu.VMEM)


def onehot_rows(tok):
    i = lax.broadcasted_iota(jnp.int32, (tok, tok), 0)
    t = lax.broadcasted_iota(jnp.int32, (tok, tok), 1)
    return ((i % 128) * 4 + class_slot(i // 128) == t).astype(bf16)


def onehot_cols(tok):
    t = lax.broadcasted_iota(jnp.int32, (tok, tok), 0)
    i = lax.broadcasted_iota(jnp.int32, (tok, tok), 1)
    return ((i % 128) * 4 + class_slot(i // 128) == t).astype(bf16)


def normalize(x):
    c = x - jnp.mean(x, axis=-1, keepdims=True)
    rstd = lax.rsqrt(jnp.mean(c * c, axis=-1, keepdims=True) + EPS)
    return c * rstd, rstd


def norm_back(grad, gain, xhat, rstd):
    dn = grad * gain
    low = jnp.mean(dn, axis=-1, keepdims=True)
    along = jnp.mean(dn * xhat, axis=-1, keepdims=True)
    dx = rstd * (dn - low - xhat * along)
    return dx, jnp.sum(grad * xhat, 0, keepdims=True), jnp.sum(grad, 0, keepdims=True)


CHUNK = 512
SQRT_HALF = 0.7071067811865476
INV_SQRT_2PI = 0.3989422804014327


def ffn_body(
    own_ref,
    got_hbm,
    xp_ref,
    cot_ref,
    wo_hbm,
    wu_hbm,
    wd_hbm,
    mg_ref,
    mb_ref,
    bg_ref,
    bb_ref,
    hg_ref,
    hb_ref,
    out_ref,
    ng_ref,
    nh_ref,
    branch_out,
    mix_out,
    low_out,
    hid_out,
    dup_out,
    brl_out,
    cotp_out,
    da0_out,
    da1_out,
    wo,
    wu,
    wd,
    g_scr,
    dg_scr,
    dn_scr,
    am_scr,
    acc_scr,
    att_scr,
    da_scr,
    branch,
    mix,
    low,
    hid,
    dup,
    brl,
    cotp,
    load_sems,
    out_sems,
    att_sems,
    da_sems,
    own_sems,
):
    micros, tok, width = xp_ref.shape
    hidden = hid.shape[1]
    chunks = hidden // CHUNK
    reps, cols = own_ref.shape[1:3]
    me = lax.axis_index("rep")
    loads = [
        pltpu.make_async_copy(a, b, load_sems.at[n])
        for n, (a, b) in enumerate(
            ((wo_hbm, wo), (wu_hbm, wu), (wd_hbm, wd), (got_hbm, att_scr.at[0]))
        )
    ]
    for n in (3, 0, 1, 2):
        loads[n].start()
    barrier = pltpu.get_barrier_semaphore()
    for k in range(1, 4):
        pl.semaphore_signal(
            barrier, inc=1, device_id={"rep": rep_peer(k)}, device_id_type=pl.DeviceIdType.MESH
        )
    pl.semaphore_wait(barrier, 3)

    def att_copy(k, source):
        return remote(
            own_ref.at[1, rep_peer(k)],
            att_scr.at[1, source],
            att_sems.at[0, k - 1],
            att_sems.at[1, k - 1],
            "rep",
            rep_peer(k),
        )

    def da_copy(k, source):
        return remote(
            da_scr.at[0, rep_peer(k)],
            da0_out.at[source],
            da_sems.at[0, k - 1],
            da_sems.at[1, k - 1],
            "rep",
            rep_peer(k),
        )

    da_own = pltpu.make_async_copy(da_scr.at[0, me], da0_out.at[me], own_sems.at[0])
    da_last = pltpu.make_async_copy(da_scr.at[1], da1_out, own_sems.at[1])
    for k in range(1, 4):
        att_copy(k, me).start()
    att_scr[1, me] = own_ref[1, me]
    pairs = (
        (branch, branch_out),
        (mix, mix_out),
        (low, low_out),
        (hid, hid_out),
        (dup, dup_out),
        (brl, brl_out),
        (cotp, cotp_out),
    )

    def out_copy(n, m):
        return pltpu.make_async_copy(pairs[n][0], pairs[n][1].at[m], out_sems.at[n])

    def lanes(n):
        return slice(n * CHUNK, (n + 1) * CHUNK)

    def row(ref, at=slice(None)):
        return ref[at].reshape(1, -1)

    def micro(m, carry):
        def before(n):
            @pl.when(m == 1)
            def _():
                out_copy(n, 0).wait()

        @pl.when(m == 0)
        def _():
            loads[3].wait()

        @pl.when(m == 1)
        def _():
            for k in range(1, 4):
                att_copy(k, (me + reps - k) % reps).wait_recv()

        before(6)
        cotp[...] = dot_nn(onehot_rows(tok), cot_ref[m]).astype(bf16)
        out_copy(6, m).start()
        att = att_scr[m].reshape(width, tok).T.astype(f32)
        ahat, _ = normalize(att)
        before(1)
        mix[...] = (ahat * row(mg_ref) + row(mb_ref)).astype(bf16)
        out_copy(1, m).start()

        @pl.when(m == 0)
        def _():
            loads[0].wait()

        am = xp_ref[m].astype(f32) + dot_nn(mix[...], wo[...])
        am_scr[...] = am
        bhat, _ = normalize(am)
        before(2)
        low[...] = (bhat * row(bg_ref) + row(bb_ref)).astype(bf16)
        out_copy(2, m).start()

        @pl.when(m == 0)
        def _():
            loads[1].wait()

        total = jnp.zeros((tok, 1), f32)
        for n in range(chunks):
            u = dot_nn(low[...], wu[:, lanes(n)])
            cdf = 0.5 + 0.5 * lax.erf(u * SQRT_HALF)
            g = u * cdf
            g_scr[:, lanes(n)] = g
            dg_scr[:, lanes(n)] = cdf + u * (jnp.exp(u * u * -0.5) * INV_SQRT_2PI)
            total = total + jnp.sum(g, 1, keepdims=True)
        mean = total / hidden
        total = jnp.zeros((tok, 1), f32)
        for n in range(chunks):
            c = g_scr[:, lanes(n)] - mean
            total = total + jnp.sum(c * c, 1, keepdims=True)
        rstd = lax.rsqrt(total / hidden + EPS)

        @pl.when(m == 0)
        def _():
            loads[2].wait()

        before(3)
        first = second = jnp.zeros((tok, 1), f32)
        for n in range(chunks):
            ghat = (g_scr[:, lanes(n)] - mean) * rstd
            g_scr[:, lanes(n)] = ghat
            gain = row(hg_ref, lanes(n))
            h = (ghat * gain + row(hb_ref, lanes(n))).astype(bf16)
            hid[:, lanes(n)] = h
            part = dot_nn(h, wd[lanes(n), :])
            if n == 0:
                acc_scr[...] = part
            else:
                acc_scr[...] += part
            back = dot_nt(cotp[...], wd[lanes(n), :])
            nh_ref[m, 0:1, lanes(n)] = jnp.sum(back * ghat, 0, keepdims=True)
            nh_ref[m, 1:2, lanes(n)] = jnp.sum(back, 0, keepdims=True)
            dn = back * gain
            dn_scr[:, lanes(n)] = dn
            first = first + jnp.sum(dn, 1, keepdims=True)
            second = second + jnp.sum(dn * ghat, 1, keepdims=True)
        first, second = first / hidden, second / hidden
        out_copy(3, m).start()
        out_ref[m] = (am_scr[...] + acc_scr[...]).astype(bf16)
        before(4)
        for n in range(chunks):
            d = rstd * (dn_scr[:, lanes(n)] - first - g_scr[:, lanes(n)] * second)
            t = (d * dg_scr[:, lanes(n)]).astype(bf16)
            dup[:, lanes(n)] = t
            part = dot_nt(t, wu[:, lanes(n)])
            if n == 0:
                acc_scr[...] = part
            else:
                acc_scr[...] += part
        out_copy(4, m).start()
        bhat, brstd = normalize(am_scr[...])
        middle, gain_b, bias_b = norm_back(acc_scr[...], row(bg_ref), bhat, brstd)
        total = cotp[...].astype(f32) + middle
        before(0)
        branch[...] = total
        out_copy(0, m).start()
        before(5)
        brl[...] = total.astype(bf16)
        out_copy(5, m).start()
        att = att_scr[m].reshape(width, tok).T.astype(f32)
        ahat, arstd = normalize(att)
        da, gain_m, bias_m = norm_back(dot_nt(brl[...], wo[...]), row(mg_ref), ahat, arstd)
        da_scr[m] = da.astype(bf16).T.reshape(reps, cols, tok)
        ng_ref[m, 0:1] = gain_m
        ng_ref[m, 1:2] = bias_m
        ng_ref[m, 2:3] = gain_b
        ng_ref[m, 3:4] = bias_b

        @pl.when(m == 0)
        def _():
            for k in range(1, 4):
                da_copy(k, me).start()
            da_own.start()

        return carry

    lax.fori_loop(0, micros, micro, 0)
    da_last.start()
    for n in range(len(pairs)):
        out_copy(n, 1).wait()
    for k in range(1, 4):
        att_copy(k, me).wait_send()
        da_copy(k, (me + reps - k) % reps).wait_recv()
        da_copy(k, me).wait_send()
    da_own.wait()
    da_last.wait()


def ffn_call(own, got, xp, output_grad, weights, gains):
    micros, reps, cols, tok = own.shape
    width = xp.shape[2]
    hidden = weights[1].shape[1]
    any_spec = pl.BlockSpec(memory_space=pl.ANY)
    wide, narrow = (tok, hidden), (tok, width)
    outs = [
        ((micros,) + narrow, bf16, vmem_spec()),
        ((micros, 4, width), f32, vmem_spec()),
        ((micros, 2, hidden), f32, vmem_spec()),
        ((micros,) + narrow, f32, any_spec),
        ((micros,) + narrow, bf16, any_spec),
        ((micros,) + narrow, bf16, any_spec),
        ((micros,) + wide, bf16, any_spec),
        ((micros,) + wide, bf16, any_spec),
        ((micros,) + narrow, bf16, any_spec),
        ((micros,) + narrow, bf16, any_spec),
        ((reps, cols, tok), bf16, any_spec),
        ((reps, cols, tok), bf16, any_spec),
    ]
    dma = pltpu.SemaphoreType.DMA
    return pl.pallas_call(
        ffn_body,
        in_specs=[vmem_spec(), any_spec, vmem_spec(), vmem_spec()]
        + [any_spec] * 3
        + [vmem_spec()] * len(gains),
        out_specs=[o[2] for o in outs],
        out_shape=[jax.ShapeDtypeStruct(o[0], o[1]) for o in outs],
        scratch_shapes=[pltpu.VMEM(w.shape, bf16) for w in weights]
        + [pltpu.VMEM(wide, f32)] * 3
        + [pltpu.VMEM(narrow, f32)] * 2
        + [pltpu.VMEM((2, reps, cols, tok), bf16)] * 2
        + [pltpu.VMEM(narrow, f32), pltpu.VMEM(narrow, bf16), pltpu.VMEM(narrow, bf16)]
        + [pltpu.VMEM(wide, bf16)] * 2
        + [pltpu.VMEM(narrow, bf16)] * 2
        + [dma((4,)), dma((7,)), dma((2, 3)), dma((2, 3)), dma((2,))],
        compiler_params=pltpu.CompilerParams(
            vmem_limit_bytes=60 << 20, collective_id=5, has_side_effects=True
        ),
        cost_estimate=pl.CostEstimate(
            flops=8 * tok * width * (2 * hidden + width),
            bytes_accessed=40_000_000,
            transcendentals=4 * tok * hidden,
        ),
        name="middle",
    )(own, got, xp, output_grad, *weights, *gains)


def rep_peer(k):
    count = lax.axis_size("rep")
    return (lax.axis_index("rep") + k) % count


def team_place():
    return lax.axis_index("seq") % 4


def team_member(k):
    s = lax.axis_index("seq")
    return s // 4 * 4 + (s + k) % 4


def pair_partner():
    s = lax.axis_index("seq")
    return s + 1 - 2 * (s % 2)


def remote(src, dst, send_sem, recv_sem, axis, peer):
    return pltpu.make_async_remote_copy(
        src_ref=src,
        dst_ref=dst,
        send_sem=send_sem,
        recv_sem=recv_sem,
        device_id={axis: peer},
        device_id_type=pl.DeviceIdType.MESH,
    )


def meet_peers():
    barrier = pltpu.get_barrier_semaphore()
    for k in range(1, 4):
        for axis, peer in (("rep", rep_peer(k)), ("seq", team_member(k))):
            pl.semaphore_signal(
                barrier, inc=1, device_id={axis: peer}, device_id_type=pl.DeviceIdType.MESH
            )
    pl.semaphore_wait(barrier, 6)


def head_rows(j):
    return pl.ds(pl.multiple_of(j * HD, HD), HD)


def attend(block, doc, put, ks, qs, pattern, count, lanes):
    kb = min(512, lanes)
    for s in range(0, count, kb):
        sl = slice(s, s + kb)
        r = lax.broadcasted_iota(jnp.int32, (HD, kb), 0)
        same = doc[:, sl] == r
        aux_k = jnp.where(same, 1.0, 0.0).astype(bf16)
        aux_q = jnp.where(same | (r >= 4), 0.0, NEG).astype(bf16)
        q = (block(0, s, kb).astype(f32) * 0.125).astype(bf16)
        qs[:, sl] = jnp.concatenate([q, aux_q], 0)
        ks[sl, :] = jnp.concatenate([block(1, s, kb), aux_k], 0).T

    qb = 256
    grain = 512 if pattern == 0 else 256

    def tiles(i):
        low = (i * qb) // grain * grain
        out = [(s, min(512, low - s), False) for s in range(0, low, 512)]
        return out + [(low, grain, True)]

    def scores(i):
        out = []
        for s, size, diagonal in tiles(i):
            t = dot_nn(ks[s : s + size, :], qs[:, i * qb : (i + 1) * qb])
            if diagonal:
                keep = rel_pos((size, qb), 0, s % 512, pattern) <= rel_pos(
                    (size, qb), 1, (i * qb) % 512, pattern
                )
                t = jnp.where(keep, t, NEG)
            out.append(t)
        return out

    following = scores(0)
    for i in range(count // qb):
        current = following
        if (i + 1) * qb < count:
            following = scores(i + 1)
        top = functools.reduce(jnp.maximum, [jnp.max(t, 0, keepdims=True) for t in current])
        top2 = top * LOG2E
        acc, total = None, None
        for t, (s, size, _) in zip(current, tiles(i)):
            p = jnp.exp2(t * LOG2E - top2)
            part = jnp.sum(p, 0, keepdims=True)
            out = dot_nn(block(2, s, size), p.astype(bf16))
            acc = out if acc is None else acc + out
            total = part if total is None else total + part
        lse = top + jnp.log(total)
        put(i * qb, qb, (acc / total).astype(bf16), stat_rows(split3(lse), qb))


def forward_body(
    x_ref,
    w_ref,
    gain_ref,
    bias_ref,
    len_ref,
    xp_ref,
    nt_ref,
    r_out,
    p1_out,
    p2_out,
    att_ref,
    got_ref,
    mix_ref,
    sent,
    r,
    stage1,
    stage2,
    p1,
    p2,
    o0,
    o1,
    o2,
    b1,
    b2,
    ks,
    qs,
    qkv_sems,
    p1_sems,
    p2_sems,
    b1_sems,
    b2_sems,
    att_sems,
    out_sems,
):
    micros, tok, width = x_ref.shape
    reps = r.shape[1]
    span = tok * reps
    cols = width // reps
    me = lax.axis_index("rep")
    place = team_place()
    side = place % 2
    meet_peers()

    def qkv_copy(m, j, k, source):
        return remote(
            sent.at[m, rep_peer(k), :, head_rows(j)],
            r.at[m, source, :, head_rows(j)],
            qkv_sems.at[0, m, j, k - 1],
            qkv_sems.at[1, m, j, k - 1],
            "rep",
            rep_peer(k),
        )

    def p1_copy(m, s, source):
        return remote(
            stage1.at[m, s],
            p1.at[m, source, s],
            p1_sems.at[0, m, s],
            p1_sems.at[1, m, s],
            "seq",
            pair_partner(),
        )

    def p2_copy(m, k, source):
        return remote(
            stage2.at[m, (place + k) % 4],
            p2.at[m, source],
            p2_sems.at[0, m, k - 1],
            p2_sems.at[1, m, k - 1],
            "seq",
            team_member(k),
        )

    def b1_copy(m, s, source):
        return remote(
            o1.at[m, s, 1 - side],
            b1.at[m, source, s],
            b1_sems.at[0, m, s],
            b1_sems.at[1, m, s],
            "seq",
            pair_partner(),
        )

    def b2_copy(m, k, source):
        return remote(
            o2.at[m, (place + k) % 4],
            b2.at[m, source],
            b2_sems.at[0, m, k - 1],
            b2_sems.at[1, m, k - 1],
            "seq",
            team_member(k),
        )

    def att_copy(k, source):
        return remote(
            att_ref.at[0, rep_peer(k)],
            got_ref.at[source],
            att_sems.at[0, k - 1],
            att_sems.at[1, k - 1],
            "rep",
            rep_peer(k),
        )

    def out_copies(m):
        return (
            pltpu.make_async_copy(r.at[m], r_out.at[m], out_sems.at[m, 0]),
            pltpu.make_async_copy(p1.at[m], p1_out.at[m], out_sems.at[m, 1]),
            pltpu.make_async_copy(p2.at[m], p2_out.at[m], out_sems.at[m, 2]),
        )

    def project(m, carry):
        xp = dot_nn(onehot_rows(tok), x_ref[m])
        xp_ref[m] = xp.astype(bf16)
        xhat, _ = normalize(xp)
        n = (xhat * gain_ref[...].reshape(1, -1) + bias_ref[...].reshape(1, -1)).astype(bf16)
        nt_ref[m] = n.T
        for c in range(3):
            t = dot_nn(n, w_ref[:, c * width : (c + 1) * width]).astype(bf16).T
            for d in range(reps):
                sent[m, d, c] = t[d * cols : (d + 1) * cols]
        for j in range(3):
            for k in range(1, 4):
                qkv_copy(m, j, k, me).start()
        r[m, me] = sent[m, me]
        return carry

    lax.fori_loop(0, micros, project, 0)

    def half(j):
        return pl.ds(pl.multiple_of(((3 * me + j) % 2) * 256, 256), 256)

    def quarter_at(j):
        c = (3 * me + j) % 4
        return c % 2 * 2 + c // 2

    def quarter(j):
        return pl.ds(pl.multiple_of(quarter_at(j) * 128, 128), 128)

    def send_first(m):
        for b in range(reps):
            bl = slice(b * 256, (b + 1) * 256)
            stage1[m, 0, :, :, bl] = r[m, b, :, head_rows(1 - side), half(1 - side)]
            p1[m, side, 0, :, :, bl] = r[m, b, :, head_rows(side), half(side)]
        p1_copy(m, 0, side).start()

    def send_second(m):
        for b in range(reps):
            bl = slice(b * 256, (b + 1) * 256)
            piece = r[m, b, :, head_rows(2), half(2)]
            stage1[m, 1, :, :, bl] = piece
            p1[m, side, 1, :, :, bl] = piece

        @pl.when(side != taker())
        def _():
            p1_copy(m, 1, side).start()

        for g in range(4):
            j = clamp_slot(slot_of(g))
            for b in range(reps):
                stage2[m, g, :, :, b * 128 : (b + 1) * 128] = r[m, b, :, head_rows(j), quarter(j)]
        p2[m, place] = stage2[m, place]
        for k in range(1, 4):

            @pl.when(slot_of(place + k) < 3)
            def _():
                p2_copy(m, k, place).start()

    def mix_all(m):
        b1_copy(m, 0, 1 - side).wait_recv()

        @pl.when(side != taker())
        def _():
            b1_copy(m, 1, 1 - side).wait_recv()

        for k in range(1, 4):

            @pl.when(slot_of(place + 4 - k) < 3)
            def _():
                b2_copy(m, k, (place + 4 - k) % 4).wait_recv()

        def stat(tile):
            t = tile[HD:, :].astype(f32)
            return t[0:1] + t[1:2] + t[2:3]

        mix_ref[m] = jnp.zeros(mix_ref.shape[1:], f32)
        for j in range(3):
            e, s = place1(j)
            for b in range(reps):
                for a in range(4):
                    la = slice(a * 128, (a + 1) * 128)
                    lb = b * 256 + (a % 2) * 128
                    t0 = o0[m, j, b, :, la]
                    t1 = b1[m, e, s, :, lb : lb + 128]
                    t2 = b2[m, owner_of(j), :, b * 128 : (b + 1) * 128]
                    l0 = stat(t0)
                    l1 = jnp.where((3 * me + j) % 2 == a // 2, stat(t1), NEG)
                    l2 = jnp.where(quarter_at(j) == a, stat(t2), NEG)
                    top = jnp.maximum(jnp.maximum(l0, l1), l2)
                    e0, e1, e2 = jnp.exp(l0 - top), jnp.exp(l1 - top), jnp.exp(l2 - top)
                    total = e0 + e1 + e2
                    inv = 1.0 / total
                    mixed = (
                        t0[:HD].astype(f32) * (e0 * inv)
                        + t1[:HD].astype(f32) * (e1 * inv)
                        + t2[:HD].astype(f32) * (e2 * inv)
                    )
                    att_ref[m, b, j * HD : (j + 1) * HD, la] = mixed.astype(bf16)
                    col = b * tok + a * 128
                    mix_ref[m, j : j + 1, col : col + 128] = top + jnp.log(total)

    docs_of = lambda m, pattern: doc_rows(
        len_ref, m, segment_start(pattern, span), 2**pattern, span
    )

    def micro(m, carry):
        def local(j, inner):
            for k in range(1, 4):
                qkv_copy(m, j, k, (me + reps - k) % reps).wait_recv()

            @pl.when(j == 1)
            def _():
                send_first(m)

            @pl.when(j == 2)
            def _():
                send_second(m)

            def block(c, start, size):
                at = start % tok
                return r[m, start // tok, c, head_rows(j), at : at + size]

            def put(start, size, out, stats):
                at = start % tok
                o0[m, j, start // tok, :HD, at : at + size] = out
                o0[m, j, start // tok, HD:, at : at + size] = stats

            attend(block, docs_of(m, 0), put, ks, qs, 0, span, tok)
            return inner

        lax.fori_loop(0, 3, local, 0)

        @pl.when(m == 1)
        def _():
            mix_all(0)
            for k in range(1, 4):
                att_copy(k, me).start()
            got_ref[me] = att_ref[0, me]

        wide = span // 2

        def paired(s):
            p1_copy(m, s, 1 - side).wait_recv()

            def block(c, start, size):
                at = start % wide
                return p1[m, start // wide, s, c, :, at : at + size]

            def put(start, size, out, stats):
                at = start % wide
                o1[m, s, start // wide, :HD, at : at + size] = out
                o1[m, s, start // wide, HD:, at : at + size] = stats

            attend(block, docs_of(m, 1), put, ks, qs, 1, span, wide)
            b1[m, side, s] = o1[m, s, side]
            b1_copy(m, s, side).start()

        def each_pair(s, inner):
            @pl.when((s == 0) | (side == taker()))
            def _():
                paired(s)

            return inner

        lax.fori_loop(0, 2, each_pair, 0)

        def block(c, start, size):
            at = start % tok
            return p2[m, start // tok, c, :, at : at + size]

        def put(start, size, out, stats):
            at = start % tok
            o2[m, start // tok, :HD, at : at + size] = out
            o2[m, start // tok, HD:, at : at + size] = stats

        @pl.when(slot_of(place) < 3)
        def _():
            for k in range(1, 4):
                p2_copy(m, k, (place + 4 - k) % 4).wait_recv()
            attend(block, docs_of(m, 2), put, ks, qs, 2, span, tok)
            b2[m, place] = o2[m, place]
            for k in range(1, 4):
                b2_copy(m, k, place).start()

        for c in out_copies(m):
            c.start()
        return carry

    lax.fori_loop(0, micros, micro, 0)
    mix_all(1)
    for k in range(1, 4):
        att_copy(k, (me + reps - k) % reps).wait_recv()
        att_copy(k, me).wait_send()

    def finish(m, carry):
        for c in out_copies(m):
            c.wait()
        for k in range(1, 4):
            for j in range(3):
                qkv_copy(m, j, k, me).wait_send()

            @pl.when(slot_of(place + k) < 3)
            def _():
                p2_copy(m, k, place).wait_send()

            @pl.when(slot_of(place) < 3)
            def _():
                b2_copy(m, k, place).wait_send()

        p1_copy(m, 0, side).wait_send()
        b1_copy(m, 0, side).wait_send()

        @pl.when(side != taker())
        def _():
            p1_copy(m, 1, side).wait_send()

        @pl.when(side == taker())
        def _():
            b1_copy(m, 1, side).wait_send()

        return carry

    lax.fori_loop(0, micros, finish, 0)


def forward_call(layer_in, weight, gain, bias, lengths, reps):
    micros, tok, width = layer_in.shape
    span, cols = tok * reps, width // reps
    any_spec = pl.BlockSpec(memory_space=pl.ANY)
    outs = [
        ((micros, tok, width), bf16, vmem_spec()),
        ((micros, width, tok), bf16, vmem_spec()),
        ((micros, reps, 3, cols, tok), bf16, any_spec),
        ((micros, 2, 2, 3, HD, span // 2), bf16, any_spec),
        ((micros, 4, 3, HD, span // 4), bf16, any_spec),
        ((micros, reps, cols, tok), bf16, vmem_spec()),
        ((reps, cols, tok), bf16, vmem_spec()),
        ((micros, 8, span), f32, vmem_spec()),
    ]

    def vm(*shape):
        return pltpu.VMEM(shape, bf16)

    dma = pltpu.SemaphoreType.DMA
    return pl.pallas_call(
        forward_body,
        in_specs=[vmem_spec()] * 4 + [smem_spec()],
        out_specs=[o[2] for o in outs],
        out_shape=[jax.ShapeDtypeStruct(o[0], o[1]) for o in outs],
        scratch_shapes=[
            vm(micros, reps, 3, cols, tok),
            vm(micros, reps, 3, cols, tok),
            vm(micros, 2, 3, HD, span // 2),
            vm(micros, 4, 3, HD, span // 4),
            vm(micros, 2, 2, 3, HD, span // 2),
            vm(micros, 4, 3, HD, span // 4),
            vm(micros, 3, reps, HPAD, tok),
            vm(micros, 2, 2, HPAD, span // 2),
            vm(micros, 4, HPAD, span // 4),
            vm(micros, 2, 2, HPAD, span // 2),
            vm(micros, 4, HPAD, span // 4),
            vm(span, 128),
            vm(128, span),
            dma((2, micros, 3, 3)),
            dma((2, micros, 2)),
            dma((2, micros, 3)),
            dma((2, micros, 2)),
            dma((2, micros, 3)),
            dma((2, 3)),
            dma((micros, 3)),
        ],
        compiler_params=pltpu.CompilerParams(
            vmem_limit_bytes=VMEM, collective_id=1, has_side_effects=True
        ),
        cost_estimate=pl.CostEstimate(
            flops=60_000_000_000, bytes_accessed=30_000_000, transcendentals=30_000_000
        ),
        name="forward",
    )(layer_in, weight, gain, bias, lengths)


def bit_of(axis, bit):
    return lax.axis_index(axis) // (1 << bit) % 2


def bit_peer(axis, bit):
    return lax.axis_index(axis) + (1 << bit) * (1 - 2 * bit_of(axis, bit))


def attend_back(block, gblock, doc, put, scr, pattern, count, lanes):
    ks, vs, qs, qr, gs, gr, dq = scr
    bs = min(512, lanes)
    zeros = jnp.zeros((HD, bs), bf16)
    r = lax.broadcasted_iota(jnp.int32, (HD, bs), 0)
    fill = jnp.zeros((HD - 32, bs), bf16)
    for s in range(0, count, bs):
        sl = slice(s, s + bs)
        same = doc[:, sl] == r
        aux_k = jnp.where(same | ((r >= 16) & (r < 19)), 1.0, 0.0).astype(bf16)
        aux_q = jnp.where(same | (r >= 4), 0.0, NEG).astype(bf16)
        aux_v = jnp.where((r >= 19) & (r < 21), 1.0, 0.0).astype(bf16)
        q = (block(0, s, bs).astype(f32) * 0.125).astype(bf16)
        tile = gblock(s, bs)
        g, stats = tile[:HD], tile[HD:]
        qs[:, sl] = jnp.concatenate([q, aux_q[:16], stats, fill], 0)
        gs[:, sl] = jnp.concatenate([g, zeros[:16], stats, fill], 0)
        qr[sl, :] = jnp.concatenate([q, zeros], 0).T
        gr[sl, :] = jnp.concatenate([g, zeros], 0).T
        ks[sl, :] = jnp.concatenate([block(1, s, bs), aux_k], 0).T
        vs[sl, :] = jnp.concatenate([block(2, s, bs), aux_v], 0).T

    keep = rel_pos((bs, bs), 0, 0, pattern) <= rel_pos((bs, bs), 1, 0, pattern)
    for j in range(count // bs):
        jl = slice(j * bs, (j + 1) * bs)
        dva, dka = None, None
        for i in range(j, count // bs):
            il = slice(i * bs, (i + 1) * bs)
            p = jnp.exp2(dot_nn(ks[jl, :], qs[:, il]) * LOG2E)
            if i == j:
                p = jnp.where(keep, p, 0.0)
            dp = dot_nn(vs[jl, :], gs[:, il])
            ds = (p * dp).astype(bf16)
            dvi = dot_nn(p.astype(bf16), gr[il, :])
            dki = dot_nn(ds, qr[il, :])
            dva = dvi if dva is None else dva + dvi
            dka = dki if dka is None else dka + dki
            dqi = dot_nn(block(1, j * bs, bs), ds) * 0.125
            if j == 0:
                dq[:, il] = dqi
            else:
                dq[:, il] += dqi
        put(1, j * bs, bs, dka.T[:HD].astype(bf16))
        put(2, j * bs, bs, dva.T[:HD].astype(bf16))
        put(0, j * bs, bs, dq[:, jl].astype(bf16))


class Halving:
    def __init__(self, source, steps, buffers, gathered, out, sems):
        self.source, self.steps, self.buffers = source, steps, buffers
        self.gathered, self.out, self.sems = gathered, out, sems
        self.names = ["high", "z", "x", "y"]
        self.at = 0
        self.pending = None

    def pick(self, ref, axis, name, index):
        lead = (slice(None),) * axis
        if name == "high":
            half = ref.shape[axis] // 2
            return lead + (pl.ds(index * half, half),)
        return lead + (index,)

    def start(self):
        if self.at < len(self.steps):
            name, axis_name, bit = self.steps[self.at]
            axis = self.names.index(name)
            mine = bit_of(axis_name, bit)
            target = self.buffers[self.at]
            copy = remote(
                self.source.at[self.pick(self.source, axis, name, 1 - mine)],
                target,
                self.sems.at[0, self.at],
                self.sems.at[1, self.at],
                axis_name,
                bit_peer(axis_name, bit),
            )
            copy.start()
            self.pending = ("sum", copy, target, self.pick(self.source, axis, name, mine))
            if name != "high":
                self.names.pop(axis)
            return
        stage = self.at - len(self.steps)
        y, c = bit_of("rep", 1), bit_of("rep", 0)
        if stage == 0:
            self.gathered[y, c] = self.source[0]
            part, landing, bit = (y, c), (1 - y, c), 1
        elif stage == 1:
            part, landing, bit = (slice(None), c), (slice(None), 1 - c), 0
        else:
            self.pending = None
            return
        copy = lambda place: remote(
            self.gathered.at[part],
            self.gathered.at[place],
            self.sems.at[0, self.at],
            self.sems.at[1, self.at],
            "rep",
            bit_peer("rep", bit),
        )
        copy(part).start()
        self.pending = ("gather", copy(part), copy(landing), None)

    def finish(self):
        kind, first, second, mine = self.pending
        if kind == "sum":
            first.wait()
            rows = second.shape[0]

            def add(n, carry):
                at = (n,) if mine[0] == slice(None) else None
                if at is None:
                    head = mine[0]
                    base = head.start if isinstance(head, pl.Slice) else None
                    value = self.source[(base + n,) + mine[1:]]
                else:
                    value = self.source[at + mine[1:]]
                second[n] = (second[n].astype(f32) + value.astype(f32)).astype(bf16)
                return carry

            lax.fori_loop(0, rows, add, 0)
            self.source = second
        else:
            first.wait_send()
            second.wait_recv()
        self.at += 1

    def pump(self):
        if self.pending is not None:
            self.finish()
            self.start()

    def drain(self):
        while self.pending is not None:
            self.pump()
        self.out[...] = self.gathered[...]


def reduce_steps(order, seq_bits):
    steps = []
    for name in order:
        if name == "y":
            steps.append(("y", "rep", 1))
        elif name == "x":
            steps.append(("x", "seq", 0))
        elif name == "z":
            steps.append(("z", "seq", 1))
        else:
            steps += [("high", "seq", b) for b in range(seq_bits - 1, 1, -1)]
    return steps


def reduce_buffers(shape, steps):
    high, rows, cols = shape[0], shape[4], shape[5]
    left = 3
    out = []
    for name, _, _ in steps:
        if name == "high":
            high //= 2
        else:
            left -= 1
        out.append((high,) + (2,) * left + (rows, cols))
    return out


def grad_parts(width, hidden):
    return (
        (0, slice(0, width), "yzhx"),
        (1, slice(0, hidden // 2), "zhyx"),
        (1, slice(hidden // 2, hidden), "xyzh"),
        (2, slice(0, width), "xyzh"),
    )


def backward_body(
    r_hbm,
    p1_hbm,
    p2_hbm,
    da0_ref,
    da1_ref,
    att_ref,
    mix_ref,
    len_ref,
    w0_ref,
    w1_ref,
    w2_ref,
    tg_ref,
    t0_ref,
    t1_ref,
    t2_ref,
    *scratch,
    seq_bits,
):
    (r, p1, p2, g0, g1s, g2s, g1, g2, d1, d2, e1, e2, sums, ks, vs, qs, qr, gs, gr, dq) = scratch[:20]
    load_sems, g1_sems, g2_sems, d1_sems, d2_sems, tg_sems, tg1_sems, own_sems = scratch[20:28]
    rest = list(scratch[28:])
    halvings = []
    sources, outs = (w0_ref, w1_ref, w2_ref), (t0_ref, t1_ref, t2_ref)
    for n, lanes, order in grad_parts(w0_ref.shape[-1], w1_ref.shape[-1]):
        steps = reduce_steps(order, seq_bits)
        buffers = [rest.pop(0) for _ in steps]
        gathered, sems = rest.pop(0), rest.pop(0)
        source = sources[n].at[:, :, :, :, :, lanes]
        out = outs[n].at[:, :, :, lanes]
        halvings.append(Halving(source, steps, buffers, gathered, out, sems))
    reps, cols, tok = da0_ref.shape
    micros = att_ref.shape[0]
    span = tok * reps
    wide = span // 2
    me = lax.axis_index("rep")
    place = team_place()
    side = place % 2
    scr = (ks, vs, qs, qr, gs, gr, dq)

    barrier = pltpu.get_barrier_semaphore()
    peers = [("rep", rep_peer(k)) for k in range(1, 4)]
    peers += [("seq", team_member(k)) for k in range(1, 4)]
    peers += [("seq", bit_peer("seq", b)) for b in range(2, seq_bits)]
    for axis, peer in peers:
        pl.semaphore_signal(
            barrier, inc=1, device_id={axis: peer}, device_id_type=pl.DeviceIdType.MESH
        )
    load_r = lambda m: pltpu.make_async_copy(r_hbm.at[m], r, load_sems.at[0])
    load_1 = lambda m: pltpu.make_async_copy(p1_hbm.at[m], p1, load_sems.at[1])
    load_2 = lambda m: pltpu.make_async_copy(p2_hbm.at[m], p2, load_sems.at[2])
    load_r(0).start()
    load_1(0).start()
    load_2(0).start()
    pl.semaphore_wait(barrier, len(peers))
    for h in halvings:
        h.start()

    def pump():
        for h in halvings:
            h.pump()

    def g1_copy(m, s, source):
        return remote(
            g1s.at[m, s],
            g1.at[m, source, s],
            g1_sems.at[0, m, s],
            g1_sems.at[1, m, s],
            "seq",
            pair_partner(),
        )

    def g2_copy(m, k, source):
        return remote(
            g2s.at[m, (place + k) % 4],
            g2.at[m, source],
            g2_sems.at[0, m, k - 1],
            g2_sems.at[1, m, k - 1],
            "seq",
            team_member(k),
        )

    def d1_copy(m, s, source):
        return remote(
            d1.at[m, s, 1 - side],
            e1.at[m, source, s],
            d1_sems.at[0, m, s],
            d1_sems.at[1, m, s],
            "seq",
            pair_partner(),
        )

    def d2_copy(m, k, source):
        return remote(
            d2.at[m, (place + k) % 4],
            e2.at[m, source],
            d2_sems.at[0, m, k - 1],
            d2_sems.at[1, m, k - 1],
            "seq",
            team_member(k),
        )

    def tg0_copy(k, source):
        return remote(
            sums.at[0, rep_peer(k)],
            tg_ref.at[0, source],
            tg_sems.at[0, k - 1],
            tg_sems.at[1, k - 1],
            "rep",
            rep_peer(k),
        )

    def tg1_copy(j, k, source):
        return remote(
            sums.at[1, rep_peer(k), :, head_rows(j)],
            tg_ref.at[1, source, :, head_rows(j)],
            tg1_sems.at[0, j, k - 1],
            tg1_sems.at[1, j, k - 1],
            "rep",
            rep_peer(k),
        )

    own_copy = lambda m: pltpu.make_async_copy(sums.at[m, me], tg_ref.at[m, me], own_sems.at[m])

    def half(j):
        return pl.ds(pl.multiple_of(((3 * me + j) % 2) * 256, 256), 256)

    def quarter_at(j):
        c = (3 * me + j) % 4
        return c % 2 * 2 + c // 2

    def quarter(j):
        return pl.ds(pl.multiple_of(quarter_at(j) * 128, 128), 128)

    for m, da_ref in enumerate((da0_ref, da1_ref)):
        for j in range(3):
            rows = slice(j * HD, (j + 1) * HD)
            for b in range(reps):
                g = da_ref[b, rows, :]
                inner = jnp.sum(
                    g.astype(f32) * att_ref[m, b, rows, :].astype(f32), 0, keepdims=True
                )
                total = mix_ref[m, j : j + 1, b * tok : (b + 1) * tok]
                high, mid, low = split3(-total)
                inner_high, inner_mid, _ = split3(-inner)
                g0[m, j, b, :HD, :] = g
                g0[m, j, b, HD:, :] = stat_rows((high, mid, low, inner_high, inner_mid), tok)
        for b in range(reps):
            bl = slice(b * 256, (b + 1) * 256)
            g1s[m, 0, :, bl] = g0[m, 1 - side, b, :, half(1 - side)]
            g1[m, side, 0, :, bl] = g0[m, side, b, :, half(side)]
            piece = g0[m, 2, b, :, half(2)]
            g1s[m, 1, :, bl] = piece
            g1[m, side, 1, :, bl] = piece
            for g in range(4):
                j = clamp_slot(slot_of(g))
                g2s[m, g, :, b * 128 : (b + 1) * 128] = g0[m, j, b, :, quarter(j)]
        g2[m, place] = g2s[m, place]
        g1_copy(m, 0, side).start()

        @pl.when(side != taker())
        def _():
            g1_copy(m, 1, side).start()

        for k in range(1, 4):

            @pl.when(slot_of(place + k) < 3)
            def _():
                g2_copy(m, k, place).start()

    def docs(m, pattern):
        return doc_rows(len_ref, m, segment_start(pattern, span), 2**pattern, span)

    def own_head(m, j):
        def block(c, start, size):
            at = start % tok
            return r[start // tok, c, head_rows(j), at : at + size]

        def gblock(start, size):
            at = start % tok
            return g0[m, j, start // tok, :, at : at + size]

        def put(c, start, size, value):
            at = start % tok
            sums[m, start // tok, c, head_rows(j), at : at + size] = value

        attend_back(block, gblock, docs(m, 0), put, scr, 0, span, tok)

    def add_others(m, j):
        e, s = place1(j)
        for b in range(reps):
            bl = slice(b * 256, (b + 1) * 256)
            t = sums[m, b, :, j * HD : (j + 1) * HD, half(j)].astype(f32)
            t = t + e1[m, e, s, :, :, bl].astype(f32)
            sums[m, b, :, j * HD : (j + 1) * HD, half(j)] = t.astype(bf16)
            t = sums[m, b, :, j * HD : (j + 1) * HD, quarter(j)].astype(f32)
            t = t + e2[m, owner_of(j), :, :, b * 128 : (b + 1) * 128].astype(f32)
            sums[m, b, :, j * HD : (j + 1) * HD, quarter(j)] = t.astype(bf16)

    def wait_others(m):
        d1_copy(m, 0, 1 - side).wait_recv()

        @pl.when(side != taker())
        def _():
            d1_copy(m, 1, 1 - side).wait_recv()

        for k in range(1, 4):

            @pl.when(slot_of(place + 4 - k) < 3)
            def _():
                d2_copy(m, k, (place + 4 - k) % 4).wait_recv()

    load_r(0).wait()

    def first_heads(j, carry):
        own_head(0, j)
        return carry

    lax.fori_loop(0, 3, first_heads, 0)
    load_r(1).start()

    def others(m):
        def paired(s):
            g1_copy(m, s, 1 - side).wait_recv()

            def block(c, start, size):
                at = start % wide
                return p1[start // wide, s, c, :, at : at + size]

            def gblock(start, size):
                at = start % wide
                return g1[m, start // wide, s, :, at : at + size]

            def put(c, start, size, value):
                at = start % wide
                d1[m, s, start // wide, c, :, at : at + size] = value

            attend_back(block, gblock, docs(m, 1), put, scr, 1, span, wide)
            e1[m, side, s] = d1[m, s, side]
            d1_copy(m, s, side).start()

        def each_pair(s, inner):
            @pl.when((s == 0) | (side == taker()))
            def _():
                paired(s)

            return inner

        load_1(m).wait()
        lax.fori_loop(0, 2, each_pair, 0)
        if m + 1 < micros:
            load_1(m + 1).start()
        pump()
        if m == 1:
            wait_others(0)
            for j in range(3):
                add_others(0, j)
            for k in range(1, 4):
                tg0_copy(k, me).start()
            own_copy(0).start()
        load_2(m).wait()

        def block(c, start, size):
            at = start % tok
            return p2[start // tok, c, :, at : at + size]

        def gblock(start, size):
            at = start % tok
            return g2[m, start // tok, :, at : at + size]

        def put(c, start, size, value):
            at = start % tok
            d2[m, start // tok, c, :, at : at + size] = value

        @pl.when(slot_of(place) < 3)
        def _():
            for k in range(1, 4):
                g2_copy(m, k, (place + 4 - k) % 4).wait_recv()
            attend_back(block, gblock, docs(m, 2), put, scr, 2, span, tok)
            e2[m, place] = d2[m, place]
            for k in range(1, 4):
                d2_copy(m, k, place).start()

        if m + 1 < micros:
            load_2(m + 1).start()

    others(0)
    others(1)
    load_r(1).wait()
    for j in range(3):
        own_head(1, j)
        if j == 0:
            wait_others(1)
        add_others(1, j)
        for k in range(1, 4):
            tg1_copy(j, k, me).start()
        pump()
    own_copy(1).start()
    for h in halvings:
        h.drain()
    for m in range(micros):
        own_copy(m).wait()
        g1_copy(m, 0, side).wait_send()
        d1_copy(m, 0, side).wait_send()

        @pl.when(side != taker())
        def _():
            g1_copy(m, 1, side).wait_send()

        @pl.when(side == taker())
        def _():
            d1_copy(m, 1, side).wait_send()

        for k in range(1, 4):

            @pl.when(slot_of(place + k) < 3)
            def _():
                g2_copy(m, k, place).wait_send()

            @pl.when(slot_of(place) < 3)
            def _():
                d2_copy(m, k, place).wait_send()

    for k in range(1, 4):
        source = (me + reps - k) % reps
        tg0_copy(k, source).wait_recv()
        tg0_copy(k, me).wait_send()
        for j in range(3):
            tg1_copy(j, k, source).wait_recv()
            tg1_copy(j, k, me).wait_send()


def backward_call(pieces, da, att, totals, lengths, grads, seq_bits):
    micros, reps, cols, tok = att.shape
    span = tok * reps
    any_spec = pl.BlockSpec(memory_space=pl.ANY)

    def vm(*shape):
        return pltpu.VMEM(shape, bf16)

    dma = pltpu.SemaphoreType.DMA
    halving = []
    for n, lanes, order in grad_parts(grads[0].shape[-1], grads[1].shape[-1]):
        steps = reduce_steps(order, seq_bits)
        shape = grads[n].shape[:5] + (lanes.stop - lanes.start,)
        halving += [vm(*b) for b in reduce_buffers(shape, steps)]
        halving += [vm(2, 2, *shape[4:]), dma((2, len(steps) + 2))]
    tall, flat = vm(span, 128), vm(128, span)
    outs = [((micros, reps, 3, cols, tok), bf16, any_spec)]
    outs += [((2, 2) + g.shape[4:], bf16, vmem_spec()) for g in grads]
    return pl.pallas_call(
        functools.partial(backward_body, seq_bits=seq_bits),
        in_specs=[any_spec] * 3 + [vmem_spec()] * 4 + [smem_spec()] + [vmem_spec()] * 3,
        out_specs=[o[2] for o in outs],
        out_shape=[jax.ShapeDtypeStruct(o[0], o[1]) for o in outs],
        scratch_shapes=[
            vm(reps, 3, cols, tok),
            vm(2, 2, 3, HD, span // 2),
            vm(4, 3, HD, span // 4),
            vm(micros, 3, reps, HPAD, tok),
            vm(micros, 2, HPAD, span // 2),
            vm(micros, 4, HPAD, span // 4),
            vm(micros, 2, 2, HPAD, span // 2),
            vm(micros, 4, HPAD, span // 4),
            vm(micros, 2, 2, 3, HD, span // 2),
            vm(micros, 4, 3, HD, span // 4),
            vm(micros, 2, 2, 3, HD, span // 2),
            vm(micros, 4, 3, HD, span // 4),
            vm(micros, reps, 3, cols, tok),
            tall,
            tall,
            flat,
            tall,
            flat,
            tall,
            pltpu.VMEM((HD, span), f32),
            dma((3,)),
            dma((2, micros, 2)),
            dma((2, micros, 3)),
            dma((2, micros, 2)),
            dma((2, micros, 3)),
            dma((2, 3)),
            dma((2, 3, 3)),
            dma((micros,)),
            *halving,
        ],
        compiler_params=pltpu.CompilerParams(
            vmem_limit_bytes=60 << 20, collective_id=2, has_side_effects=True
        ),
        cost_estimate=pl.CostEstimate(
            flops=100_000_000_000, bytes_accessed=40_000_000, transcendentals=30_000_000
        ),
        name="backward",
    )(*pieces, *da, att, totals, lengths, *grads)


def store_parts(ref, value):
    parts, _, rows, _ = ref.shape
    for n in range(2 * parts):
        ref[n // 2, n % 2] = value[n * rows : (n + 1) * rows].astype(bf16)


def weight_grad_body(*refs, chunks):
    ins, da_ref, refs = refs[:12], refs[12], refs[13:]
    down_ref, up_ref, proj_ref, da_out, lt = refs[:5]
    values, gets, sems = refs[5:8], refs[8:11], refs[11:14]
    da_sems, own_sems = refs[14:]
    core = bit_of("rep", 0)
    me = lax.axis_index("rep")
    groups = [ins[:6], ins[6:]]
    n = pl.program_id(0)

    def copy(t, slot):
        return remote(
            values[t].at[slot, :, 1 - core],
            gets[t].at[slot],
            sems[t].at[0, slot],
            sems[t].at[1, slot],
            "rep",
            bit_peer("rep", 0),
        )

    def spread(t, slot, value):
        store_parts(values[t].at[slot], value)
        copy(t, slot).start()

    def da_copy(k, source):
        return remote(
            da_ref.at[rep_peer(k)],
            da_out.at[source],
            da_sems.at[0, k - 1],
            da_sems.at[1, k - 1],
            "rep",
            rep_peer(k),
        )

    da_own = pltpu.make_async_copy(da_ref.at[me], da_out.at[me], own_sems.at[0])

    @pl.when(n == 0)
    def _():
        barrier = pltpu.get_barrier_semaphore()
        for k in range(1, 4):
            pl.semaphore_signal(
                barrier, inc=1, device_id={"rep": rep_peer(k)}, device_id_type=pl.DeviceIdType.MESH
            )
        pl.semaphore_wait(barrier, 3)
        for k in range(1, 4):
            da_copy(k, me).start()
        da_own.start()
        total = None
        for k, (low, dup, hid, cot, mix, brl) in enumerate(groups):
            lt[k] = low[...].T
            part = dot_tn(mix[...], brl[...])
            total = part if total is None else total + part
        spread(2, 0, total)

    @pl.when(n < chunks)
    def _():
        up = down = None
        for k, (low, dup, hid, cot, mix, brl) in enumerate(groups):
            u = dot_nn(lt[k], dup[...])
            d = dot_tn(hid[...], cot[...])
            up = u if up is None else up + u
            down = d if down is None else down + d
        spread(0, n, down)
        spread(1, n, up)

    def merged(t, slot, out_ref):
        copy(t, slot).wait()
        value, got = values[t], gets[t]
        for k in range(got.shape[1]):
            out_ref[k] = (value[slot, k, core].astype(f32) + got[slot, k].astype(f32)).astype(bf16)

    @pl.when(n > 0)
    def _():
        merged(0, n - 1, down_ref)
        merged(1, n - 1, up_ref)

    @pl.when(n == chunks)
    def _():
        merged(2, 0, proj_ref)
        da_own.wait()
        for k in range(1, 4):
            da_copy(k, (me + 4 - k) % 4).wait_recv()
            da_copy(k, me).wait_send()


def weight_grads(group, da, width, hidden, seqs, reps):
    tok = group[0].shape[1]
    chunk = 768
    chunks = hidden // chunk
    last = chunks - 1

    def full(k):
        return pl.BlockSpec((None, tok, width), lambda n: (k, 0, 0))

    def part(k):
        return pl.BlockSpec((None, tok, chunk), lambda n: (k, 0, jnp.minimum(n, last)))

    def specs(k):
        return [full(k), part(k), part(k), full(k), full(k), full(k)]

    down_rows, up_rows = hidden // seqs // reps, width // seqs // reps
    per = chunk // down_rows // 2
    blocks = seqs * reps // 2
    shapes = [(chunks, per, down_rows, width), (chunks, blocks, up_rows, chunk), (1, blocks, up_rows, width)]
    return pl.pallas_call(
        functools.partial(weight_grad_body, chunks=chunks),
        grid=(chunks + 1,),
        in_specs=specs(0) + specs(1) + [vmem_spec()],
        out_specs=[
            pl.BlockSpec((per, down_rows, width), lambda n: (jnp.maximum(n - 1, 0), 0, 0)),
            pl.BlockSpec((blocks, up_rows, chunk), lambda n: (0, 0, jnp.maximum(n - 1, 0))),
            pl.BlockSpec((blocks, up_rows, width), lambda n: (0, 0, 0)),
            pl.BlockSpec(memory_space=pl.ANY),
        ],
        out_shape=[
            jax.ShapeDtypeStruct((blocks, down_rows, width), bf16),
            jax.ShapeDtypeStruct((blocks, up_rows, hidden), bf16),
            jax.ShapeDtypeStruct((blocks, up_rows, width), bf16),
            jax.ShapeDtypeStruct(da.shape, bf16),
        ],
        scratch_shapes=[pltpu.VMEM((2, width, tok), bf16)]
        + [pltpu.VMEM(b[:2] + (2,) + b[2:], bf16) for b in shapes]
        + [pltpu.VMEM(b, bf16) for b in shapes]
        + [pltpu.SemaphoreType.DMA((2, s[0])) for s in shapes]
        + [pltpu.SemaphoreType.DMA((2, 3)), pltpu.SemaphoreType.DMA((1,))],
        compiler_params=pltpu.CompilerParams(
            vmem_limit_bytes=VMEM, collective_id=3, has_side_effects=True
        ),
        cost_estimate=pl.CostEstimate(
            flops=4 * tok * width * (2 * hidden + width),
            bytes_accessed=30_000_000,
            transcendentals=0,
        ),
        name="weight_grads",
    )(*group, *group, da)


TAIL_ORDERS = ("yxzh", "xzhy", "zhyx")


def vec_rounds(seq_bits):
    rounds = [
        ("rep", lax.axis_index("rep"), [rep_peer(k) for k in range(1, 4)]),
        ("seq", team_place(), [team_member(k) for k in range(1, 4)]),
    ]
    for b in range(2, seq_bits):
        rounds.append(("seq", bit_of("seq", b), [bit_peer("seq", b)]))
    return rounds


def tail_body(
    tg_hbm,
    w_hbm,
    branch_hbm,
    xp_ref,
    nt_ref,
    gain_ref,
    ng_ref,
    nh_ref,
    out_ref,
    total_ref,
    norm_ref,
    hidden_ref,
    *scratch,
    seq_bits,
):
    tg, w, branch, acc, value, get, vec, load_sems, core_sems = scratch[:9]
    rest = list(scratch[9:])
    micros, tok, width = xp_ref.shape
    reps = tg.shape[2]
    parts = get.shape[1]
    core = bit_of("rep", 0)
    rounds = vec_rounds(seq_bits)

    barrier = pltpu.get_barrier_semaphore()
    peers = [(axis, peer) for axis, _, others in rounds for peer in others]
    for axis, peer in peers:
        pl.semaphore_signal(
            barrier, inc=1, device_id={axis: peer}, device_id_type=pl.DeviceIdType.MESH
        )
    loads = [
        pltpu.make_async_copy(tg_hbm.at[m, :, c], tg.at[m, c], load_sems.at[m * 3 + c])
        for c in range(3)
        for m in range(micros)
    ]
    loads += [pltpu.make_async_copy(w_hbm, w, load_sems.at[6])]
    loads += [
        pltpu.make_async_copy(branch_hbm.at[m], branch.at[m], load_sems.at[7 + m])
        for m in range(micros)
    ]
    for c in loads:
        c.start()
    pl.semaphore_wait(barrier, len(peers))

    def core_copy(c):
        return remote(
            value.at[c, :, 1 - core],
            get.at[c],
            core_sems.at[0, c],
            core_sems.at[1, c],
            "rep",
            bit_peer("rep", 0),
        )

    def piece(m, c):
        return jnp.concatenate([tg[m, c, r] for r in range(reps)], 0)

    for c in range(3):
        total = None
        for m in range(micros):
            loads[c * micros + m].wait()
            part = dot_nt(nt_ref[m], piece(m, c))
            total = part if total is None else total + part
        store_parts(value.at[c], total)
        core_copy(c).start()

    halvings = []
    for c, order in enumerate(TAIL_ORDERS):
        steps = reduce_steps(order, seq_bits)
        summed = rest.pop(0)
        buffers = [rest.pop(0) for _ in steps]
        gathered, sems = rest.pop(0), rest.pop(0)
        out = total_ref.at[:, :, :, c * width : (c + 1) * width]
        halvings.append(Halving(summed, steps, buffers, gathered, out, sems))

    def core_sum(c):
        core_copy(c).wait()
        summed = halvings[c].source

        def add(z, carry):
            for n in range(8):
                k = z * 8 + n
                total = value[c, k, core].astype(f32) + get[c, k].astype(f32)
                summed[z, n // 4, n // 2 % 2, n % 2] = total.astype(bf16)
            return carry

        lax.fori_loop(0, parts // 8, add, 0)
        halvings[c].start()

    loads[6].wait()

    def grad_part(m, c):
        part = dot_nn(w[:, c * width : (c + 1) * width], piece(m, c))
        if c == 0:
            acc[...] = part
        else:
            acc[...] += part

    def grad_end(m):
        xhat, rstd = normalize(xp_ref[m].astype(f32))
        dx, gain_i, bias_i = norm_back(acc[...].T, gain_ref[...].reshape(1, -1), xhat, rstd)
        loads[7 + m].wait()
        out_ref[m] = (branch[m] + dx).astype(bf16)
        return gain_i, bias_i

    core_sum(0)
    grad_part(0, 0)
    core_sum(1)
    grad_part(0, 1)
    core_sum(2)
    grad_part(0, 2)
    gain0, bias0 = grad_end(0)

    def pump():
        for h in halvings:
            h.pump()

    pump()
    grad_part(1, 0)
    grad_part(1, 1)
    pump()
    grad_part(1, 2)
    gain1, bias1 = grad_end(1)
    terms = [gain0 + gain1, bias0 + bias1]
    terms += [ng_ref[0, n : n + 1] + ng_ref[1, n : n + 1] for n in range(4)]
    terms += [jnp.zeros((2, width), f32)]
    fold = nh_ref.shape[2] // width
    for n in range(2):
        for k in range(fold):
            cl = slice(k * width, (k + 1) * width)
            terms.append(nh_ref[0, n : n + 1, cl] + nh_ref[1, n : n + 1, cl])
    terms = jnp.concatenate(terms, 0)
    for n, (axis, place, others) in enumerate(rounds):
        box, sems = vec[2 * n], vec[2 * n + 1]
        box[place] = terms
        copies = []
        for k, peer in enumerate(others):
            copies.append(
                remote(box.at[place], box.at[place], sems.at[0, k], sems.at[1, k], axis, peer)
            )
            copies[-1].start()
        pump()
        size = box.shape[0]
        for k in range(1, size):
            landing = (place + size - k) % size
            remote(
                box.at[landing],
                box.at[landing],
                sems.at[0, k - 1],
                sems.at[1, k - 1],
                axis,
                others[k - 1],
            ).wait_recv()
        terms = box[0]
        for k in range(1, size):
            terms = terms + box[k]
        for c in copies:
            c.wait_send()
    s = lax.axis_index("seq")
    seqs = 1 << seq_bits
    cols = terms.T
    acc[:, : cols.shape[1]] = cols


    def rows_at(block, size):
        if size % 8 == 0:
            return acc[pl.ds(pl.multiple_of(block * size, 8), size), :16]
        out = cols[:size]
        for n in range(1, width // size):
            out = jnp.where(block == n, cols[n * size : (n + 1) * size], out)
        return out

    norm_ref[...] = rows_at(s, norm_ref.shape[1]).T[:6]
    own = hidden_ref.shape[1]
    per = width // own
    picked = rows_at(s % per, own)
    out = jnp.zeros((own, 2), f32)
    for k in range(fold):
        pair = jnp.concatenate(
            [picked[:, 8 + k : 9 + k], picked[:, 8 + fold + k : 9 + fold + k]], 1
        )
        out = jnp.where(s // per == k, pair, out)
    hidden_ref[...] = out.T
    for h in halvings:
        h.drain()


def tail_call(tg, weight, branch, xp, nt, gain, ng, nh, seq_bits):
    micros, tok, width = xp.shape
    reps, _, cols = tg.shape[1:4]
    hidden = nh.shape[2]
    seqs = 1 << seq_bits
    rows = width // seqs // reps
    parts = seqs * reps // 2
    any_spec = pl.BlockSpec(memory_space=pl.ANY)

    def vm(*shape):
        return pltpu.VMEM(shape, bf16)

    dma = pltpu.SemaphoreType.DMA
    shape = (seqs // 4, 2, 2, reps // 2, rows, width)
    halving = []
    for order in TAIL_ORDERS:
        steps = reduce_steps(order, seq_bits)
        halving += [vm(*shape)] + [vm(*b) for b in reduce_buffers(shape, steps)]
        halving += [vm(2, 2, rows, width), dma((2, len(steps) + 2))]
    vec = []
    for size in (4, 4) + (2,) * (seq_bits - 2):
        vec += [pltpu.VMEM((size, 16, width), f32), dma((2, size - 1))]
    outs = [
        ((micros, tok, width), bf16),
        ((2, 2, rows, 3 * width), bf16),
        ((6, width // seqs), f32),
        ((2, hidden // seqs), f32),
    ]
    return pl.pallas_call(
        functools.partial(tail_body, seq_bits=seq_bits),
        in_specs=[any_spec] * 3 + [vmem_spec()] * 5,
        out_specs=[vmem_spec()] * 4,
        out_shape=[jax.ShapeDtypeStruct(s, d) for s, d in outs],
        scratch_shapes=[
            vm(micros, 3, reps, cols, tok),
            vm(width, 3 * width),
            pltpu.VMEM((micros, tok, width), f32),
            pltpu.VMEM((width, tok), f32),
            vm(3, parts, 2, rows, width),
            vm(3, parts, rows, width),
            vec,
            dma((9,)),
            dma((2, 3)),
            *halving,
        ],
        compiler_params=pltpu.CompilerParams(
            vmem_limit_bytes=VMEM, collective_id=4, has_side_effects=True
        ),
        cost_estimate=pl.CostEstimate(
            flops=24 * tok * width * width, bytes_accessed=20_000_000, transcendentals=0
        ),
        name="tail",
    )(tg, weight, branch, xp, nt, gain, ng, nh)


def finish_body(*refs):
    half = len(refs) // 2
    ins, outs = refs[:half], refs[half:]
    micros, tok, _ = ins[0].shape
    back = onehot_cols(tok)
    for a, o in zip(ins[:2], outs[:2]):
        for m in range(micros):
            o[m] = dot_nn(back, a[m]).astype(bf16)
    for a, o in zip(ins[2:], outs[2:]):
        o[...] = a[...].astype(f32)


def finish_call(tokens, grads):
    args = (*tokens, *grads)
    return pl.pallas_call(
        finish_body,
        in_specs=[vmem_spec()] * len(args),
        out_specs=[vmem_spec()] * len(args),
        out_shape=[jax.ShapeDtypeStruct(a.shape, bf16) for a in tokens]
        + [jax.ShapeDtypeStruct(a.shape, f32) for a in grads],
        compiler_params=pltpu.CompilerParams(vmem_limit_bytes=VMEM),
        cost_estimate=pl.CostEstimate(
            flops=2_000_000_000, bytes_accessed=12_000_000, transcendentals=0
        ),
        name="finish",
    )(*args)


def bits_of(count):
    return count.bit_length() - 1


def on_device(
    layer_in,
    qkv_weight,
    out_weight,
    up_weight,
    down_weight,
    input_gain,
    input_bias,
    mixer_gain,
    mixer_bias,
    block_gain,
    block_bias,
    hidden_gain,
    hidden_bias,
    output_grad,
    seq_lengths,
):
    micro_count, tok, width = layer_in.shape
    reps = lax.axis_size("rep")
    seqs = lax.axis_size("seq")
    seq_bits = bits_of(seqs)
    hidden = up_weight.shape[1]
    xp, nt, got_qkv, got_pair, got_four, own_att, got_att, totals = forward_call(
        layer_in, qkv_weight, input_gain, input_bias, seq_lengths, reps
    )
    out, ng, nh, branch, mix, low, hid, dup, brl, cotp, da0, da1 = ffn_call(
        own_att,
        got_att,
        xp,
        output_grad,
        (out_weight, up_weight, down_weight),
        (mixer_gain, mixer_bias, block_gain, block_bias, hidden_gain, hidden_bias),
    )
    *grads, da1 = weight_grads((low, dup, hid, cotp, mix, brl), da1, width, hidden, seqs, reps)
    grads = [g.reshape((seqs // 4, 2, 2, reps // 2) + g.shape[1:]) for g in grads]
    token_grad, *totals = backward_call(
        (got_qkv, got_pair, got_four), (da0, da1), own_att, totals, seq_lengths, grads, seq_bits
    )
    input_grad, qkv_total, norm_total, hidden_total = tail_call(
        token_grad, qkv_weight, branch, xp, nt, input_gain, ng, nh, seq_bits
    )
    down_total, up_total, proj_total, qkv_total = (
        t.reshape(-1, t.shape[-1]) for t in (*totals, qkv_total)
    )
    *results, norm_total, hidden_total = finish_call(
        (out, input_grad), (qkv_total, proj_total, up_total, down_total, norm_total, hidden_total)
    )
    return (*results, norm_total.T, hidden_total.T)


def solution(mesh):
    tokens = P(None, ("seq", "rep"), None)
    rows = P("seq", None)
    return jax.shard_map(
        on_device,
        mesh=mesh,
        in_specs=(tokens,) + (P(),) * 12 + (tokens, P()),
        out_specs=(tokens, tokens) + (rows,) * 6,
        check_vma=False,
    )
```

```python
import functools
import math

import jax
import jax.numpy as jnp
from jax import lax
from jax.experimental import pallas as pl
from jax.experimental.pallas import tpu as pltpu
from jax.sharding import PartitionSpec as P

HEADS = 12
HD = 64
HPAD = 80
CLASS_SLOT = (0, 2, 1, 3)
LOG2E = 1.4426950408889634
NEG = -1e30
EPS = 1e-05
VMEM = 56 << 20

f32 = jnp.float32
bf16 = jnp.bfloat16


def dot_nn(a, b):
    return lax.dot_general(a, b, (((1,), (0,)), ((), ())), preferred_element_type=f32)


def dot_nt(a, b):
    return lax.dot_general(a, b, (((1,), (1,)), ((), ())), preferred_element_type=f32)


def dot_tn(a, b):
    return lax.dot_general(a, b, (((0,), (0,)), ((), ())), preferred_element_type=f32)


def class_slot(cls):
    return jnp.where(cls == 1, 2, jnp.where(cls == 2, 1, cls))


def rel_pos(shape, dim, offset, pattern):
    i = lax.broadcasted_iota(jnp.int32, shape, dim) + offset
    if pattern == 0:
        return (i % 128) * 4 + class_slot((i // 128) % 4)
    if pattern == 1:
        return (i // 256) * 512 + (i % 128) * 4 + ((i // 128) % 2) * 2
    return i


def doc_rows(len_ref, micro, start, dilation, count):
    pos = lax.broadcasted_iota(jnp.int32, (1, count), 1) * dilation + start
    edge = len_ref[micro, 0]
    doc = (pos >= edge).astype(jnp.int32)
    for n in range(1, len_ref.shape[1] - 1):
        edge = edge + len_ref[micro, n]
        doc = doc + (pos >= edge).astype(jnp.int32)
    return doc


def segment_start(pattern, span):
    team = 2**pattern
    return (lax.axis_index("seq") // team) * (team * span)


def split3(x):
    hi = x.astype(bf16).astype(f32)
    mid = (x - hi).astype(bf16).astype(f32)
    return hi, mid, x - hi - mid


def stat_rows(rows, count):
    r = lax.broadcasted_iota(jnp.int32, (HPAD - HD, count), 0)
    out = jnp.zeros((HPAD - HD, count), f32)
    for n, row in enumerate(rows):
        out = jnp.where(r == n, row, out)
    return out.astype(bf16)


def shift():
    return lax.axis_index("rep") % 2


def taker():
    return shift()


def owner_of(j):
    return (j + shift()) % 4


def slot_of(place):
    return (place + 4 - shift()) % 4


def clamp_slot(j):
    return j - j // 3


def place1(j):
    return (taker(), 1) if j == 2 else (j, 0)


def smem_spec():
    return pl.BlockSpec(memory_space=pltpu.SMEM)


def vmem_spec():
    return pl.BlockSpec(memory_space=pltpu.VMEM)


def onehot_rows(tok):
    i = lax.broadcasted_iota(jnp.int32, (tok, tok), 0)
    t = lax.broadcasted_iota(jnp.int32, (tok, tok), 1)
    return ((i % 128) * 4 + class_slot(i // 128) == t).astype(bf16)


def onehot_cols(tok):
    t = lax.broadcasted_iota(jnp.int32, (tok, tok), 0)
    i = lax.broadcasted_iota(jnp.int32, (tok, tok), 1)
    return ((i % 128) * 4 + class_slot(i // 128) == t).astype(bf16)


def normalize(x):
    c = x - jnp.mean(x, axis=-1, keepdims=True)
    rstd = lax.rsqrt(jnp.mean(c * c, axis=-1, keepdims=True) + EPS)
    return c * rstd, rstd


def norm_back(grad, gain, xhat, rstd):
    dn = grad * gain
    low = jnp.mean(dn, axis=-1, keepdims=True)
    along = jnp.mean(dn * xhat, axis=-1, keepdims=True)
    dx = rstd * (dn - low - xhat * along)
    return dx, jnp.sum(grad * xhat, 0, keepdims=True), jnp.sum(grad, 0, keepdims=True)


CHUNK = 512
SQRT_HALF = 0.7071067811865476
INV_SQRT_2PI = 0.3989422804014327


def ffn_body(
    own_ref,
    got_hbm,
    xp_ref,
    cot_ref,
    wo_hbm,
    wu_hbm,
    wd_hbm,
    mg_ref,
    mb_ref,
    bg_ref,
    bb_ref,
    hg_ref,
    hb_ref,
    out_ref,
    ng_ref,
    nh_ref,
    branch_out,
    mix_out,
    low_out,
    hid_out,
    dup_out,
    brl_out,
    cotp_out,
    da0_out,
    da1_out,
    wo,
    wu,
    wd,
    g_scr,
    dg_scr,
    dn_scr,
    am_scr,
    acc_scr,
    att_scr,
    da_scr,
    branch,
    mix,
    low,
    hid,
    dup,
    brl,
    cotp,
    load_sems,
    out_sems,
    att_sems,
    da_sems,
    own_sems,
):
    micros, tok, width = xp_ref.shape
    hidden = hid.shape[1]
    chunks = hidden // CHUNK
    reps, cols = own_ref.shape[1:3]
    me = lax.axis_index("rep")
    loads = [
        pltpu.make_async_copy(a, b, load_sems.at[n])
        for n, (a, b) in enumerate(
            ((wo_hbm, wo), (wu_hbm, wu), (wd_hbm, wd), (got_hbm, att_scr.at[0]))
        )
    ]
    for n in (3, 0, 1, 2):
        loads[n].start()
    barrier = pltpu.get_barrier_semaphore()
    for k in range(1, 4):
        pl.semaphore_signal(
            barrier, inc=1, device_id={"rep": rep_peer(k)}, device_id_type=pl.DeviceIdType.MESH
        )
    pl.semaphore_wait(barrier, 3)

    def att_copy(k, source):
        return remote(
            own_ref.at[1, rep_peer(k)],
            att_scr.at[1, source],
            att_sems.at[0, k - 1],
            att_sems.at[1, k - 1],
            "rep",
            rep_peer(k),
        )

    def da_copy(k, source):
        return remote(
            da_scr.at[0, rep_peer(k)],
            da0_out.at[source],
            da_sems.at[0, k - 1],
            da_sems.at[1, k - 1],
            "rep",
            rep_peer(k),
        )

    da_own = pltpu.make_async_copy(da_scr.at[0, me], da0_out.at[me], own_sems.at[0])
    da_last = pltpu.make_async_copy(da_scr.at[1], da1_out, own_sems.at[1])
    for k in range(1, 4):
        att_copy(k, me).start()
    att_scr[1, me] = own_ref[1, me]
    pairs = (
        (branch, branch_out),
        (mix, mix_out),
        (low, low_out),
        (hid, hid_out),
        (dup, dup_out),
        (brl, brl_out),
        (cotp, cotp_out),
    )

    def out_copy(n, m):
        return pltpu.make_async_copy(pairs[n][0], pairs[n][1].at[m], out_sems.at[n])

    def lanes(n):
        return slice(n * CHUNK, (n + 1) * CHUNK)

    def row(ref, at=slice(None)):
        return ref[at].reshape(1, -1)

    def micro(m, carry):
        def before(n):
            @pl.when(m == 1)
            def _():
                out_copy(n, 0).wait()

        @pl.when(m == 0)
        def _():
            loads[3].wait()

        @pl.when(m == 1)
        def _():
            for k in range(1, 4):
                att_copy(k, (me + reps - k) % reps).wait_recv()

        before(6)
        cotp[...] = dot_nn(onehot_rows(tok), cot_ref[m]).astype(bf16)
        out_copy(6, m).start()
        att = att_scr[m].reshape(width, tok).T.astype(f32)
        ahat, _ = normalize(att)
        before(1)
        mix[...] = (ahat * row(mg_ref) + row(mb_ref)).astype(bf16)
        out_copy(1, m).start()

        @pl.when(m == 0)
        def _():
            loads[0].wait()

        am = xp_ref[m].astype(f32) + dot_nn(mix[...], wo[...])
        am_scr[...] = am
        bhat, _ = normalize(am)
        before(2)
        low[...] = (bhat * row(bg_ref) + row(bb_ref)).astype(bf16)
        out_copy(2, m).start()

        @pl.when(m == 0)
        def _():
            loads[1].wait()

        total = jnp.zeros((tok, 1), f32)
        for n in range(chunks):
            u = dot_nn(low[...], wu[:, lanes(n)])
            cdf = 0.5 + 0.5 * lax.erf(u * SQRT_HALF)
            g = u * cdf
            g_scr[:, lanes(n)] = g
            dg_scr[:, lanes(n)] = cdf + u * (jnp.exp(u * u * -0.5) * INV_SQRT_2PI)
            total = total + jnp.sum(g, 1, keepdims=True)
        mean = total / hidden
        total = jnp.zeros((tok, 1), f32)
        for n in range(chunks):
            c = g_scr[:, lanes(n)] - mean
            total = total + jnp.sum(c * c, 1, keepdims=True)
        rstd = lax.rsqrt(total / hidden + EPS)

        @pl.when(m == 0)
        def _():
            loads[2].wait()

        before(3)
        first = second = jnp.zeros((tok, 1), f32)
        for n in range(chunks):
            ghat = (g_scr[:, lanes(n)] - mean) * rstd
            g_scr[:, lanes(n)] = ghat
            gain = row(hg_ref, lanes(n))
            h = (ghat * gain + row(hb_ref, lanes(n))).astype(bf16)
            hid[:, lanes(n)] = h
            part = dot_nn(h, wd[lanes(n), :])
            if n == 0:
                acc_scr[...] = part
            else:
                acc_scr[...] += part
            back = dot_nt(cotp[...], wd[lanes(n), :])
            nh_ref[m, 0:1, lanes(n)] = jnp.sum(back * ghat, 0, keepdims=True)
            nh_ref[m, 1:2, lanes(n)] = jnp.sum(back, 0, keepdims=True)
            dn = back * gain
            dn_scr[:, lanes(n)] = dn
            first = first + jnp.sum(dn, 1, keepdims=True)
            second = second + jnp.sum(dn * ghat, 1, keepdims=True)
        first, second = first / hidden, second / hidden
        out_copy(3, m).start()
        out_ref[m] = (am_scr[...] + acc_scr[...]).astype(bf16)
        before(4)
        for n in range(chunks):
            d = rstd * (dn_scr[:, lanes(n)] - first - g_scr[:, lanes(n)] * second)
            t = (d * dg_scr[:, lanes(n)]).astype(bf16)
            dup[:, lanes(n)] = t
            part = dot_nt(t, wu[:, lanes(n)])
            if n == 0:
                acc_scr[...] = part
            else:
                acc_scr[...] += part
        out_copy(4, m).start()
        bhat, brstd = normalize(am_scr[...])
        middle, gain_b, bias_b = norm_back(acc_scr[...], row(bg_ref), bhat, brstd)
        total = cotp[...].astype(f32) + middle
        before(0)
        branch[...] = total
        out_copy(0, m).start()
        before(5)
        brl[...] = total.astype(bf16)
        out_copy(5, m).start()
        att = att_scr[m].reshape(width, tok).T.astype(f32)
        ahat, arstd = normalize(att)
        da, gain_m, bias_m = norm_back(dot_nt(brl[...], wo[...]), row(mg_ref), ahat, arstd)
        da_scr[m] = da.astype(bf16).T.reshape(reps, cols, tok)
        ng_ref[m, 0:1] = gain_m
        ng_ref[m, 1:2] = bias_m
        ng_ref[m, 2:3] = gain_b
        ng_ref[m, 3:4] = bias_b

        @pl.when(m == 0)
        def _():
            for k in range(1, 4):
                da_copy(k, me).start()
            da_own.start()

        return carry

    lax.fori_loop(0, micros, micro, 0)
    da_last.start()
    for n in range(len(pairs)):
        out_copy(n, 1).wait()
    for k in range(1, 4):
        att_copy(k, me).wait_send()
        da_copy(k, (me + reps - k) % reps).wait_recv()
        da_copy(k, me).wait_send()
    da_own.wait()
    da_last.wait()


def ffn_call(own, got, xp, output_grad, weights, gains):
    micros, reps, cols, tok = own.shape
    width = xp.shape[2]
    hidden = weights[1].shape[1]
    any_spec = pl.BlockSpec(memory_space=pl.ANY)
    wide, narrow = (tok, hidden), (tok, width)
    outs = [
        ((micros,) + narrow, bf16, vmem_spec()),
        ((micros, 4, width), f32, vmem_spec()),
        ((micros, 2, hidden), f32, vmem_spec()),
        ((micros,) + narrow, f32, any_spec),
        ((micros,) + narrow, bf16, any_spec),
        ((micros,) + narrow, bf16, any_spec),
        ((micros,) + wide, bf16, any_spec),
        ((micros,) + wide, bf16, any_spec),
        ((micros,) + narrow, bf16, any_spec),
        ((micros,) + narrow, bf16, any_spec),
        ((reps, cols, tok), bf16, any_spec),
        ((reps, cols, tok), bf16, any_spec),
    ]
    dma = pltpu.SemaphoreType.DMA
    return pl.pallas_call(
        ffn_body,
        in_specs=[vmem_spec(), any_spec, vmem_spec(), vmem_spec()]
        + [any_spec] * 3
        + [vmem_spec()] * len(gains),
        out_specs=[o[2] for o in outs],
        out_shape=[jax.ShapeDtypeStruct(o[0], o[1]) for o in outs],
        scratch_shapes=[pltpu.VMEM(w.shape, bf16) for w in weights]
        + [pltpu.VMEM(wide, f32)] * 3
        + [pltpu.VMEM(narrow, f32)] * 2
        + [pltpu.VMEM((2, reps, cols, tok), bf16)] * 2
        + [pltpu.VMEM(narrow, f32), pltpu.VMEM(narrow, bf16), pltpu.VMEM(narrow, bf16)]
        + [pltpu.VMEM(wide, bf16)] * 2
        + [pltpu.VMEM(narrow, bf16)] * 2
        + [dma((4,)), dma((7,)), dma((2, 3)), dma((2, 3)), dma((2,))],
        compiler_params=pltpu.CompilerParams(
            vmem_limit_bytes=60 << 20, collective_id=5, has_side_effects=True
        ),
        cost_estimate=pl.CostEstimate(
            flops=8 * tok * width * (2 * hidden + width),
            bytes_accessed=40_000_000,
            transcendentals=4 * tok * hidden,
        ),
        name="middle",
    )(own, got, xp, output_grad, *weights, *gains)


def rep_peer(k):
    count = lax.axis_size("rep")
    return (lax.axis_index("rep") + k) % count


def team_place():
    return lax.axis_index("seq") % 4


def team_member(k):
    s = lax.axis_index("seq")
    return s // 4 * 4 + (s + k) % 4


def pair_partner():
    s = lax.axis_index("seq")
    return s + 1 - 2 * (s % 2)


def remote(src, dst, send_sem, recv_sem, axis, peer):
    return pltpu.make_async_remote_copy(
        src_ref=src,
        dst_ref=dst,
        send_sem=send_sem,
        recv_sem=recv_sem,
        device_id={axis: peer},
        device_id_type=pl.DeviceIdType.MESH,
    )


def meet_peers():
    barrier = pltpu.get_barrier_semaphore()
    for k in range(1, 4):
        for axis, peer in (("rep", rep_peer(k)), ("seq", team_member(k))):
            pl.semaphore_signal(
                barrier, inc=1, device_id={axis: peer}, device_id_type=pl.DeviceIdType.MESH
            )
    pl.semaphore_wait(barrier, 6)


def head_rows(j):
    return pl.ds(pl.multiple_of(j * HD, HD), HD)


def attend(block, doc, put, ks, qs, pattern, count, lanes):
    kb = min(512, lanes)
    for s in range(0, count, kb):
        sl = slice(s, s + kb)
        r = lax.broadcasted_iota(jnp.int32, (HD, kb), 0)
        same = doc[:, sl] == r
        aux_k = jnp.where(same, 1.0, 0.0).astype(bf16)
        aux_q = jnp.where(same | (r >= 4), 0.0, NEG).astype(bf16)
        q = (block(0, s, kb).astype(f32) * 0.125).astype(bf16)
        qs[:, sl] = jnp.concatenate([q, aux_q], 0)
        ks[sl, :] = jnp.concatenate([block(1, s, kb), aux_k], 0).T

    qb = 256
    grain = 512 if pattern == 0 else 256

    def tiles(i):
        low = (i * qb) // grain * grain
        out = [(s, min(512, low - s), False) for s in range(0, low, 512)]
        return out + [(low, grain, True)]

    def scores(i):
        out = []
        for s, size, diagonal in tiles(i):
            t = dot_nn(ks[s : s + size, :], qs[:, i * qb : (i + 1) * qb])
            if diagonal:
                keep = rel_pos((size, qb), 0, s % 512, pattern) <= rel_pos(
                    (size, qb), 1, (i * qb) % 512, pattern
                )
                t = jnp.where(keep, t, NEG)
            out.append(t)
        return out

    following = scores(0)
    for i in range(count // qb):
        current = following
        if (i + 1) * qb < count:
            following = scores(i + 1)
        top = functools.reduce(jnp.maximum, [jnp.max(t, 0, keepdims=True) for t in current])
        top2 = top * LOG2E
        acc, total = None, None
        for t, (s, size, _) in zip(current, tiles(i)):
            p = jnp.exp2(t * LOG2E - top2)
            part = jnp.sum(p, 0, keepdims=True)
            out = dot_nn(block(2, s, size), p.astype(bf16))
            acc = out if acc is None else acc + out
            total = part if total is None else total + part
        lse = top + jnp.log(total)
        put(i * qb, qb, (acc / total).astype(bf16), stat_rows(split3(lse), qb))


def forward_body(
    x_ref,
    w_ref,
    gain_ref,
    bias_ref,
    len_ref,
    xp_ref,
    nt_ref,
    r_out,
    p1_out,
    p2_out,
    att_ref,
    got_ref,
    mix_ref,
    sent,
    r,
    stage1,
    stage2,
    p1,
    p2,
    o0,
    o1,
    o2,
    b1,
    b2,
    ks,
    qs,
    qkv_sems,
    p1_sems,
    p2_sems,
    b1_sems,
    b2_sems,
    att_sems,
    out_sems,
):
    micros, tok, width = x_ref.shape
    reps = r.shape[1]
    span = tok * reps
    cols = width // reps
    me = lax.axis_index("rep")
    place = team_place()
    side = place % 2
    meet_peers()

    def qkv_copy(m, j, k, source):
        return remote(
            sent.at[m, rep_peer(k), :, head_rows(j)],
            r.at[m, source, :, head_rows(j)],
            qkv_sems.at[0, m, j, k - 1],
            qkv_sems.at[1, m, j, k - 1],
            "rep",
            rep_peer(k),
        )

    def p1_copy(m, s, source):
        return remote(
            stage1.at[m, s],
            p1.at[m, source, s],
            p1_sems.at[0, m, s],
            p1_sems.at[1, m, s],
            "seq",
            pair_partner(),
        )

    def p2_copy(m, k, source):
        return remote(
            stage2.at[m, (place + k) % 4],
            p2.at[m, source],
            p2_sems.at[0, m, k - 1],
            p2_sems.at[1, m, k - 1],
            "seq",
            team_member(k),
        )

    def b1_copy(m, s, source):
        return remote(
            o1.at[m, s, 1 - side],
            b1.at[m, source, s],
            b1_sems.at[0, m, s],
            b1_sems.at[1, m, s],
            "seq",
            pair_partner(),
        )

    def b2_copy(m, k, source):
        return remote(
            o2.at[m, (place + k) % 4],
            b2.at[m, source],
            b2_sems.at[0, m, k - 1],
            b2_sems.at[1, m, k - 1],
            "seq",
            team_member(k),
        )

    def att_copy(k, source):
        return remote(
            att_ref.at[0, rep_peer(k)],
            got_ref.at[source],
            att_sems.at[0, k - 1],
            att_sems.at[1, k - 1],
            "rep",
            rep_peer(k),
        )

    def out_copies(m):
        return (
            pltpu.make_async_copy(r.at[m], r_out.at[m], out_sems.at[m, 0]),
            pltpu.make_async_copy(p1.at[m], p1_out.at[m], out_sems.at[m, 1]),
            pltpu.make_async_copy(p2.at[m], p2_out.at[m], out_sems.at[m, 2]),
        )

    def project(m, carry):
        xp = dot_nn(onehot_rows(tok), x_ref[m])
        xp_ref[m] = xp.astype(bf16)
        xhat, _ = normalize(xp)
        n = (xhat * gain_ref[...].reshape(1, -1) + bias_ref[...].reshape(1, -1)).astype(bf16)
        nt_ref[m] = n.T
        for c in range(3):
            t = dot_nn(n, w_ref[:, c * width : (c + 1) * width]).astype(bf16).T
            for d in range(reps):
                sent[m, d, c] = t[d * cols : (d + 1) * cols]
        for j in range(3):
            for k in range(1, 4):
                qkv_copy(m, j, k, me).start()
        r[m, me] = sent[m, me]
        return carry

    lax.fori_loop(0, micros, project, 0)

    def half(j):
        return pl.ds(pl.multiple_of(((3 * me + j) % 2) * 256, 256), 256)

    def quarter_at(j):
        c = (3 * me + j) % 4
        return c % 2 * 2 + c // 2

    def quarter(j):
        return pl.ds(pl.multiple_of(quarter_at(j) * 128, 128), 128)

    def send_first(m):
        for b in range(reps):
            bl = slice(b * 256, (b + 1) * 256)
            stage1[m, 0, :, :, bl] = r[m, b, :, head_rows(1 - side), half(1 - side)]
            p1[m, side, 0, :, :, bl] = r[m, b, :, head_rows(side), half(side)]
        p1_copy(m, 0, side).start()

    def send_second(m):
        for b in range(reps):
            bl = slice(b * 256, (b + 1) * 256)
            piece = r[m, b, :, head_rows(2), half(2)]
            stage1[m, 1, :, :, bl] = piece
            p1[m, side, 1, :, :, bl] = piece

        @pl.when(side != taker())
        def _():
            p1_copy(m, 1, side).start()

        for g in range(4):
            j = clamp_slot(slot_of(g))
            for b in range(reps):
                stage2[m, g, :, :, b * 128 : (b + 1) * 128] = r[m, b, :, head_rows(j), quarter(j)]
        p2[m, place] = stage2[m, place]
        for k in range(1, 4):

            @pl.when(slot_of(place + k) < 3)
            def _():
                p2_copy(m, k, place).start()

    def mix_all(m):
        b1_copy(m, 0, 1 - side).wait_recv()

        @pl.when(side != taker())
        def _():
            b1_copy(m, 1, 1 - side).wait_recv()

        for k in range(1, 4):

            @pl.when(slot_of(place + 4 - k) < 3)
            def _():
                b2_copy(m, k, (place + 4 - k) % 4).wait_recv()

        def stat(tile):
            t = tile[HD:, :].astype(f32)
            return t[0:1] + t[1:2] + t[2:3]

        mix_ref[m] = jnp.zeros(mix_ref.shape[1:], f32)
        for j in range(3):
            e, s = place1(j)
            for b in range(reps):
                for a in range(4):
                    la = slice(a * 128, (a + 1) * 128)
                    lb = b * 256 + (a % 2) * 128
                    t0 = o0[m, j, b, :, la]
                    t1 = b1[m, e, s, :, lb : lb + 128]
                    t2 = b2[m, owner_of(j), :, b * 128 : (b + 1) * 128]
                    l0 = stat(t0)
                    l1 = jnp.where((3 * me + j) % 2 == a // 2, stat(t1), NEG)
                    l2 = jnp.where(quarter_at(j) == a, stat(t2), NEG)
                    top = jnp.maximum(jnp.maximum(l0, l1), l2)
                    e0, e1, e2 = jnp.exp(l0 - top), jnp.exp(l1 - top), jnp.exp(l2 - top)
                    total = e0 + e1 + e2
                    inv = 1.0 / total
                    mixed = (
                        t0[:HD].astype(f32) * (e0 * inv)
                        + t1[:HD].astype(f32) * (e1 * inv)
                        + t2[:HD].astype(f32) * (e2 * inv)
                    )
                    att_ref[m, b, j * HD : (j + 1) * HD, la] = mixed.astype(bf16)
                    col = b * tok + a * 128
                    mix_ref[m, j : j + 1, col : col + 128] = top + jnp.log(total)

    docs_of = lambda m, pattern: doc_rows(
        len_ref, m, segment_start(pattern, span), 2**pattern, span
    )

    def micro(m, carry):
        def local(j, inner):
            for k in range(1, 4):
                qkv_copy(m, j, k, (me + reps - k) % reps).wait_recv()

            @pl.when(j == 1)
            def _():
                send_first(m)

            @pl.when(j == 2)
            def _():
                send_second(m)

            def block(c, start, size):
                at = start % tok
                return r[m, start // tok, c, head_rows(j), at : at + size]

            def put(start, size, out, stats):
                at = start % tok
                o0[m, j, start // tok, :HD, at : at + size] = out
                o0[m, j, start // tok, HD:, at : at + size] = stats

            attend(block, docs_of(m, 0), put, ks, qs, 0, span, tok)
            return inner

        lax.fori_loop(0, 3, local, 0)

        @pl.when(m == 1)
        def _():
            mix_all(0)
            for k in range(1, 4):
                att_copy(k, me).start()
            got_ref[me] = att_ref[0, me]

        wide = span // 2

        def paired(s):
            p1_copy(m, s, 1 - side).wait_recv()

            def block(c, start, size):
                at = start % wide
                return p1[m, start // wide, s, c, :, at : at + size]

            def put(start, size, out, stats):
                at = start % wide
                o1[m, s, start // wide, :HD, at : at + size] = out
                o1[m, s, start // wide, HD:, at : at + size] = stats

            attend(block, docs_of(m, 1), put, ks, qs, 1, span, wide)
            b1[m, side, s] = o1[m, s, side]
            b1_copy(m, s, side).start()

        def each_pair(s, inner):
            @pl.when((s == 0) | (side == taker()))
            def _():
                paired(s)

            return inner

        lax.fori_loop(0, 2, each_pair, 0)

        def block(c, start, size):
            at = start % tok
            return p2[m, start // tok, c, :, at : at + size]

        def put(start, size, out, stats):
            at = start % tok
            o2[m, start // tok, :HD, at : at + size] = out
            o2[m, start // tok, HD:, at : at + size] = stats

        @pl.when(slot_of(place) < 3)
        def _():
            for k in range(1, 4):
                p2_copy(m, k, (place + 4 - k) % 4).wait_recv()
            attend(block, docs_of(m, 2), put, ks, qs, 2, span, tok)
            b2[m, place] = o2[m, place]
            for k in range(1, 4):
                b2_copy(m, k, place).start()

        for c in out_copies(m):
            c.start()
        return carry

    lax.fori_loop(0, micros, micro, 0)
    mix_all(1)
    for k in range(1, 4):
        att_copy(k, (me + reps - k) % reps).wait_recv()
        att_copy(k, me).wait_send()

    def finish(m, carry):
        for c in out_copies(m):
            c.wait()
        for k in range(1, 4):
            for j in range(3):
                qkv_copy(m, j, k, me).wait_send()

            @pl.when(slot_of(place + k) < 3)
            def _():
                p2_copy(m, k, place).wait_send()

            @pl.when(slot_of(place) < 3)
            def _():
                b2_copy(m, k, place).wait_send()

        p1_copy(m, 0, side).wait_send()
        b1_copy(m, 0, side).wait_send()

        @pl.when(side != taker())
        def _():
            p1_copy(m, 1, side).wait_send()

        @pl.when(side == taker())
        def _():
            b1_copy(m, 1, side).wait_send()

        return carry

    lax.fori_loop(0, micros, finish, 0)


def forward_call(layer_in, weight, gain, bias, lengths, reps):
    micros, tok, width = layer_in.shape
    span, cols = tok * reps, width // reps
    any_spec = pl.BlockSpec(memory_space=pl.ANY)
    outs = [
        ((micros, tok, width), bf16, vmem_spec()),
        ((micros, width, tok), bf16, vmem_spec()),
        ((micros, reps, 3, cols, tok), bf16, any_spec),
        ((micros, 2, 2, 3, HD, span // 2), bf16, any_spec),
        ((micros, 4, 3, HD, span // 4), bf16, any_spec),
        ((micros, reps, cols, tok), bf16, vmem_spec()),
        ((reps, cols, tok), bf16, vmem_spec()),
        ((micros, 8, span), f32, vmem_spec()),
    ]

    def vm(*shape):
        return pltpu.VMEM(shape, bf16)

    dma = pltpu.SemaphoreType.DMA
    return pl.pallas_call(
        forward_body,
        in_specs=[vmem_spec()] * 4 + [smem_spec()],
        out_specs=[o[2] for o in outs],
        out_shape=[jax.ShapeDtypeStruct(o[0], o[1]) for o in outs],
        scratch_shapes=[
            vm(micros, reps, 3, cols, tok),
            vm(micros, reps, 3, cols, tok),
            vm(micros, 2, 3, HD, span // 2),
            vm(micros, 4, 3, HD, span // 4),
            vm(micros, 2, 2, 3, HD, span // 2),
            vm(micros, 4, 3, HD, span // 4),
            vm(micros, 3, reps, HPAD, tok),
            vm(micros, 2, 2, HPAD, span // 2),
            vm(micros, 4, HPAD, span // 4),
            vm(micros, 2, 2, HPAD, span // 2),
            vm(micros, 4, HPAD, span // 4),
            vm(span, 128),
            vm(128, span),
            dma((2, micros, 3, 3)),
            dma((2, micros, 2)),
            dma((2, micros, 3)),
            dma((2, micros, 2)),
            dma((2, micros, 3)),
            dma((2, 3)),
            dma((micros, 3)),
        ],
        compiler_params=pltpu.CompilerParams(
            vmem_limit_bytes=VMEM, collective_id=1, has_side_effects=True
        ),
        cost_estimate=pl.CostEstimate(
            flops=60_000_000_000, bytes_accessed=30_000_000, transcendentals=30_000_000
        ),
        name="forward",
    )(layer_in, weight, gain, bias, lengths)


def bit_of(axis, bit):
    return lax.axis_index(axis) // (1 << bit) % 2


def bit_peer(axis, bit):
    return lax.axis_index(axis) + (1 << bit) * (1 - 2 * bit_of(axis, bit))


def attend_back(block, gblock, doc, put, scr, pattern, count, lanes, done=None):
    ks, vs, qs, qr, gs, gr, dq = scr
    bs = min(512, lanes)
    zeros = jnp.zeros((HD, bs), bf16)
    r = lax.broadcasted_iota(jnp.int32, (HD, bs), 0)
    fill = jnp.zeros((HD - 32, bs), bf16)
    for s in range(0, count, bs):
        sl = slice(s, s + bs)
        same = doc[:, sl] == r
        aux_k = jnp.where(same | ((r >= 16) & (r < 19)), 1.0, 0.0).astype(bf16)
        aux_q = jnp.where(same | (r >= 4), 0.0, NEG).astype(bf16)
        aux_v = jnp.where((r >= 19) & (r < 21), 1.0, 0.0).astype(bf16)
        q = (block(0, s, bs).astype(f32) * 0.125).astype(bf16)
        tile = gblock(s, bs)
        g, stats = tile[:HD], tile[HD:]
        qs[:, sl] = jnp.concatenate([q, aux_q[:16], stats, fill], 0)
        gs[:, sl] = jnp.concatenate([g, zeros[:16], stats, fill], 0)
        qr[sl, :] = jnp.concatenate([q, zeros], 0).T
        gr[sl, :] = jnp.concatenate([g, zeros], 0).T
        ks[sl, :] = jnp.concatenate([block(1, s, bs), aux_k], 0).T
        vs[sl, :] = jnp.concatenate([block(2, s, bs), aux_v], 0).T

    def tile(k, ksize, q, qsize, diagonal):
        kl, ql = slice(k, k + ksize), slice(q, q + qsize)
        p = jnp.exp2(dot_nn(ks[kl, :], qs[:, ql]) * LOG2E)
        if diagonal:
            keep = rel_pos((ksize, qsize), 0, k % bs, pattern) <= rel_pos(
                (ksize, qsize), 1, q % bs, pattern
            )
            p = jnp.where(keep, p, 0.0)
        dp = dot_nn(vs[kl, :], gs[:, ql])
        ds = (p * dp).astype(bf16)
        dv = dot_nn(p.astype(bf16), gr[ql, :])
        dk = dot_nn(ds, qr[ql, :])
        return dv, dk, dot_nn(block(1, k, ksize), ds) * 0.125

    def add_dq(k, q, qsize, value):
        if k == 0:
            dq[:, q : q + qsize] = value
        else:
            dq[:, q : q + qsize] += value

    for j in range(count // bs):
        at = j * bs
        jl = slice(at, at + bs)
        if pattern == 0:
            dva, dka, dqi = tile(at, bs, at, bs, True)
            add_dq(at, at, bs, dqi)
        else:
            h = bs // 2
            dv0, dk0, dqi = tile(at, h, at, bs, True)
            add_dq(at, at, bs, dqi)
            dv1, dk1, dqi = tile(at + h, h, at + h, h, True)
            add_dq(at + h, at + h, h, dqi)
            dva, dka = jnp.concatenate([dv0, dv1], 0), jnp.concatenate([dk0, dk1], 0)
        for i in range(j + 1, count // bs):
            dvi, dki, dqi = tile(at, bs, i * bs, bs, False)
            dva, dka = dva + dvi, dka + dki
            add_dq(at, i * bs, bs, dqi)
        put(1, j * bs, bs, dka.T[:HD].astype(bf16))
        put(2, j * bs, bs, dva.T[:HD].astype(bf16))
        put(0, j * bs, bs, dq[:, jl].astype(bf16))
        if done is not None:
            done(j)


class Halving:
    def __init__(self, source, steps, buffers, gathered, out, sems):
        self.source, self.steps, self.buffers = source, steps, buffers
        self.gathered, self.out, self.sems = gathered, out, sems
        self.names = ["high", "z", "x", "y"]
        self.at = 0
        self.pending = None

    def pick(self, ref, axis, name, index):
        lead = (slice(None),) * axis
        if name == "high":
            half = ref.shape[axis] // 2
            return lead + (pl.ds(index * half, half),)
        return lead + (index,)

    def start(self):
        if self.at < len(self.steps):
            name, axis_name, bit = self.steps[self.at]
            axis = self.names.index(name)
            mine = bit_of(axis_name, bit)
            target = self.buffers[self.at]
            copy = remote(
                self.source.at[self.pick(self.source, axis, name, 1 - mine)],
                target,
                self.sems.at[0, self.at],
                self.sems.at[1, self.at],
                axis_name,
                bit_peer(axis_name, bit),
            )
            copy.start()
            self.pending = ("sum", copy, target, self.pick(self.source, axis, name, mine))
            if name != "high":
                self.names.pop(axis)
            return
        if self.at > len(self.steps):
            self.pending = None
            return
        me = lax.axis_index("rep")
        self.gathered[me // 2, me % 2] = self.source[0]

        def copy(k, source):
            place = (source // 2, source % 2)
            return remote(
                self.gathered.at[place],
                self.gathered.at[place],
                self.sems.at[0, self.at + k - 1],
                self.sems.at[1, self.at + k - 1],
                "rep",
                rep_peer(k),
            )

        pairs = []
        for k in range(1, 4):
            copy(k, me).start()
            pairs.append((copy(k, me), copy(k, (me + 4 - k) % 4)))
        self.pending = ("gather", pairs, None, None)

    def finish(self):
        kind, first, second, mine = self.pending
        if kind == "sum":
            first.wait()
            rows = second.shape[0]

            def add(n, carry):
                at = (n,) if mine[0] == slice(None) else None
                if at is None:
                    head = mine[0]
                    base = head.start if isinstance(head, pl.Slice) else None
                    value = self.source[(base + n,) + mine[1:]]
                else:
                    value = self.source[at + mine[1:]]
                second[n] = (second[n].astype(f32) + value.astype(f32)).astype(bf16)
                return carry

            lax.fori_loop(0, rows, add, 0)
            self.source = second
        else:
            for sent, landed in first:
                sent.wait_send()
                landed.wait_recv()
        self.at += 1

    def pump(self):
        if self.pending is not None:
            self.finish()
            self.start()

    def drain(self):
        while self.pending is not None:
            self.pump()
        self.out[...] = self.gathered[...]


def reduce_steps(order, seq_bits):
    steps = []
    for name in order:
        if name == "y":
            steps.append(("y", "rep", 1))
        elif name == "x":
            steps.append(("x", "seq", 0))
        elif name == "z":
            steps.append(("z", "seq", 1))
        else:
            steps += [("high", "seq", b) for b in range(seq_bits - 1, 1, -1)]
    return steps


def reduce_buffers(shape, steps):
    high, rows, cols = shape[0], shape[4], shape[5]
    left = 3
    out = []
    for name, _, _ in steps:
        if name == "high":
            high //= 2
        else:
            left -= 1
        out.append((high,) + (2,) * left + (rows, cols))
    return out


def grad_parts(width, hidden):
    return (
        (0, slice(0, width), "yzhx"),
        (1, slice(0, hidden // 2), "zhyx"),
        (1, slice(hidden // 2, hidden), "yxzh"),
        (2, slice(0, width), "zhyx"),
    )


def backward_body(
    r_hbm,
    p1_hbm,
    p2_hbm,
    da0_ref,
    da1_ref,
    att_ref,
    mix_ref,
    len_ref,
    w0_ref,
    w1_ref,
    w2_ref,
    tg_ref,
    t0_ref,
    t1_ref,
    t2_ref,
    *scratch,
    seq_bits,
):
    (r, p1, p2, g0, g1s, g2s, g1, g2, d1, d2, e1, e2, sums, ks, vs, qs, qr, gs, gr, dq) = scratch[:20]
    load_sems, g1_sems, g2_sems, d1_sems, d2_sems, tg_sems, own_sems = scratch[20:27]
    rest = list(scratch[27:])
    halvings = []
    sources, outs = (w0_ref, w1_ref, w2_ref), (t0_ref, t1_ref, t2_ref)
    for n, lanes, order in grad_parts(w0_ref.shape[-1], w1_ref.shape[-1]):
        steps = reduce_steps(order, seq_bits)
        buffers = [rest.pop(0) for _ in steps]
        gathered, sems = rest.pop(0), rest.pop(0)
        source = sources[n].at[:, :, :, :, :, lanes]
        out = outs[n].at[:, :, :, lanes]
        halvings.append(Halving(source, steps, buffers, gathered, out, sems))
    reps, cols, tok = da0_ref.shape
    micros = att_ref.shape[0]
    span = tok * reps
    wide = span // 2
    me = lax.axis_index("rep")
    place = team_place()
    side = place % 2
    scr = (ks, vs, qs, qr, gs, gr, dq)

    barrier = pltpu.get_barrier_semaphore()
    peers = [("rep", rep_peer(k)) for k in range(1, 4)]
    peers += [("seq", team_member(k)) for k in range(1, 4)]
    peers += [("seq", bit_peer("seq", b)) for b in range(2, seq_bits)]
    for axis, peer in peers:
        pl.semaphore_signal(
            barrier, inc=1, device_id={axis: peer}, device_id_type=pl.DeviceIdType.MESH
        )
    load_r = lambda m: pltpu.make_async_copy(r_hbm.at[m], r, load_sems.at[0])
    load_1 = lambda m: pltpu.make_async_copy(p1_hbm.at[m], p1, load_sems.at[1])
    load_2 = lambda m: pltpu.make_async_copy(p2_hbm.at[m], p2, load_sems.at[2])
    load_r(0).start()
    load_1(0).start()
    load_2(0).start()
    pl.semaphore_wait(barrier, len(peers))
    for h in halvings:
        h.start()

    def pump():
        for h in halvings:
            h.pump()

    def g1_copy(m, s, source):
        return remote(
            g1s.at[m, s],
            g1.at[m, source, s],
            g1_sems.at[0, m, s],
            g1_sems.at[1, m, s],
            "seq",
            pair_partner(),
        )

    def g2_copy(m, k, source):
        return remote(
            g2s.at[m, (place + k) % 4],
            g2.at[m, source],
            g2_sems.at[0, m, k - 1],
            g2_sems.at[1, m, k - 1],
            "seq",
            team_member(k),
        )

    def d1_copy(m, s, source):
        return remote(
            d1.at[m, s, 1 - side],
            e1.at[m, source, s],
            d1_sems.at[0, m, s],
            d1_sems.at[1, m, s],
            "seq",
            pair_partner(),
        )

    def d2_copy(m, k, source):
        return remote(
            d2.at[m, (place + k) % 4],
            e2.at[m, source],
            d2_sems.at[0, m, k - 1],
            d2_sems.at[1, m, k - 1],
            "seq",
            team_member(k),
        )

    def tg_copy(m, j, k, source):
        return remote(
            sums.at[m, rep_peer(k), :, head_rows(j)],
            tg_ref.at[m, source, :, head_rows(j)],
            tg_sems.at[0, m, j, k - 1],
            tg_sems.at[1, m, j, k - 1],
            "rep",
            rep_peer(k),
        )

    own_copy = lambda m: pltpu.make_async_copy(sums.at[m, me], tg_ref.at[m, me], own_sems.at[m])

    def half(j):
        return pl.ds(pl.multiple_of(((3 * me + j) % 2) * 256, 256), 256)

    def quarter_at(j):
        c = (3 * me + j) % 4
        return c % 2 * 2 + c // 2

    def quarter(j):
        return pl.ds(pl.multiple_of(quarter_at(j) * 128, 128), 128)

    for m, da_ref in enumerate((da0_ref, da1_ref)):
        for j in range(3):
            rows = slice(j * HD, (j + 1) * HD)
            for b in range(reps):
                g = da_ref[b, rows, :]
                inner = jnp.sum(
                    g.astype(f32) * att_ref[m, b, rows, :].astype(f32), 0, keepdims=True
                )
                total = mix_ref[m, j : j + 1, b * tok : (b + 1) * tok]
                high, mid, low = split3(-total)
                inner_high, inner_mid, _ = split3(-inner)
                g0[m, j, b, :HD, :] = g
                g0[m, j, b, HD:, :] = stat_rows((high, mid, low, inner_high, inner_mid), tok)
        for b in range(reps):
            bl = slice(b * 256, (b + 1) * 256)
            g1s[m, 0, :, bl] = g0[m, 1 - side, b, :, half(1 - side)]
            g1[m, side, 0, :, bl] = g0[m, side, b, :, half(side)]
            piece = g0[m, 2, b, :, half(2)]
            g1s[m, 1, :, bl] = piece
            g1[m, side, 1, :, bl] = piece
            for g in range(4):
                j = clamp_slot(slot_of(g))
                g2s[m, g, :, b * 128 : (b + 1) * 128] = g0[m, j, b, :, quarter(j)]
        g2[m, place] = g2s[m, place]
        g1_copy(m, 0, side).start()

        @pl.when(side != taker())
        def _():
            g1_copy(m, 1, side).start()

        for k in range(1, 4):

            @pl.when(slot_of(place + k) < 3)
            def _():
                g2_copy(m, k, place).start()

    def docs(m, pattern):
        return doc_rows(len_ref, m, segment_start(pattern, span), 2**pattern, span)

    def own_head(m, j, done=None):
        def block(c, start, size):
            at = start % tok
            return r[start // tok, c, head_rows(j), at : at + size]

        def gblock(start, size):
            at = start % tok
            return g0[m, j, start // tok, :, at : at + size]

        def put(c, start, size, value):
            at = start % tok
            sums[m, start // tok, c, head_rows(j), at : at + size] = value

        attend_back(block, gblock, docs(m, 0), put, scr, 0, span, tok, done)

    def add_others(m, j, b):
        s = j // 2
        e = s * taker() + (1 - s) * j
        bl = slice(b * 256, (b + 1) * 256)
        t = sums[m, b, :, head_rows(j), half(j)].astype(f32)
        t = t + e1[m, e, s, :, :, bl].astype(f32)
        sums[m, b, :, head_rows(j), half(j)] = t.astype(bf16)
        t = sums[m, b, :, head_rows(j), quarter(j)].astype(f32)
        t = t + e2[m, owner_of(j), :, :, b * 128 : (b + 1) * 128].astype(f32)
        sums[m, b, :, head_rows(j), quarter(j)] = t.astype(bf16)

    def wait_others(m):
        d1_copy(m, 0, 1 - side).wait_recv()

        @pl.when(side != taker())
        def _():
            d1_copy(m, 1, 1 - side).wait_recv()

        for k in range(1, 4):

            @pl.when(slot_of(place + 4 - k) < 3)
            def _():
                d2_copy(m, k, (place + 4 - k) % 4).wait_recv()

    def complete(m, j, b):
        add_others(m, j, b)
        k = (b + reps - me) % reps

        @pl.when(k > 0)
        def _():
            tg_copy(m, j, k, me).start()

    def heads(m, first, last):
        def step(j, carry):
            def done(b):
                @pl.when(j > first)
                def _():
                    complete(m, j, b)

            own_head(m, j, done)

            @pl.when(j == first)
            def _():
                wait_others(m)
                for n in range(first + 1):
                    for b in range(reps):
                        complete(m, n, b)

            return carry

        lax.fori_loop(first, last, step, 0)

    load_r(0).wait()
    own_head(0, 0)

    def others(m):
        def paired(s):
            g1_copy(m, s, 1 - side).wait_recv()

            def block(c, start, size):
                at = start % wide
                return p1[start // wide, s, c, :, at : at + size]

            def gblock(start, size):
                at = start % wide
                return g1[m, start // wide, s, :, at : at + size]

            def put(c, start, size, value):
                at = start % wide
                d1[m, s, start // wide, c, :, at : at + size] = value

            attend_back(block, gblock, docs(m, 1), put, scr, 1, span, wide)
            e1[m, side, s] = d1[m, s, side]
            d1_copy(m, s, side).start()

        def each_pair(s, inner):
            @pl.when((s == 0) | (side == taker()))
            def _():
                paired(s)

            return inner

        load_1(m).wait()
        lax.fori_loop(0, 2, each_pair, 0)
        if m + 1 < micros:
            load_1(m + 1).start()
            halvings[1].pump()
            halvings[3].pump()
        else:
            pump()
        load_2(m).wait()

        def block(c, start, size):
            at = start % tok
            return p2[start // tok, c, :, at : at + size]

        def gblock(start, size):
            at = start % tok
            return g2[m, start // tok, :, at : at + size]

        def put(c, start, size, value):
            at = start % tok
            d2[m, start // tok, c, :, at : at + size] = value

        @pl.when(slot_of(place) < 3)
        def _():
            for k in range(1, 4):
                g2_copy(m, k, (place + 4 - k) % 4).wait_recv()
            attend_back(block, gblock, docs(m, 2), put, scr, 2, span, tok)
            e2[m, place] = d2[m, place]
            for k in range(1, 4):
                d2_copy(m, k, place).start()

        if m + 1 < micros:
            load_2(m + 1).start()

    others(0)
    heads(0, 1, 3)
    own_copy(0).start()
    load_r(1).start()
    pump()
    others(1)
    pump()
    load_r(1).wait()
    heads(1, 0, 1)
    pump()

    def last_heads(j, carry):
        own_head(1, j, lambda b: complete(1, j, b))
        return carry

    lax.fori_loop(1, 3, last_heads, 0)
    own_copy(1).start()
    for h in halvings:
        h.drain()
    for m in range(micros):
        own_copy(m).wait()
        g1_copy(m, 0, side).wait_send()
        d1_copy(m, 0, side).wait_send()

        @pl.when(side != taker())
        def _():
            g1_copy(m, 1, side).wait_send()

        @pl.when(side == taker())
        def _():
            d1_copy(m, 1, side).wait_send()

        for k in range(1, 4):

            @pl.when(slot_of(place + k) < 3)
            def _():
                g2_copy(m, k, place).wait_send()

            @pl.when(slot_of(place) < 3)
            def _():
                d2_copy(m, k, place).wait_send()


    def settle(j, carry):
        for m in range(micros):
            for k in range(1, 4):
                tg_copy(m, j, k, (me + reps - k) % reps).wait_recv()
                tg_copy(m, j, k, me).wait_send()
        return carry

    lax.fori_loop(0, 3, settle, 0)


def backward_call(pieces, da, att, totals, lengths, grads, seq_bits):
    micros, reps, cols, tok = att.shape
    span = tok * reps
    any_spec = pl.BlockSpec(memory_space=pl.ANY)

    def vm(*shape):
        return pltpu.VMEM(shape, bf16)

    dma = pltpu.SemaphoreType.DMA
    halving = []
    for n, lanes, order in grad_parts(grads[0].shape[-1], grads[1].shape[-1]):
        steps = reduce_steps(order, seq_bits)
        shape = grads[n].shape[:5] + (lanes.stop - lanes.start,)
        halving += [vm(*b) for b in reduce_buffers(shape, steps)]
        halving += [vm(2, 2, *shape[4:]), dma((2, len(steps) + 3))]
    tall, flat = vm(span, 128), vm(128, span)
    outs = [((micros, reps, 3, cols, tok), bf16, any_spec)]
    outs += [((2, 2) + g.shape[4:], bf16, vmem_spec()) for g in grads]
    return pl.pallas_call(
        functools.partial(backward_body, seq_bits=seq_bits),
        in_specs=[any_spec] * 3 + [vmem_spec()] * 4 + [smem_spec()] + [vmem_spec()] * 3,
        out_specs=[o[2] for o in outs],
        out_shape=[jax.ShapeDtypeStruct(o[0], o[1]) for o in outs],
        scratch_shapes=[
            vm(reps, 3, cols, tok),
            vm(2, 2, 3, HD, span // 2),
            vm(4, 3, HD, span // 4),
            vm(micros, 3, reps, HPAD, tok),
            vm(micros, 2, HPAD, span // 2),
            vm(micros, 4, HPAD, span // 4),
            vm(micros, 2, 2, HPAD, span // 2),
            vm(micros, 4, HPAD, span // 4),
            vm(micros, 2, 2, 3, HD, span // 2),
            vm(micros, 4, 3, HD, span // 4),
            vm(micros, 2, 2, 3, HD, span // 2),
            vm(micros, 4, 3, HD, span // 4),
            vm(micros, reps, 3, cols, tok),
            tall,
            tall,
            flat,
            tall,
            flat,
            tall,
            pltpu.VMEM((HD, span), f32),
            dma((3,)),
            dma((2, micros, 2)),
            dma((2, micros, 3)),
            dma((2, micros, 2)),
            dma((2, micros, 3)),
            dma((2, micros, 3, 3)),
            dma((micros,)),
            *halving,
        ],
        compiler_params=pltpu.CompilerParams(
            vmem_limit_bytes=60 << 20, collective_id=2, has_side_effects=True
        ),
        cost_estimate=pl.CostEstimate(
            flops=100_000_000_000, bytes_accessed=40_000_000, transcendentals=30_000_000
        ),
        name="backward",
    )(*pieces, *da, att, totals, lengths, *grads)


def store_parts(ref, value):
    parts, _, rows, _ = ref.shape
    for n in range(2 * parts):
        ref[n // 2, n % 2] = value[n * rows : (n + 1) * rows].astype(bf16)


def weight_grad_body(*refs, chunks):
    ins, da_ref, refs = refs[:12], refs[12], refs[13:]
    down_ref, up_ref, proj_ref, da_out, lt = refs[:5]
    values, gets, sems = refs[5:8], refs[8:11], refs[11:14]
    da_sems, own_sems = refs[14:]
    core = bit_of("rep", 0)
    me = lax.axis_index("rep")
    groups = [ins[:6], ins[6:]]
    n = pl.program_id(0)

    def copy(t, slot):
        return remote(
            values[t].at[slot, :, 1 - core],
            gets[t].at[slot],
            sems[t].at[0, slot],
            sems[t].at[1, slot],
            "rep",
            bit_peer("rep", 0),
        )

    def spread(t, slot, value):
        store_parts(values[t].at[slot], value)
        copy(t, slot).start()

    def da_copy(k, source):
        return remote(
            da_ref.at[rep_peer(k)],
            da_out.at[source],
            da_sems.at[0, k - 1],
            da_sems.at[1, k - 1],
            "rep",
            rep_peer(k),
        )

    da_own = pltpu.make_async_copy(da_ref.at[me], da_out.at[me], own_sems.at[0])

    @pl.when(n == 0)
    def _():
        barrier = pltpu.get_barrier_semaphore()
        for k in range(1, 4):
            pl.semaphore_signal(
                barrier, inc=1, device_id={"rep": rep_peer(k)}, device_id_type=pl.DeviceIdType.MESH
            )
        pl.semaphore_wait(barrier, 3)
        for k in range(1, 4):
            da_copy(k, me).start()
        da_own.start()
        total = None
        for k, (low, dup, hid, cot, mix, brl) in enumerate(groups):
            lt[k] = low[...].T
            part = dot_tn(mix[...], brl[...])
            total = part if total is None else total + part
        spread(2, 0, total)

    @pl.when(n < chunks)
    def _():
        up = down = None
        for k, (low, dup, hid, cot, mix, brl) in enumerate(groups):
            u = dot_nn(lt[k], dup[...])
            d = dot_tn(hid[...], cot[...])
            up = u if up is None else up + u
            down = d if down is None else down + d
        spread(0, n, down)
        spread(1, n, up)

    def merged(t, slot, out_ref):
        copy(t, slot).wait()
        value, got = values[t], gets[t]
        for k in range(got.shape[1]):
            out_ref[k] = (value[slot, k, core].astype(f32) + got[slot, k].astype(f32)).astype(bf16)

    @pl.when(n > 0)
    def _():
        merged(0, n - 1, down_ref)
        merged(1, n - 1, up_ref)

    @pl.when(n == chunks)
    def _():
        merged(2, 0, proj_ref)
        da_own.wait()
        for k in range(1, 4):
            da_copy(k, (me + 4 - k) % 4).wait_recv()
            da_copy(k, me).wait_send()


def weight_grads(group, da, width, hidden, seqs, reps):
    tok = group[0].shape[1]
    chunk = 768
    chunks = hidden // chunk
    last = chunks - 1

    def full(k):
        return pl.BlockSpec((None, tok, width), lambda n: (k, 0, 0))

    def part(k):
        return pl.BlockSpec((None, tok, chunk), lambda n: (k, 0, jnp.minimum(n, last)))

    def specs(k):
        return [full(k), part(k), part(k), full(k), full(k), full(k)]

    down_rows, up_rows = hidden // seqs // reps, width // seqs // reps
    per = chunk // down_rows // 2
    blocks = seqs * reps // 2
    shapes = [(chunks, per, down_rows, width), (chunks, blocks, up_rows, chunk), (1, blocks, up_rows, width)]
    return pl.pallas_call(
        functools.partial(weight_grad_body, chunks=chunks),
        grid=(chunks + 1,),
        in_specs=specs(0) + specs(1) + [vmem_spec()],
        out_specs=[
            pl.BlockSpec((per, down_rows, width), lambda n: (jnp.maximum(n - 1, 0), 0, 0)),
            pl.BlockSpec((blocks, up_rows, chunk), lambda n: (0, 0, jnp.maximum(n - 1, 0))),
            pl.BlockSpec((blocks, up_rows, width), lambda n: (0, 0, 0)),
            pl.BlockSpec(memory_space=pl.ANY),
        ],
        out_shape=[
            jax.ShapeDtypeStruct((blocks, down_rows, width), bf16),
            jax.ShapeDtypeStruct((blocks, up_rows, hidden), bf16),
            jax.ShapeDtypeStruct((blocks, up_rows, width), bf16),
            jax.ShapeDtypeStruct(da.shape, bf16),
        ],
        scratch_shapes=[pltpu.VMEM((2, width, tok), bf16)]
        + [pltpu.VMEM(b[:2] + (2,) + b[2:], bf16) for b in shapes]
        + [pltpu.VMEM(b, bf16) for b in shapes]
        + [pltpu.SemaphoreType.DMA((2, s[0])) for s in shapes]
        + [pltpu.SemaphoreType.DMA((2, 3)), pltpu.SemaphoreType.DMA((1,))],
        compiler_params=pltpu.CompilerParams(
            vmem_limit_bytes=VMEM, collective_id=3, has_side_effects=True
        ),
        cost_estimate=pl.CostEstimate(
            flops=4 * tok * width * (2 * hidden + width),
            bytes_accessed=30_000_000,
            transcendentals=0,
        ),
        name="weight_grads",
    )(*group, *group, da)


TAIL_ORDERS = ("yxzh", "xzhy", "zhyx")


def vec_rounds(seq_bits):
    rounds = [
        ("rep", lax.axis_index("rep"), [rep_peer(k) for k in range(1, 4)]),
        ("seq", team_place(), [team_member(k) for k in range(1, 4)]),
    ]
    for b in range(2, seq_bits):
        rounds.append(("seq", bit_of("seq", b), [bit_peer("seq", b)]))
    return rounds


def tail_body(
    tg_hbm,
    w_hbm,
    branch_hbm,
    xp_ref,
    nt_ref,
    gain_ref,
    ng_ref,
    nh_ref,
    out_ref,
    total_ref,
    norm_ref,
    hidden_ref,
    *scratch,
    seq_bits,
):
    tg, w, branch, acc, value, get, vec, load_sems, core_sems = scratch[:9]
    rest = list(scratch[9:])
    micros, tok, width = xp_ref.shape
    reps = tg.shape[2]
    parts = get.shape[1]
    core = bit_of("rep", 0)
    rounds = vec_rounds(seq_bits)

    barrier = pltpu.get_barrier_semaphore()
    peers = [(axis, peer) for axis, _, others in rounds for peer in others]
    for axis, peer in peers:
        pl.semaphore_signal(
            barrier, inc=1, device_id={axis: peer}, device_id_type=pl.DeviceIdType.MESH
        )
    loads = [
        pltpu.make_async_copy(tg_hbm.at[m, :, c], tg.at[m, c], load_sems.at[m * 3 + c])
        for c in range(3)
        for m in range(micros)
    ]
    loads += [pltpu.make_async_copy(w_hbm, w, load_sems.at[6])]
    loads += [
        pltpu.make_async_copy(branch_hbm.at[m], branch.at[m], load_sems.at[7 + m])
        for m in range(micros)
    ]
    for c in loads:
        c.start()
    pl.semaphore_wait(barrier, len(peers))

    def core_copy(c):
        return remote(
            value.at[c, :, 1 - core],
            get.at[c],
            core_sems.at[0, c],
            core_sems.at[1, c],
            "rep",
            bit_peer("rep", 0),
        )

    def piece(m, c):
        return jnp.concatenate([tg[m, c, r] for r in range(reps)], 0)

    for c in range(3):
        total = None
        for m in range(micros):
            loads[c * micros + m].wait()
            part = dot_nt(nt_ref[m], piece(m, c))
            total = part if total is None else total + part
        store_parts(value.at[c], total)
        core_copy(c).start()

    halvings = []
    for c, order in enumerate(TAIL_ORDERS):
        steps = reduce_steps(order, seq_bits)
        summed = rest.pop(0)
        buffers = [rest.pop(0) for _ in steps]
        gathered, sems = rest.pop(0), rest.pop(0)
        out = total_ref.at[:, :, :, c * width : (c + 1) * width]
        halvings.append(Halving(summed, steps, buffers, gathered, out, sems))

    def core_sum(c):
        core_copy(c).wait()
        summed = halvings[c].source

        def add(z, carry):
            for n in range(8):
                k = z * 8 + n
                total = value[c, k, core].astype(f32) + get[c, k].astype(f32)
                summed[z, n // 4, n // 2 % 2, n % 2] = total.astype(bf16)
            return carry

        lax.fori_loop(0, parts // 8, add, 0)
        halvings[c].start()

    loads[6].wait()

    def grad_part(m, c):
        part = dot_nn(w[:, c * width : (c + 1) * width], piece(m, c))
        if c == 0:
            acc[...] = part
        else:
            acc[...] += part

    def grad_end(m):
        xhat, rstd = normalize(xp_ref[m].astype(f32))
        dx, gain_i, bias_i = norm_back(acc[...].T, gain_ref[...].reshape(1, -1), xhat, rstd)
        loads[7 + m].wait()
        out_ref[m] = (branch[m] + dx).astype(bf16)
        return gain_i, bias_i

    core_sum(0)
    grad_part(0, 0)
    core_sum(1)
    grad_part(0, 1)
    core_sum(2)
    grad_part(0, 2)
    gain0, bias0 = grad_end(0)

    def pump():
        for h in halvings:
            h.pump()

    for c in range(3):
        grad_part(1, c)
    pump()
    gain1, bias1 = grad_end(1)
    terms = [gain0 + gain1, bias0 + bias1]
    terms += [ng_ref[0, n : n + 1] + ng_ref[1, n : n + 1] for n in range(4)]
    terms += [jnp.zeros((2, width), f32)]
    fold = nh_ref.shape[2] // width
    for n in range(2):
        for k in range(fold):
            cl = slice(k * width, (k + 1) * width)
            terms.append(nh_ref[0, n : n + 1, cl] + nh_ref[1, n : n + 1, cl])
    terms = jnp.concatenate(terms, 0)
    for n, (axis, place, others) in enumerate(rounds):
        box, sems = vec[2 * n], vec[2 * n + 1]
        box[place] = terms
        copies = []
        for k, peer in enumerate(others):
            copies.append(
                remote(box.at[place], box.at[place], sems.at[0, k], sems.at[1, k], axis, peer)
            )
            copies[-1].start()
        pump()
        size = box.shape[0]
        for k in range(1, size):
            landing = (place + size - k) % size
            remote(
                box.at[landing],
                box.at[landing],
                sems.at[0, k - 1],
                sems.at[1, k - 1],
                axis,
                others[k - 1],
            ).wait_recv()
        terms = box[0]
        for k in range(1, size):
            terms = terms + box[k]
        for c in copies:
            c.wait_send()
    s = lax.axis_index("seq")
    seqs = 1 << seq_bits
    cols = terms.T
    acc[:, : cols.shape[1]] = cols


    def rows_at(block, size):
        if size % 8 == 0:
            return acc[pl.ds(pl.multiple_of(block * size, 8), size), :16]
        out = cols[:size]
        for n in range(1, width // size):
            out = jnp.where(block == n, cols[n * size : (n + 1) * size], out)
        return out

    norm_ref[...] = rows_at(s, norm_ref.shape[1]).T[:6]
    own = hidden_ref.shape[1]
    per = width // own
    picked = rows_at(s % per, own)
    out = jnp.zeros((own, 2), f32)
    for k in range(fold):
        pair = jnp.concatenate(
            [picked[:, 8 + k : 9 + k], picked[:, 8 + fold + k : 9 + fold + k]], 1
        )
        out = jnp.where(s // per == k, pair, out)
    hidden_ref[...] = out.T
    for h in halvings:
        h.drain()


def tail_call(tg, weight, branch, xp, nt, gain, ng, nh, seq_bits):
    micros, tok, width = xp.shape
    reps, _, cols = tg.shape[1:4]
    hidden = nh.shape[2]
    seqs = 1 << seq_bits
    rows = width // seqs // reps
    parts = seqs * reps // 2
    any_spec = pl.BlockSpec(memory_space=pl.ANY)

    def vm(*shape):
        return pltpu.VMEM(shape, bf16)

    dma = pltpu.SemaphoreType.DMA
    shape = (seqs // 4, 2, 2, reps // 2, rows, width)
    halving = []
    for order in TAIL_ORDERS:
        steps = reduce_steps(order, seq_bits)
        halving += [vm(*shape)] + [vm(*b) for b in reduce_buffers(shape, steps)]
        halving += [vm(2, 2, rows, width), dma((2, len(steps) + 3))]
    vec = []
    for size in (4, 4) + (2,) * (seq_bits - 2):
        vec += [pltpu.VMEM((size, 16, width), f32), dma((2, size - 1))]
    outs = [
        ((micros, tok, width), bf16),
        ((2, 2, rows, 3 * width), bf16),
        ((6, width // seqs), f32),
        ((2, hidden // seqs), f32),
    ]
    return pl.pallas_call(
        functools.partial(tail_body, seq_bits=seq_bits),
        in_specs=[any_spec] * 3 + [vmem_spec()] * 5,
        out_specs=[vmem_spec()] * 4,
        out_shape=[jax.ShapeDtypeStruct(s, d) for s, d in outs],
        scratch_shapes=[
            vm(micros, 3, reps, cols, tok),
            vm(width, 3 * width),
            pltpu.VMEM((micros, tok, width), f32),
            pltpu.VMEM((width, tok), f32),
            vm(3, parts, 2, rows, width),
            vm(3, parts, rows, width),
            vec,
            dma((9,)),
            dma((2, 3)),
            *halving,
        ],
        compiler_params=pltpu.CompilerParams(
            vmem_limit_bytes=VMEM, collective_id=4, has_side_effects=True
        ),
        cost_estimate=pl.CostEstimate(
            flops=24 * tok * width * width, bytes_accessed=20_000_000, transcendentals=0
        ),
        name="tail",
    )(tg, weight, branch, xp, nt, gain, ng, nh)


def finish_body(*refs):
    half = len(refs) // 2
    ins, outs = refs[:half], refs[half:]
    micros, tok, _ = ins[0].shape
    back = onehot_cols(tok)
    for a, o in zip(ins[:2], outs[:2]):
        for m in range(micros):
            o[m] = dot_nn(back, a[m]).astype(bf16)
    for a, o in zip(ins[2:], outs[2:]):
        o[...] = a[...].astype(f32)


def finish_call(tokens, grads):
    args = (*tokens, *grads)
    return pl.pallas_call(
        finish_body,
        in_specs=[vmem_spec()] * len(args),
        out_specs=[vmem_spec()] * len(args),
        out_shape=[jax.ShapeDtypeStruct(a.shape, bf16) for a in tokens]
        + [jax.ShapeDtypeStruct(a.shape, f32) for a in grads],
        compiler_params=pltpu.CompilerParams(vmem_limit_bytes=VMEM),
        cost_estimate=pl.CostEstimate(
            flops=2_000_000_000, bytes_accessed=12_000_000, transcendentals=0
        ),
        name="finish",
    )(*args)


def bits_of(count):
    return count.bit_length() - 1


def on_device(
    layer_in,
    qkv_weight,
    out_weight,
    up_weight,
    down_weight,
    input_gain,
    input_bias,
    mixer_gain,
    mixer_bias,
    block_gain,
    block_bias,
    hidden_gain,
    hidden_bias,
    output_grad,
    seq_lengths,
):
    micro_count, tok, width = layer_in.shape
    reps = lax.axis_size("rep")
    seqs = lax.axis_size("seq")
    seq_bits = bits_of(seqs)
    hidden = up_weight.shape[1]
    xp, nt, got_qkv, got_pair, got_four, own_att, got_att, totals = forward_call(
        layer_in, qkv_weight, input_gain, input_bias, seq_lengths, reps
    )
    out, ng, nh, branch, mix, low, hid, dup, brl, cotp, da0, da1 = ffn_call(
        own_att,
        got_att,
        xp,
        output_grad,
        (out_weight, up_weight, down_weight),
        (mixer_gain, mixer_bias, block_gain, block_bias, hidden_gain, hidden_bias),
    )
    *grads, da1 = weight_grads((low, dup, hid, cotp, mix, brl), da1, width, hidden, seqs, reps)
    grads = [g.reshape((seqs // 4, 2, 2, reps // 2) + g.shape[1:]) for g in grads]
    token_grad, *totals = backward_call(
        (got_qkv, got_pair, got_four), (da0, da1), own_att, totals, seq_lengths, grads, seq_bits
    )
    input_grad, qkv_total, norm_total, hidden_total = tail_call(
        token_grad, qkv_weight, branch, xp, nt, input_gain, ng, nh, seq_bits
    )
    down_total, up_total, proj_total, qkv_total = (
        t.reshape(-1, t.shape[-1]) for t in (*totals, qkv_total)
    )
    *results, norm_total, hidden_total = finish_call(
        (out, input_grad), (qkv_total, proj_total, up_total, down_total, norm_total, hidden_total)
    )
    return (*results, norm_total.T, hidden_total.T)


def solution(mesh):
    tokens = P(None, ("seq", "rep"), None)
    rows = P("seq", None)
    return jax.shard_map(
        on_device,
        mesh=mesh,
        in_specs=(tokens,) + (P(),) * 12 + (tokens, P()),
        out_specs=(tokens, tokens) + (rows,) * 6,
        check_vma=False,
    )
```

```python
import functools
import math

import jax
import jax.numpy as jnp
from jax import lax
from jax.experimental import pallas as pl
from jax.experimental.pallas import tpu as pltpu
from jax.sharding import PartitionSpec as P

HEADS = 12
HD = 64
HPAD = 80
CLASS_SLOT = (0, 2, 1, 3)
LOG2E = 1.4426950408889634
NEG = -1e30
EPS = 1e-05
VMEM = 56 << 20

f32 = jnp.float32
bf16 = jnp.bfloat16


def dot_nn(a, b):
    return lax.dot_general(a, b, (((1,), (0,)), ((), ())), preferred_element_type=f32)


def dot_nt(a, b):
    return lax.dot_general(a, b, (((1,), (1,)), ((), ())), preferred_element_type=f32)


def dot_tn(a, b):
    return lax.dot_general(a, b, (((0,), (0,)), ((), ())), preferred_element_type=f32)


def class_slot(cls):
    return jnp.where(cls == 1, 2, jnp.where(cls == 2, 1, cls))


def rel_pos(shape, dim, offset, pattern):
    i = lax.broadcasted_iota(jnp.int32, shape, dim) + offset
    if pattern == 0:
        return (i % 128) * 4 + class_slot((i // 128) % 4)
    if pattern == 1:
        return (i // 256) * 512 + (i % 128) * 4 + ((i // 128) % 2) * 2
    return i


def doc_rows(len_ref, micro, start, dilation, count):
    pos = lax.broadcasted_iota(jnp.int32, (1, count), 1) * dilation + start
    edge = len_ref[micro, 0]
    doc = (pos >= edge).astype(jnp.int32)
    for n in range(1, len_ref.shape[1] - 1):
        edge = edge + len_ref[micro, n]
        doc = doc + (pos >= edge).astype(jnp.int32)
    return doc


def segment_start(pattern, span):
    team = 2**pattern
    return (lax.axis_index("seq") // team) * (team * span)


def split3(x):
    hi = x.astype(bf16).astype(f32)
    mid = (x - hi).astype(bf16).astype(f32)
    return hi, mid, x - hi - mid


def stat_rows(rows, count):
    r = lax.broadcasted_iota(jnp.int32, (HPAD - HD, count), 0)
    out = jnp.zeros((HPAD - HD, count), f32)
    for n, row in enumerate(rows):
        out = jnp.where(r == n, row, out)
    return out.astype(bf16)


def shift():
    return lax.axis_index("rep") % 2


def taker():
    return shift()


def owner_of(j):
    return (j + shift()) % 4


def slot_of(place):
    return (place + 4 - shift()) % 4


def clamp_slot(j):
    return j - j // 3


def place1(j):
    return (taker(), 1) if j == 2 else (j, 0)


def smem_spec():
    return pl.BlockSpec(memory_space=pltpu.SMEM)


def vmem_spec():
    return pl.BlockSpec(memory_space=pltpu.VMEM)


def onehot_rows(tok):
    i = lax.broadcasted_iota(jnp.int32, (tok, tok), 0)
    t = lax.broadcasted_iota(jnp.int32, (tok, tok), 1)
    return ((i % 128) * 4 + class_slot(i // 128) == t).astype(bf16)


def onehot_cols(tok):
    t = lax.broadcasted_iota(jnp.int32, (tok, tok), 0)
    i = lax.broadcasted_iota(jnp.int32, (tok, tok), 1)
    return ((i % 128) * 4 + class_slot(i // 128) == t).astype(bf16)


def normalize(x):
    c = x - jnp.mean(x, axis=-1, keepdims=True)
    rstd = lax.rsqrt(jnp.mean(c * c, axis=-1, keepdims=True) + EPS)
    return c * rstd, rstd


def norm_back(grad, gain, xhat, rstd):
    dn = grad * gain
    low = jnp.mean(dn, axis=-1, keepdims=True)
    along = jnp.mean(dn * xhat, axis=-1, keepdims=True)
    dx = rstd * (dn - low - xhat * along)
    return dx, jnp.sum(grad * xhat, 0, keepdims=True), jnp.sum(grad, 0, keepdims=True)


CHUNK = 512
SQRT_HALF = 0.7071067811865476
INV_SQRT_2PI = 0.3989422804014327


def ffn_body(
    own_ref,
    got_hbm,
    xp_ref,
    cot_ref,
    wo_hbm,
    wu_hbm,
    wd_hbm,
    mg_ref,
    mb_ref,
    bg_ref,
    bb_ref,
    hg_ref,
    hb_ref,
    out_ref,
    ng_ref,
    nh_ref,
    branch_out,
    mix_out,
    low_out,
    hid_out,
    dup_out,
    brl_out,
    cotp_out,
    da0_out,
    da1_out,
    wo,
    wu,
    wd,
    g_scr,
    dg_scr,
    dn_scr,
    am_scr,
    acc_scr,
    att_scr,
    da_scr,
    branch,
    mix,
    low,
    hid,
    dup,
    brl,
    cotp,
    load_sems,
    out_sems,
    att_sems,
    da_sems,
    own_sems,
):
    micros, tok, width = xp_ref.shape
    hidden = hid.shape[1]
    chunks = hidden // CHUNK
    reps, cols = own_ref.shape[1:3]
    me = lax.axis_index("rep")
    loads = [
        pltpu.make_async_copy(a, b, load_sems.at[n])
        for n, (a, b) in enumerate(
            ((wo_hbm, wo), (wu_hbm, wu), (wd_hbm, wd), (got_hbm, att_scr.at[0]))
        )
    ]
    for n in (3, 0, 1, 2):
        loads[n].start()
    barrier = pltpu.get_barrier_semaphore()
    for k in range(1, 4):
        pl.semaphore_signal(
            barrier, inc=1, device_id={"rep": rep_peer(k)}, device_id_type=pl.DeviceIdType.MESH
        )
    pl.semaphore_wait(barrier, 3)

    def att_copy(k, source):
        return remote(
            own_ref.at[1, rep_peer(k)],
            att_scr.at[1, source],
            att_sems.at[0, k - 1],
            att_sems.at[1, k - 1],
            "rep",
            rep_peer(k),
        )

    def da_copy(k, source):
        return remote(
            da_scr.at[0, rep_peer(k)],
            da0_out.at[source],
            da_sems.at[0, k - 1],
            da_sems.at[1, k - 1],
            "rep",
            rep_peer(k),
        )

    da_own = pltpu.make_async_copy(da_scr.at[0, me], da0_out.at[me], own_sems.at[0])
    da_last = pltpu.make_async_copy(da_scr.at[1], da1_out, own_sems.at[1])
    for k in range(1, 4):
        att_copy(k, me).start()
    att_scr[1, me] = own_ref[1, me]
    pairs = (
        (branch, branch_out),
        (mix, mix_out),
        (low, low_out),
        (hid, hid_out),
        (dup, dup_out),
        (brl, brl_out),
        (cotp, cotp_out),
    )

    def out_copy(n, m):
        return pltpu.make_async_copy(pairs[n][0], pairs[n][1].at[m], out_sems.at[n])

    def lanes(n):
        return slice(n * CHUNK, (n + 1) * CHUNK)

    def row(ref, at=slice(None)):
        return ref[at].reshape(1, -1)

    def micro(m, carry):
        def before(n):
            @pl.when(m == 1)
            def _():
                out_copy(n, 0).wait()

        @pl.when(m == 0)
        def _():
            loads[3].wait()

        @pl.when(m == 1)
        def _():
            for k in range(1, 4):
                att_copy(k, (me + reps - k) % reps).wait_recv()

        before(6)
        cotp[...] = dot_nn(onehot_rows(tok), cot_ref[m]).astype(bf16)
        out_copy(6, m).start()
        att = att_scr[m].reshape(width, tok).T.astype(f32)
        ahat, _ = normalize(att)
        before(1)
        mix[...] = (ahat * row(mg_ref) + row(mb_ref)).astype(bf16)
        out_copy(1, m).start()

        @pl.when(m == 0)
        def _():
            loads[0].wait()

        am = xp_ref[m].astype(f32) + dot_nn(mix[...], wo[...])
        am_scr[...] = am
        bhat, _ = normalize(am)
        before(2)
        low[...] = (bhat * row(bg_ref) + row(bb_ref)).astype(bf16)
        out_copy(2, m).start()

        @pl.when(m == 0)
        def _():
            loads[1].wait()

        total = jnp.zeros((tok, 1), f32)
        for n in range(chunks):
            u = dot_nn(low[...], wu[:, lanes(n)])
            cdf = 0.5 + 0.5 * lax.erf(u * SQRT_HALF)
            g = u * cdf
            g_scr[:, lanes(n)] = g
            dg_scr[:, lanes(n)] = cdf + u * (jnp.exp(u * u * -0.5) * INV_SQRT_2PI)
            total = total + jnp.sum(g, 1, keepdims=True)
        mean = total / hidden
        total = jnp.zeros((tok, 1), f32)
        for n in range(chunks):
            c = g_scr[:, lanes(n)] - mean
            total = total + jnp.sum(c * c, 1, keepdims=True)
        rstd = lax.rsqrt(total / hidden + EPS)

        @pl.when(m == 0)
        def _():
            loads[2].wait()

        before(3)
        first = second = jnp.zeros((tok, 1), f32)
        for n in range(chunks):
            ghat = (g_scr[:, lanes(n)] - mean) * rstd
            g_scr[:, lanes(n)] = ghat
            gain = row(hg_ref, lanes(n))
            h = (ghat * gain + row(hb_ref, lanes(n))).astype(bf16)
            hid[:, lanes(n)] = h
            part = dot_nn(h, wd[lanes(n), :])
            if n == 0:
                acc_scr[...] = part
            else:
                acc_scr[...] += part
            back = dot_nt(cotp[...], wd[lanes(n), :])
            nh_ref[m, 0:1, lanes(n)] = jnp.sum(back * ghat, 0, keepdims=True)
            nh_ref[m, 1:2, lanes(n)] = jnp.sum(back, 0, keepdims=True)
            dn = back * gain
            dn_scr[:, lanes(n)] = dn
            first = first + jnp.sum(dn, 1, keepdims=True)
            second = second + jnp.sum(dn * ghat, 1, keepdims=True)
        first, second = first / hidden, second / hidden
        out_copy(3, m).start()
        out_ref[m] = (am_scr[...] + acc_scr[...]).astype(bf16)
        before(4)
        for n in range(chunks):
            d = rstd * (dn_scr[:, lanes(n)] - first - g_scr[:, lanes(n)] * second)
            t = (d * dg_scr[:, lanes(n)]).astype(bf16)
            dup[:, lanes(n)] = t
            part = dot_nt(t, wu[:, lanes(n)])
            if n == 0:
                acc_scr[...] = part
            else:
                acc_scr[...] += part
        out_copy(4, m).start()
        bhat, brstd = normalize(am_scr[...])
        middle, gain_b, bias_b = norm_back(acc_scr[...], row(bg_ref), bhat, brstd)
        total = cotp[...].astype(f32) + middle
        before(0)
        branch[...] = total
        out_copy(0, m).start()
        before(5)
        brl[...] = total.astype(bf16)
        out_copy(5, m).start()
        att = att_scr[m].reshape(width, tok).T.astype(f32)
        ahat, arstd = normalize(att)
        da, gain_m, bias_m = norm_back(dot_nt(brl[...], wo[...]), row(mg_ref), ahat, arstd)
        da_scr[m] = da.astype(bf16).T.reshape(reps, cols, tok)
        ng_ref[m, 0:1] = gain_m
        ng_ref[m, 1:2] = bias_m
        ng_ref[m, 2:3] = gain_b
        ng_ref[m, 3:4] = bias_b

        @pl.when(m == 0)
        def _():
            for k in range(1, 4):
                da_copy(k, me).start()
            da_own.start()

        return carry

    lax.fori_loop(0, micros, micro, 0)
    da_last.start()
    for n in range(len(pairs)):
        out_copy(n, 1).wait()
    for k in range(1, 4):
        att_copy(k, me).wait_send()
        da_copy(k, (me + reps - k) % reps).wait_recv()
        da_copy(k, me).wait_send()
    da_own.wait()
    da_last.wait()


def ffn_call(own, got, xp, output_grad, weights, gains):
    micros, reps, cols, tok = own.shape
    width = xp.shape[2]
    hidden = weights[1].shape[1]
    any_spec = pl.BlockSpec(memory_space=pl.ANY)
    wide, narrow = (tok, hidden), (tok, width)
    outs = [
        ((micros,) + narrow, bf16, vmem_spec()),
        ((micros, 4, width), f32, vmem_spec()),
        ((micros, 2, hidden), f32, vmem_spec()),
        ((micros,) + narrow, f32, any_spec),
        ((micros,) + narrow, bf16, any_spec),
        ((micros,) + narrow, bf16, any_spec),
        ((micros,) + wide, bf16, any_spec),
        ((micros,) + wide, bf16, any_spec),
        ((micros,) + narrow, bf16, any_spec),
        ((micros,) + narrow, bf16, any_spec),
        ((reps, cols, tok), bf16, any_spec),
        ((reps, cols, tok), bf16, any_spec),
    ]
    dma = pltpu.SemaphoreType.DMA
    return pl.pallas_call(
        ffn_body,
        in_specs=[vmem_spec(), any_spec, vmem_spec(), vmem_spec()]
        + [any_spec] * 3
        + [vmem_spec()] * len(gains),
        out_specs=[o[2] for o in outs],
        out_shape=[jax.ShapeDtypeStruct(o[0], o[1]) for o in outs],
        scratch_shapes=[pltpu.VMEM(w.shape, bf16) for w in weights]
        + [pltpu.VMEM(wide, f32)] * 3
        + [pltpu.VMEM(narrow, f32)] * 2
        + [pltpu.VMEM((2, reps, cols, tok), bf16)] * 2
        + [pltpu.VMEM(narrow, f32), pltpu.VMEM(narrow, bf16), pltpu.VMEM(narrow, bf16)]
        + [pltpu.VMEM(wide, bf16)] * 2
        + [pltpu.VMEM(narrow, bf16)] * 2
        + [dma((4,)), dma((7,)), dma((2, 3)), dma((2, 3)), dma((2,))],
        compiler_params=pltpu.CompilerParams(
            vmem_limit_bytes=60 << 20, collective_id=5, has_side_effects=True
        ),
        cost_estimate=pl.CostEstimate(
            flops=8 * tok * width * (2 * hidden + width),
            bytes_accessed=40_000_000,
            transcendentals=4 * tok * hidden,
        ),
        name="middle",
    )(own, got, xp, output_grad, *weights, *gains)


def rep_peer(k):
    count = lax.axis_size("rep")
    return (lax.axis_index("rep") + k) % count


def team_place():
    return lax.axis_index("seq") % 4


def team_member(k):
    s = lax.axis_index("seq")
    return s // 4 * 4 + (s + k) % 4


def pair_partner():
    s = lax.axis_index("seq")
    return s + 1 - 2 * (s % 2)


def remote(src, dst, send_sem, recv_sem, axis, peer):
    return pltpu.make_async_remote_copy(
        src_ref=src,
        dst_ref=dst,
        send_sem=send_sem,
        recv_sem=recv_sem,
        device_id={axis: peer},
        device_id_type=pl.DeviceIdType.MESH,
    )


def meet_peers():
    barrier = pltpu.get_barrier_semaphore()
    for k in range(1, 4):
        for axis, peer in (("rep", rep_peer(k)), ("seq", team_member(k))):
            pl.semaphore_signal(
                barrier, inc=1, device_id={axis: peer}, device_id_type=pl.DeviceIdType.MESH
            )
    pl.semaphore_wait(barrier, 6)


def head_rows(j):
    return pl.ds(pl.multiple_of(j * HD, HD), HD)


def attend(block, doc, put, ks, qs, pattern, count, lanes):
    kb = min(512, lanes)
    for s in range(0, count, kb):
        sl = slice(s, s + kb)
        r = lax.broadcasted_iota(jnp.int32, (HD, kb), 0)
        same = doc[:, sl] == r
        aux_k = jnp.where(same, 1.0, 0.0).astype(bf16)
        aux_q = jnp.where(same | (r >= 4), 0.0, NEG).astype(bf16)
        q = (block(0, s, kb).astype(f32) * 0.125).astype(bf16)
        qs[:, sl] = jnp.concatenate([q, aux_q], 0)
        ks[sl, :] = jnp.concatenate([block(1, s, kb), aux_k], 0).T

    qb = 256
    grain = 512 if pattern == 0 else 256

    def tiles(i):
        low = (i * qb) // grain * grain
        out = [(s, min(512, low - s), False) for s in range(0, low, 512)]
        return out + [(low, grain, True)]

    def scores(i):
        out = []
        for s, size, diagonal in tiles(i):
            t = dot_nn(ks[s : s + size, :], qs[:, i * qb : (i + 1) * qb])
            if diagonal:
                keep = rel_pos((size, qb), 0, s % 512, pattern) <= rel_pos(
                    (size, qb), 1, (i * qb) % 512, pattern
                )
                t = jnp.where(keep, t, NEG)
            out.append(t)
        return out

    following = scores(0)
    for i in range(count // qb):
        current = following
        if (i + 1) * qb < count:
            following = scores(i + 1)
        top = functools.reduce(jnp.maximum, [jnp.max(t, 0, keepdims=True) for t in current])
        top2 = top * LOG2E
        acc, total = None, None
        for t, (s, size, _) in zip(current, tiles(i)):
            p = jnp.exp2(t * LOG2E - top2)
            part = jnp.sum(p, 0, keepdims=True)
            out = dot_nn(block(2, s, size), p.astype(bf16))
            acc = out if acc is None else acc + out
            total = part if total is None else total + part
        lse = top + jnp.log(total)
        put(i * qb, qb, (acc / total).astype(bf16), stat_rows(split3(lse), qb))


def forward_body(
    x_ref,
    w_ref,
    gain_ref,
    bias_ref,
    len_ref,
    xp_ref,
    nt_ref,
    r_out,
    p1_out,
    p2_out,
    att_ref,
    got_ref,
    mix_ref,
    sent,
    r,
    stage1,
    stage2,
    p1,
    p2,
    o0,
    o1,
    o2,
    b1,
    b2,
    ks,
    qs,
    qkv_sems,
    p1_sems,
    p2_sems,
    b1_sems,
    b2_sems,
    att_sems,
    out_sems,
):
    micros, tok, width = x_ref.shape
    reps = r.shape[1]
    span = tok * reps
    cols = width // reps
    me = lax.axis_index("rep")
    place = team_place()
    side = place % 2
    meet_peers()

    def qkv_copy(m, j, k, source):
        return remote(
            sent.at[m, rep_peer(k), :, head_rows(j)],
            r.at[m, source, :, head_rows(j)],
            qkv_sems.at[0, m, j, k - 1],
            qkv_sems.at[1, m, j, k - 1],
            "rep",
            rep_peer(k),
        )

    def p1_copy(m, s, source):
        return remote(
            stage1.at[m, s],
            p1.at[m, source, s],
            p1_sems.at[0, m, s],
            p1_sems.at[1, m, s],
            "seq",
            pair_partner(),
        )

    def p2_copy(m, k, source):
        return remote(
            stage2.at[m, (place + k) % 4],
            p2.at[m, source],
            p2_sems.at[0, m, k - 1],
            p2_sems.at[1, m, k - 1],
            "seq",
            team_member(k),
        )

    def b1_copy(m, s, source):
        return remote(
            o1.at[m, s, 1 - side],
            b1.at[m, source, s],
            b1_sems.at[0, m, s],
            b1_sems.at[1, m, s],
            "seq",
            pair_partner(),
        )

    def b2_copy(m, k, source):
        return remote(
            o2.at[m, (place + k) % 4],
            b2.at[m, source],
            b2_sems.at[0, m, k - 1],
            b2_sems.at[1, m, k - 1],
            "seq",
            team_member(k),
        )

    def att_copy(k, source):
        return remote(
            att_ref.at[0, rep_peer(k)],
            got_ref.at[source],
            att_sems.at[0, k - 1],
            att_sems.at[1, k - 1],
            "rep",
            rep_peer(k),
        )

    def out_copies(m):
        return (
            pltpu.make_async_copy(r.at[m], r_out.at[m], out_sems.at[m, 0]),
            pltpu.make_async_copy(p1.at[m], p1_out.at[m], out_sems.at[m, 1]),
            pltpu.make_async_copy(p2.at[m], p2_out.at[m], out_sems.at[m, 2]),
        )

    def project(m, carry):
        xp = dot_nn(onehot_rows(tok), x_ref[m])
        xp_ref[m] = xp.astype(bf16)
        xhat, _ = normalize(xp)
        n = (xhat * gain_ref[...].reshape(1, -1) + bias_ref[...].reshape(1, -1)).astype(bf16)
        nt_ref[m] = n.T
        for c in range(3):
            t = dot_nn(n, w_ref[:, c * width : (c + 1) * width]).astype(bf16).T
            for d in range(reps):
                sent[m, d, c] = t[d * cols : (d + 1) * cols]
        for j in range(3):
            for k in range(1, 4):
                qkv_copy(m, j, k, me).start()
        r[m, me] = sent[m, me]
        return carry

    lax.fori_loop(0, micros, project, 0)

    def half(j):
        return pl.ds(pl.multiple_of(((3 * me + j) % 2) * 256, 256), 256)

    def quarter_at(j):
        c = (3 * me + j) % 4
        return c % 2 * 2 + c // 2

    def quarter(j):
        return pl.ds(pl.multiple_of(quarter_at(j) * 128, 128), 128)

    def send_first(m):
        for b in range(reps):
            bl = slice(b * 256, (b + 1) * 256)
            stage1[m, 0, :, :, bl] = r[m, b, :, head_rows(1 - side), half(1 - side)]
            p1[m, side, 0, :, :, bl] = r[m, b, :, head_rows(side), half(side)]
        p1_copy(m, 0, side).start()

    def send_second(m):
        for b in range(reps):
            bl = slice(b * 256, (b + 1) * 256)
            piece = r[m, b, :, head_rows(2), half(2)]
            stage1[m, 1, :, :, bl] = piece
            p1[m, side, 1, :, :, bl] = piece

        @pl.when(side != taker())
        def _():
            p1_copy(m, 1, side).start()

        for g in range(4):
            j = clamp_slot(slot_of(g))
            for b in range(reps):
                stage2[m, g, :, :, b * 128 : (b + 1) * 128] = r[m, b, :, head_rows(j), quarter(j)]
        p2[m, place] = stage2[m, place]
        for k in range(1, 4):

            @pl.when(slot_of(place + k) < 3)
            def _():
                p2_copy(m, k, place).start()

    def mix_all(m):
        b1_copy(m, 0, 1 - side).wait_recv()

        @pl.when(side != taker())
        def _():
            b1_copy(m, 1, 1 - side).wait_recv()

        for k in range(1, 4):

            @pl.when(slot_of(place + 4 - k) < 3)
            def _():
                b2_copy(m, k, (place + 4 - k) % 4).wait_recv()

        def stat(tile):
            t = tile[HD:, :].astype(f32)
            return t[0:1] + t[1:2] + t[2:3]

        mix_ref[m] = jnp.zeros(mix_ref.shape[1:], f32)
        for j in range(3):
            e, s = place1(j)
            for b in range(reps):
                for a in range(4):
                    la = slice(a * 128, (a + 1) * 128)
                    lb = b * 256 + (a % 2) * 128
                    t0 = o0[m, j, b, :, la]
                    t1 = b1[m, e, s, :, lb : lb + 128]
                    t2 = b2[m, owner_of(j), :, b * 128 : (b + 1) * 128]
                    l0 = stat(t0)
                    l1 = jnp.where((3 * me + j) % 2 == a // 2, stat(t1), NEG)
                    l2 = jnp.where(quarter_at(j) == a, stat(t2), NEG)
                    top = jnp.maximum(jnp.maximum(l0, l1), l2)
                    e0, e1, e2 = jnp.exp(l0 - top), jnp.exp(l1 - top), jnp.exp(l2 - top)
                    total = e0 + e1 + e2
                    inv = 1.0 / total
                    mixed = (
                        t0[:HD].astype(f32) * (e0 * inv)
                        + t1[:HD].astype(f32) * (e1 * inv)
                        + t2[:HD].astype(f32) * (e2 * inv)
                    )
                    att_ref[m, b, j * HD : (j + 1) * HD, la] = mixed.astype(bf16)
                    col = b * tok + a * 128
                    mix_ref[m, j : j + 1, col : col + 128] = top + jnp.log(total)

    docs_of = lambda m, pattern: doc_rows(
        len_ref, m, segment_start(pattern, span), 2**pattern, span
    )

    def micro(m, carry):
        def local(j, inner):
            for k in range(1, 4):
                qkv_copy(m, j, k, (me + reps - k) % reps).wait_recv()

            @pl.when(j == 1)
            def _():
                send_first(m)

            @pl.when(j == 2)
            def _():
                send_second(m)

            def block(c, start, size):
                at = start % tok
                return r[m, start // tok, c, head_rows(j), at : at + size]

            def put(start, size, out, stats):
                at = start % tok
                o0[m, j, start // tok, :HD, at : at + size] = out
                o0[m, j, start // tok, HD:, at : at + size] = stats

            attend(block, docs_of(m, 0), put, ks, qs, 0, span, tok)
            return inner

        lax.fori_loop(0, 3, local, 0)

        @pl.when(m == 1)
        def _():
            mix_all(0)
            for k in range(1, 4):
                att_copy(k, me).start()
            got_ref[me] = att_ref[0, me]

        wide = span // 2

        def paired(s):
            p1_copy(m, s, 1 - side).wait_recv()

            def block(c, start, size):
                at = start % wide
                return p1[m, start // wide, s, c, :, at : at + size]

            def put(start, size, out, stats):
                at = start % wide
                o1[m, s, start // wide, :HD, at : at + size] = out
                o1[m, s, start // wide, HD:, at : at + size] = stats

            attend(block, docs_of(m, 1), put, ks, qs, 1, span, wide)
            b1[m, side, s] = o1[m, s, side]
            b1_copy(m, s, side).start()

        def each_pair(s, inner):
            @pl.when((s == 0) | (side == taker()))
            def _():
                paired(s)

            return inner

        lax.fori_loop(0, 2, each_pair, 0)

        def block(c, start, size):
            at = start % tok
            return p2[m, start // tok, c, :, at : at + size]

        def put(start, size, out, stats):
            at = start % tok
            o2[m, start // tok, :HD, at : at + size] = out
            o2[m, start // tok, HD:, at : at + size] = stats

        @pl.when(slot_of(place) < 3)
        def _():
            for k in range(1, 4):
                p2_copy(m, k, (place + 4 - k) % 4).wait_recv()
            attend(block, docs_of(m, 2), put, ks, qs, 2, span, tok)
            b2[m, place] = o2[m, place]
            for k in range(1, 4):
                b2_copy(m, k, place).start()

        for c in out_copies(m):
            c.start()
        return carry

    lax.fori_loop(0, micros, micro, 0)
    mix_all(1)
    for k in range(1, 4):
        att_copy(k, (me + reps - k) % reps).wait_recv()
        att_copy(k, me).wait_send()

    def finish(m, carry):
        for c in out_copies(m):
            c.wait()
        for k in range(1, 4):
            for j in range(3):
                qkv_copy(m, j, k, me).wait_send()

            @pl.when(slot_of(place + k) < 3)
            def _():
                p2_copy(m, k, place).wait_send()

            @pl.when(slot_of(place) < 3)
            def _():
                b2_copy(m, k, place).wait_send()

        p1_copy(m, 0, side).wait_send()
        b1_copy(m, 0, side).wait_send()

        @pl.when(side != taker())
        def _():
            p1_copy(m, 1, side).wait_send()

        @pl.when(side == taker())
        def _():
            b1_copy(m, 1, side).wait_send()

        return carry

    lax.fori_loop(0, micros, finish, 0)


def forward_call(layer_in, weight, gain, bias, lengths, reps):
    micros, tok, width = layer_in.shape
    span, cols = tok * reps, width // reps
    any_spec = pl.BlockSpec(memory_space=pl.ANY)
    outs = [
        ((micros, tok, width), bf16, vmem_spec()),
        ((micros, width, tok), bf16, vmem_spec()),
        ((micros, reps, 3, cols, tok), bf16, any_spec),
        ((micros, 2, 2, 3, HD, span // 2), bf16, any_spec),
        ((micros, 4, 3, HD, span // 4), bf16, any_spec),
        ((micros, reps, cols, tok), bf16, vmem_spec()),
        ((reps, cols, tok), bf16, vmem_spec()),
        ((micros, 8, span), f32, vmem_spec()),
    ]

    def vm(*shape):
        return pltpu.VMEM(shape, bf16)

    dma = pltpu.SemaphoreType.DMA
    return pl.pallas_call(
        forward_body,
        in_specs=[vmem_spec()] * 4 + [smem_spec()],
        out_specs=[o[2] for o in outs],
        out_shape=[jax.ShapeDtypeStruct(o[0], o[1]) for o in outs],
        scratch_shapes=[
            vm(micros, reps, 3, cols, tok),
            vm(micros, reps, 3, cols, tok),
            vm(micros, 2, 3, HD, span // 2),
            vm(micros, 4, 3, HD, span // 4),
            vm(micros, 2, 2, 3, HD, span // 2),
            vm(micros, 4, 3, HD, span // 4),
            vm(micros, 3, reps, HPAD, tok),
            vm(micros, 2, 2, HPAD, span // 2),
            vm(micros, 4, HPAD, span // 4),
            vm(micros, 2, 2, HPAD, span // 2),
            vm(micros, 4, HPAD, span // 4),
            vm(span, 128),
            vm(128, span),
            dma((2, micros, 3, 3)),
            dma((2, micros, 2)),
            dma((2, micros, 3)),
            dma((2, micros, 2)),
            dma((2, micros, 3)),
            dma((2, 3)),
            dma((micros, 3)),
        ],
        compiler_params=pltpu.CompilerParams(
            vmem_limit_bytes=VMEM, collective_id=1, has_side_effects=True
        ),
        cost_estimate=pl.CostEstimate(
            flops=60_000_000_000, bytes_accessed=30_000_000, transcendentals=30_000_000
        ),
        name="forward",
    )(layer_in, weight, gain, bias, lengths)


def bit_of(axis, bit):
    return lax.axis_index(axis) // (1 << bit) % 2


def bit_peer(axis, bit):
    return lax.axis_index(axis) + (1 << bit) * (1 - 2 * bit_of(axis, bit))


def attend_back(block, gblock, doc, put, scr, pattern, count, lanes, done=None):
    ks, vs, qs, qr, gs, gr, dq = scr
    bs = min(512, lanes)
    zeros = jnp.zeros((HD, bs), bf16)
    r = lax.broadcasted_iota(jnp.int32, (HD, bs), 0)
    fill = jnp.zeros((HD - 32, bs), bf16)
    for s in range(0, count, bs):
        sl = slice(s, s + bs)
        same = doc[:, sl] == r
        aux_k = jnp.where(same | ((r >= 16) & (r < 19)), 1.0, 0.0).astype(bf16)
        aux_q = jnp.where(same | (r >= 4), 0.0, NEG).astype(bf16)
        aux_v = jnp.where((r >= 19) & (r < 21), 1.0, 0.0).astype(bf16)
        q = (block(0, s, bs).astype(f32) * 0.125).astype(bf16)
        tile = gblock(s, bs)
        g, stats = tile[:HD], tile[HD:]
        qs[:, sl] = jnp.concatenate([q, aux_q[:16], stats, fill], 0)
        gs[:, sl] = jnp.concatenate([g, zeros[:16], stats, fill], 0)
        qr[sl, :] = jnp.concatenate([q, zeros], 0).T
        gr[sl, :] = jnp.concatenate([g, zeros], 0).T
        ks[sl, :] = jnp.concatenate([block(1, s, bs), aux_k], 0).T
        vs[sl, :] = jnp.concatenate([block(2, s, bs), aux_v], 0).T

    def tile(k, ksize, q, qsize, diagonal):
        kl, ql = slice(k, k + ksize), slice(q, q + qsize)
        p = jnp.exp2(dot_nn(ks[kl, :], qs[:, ql]) * LOG2E)
        if diagonal:
            keep = rel_pos((ksize, qsize), 0, k % bs, pattern) <= rel_pos(
                (ksize, qsize), 1, q % bs, pattern
            )
            p = jnp.where(keep, p, 0.0)
        dp = dot_nn(vs[kl, :], gs[:, ql])
        ds = (p * dp).astype(bf16)
        dv = dot_nn(p.astype(bf16), gr[ql, :])
        dk = dot_nn(ds, qr[ql, :])
        return dv, dk, dot_nn(block(1, k, ksize), ds) * 0.125

    def add_dq(k, q, qsize, value):
        if k == 0:
            dq[:, q : q + qsize] = value
        else:
            dq[:, q : q + qsize] += value

    for j in range(count // bs):
        at = j * bs
        jl = slice(at, at + bs)
        if pattern == 0:
            dva, dka, dqi = tile(at, bs, at, bs, True)
            add_dq(at, at, bs, dqi)
        else:
            h = bs // 2
            dv0, dk0, dqi = tile(at, h, at, bs, True)
            add_dq(at, at, bs, dqi)
            dv1, dk1, dqi = tile(at + h, h, at + h, h, True)
            add_dq(at + h, at + h, h, dqi)
            dva, dka = jnp.concatenate([dv0, dv1], 0), jnp.concatenate([dk0, dk1], 0)
        for i in range(j + 1, count // bs):
            dvi, dki, dqi = tile(at, bs, i * bs, bs, False)
            dva, dka = dva + dvi, dka + dki
            add_dq(at, i * bs, bs, dqi)
        put(1, j * bs, bs, dka.T[:HD].astype(bf16))
        put(2, j * bs, bs, dva.T[:HD].astype(bf16))
        put(0, j * bs, bs, dq[:, jl].astype(bf16))
        if done is not None:
            done(j)


class Halving:
    def __init__(self, source, steps, buffers, gathered, out, sems):
        self.source, self.steps, self.buffers = source, steps, buffers
        self.gathered, self.out, self.sems = gathered, out, sems
        self.names = ["high", "z", "x", "y"]
        self.at = 0
        self.pending = None

    def pick(self, ref, axis, name, index):
        lead = (slice(None),) * axis
        if name == "high":
            half = ref.shape[axis] // 2
            return lead + (pl.ds(index * half, half),)
        return lead + (index,)

    def start(self):
        if self.at < len(self.steps):
            name, axis_name, bit = self.steps[self.at]
            axis = self.names.index(name)
            mine = bit_of(axis_name, bit)
            target = self.buffers[self.at]
            copy = remote(
                self.source.at[self.pick(self.source, axis, name, 1 - mine)],
                target,
                self.sems.at[0, self.at],
                self.sems.at[1, self.at],
                axis_name,
                bit_peer(axis_name, bit),
            )
            copy.start()
            self.pending = ("sum", copy, target, self.pick(self.source, axis, name, mine))
            if name != "high":
                self.names.pop(axis)
            return
        if self.at > len(self.steps):
            self.pending = None
            return
        me = lax.axis_index("rep")
        self.gathered[me // 2, me % 2] = self.source[0]

        def copy(k, source):
            place = (source // 2, source % 2)
            return remote(
                self.gathered.at[place],
                self.gathered.at[place],
                self.sems.at[0, self.at + k - 1],
                self.sems.at[1, self.at + k - 1],
                "rep",
                rep_peer(k),
            )

        pairs = []
        for k in range(1, 4):
            copy(k, me).start()
            pairs.append((copy(k, me), copy(k, (me + 4 - k) % 4)))
        self.pending = ("gather", pairs, None, None)

    def finish(self):
        kind, first, second, mine = self.pending
        if kind == "sum":
            first.wait()
            rows = second.shape[0]

            def add(n, carry):
                at = (n,) if mine[0] == slice(None) else None
                if at is None:
                    head = mine[0]
                    base = head.start if isinstance(head, pl.Slice) else None
                    value = self.source[(base + n,) + mine[1:]]
                else:
                    value = self.source[at + mine[1:]]
                second[n] = (second[n].astype(f32) + value.astype(f32)).astype(bf16)
                return carry

            lax.fori_loop(0, rows, add, 0)
            self.source = second
        else:
            for sent, landed in first:
                sent.wait_send()
                landed.wait_recv()
        self.at += 1

    def pump(self):
        if self.pending is not None:
            self.finish()
            self.start()

    def drain(self):
        while self.pending is not None:
            self.pump()
        self.out[...] = self.gathered[...]


def reduce_steps(order, seq_bits):
    steps = []
    for name in order:
        if name == "y":
            steps.append(("y", "rep", 1))
        elif name == "x":
            steps.append(("x", "seq", 0))
        elif name == "z":
            steps.append(("z", "seq", 1))
        else:
            steps += [("high", "seq", b) for b in range(seq_bits - 1, 1, -1)]
    return steps


def reduce_buffers(shape, steps):
    high, rows, cols = shape[0], shape[4], shape[5]
    left = 3
    out = []
    for name, _, _ in steps:
        if name == "high":
            high //= 2
        else:
            left -= 1
        out.append((high,) + (2,) * left + (rows, cols))
    return out


def grad_parts(width, hidden):
    return (
        (0, slice(0, width), "yzhx"),
        (1, slice(0, hidden // 2), "zhyx"),
        (1, slice(hidden // 2, hidden), "yxzh"),
        (2, slice(0, width), "zhyx"),
    )


def backward_body(
    r_hbm,
    p1_hbm,
    p2_hbm,
    da0_ref,
    da1_ref,
    att_ref,
    mix_ref,
    len_ref,
    w0_ref,
    w1_ref,
    w2_ref,
    tg_ref,
    t0_ref,
    t1_ref,
    t2_ref,
    *scratch,
    seq_bits,
):
    (r, p1, p2, g0, g1s, g2s, g1, g2, d1, d2, e1, e2, sums, ks, vs, qs, qr, gs, gr, dq) = scratch[:20]
    load_sems, g1_sems, g2_sems, d1_sems, d2_sems, tg_sems, own_sems = scratch[20:27]
    rest = list(scratch[27:])
    halvings = []
    sources, outs = (w0_ref, w1_ref, w2_ref), (t0_ref, t1_ref, t2_ref)
    for n, lanes, order in grad_parts(w0_ref.shape[-1], w1_ref.shape[-1]):
        steps = reduce_steps(order, seq_bits)
        buffers = [rest.pop(0) for _ in steps]
        gathered, sems = rest.pop(0), rest.pop(0)
        source = sources[n].at[:, :, :, :, :, lanes]
        out = outs[n].at[:, :, :, lanes]
        halvings.append(Halving(source, steps, buffers, gathered, out, sems))
    reps, cols, tok = da0_ref.shape
    micros = att_ref.shape[0]
    span = tok * reps
    wide = span // 2
    me = lax.axis_index("rep")
    place = team_place()
    side = place % 2
    scr = (ks, vs, qs, qr, gs, gr, dq)

    barrier = pltpu.get_barrier_semaphore()
    peers = [("rep", rep_peer(k)) for k in range(1, 4)]
    peers += [("seq", team_member(k)) for k in range(1, 4)]
    peers += [("seq", bit_peer("seq", b)) for b in range(2, seq_bits)]
    for axis, peer in peers:
        pl.semaphore_signal(
            barrier, inc=1, device_id={axis: peer}, device_id_type=pl.DeviceIdType.MESH
        )
    load_r = lambda m: pltpu.make_async_copy(r_hbm.at[m], r, load_sems.at[0])
    load_1 = lambda m: pltpu.make_async_copy(p1_hbm.at[m], p1, load_sems.at[1])
    load_2 = lambda m: pltpu.make_async_copy(p2_hbm.at[m], p2, load_sems.at[2])
    load_r(0).start()
    load_1(0).start()
    load_2(0).start()
    pl.semaphore_wait(barrier, len(peers))
    for h in halvings:
        h.start()

    def pump():
        for h in halvings:
            h.pump()

    def g1_copy(m, s, source):
        return remote(
            g1s.at[m, s],
            g1.at[m, source, s],
            g1_sems.at[0, m, s],
            g1_sems.at[1, m, s],
            "seq",
            pair_partner(),
        )

    def g2_copy(m, k, source):
        return remote(
            g2s.at[m, (place + k) % 4],
            g2.at[m, source],
            g2_sems.at[0, m, k - 1],
            g2_sems.at[1, m, k - 1],
            "seq",
            team_member(k),
        )

    def d1_copy(m, s, source):
        return remote(
            d1.at[m, s, 1 - side],
            e1.at[m, source, s],
            d1_sems.at[0, m, s],
            d1_sems.at[1, m, s],
            "seq",
            pair_partner(),
        )

    def d2_copy(m, k, source):
        return remote(
            d2.at[m, (place + k) % 4],
            e2.at[m, source],
            d2_sems.at[0, m, k - 1],
            d2_sems.at[1, m, k - 1],
            "seq",
            team_member(k),
        )

    def tg_copy(m, j, k, source):
        return remote(
            sums.at[m, rep_peer(k), :, head_rows(j)],
            tg_ref.at[m, source, :, head_rows(j)],
            tg_sems.at[0, m, j, k - 1],
            tg_sems.at[1, m, j, k - 1],
            "rep",
            rep_peer(k),
        )

    own_copy = lambda m: pltpu.make_async_copy(sums.at[m, me], tg_ref.at[m, me], own_sems.at[m])

    def half(j):
        return pl.ds(pl.multiple_of(((3 * me + j) % 2) * 256, 256), 256)

    def quarter_at(j):
        c = (3 * me + j) % 4
        return c % 2 * 2 + c // 2

    def quarter(j):
        return pl.ds(pl.multiple_of(quarter_at(j) * 128, 128), 128)

    for m, da_ref in enumerate((da0_ref, da1_ref)):
        for j in range(3):
            rows = slice(j * HD, (j + 1) * HD)
            for b in range(reps):
                g = da_ref[b, rows, :]
                inner = jnp.sum(
                    g.astype(f32) * att_ref[m, b, rows, :].astype(f32), 0, keepdims=True
                )
                total = mix_ref[m, j : j + 1, b * tok : (b + 1) * tok]
                high, mid, low = split3(-total)
                inner_high, inner_mid, _ = split3(-inner)
                g0[m, j, b, :HD, :] = g
                g0[m, j, b, HD:, :] = stat_rows((high, mid, low, inner_high, inner_mid), tok)
        for b in range(reps):
            bl = slice(b * 256, (b + 1) * 256)
            g1s[m, 0, :, bl] = g0[m, 1 - side, b, :, half(1 - side)]
            g1[m, side, 0, :, bl] = g0[m, side, b, :, half(side)]
            piece = g0[m, 2, b, :, half(2)]
            g1s[m, 1, :, bl] = piece
            g1[m, side, 1, :, bl] = piece
            for g in range(4):
                j = clamp_slot(slot_of(g))
                g2s[m, g, :, b * 128 : (b + 1) * 128] = g0[m, j, b, :, quarter(j)]
        g2[m, place] = g2s[m, place]
        g1_copy(m, 0, side).start()

        @pl.when(side != taker())
        def _():
            g1_copy(m, 1, side).start()

        for k in range(1, 4):

            @pl.when(slot_of(place + k) < 3)
            def _():
                g2_copy(m, k, place).start()

    def docs(m, pattern):
        return doc_rows(len_ref, m, segment_start(pattern, span), 2**pattern, span)

    def own_head(m, j, done=None):
        def block(c, start, size):
            at = start % tok
            return r[start // tok, c, head_rows(j), at : at + size]

        def gblock(start, size):
            at = start % tok
            return g0[m, j, start // tok, :, at : at + size]

        def put(c, start, size, value):
            at = start % tok
            sums[m, start // tok, c, head_rows(j), at : at + size] = value

        attend_back(block, gblock, docs(m, 0), put, scr, 0, span, tok, done)

    def add_others(m, j, b):
        s = j // 2
        e = s * taker() + (1 - s) * j
        bl = slice(b * 256, (b + 1) * 256)
        t = sums[m, b, :, head_rows(j), half(j)].astype(f32)
        t = t + e1[m, e, s, :, :, bl].astype(f32)
        sums[m, b, :, head_rows(j), half(j)] = t.astype(bf16)
        t = sums[m, b, :, head_rows(j), quarter(j)].astype(f32)
        t = t + e2[m, owner_of(j), :, :, b * 128 : (b + 1) * 128].astype(f32)
        sums[m, b, :, head_rows(j), quarter(j)] = t.astype(bf16)

    def wait_others(m):
        d1_copy(m, 0, 1 - side).wait_recv()

        @pl.when(side != taker())
        def _():
            d1_copy(m, 1, 1 - side).wait_recv()

        for k in range(1, 4):

            @pl.when(slot_of(place + 4 - k) < 3)
            def _():
                d2_copy(m, k, (place + 4 - k) % 4).wait_recv()

    def complete(m, j, b):
        add_others(m, j, b)
        k = (b + reps - me) % reps

        @pl.when(k > 0)
        def _():
            tg_copy(m, j, k, me).start()

    def heads(m, first, last):
        def step(j, carry):
            def done(b):
                @pl.when(j > first)
                def _():
                    complete(m, j, b)

            own_head(m, j, done)

            @pl.when(j == first)
            def _():
                wait_others(m)
                for n in range(first + 1):
                    for b in range(reps):
                        complete(m, n, b)

            return carry

        lax.fori_loop(first, last, step, 0)

    load_r(0).wait()
    own_head(0, 0)

    def others(m):
        def paired(s):
            g1_copy(m, s, 1 - side).wait_recv()

            def block(c, start, size):
                at = start % wide
                return p1[start // wide, s, c, :, at : at + size]

            def gblock(start, size):
                at = start % wide
                return g1[m, start // wide, s, :, at : at + size]

            def put(c, start, size, value):
                at = start % wide
                d1[m, s, start // wide, c, :, at : at + size] = value

            attend_back(block, gblock, docs(m, 1), put, scr, 1, span, wide)
            e1[m, side, s] = d1[m, s, side]
            d1_copy(m, s, side).start()

        def each_pair(s, inner):
            @pl.when((s == 0) | (side == taker()))
            def _():
                paired(s)

            return inner

        load_1(m).wait()
        lax.fori_loop(0, 2, each_pair, 0)
        if m + 1 < micros:
            load_1(m + 1).start()
            halvings[1].pump()
            halvings[3].pump()
        else:
            pump()
        load_2(m).wait()

        def block(c, start, size):
            at = start % tok
            return p2[start // tok, c, :, at : at + size]

        def gblock(start, size):
            at = start % tok
            return g2[m, start // tok, :, at : at + size]

        def put(c, start, size, value):
            at = start % tok
            d2[m, start // tok, c, :, at : at + size] = value

        @pl.when(slot_of(place) < 3)
        def _():
            for k in range(1, 4):
                g2_copy(m, k, (place + 4 - k) % 4).wait_recv()
            attend_back(block, gblock, docs(m, 2), put, scr, 2, span, tok)
            e2[m, place] = d2[m, place]
            for k in range(1, 4):
                d2_copy(m, k, place).start()

        if m + 1 < micros:
            load_2(m + 1).start()

    others(0)
    heads(0, 1, 3)
    own_copy(0).start()
    load_r(1).start()
    pump()
    others(1)
    pump()
    load_r(1).wait()
    heads(1, 0, 1)
    pump()

    def last_heads(j, carry):
        own_head(1, j, lambda b: complete(1, j, b))
        return carry

    lax.fori_loop(1, 3, last_heads, 0)
    own_copy(1).start()
    for h in halvings:
        h.drain()
    for m in range(micros):
        own_copy(m).wait()
        g1_copy(m, 0, side).wait_send()
        d1_copy(m, 0, side).wait_send()

        @pl.when(side != taker())
        def _():
            g1_copy(m, 1, side).wait_send()

        @pl.when(side == taker())
        def _():
            d1_copy(m, 1, side).wait_send()

        for k in range(1, 4):

            @pl.when(slot_of(place + k) < 3)
            def _():
                g2_copy(m, k, place).wait_send()

            @pl.when(slot_of(place) < 3)
            def _():
                d2_copy(m, k, place).wait_send()


    def settle(j, carry):
        for m in range(micros):
            for k in range(1, 4):
                tg_copy(m, j, k, (me + reps - k) % reps).wait_recv()
                tg_copy(m, j, k, me).wait_send()
        return carry

    lax.fori_loop(0, 3, settle, 0)


def backward_call(pieces, da, att, totals, lengths, grads, seq_bits):
    micros, reps, cols, tok = att.shape
    span = tok * reps
    any_spec = pl.BlockSpec(memory_space=pl.ANY)

    def vm(*shape):
        return pltpu.VMEM(shape, bf16)

    dma = pltpu.SemaphoreType.DMA
    halving = []
    for n, lanes, order in grad_parts(grads[0].shape[-1], grads[1].shape[-1]):
        steps = reduce_steps(order, seq_bits)
        shape = grads[n].shape[:5] + (lanes.stop - lanes.start,)
        halving += [vm(*b) for b in reduce_buffers(shape, steps)]
        halving += [vm(2, 2, *shape[4:]), dma((2, len(steps) + 3))]
    tall, flat = vm(span, 128), vm(128, span)
    outs = [((micros, reps, 3, cols, tok), bf16, any_spec)]
    outs += [((2, 2) + g.shape[4:], bf16, vmem_spec()) for g in grads]
    return pl.pallas_call(
        functools.partial(backward_body, seq_bits=seq_bits),
        in_specs=[any_spec] * 3 + [vmem_spec()] * 4 + [smem_spec()] + [vmem_spec()] * 3,
        out_specs=[o[2] for o in outs],
        out_shape=[jax.ShapeDtypeStruct(o[0], o[1]) for o in outs],
        scratch_shapes=[
            vm(reps, 3, cols, tok),
            vm(2, 2, 3, HD, span // 2),
            vm(4, 3, HD, span // 4),
            vm(micros, 3, reps, HPAD, tok),
            vm(micros, 2, HPAD, span // 2),
            vm(micros, 4, HPAD, span // 4),
            vm(micros, 2, 2, HPAD, span // 2),
            vm(micros, 4, HPAD, span // 4),
            vm(micros, 2, 2, 3, HD, span // 2),
            vm(micros, 4, 3, HD, span // 4),
            vm(micros, 2, 2, 3, HD, span // 2),
            vm(micros, 4, 3, HD, span // 4),
            vm(micros, reps, 3, cols, tok),
            tall,
            tall,
            flat,
            tall,
            flat,
            tall,
            pltpu.VMEM((HD, span), f32),
            dma((3,)),
            dma((2, micros, 2)),
            dma((2, micros, 3)),
            dma((2, micros, 2)),
            dma((2, micros, 3)),
            dma((2, micros, 3, 3)),
            dma((micros,)),
            *halving,
        ],
        compiler_params=pltpu.CompilerParams(
            vmem_limit_bytes=60 << 20, collective_id=2, has_side_effects=True
        ),
        cost_estimate=pl.CostEstimate(
            flops=100_000_000_000, bytes_accessed=40_000_000, transcendentals=30_000_000
        ),
        name="backward",
    )(*pieces, *da, att, totals, lengths, *grads)


def store_parts(ref, value):
    parts, _, rows, _ = ref.shape
    for n in range(2 * parts):
        ref[n // 2, n % 2] = value[n * rows : (n + 1) * rows].astype(bf16)


def weight_grad_body(*refs, chunks):
    ins, da_ref, refs = refs[:12], refs[12], refs[13:]
    down_ref, up_ref, proj_ref, da_out, lt = refs[:5]
    values, gets, sems = refs[5:8], refs[8:11], refs[11:14]
    da_sems, own_sems = refs[14:]
    core = bit_of("rep", 0)
    me = lax.axis_index("rep")
    groups = [ins[:6], ins[6:]]
    n = pl.program_id(0)

    def copy(t, slot):
        return remote(
            values[t].at[slot, :, 1 - core],
            gets[t].at[slot],
            sems[t].at[0, slot],
            sems[t].at[1, slot],
            "rep",
            bit_peer("rep", 0),
        )

    def spread(t, slot, value):
        store_parts(values[t].at[slot], value)
        copy(t, slot).start()

    def da_copy(k, source):
        return remote(
            da_ref.at[rep_peer(k)],
            da_out.at[source],
            da_sems.at[0, k - 1],
            da_sems.at[1, k - 1],
            "rep",
            rep_peer(k),
        )

    da_own = pltpu.make_async_copy(da_ref.at[me], da_out.at[me], own_sems.at[0])

    @pl.when(n == 0)
    def _():
        barrier = pltpu.get_barrier_semaphore()
        for k in range(1, 4):
            pl.semaphore_signal(
                barrier, inc=1, device_id={"rep": rep_peer(k)}, device_id_type=pl.DeviceIdType.MESH
            )
        pl.semaphore_wait(barrier, 3)
        for k in range(1, 4):
            da_copy(k, me).start()
        da_own.start()
        total = None
        for k, (low, dup, hid, cot, mix, brl) in enumerate(groups):
            lt[k] = low[...].T
            part = dot_tn(mix[...], brl[...])
            total = part if total is None else total + part
        spread(2, 0, total)

    @pl.when(n < chunks)
    def _():
        up = down = None
        for k, (low, dup, hid, cot, mix, brl) in enumerate(groups):
            u = dot_nn(lt[k], dup[...])
            d = dot_tn(hid[...], cot[...])
            up = u if up is None else up + u
            down = d if down is None else down + d
        spread(0, n, down)
        spread(1, n, up)

    def merged(t, slot, out_ref):
        copy(t, slot).wait()
        value, got = values[t], gets[t]
        for k in range(got.shape[1]):
            out_ref[k] = (value[slot, k, core].astype(f32) + got[slot, k].astype(f32)).astype(bf16)

    @pl.when(n > 0)
    def _():
        merged(0, n - 1, down_ref)
        merged(1, n - 1, up_ref)

    @pl.when(n == chunks)
    def _():
        merged(2, 0, proj_ref)
        da_own.wait()
        for k in range(1, 4):
            da_copy(k, (me + 4 - k) % 4).wait_recv()
            da_copy(k, me).wait_send()


def weight_grads(group, da, width, hidden, seqs, reps):
    tok = group[0].shape[1]
    chunk = 768
    chunks = hidden // chunk
    last = chunks - 1

    def full(k):
        return pl.BlockSpec((None, tok, width), lambda n: (k, 0, 0))

    def part(k):
        return pl.BlockSpec((None, tok, chunk), lambda n: (k, 0, jnp.minimum(n, last)))

    def specs(k):
        return [full(k), part(k), part(k), full(k), full(k), full(k)]

    down_rows, up_rows = hidden // seqs // reps, width // seqs // reps
    per = chunk // down_rows // 2
    blocks = seqs * reps // 2
    shapes = [(chunks, per, down_rows, width), (chunks, blocks, up_rows, chunk), (1, blocks, up_rows, width)]
    return pl.pallas_call(
        functools.partial(weight_grad_body, chunks=chunks),
        grid=(chunks + 1,),
        in_specs=specs(0) + specs(1) + [vmem_spec()],
        out_specs=[
            pl.BlockSpec((per, down_rows, width), lambda n: (jnp.maximum(n - 1, 0), 0, 0)),
            pl.BlockSpec((blocks, up_rows, chunk), lambda n: (0, 0, jnp.maximum(n - 1, 0))),
            pl.BlockSpec((blocks, up_rows, width), lambda n: (0, 0, 0)),
            pl.BlockSpec(memory_space=pl.ANY),
        ],
        out_shape=[
            jax.ShapeDtypeStruct((blocks, down_rows, width), bf16),
            jax.ShapeDtypeStruct((blocks, up_rows, hidden), bf16),
            jax.ShapeDtypeStruct((blocks, up_rows, width), bf16),
            jax.ShapeDtypeStruct(da.shape, bf16),
        ],
        scratch_shapes=[pltpu.VMEM((2, width, tok), bf16)]
        + [pltpu.VMEM(b[:2] + (2,) + b[2:], bf16) for b in shapes]
        + [pltpu.VMEM(b, bf16) for b in shapes]
        + [pltpu.SemaphoreType.DMA((2, s[0])) for s in shapes]
        + [pltpu.SemaphoreType.DMA((2, 3)), pltpu.SemaphoreType.DMA((1,))],
        compiler_params=pltpu.CompilerParams(
            vmem_limit_bytes=VMEM, collective_id=3, has_side_effects=True
        ),
        cost_estimate=pl.CostEstimate(
            flops=4 * tok * width * (2 * hidden + width),
            bytes_accessed=30_000_000,
            transcendentals=0,
        ),
        name="weight_grads",
    )(*group, *group, da)


TAIL_ORDERS = ("yxzh", "xzhy", "zhyx")


def vec_rounds(seq_bits):
    rounds = [
        ("rep", lax.axis_index("rep"), [rep_peer(k) for k in range(1, 4)]),
        ("seq", team_place(), [team_member(k) for k in range(1, 4)]),
    ]
    for b in range(2, seq_bits):
        rounds.append(("seq", bit_of("seq", b), [bit_peer("seq", b)]))
    return rounds


def tail_body(
    tg_hbm,
    w_hbm,
    branch_hbm,
    xp_ref,
    nt_ref,
    gain_ref,
    ng_ref,
    nh_ref,
    out_ref,
    total_ref,
    norm_ref,
    hidden_ref,
    *scratch,
    seq_bits,
):
    tg, w, branch, acc, value, get, vec, load_sems, core_sems = scratch[:9]
    rest = list(scratch[9:])
    micros, tok, width = xp_ref.shape
    reps = tg.shape[2]
    parts = get.shape[1]
    core = bit_of("rep", 0)
    rounds = vec_rounds(seq_bits)

    barrier = pltpu.get_barrier_semaphore()
    peers = [(axis, peer) for axis, _, others in rounds for peer in others]
    for axis, peer in peers:
        pl.semaphore_signal(
            barrier, inc=1, device_id={axis: peer}, device_id_type=pl.DeviceIdType.MESH
        )
    loads = [
        pltpu.make_async_copy(tg_hbm.at[m, :, c], tg.at[m, c], load_sems.at[m * 3 + c])
        for c in range(3)
        for m in range(micros)
    ]
    loads += [pltpu.make_async_copy(w_hbm, w, load_sems.at[6])]
    loads += [
        pltpu.make_async_copy(branch_hbm.at[m], branch.at[m], load_sems.at[7 + m])
        for m in range(micros)
    ]
    for c in loads:
        c.start()
    pl.semaphore_wait(barrier, len(peers))

    def core_copy(c):
        return remote(
            value.at[c, :, 1 - core],
            get.at[c],
            core_sems.at[0, c],
            core_sems.at[1, c],
            "rep",
            bit_peer("rep", 0),
        )

    def piece(m, c):
        return jnp.concatenate([tg[m, c, r] for r in range(reps)], 0)

    for c in range(3):
        total = None
        for m in range(micros):
            loads[c * micros + m].wait()
            part = dot_nt(nt_ref[m], piece(m, c))
            total = part if total is None else total + part
        store_parts(value.at[c], total)
        core_copy(c).start()

    halvings = []
    for c, order in enumerate(TAIL_ORDERS):
        steps = reduce_steps(order, seq_bits)
        summed = rest.pop(0)
        buffers = [rest.pop(0) for _ in steps]
        gathered, sems = rest.pop(0), rest.pop(0)
        out = total_ref.at[:, :, :, c * width : (c + 1) * width]
        halvings.append(Halving(summed, steps, buffers, gathered, out, sems))

    def core_sum(c):
        core_copy(c).wait()
        summed = halvings[c].source

        def add(z, carry):
            for n in range(8):
                k = z * 8 + n
                total = value[c, k, core].astype(f32) + get[c, k].astype(f32)
                summed[z, n // 4, n // 2 % 2, n % 2] = total.astype(bf16)
            return carry

        lax.fori_loop(0, parts // 8, add, 0)
        halvings[c].start()

    loads[6].wait()

    def grad_part(m, c):
        part = dot_nn(w[:, c * width : (c + 1) * width], piece(m, c))
        if c == 0:
            acc[...] = part
        else:
            acc[...] += part

    def grad_end(m):
        xhat, rstd = normalize(xp_ref[m].astype(f32))
        dx, gain_i, bias_i = norm_back(acc[...].T, gain_ref[...].reshape(1, -1), xhat, rstd)
        loads[7 + m].wait()
        out_ref[m] = (branch[m] + dx).astype(bf16)
        return gain_i, bias_i

    core_sum(0)
    grad_part(0, 0)
    core_sum(1)
    grad_part(0, 1)
    core_sum(2)
    grad_part(0, 2)
    gain0, bias0 = grad_end(0)

    def pump():
        for h in halvings:
            h.pump()

    for c in range(3):
        grad_part(1, c)
    pump()
    gain1, bias1 = grad_end(1)
    terms = [gain0 + gain1, bias0 + bias1]
    terms += [ng_ref[0, n : n + 1] + ng_ref[1, n : n + 1] for n in range(4)]
    terms += [jnp.zeros((2, width), f32)]
    fold = nh_ref.shape[2] // width
    for n in range(2):
        for k in range(fold):
            cl = slice(k * width, (k + 1) * width)
            terms.append(nh_ref[0, n : n + 1, cl] + nh_ref[1, n : n + 1, cl])
    terms = jnp.concatenate(terms, 0)
    for n, (axis, place, others) in enumerate(rounds):
        box, sems = vec[2 * n], vec[2 * n + 1]
        box[place] = terms
        copies = []
        for k, peer in enumerate(others):
            copies.append(
                remote(box.at[place], box.at[place], sems.at[0, k], sems.at[1, k], axis, peer)
            )
            copies[-1].start()
        pump()
        size = box.shape[0]
        for k in range(1, size):
            landing = (place + size - k) % size
            remote(
                box.at[landing],
                box.at[landing],
                sems.at[0, k - 1],
                sems.at[1, k - 1],
                axis,
                others[k - 1],
            ).wait_recv()
        terms = box[0]
        for k in range(1, size):
            terms = terms + box[k]
        for c in copies:
            c.wait_send()
    s = lax.axis_index("seq")
    seqs = 1 << seq_bits
    cols = terms.T
    acc[:, : cols.shape[1]] = cols


    def rows_at(block, size):
        if size % 8 == 0:
            return acc[pl.ds(pl.multiple_of(block * size, 8), size), :16]
        out = cols[:size]
        for n in range(1, width // size):
            out = jnp.where(block == n, cols[n * size : (n + 1) * size], out)
        return out

    norm_ref[...] = rows_at(s, norm_ref.shape[1]).T[:6]
    own = hidden_ref.shape[1]
    per = width // own
    picked = rows_at(s % per, own)
    out = jnp.zeros((own, 2), f32)
    for k in range(fold):
        pair = jnp.concatenate(
            [picked[:, 8 + k : 9 + k], picked[:, 8 + fold + k : 9 + fold + k]], 1
        )
        out = jnp.where(s // per == k, pair, out)
    hidden_ref[...] = out.T
    for h in halvings:
        h.drain()


def tail_call(tg, weight, branch, xp, nt, gain, ng, nh, seq_bits):
    micros, tok, width = xp.shape
    reps, _, cols = tg.shape[1:4]
    hidden = nh.shape[2]
    seqs = 1 << seq_bits
    rows = width // seqs // reps
    parts = seqs * reps // 2
    any_spec = pl.BlockSpec(memory_space=pl.ANY)

    def vm(*shape):
        return pltpu.VMEM(shape, bf16)

    dma = pltpu.SemaphoreType.DMA
    shape = (seqs // 4, 2, 2, reps // 2, rows, width)
    halving = []
    for order in TAIL_ORDERS:
        steps = reduce_steps(order, seq_bits)
        halving += [vm(*shape)] + [vm(*b) for b in reduce_buffers(shape, steps)]
        halving += [vm(2, 2, rows, width), dma((2, len(steps) + 3))]
    vec = []
    for size in (4, 4) + (2,) * (seq_bits - 2):
        vec += [pltpu.VMEM((size, 16, width), f32), dma((2, size - 1))]
    outs = [
        ((micros, tok, width), bf16),
        ((2, 2, rows, 3 * width), bf16),
        ((6, width // seqs), f32),
        ((2, hidden // seqs), f32),
    ]
    return pl.pallas_call(
        functools.partial(tail_body, seq_bits=seq_bits),
        in_specs=[any_spec] * 3 + [vmem_spec()] * 5,
        out_specs=[vmem_spec()] * 4,
        out_shape=[jax.ShapeDtypeStruct(s, d) for s, d in outs],
        scratch_shapes=[
            vm(micros, 3, reps, cols, tok),
            vm(width, 3 * width),
            pltpu.VMEM((micros, tok, width), f32),
            pltpu.VMEM((width, tok), f32),
            vm(3, parts, 2, rows, width),
            vm(3, parts, rows, width),
            vec,
            dma((9,)),
            dma((2, 3)),
            *halving,
        ],
        compiler_params=pltpu.CompilerParams(
            vmem_limit_bytes=VMEM, collective_id=4, has_side_effects=True
        ),
        cost_estimate=pl.CostEstimate(
            flops=24 * tok * width * width, bytes_accessed=20_000_000, transcendentals=0
        ),
        name="tail",
    )(tg, weight, branch, xp, nt, gain, ng, nh)


def finish_body(*refs):
    half = len(refs) // 2
    ins, outs = refs[:half], refs[half:]
    back = onehot_cols(ins[0].shape[0])
    for a, o in zip(ins[:2], outs[:2]):
        o[...] = dot_nn(back, a[...]).astype(bf16)

    @pl.when(pl.program_id(0) == 0)
    def _():
        for a, o in zip(ins[2:], outs[2:]):
            o[...] = a[...].astype(f32)


def finish_call(tokens, grads):
    args = (*tokens, *grads)
    specs = [pl.BlockSpec((None,) + a.shape[1:], lambda m: (m, 0, 0)) for a in tokens]
    specs += [pl.BlockSpec(a.shape, lambda m: (0, 0)) for a in grads]
    return pl.pallas_call(
        finish_body,
        grid=(tokens[0].shape[0],),
        in_specs=specs,
        out_specs=specs,
        out_shape=[jax.ShapeDtypeStruct(a.shape, bf16) for a in tokens]
        + [jax.ShapeDtypeStruct(a.shape, f32) for a in grads],
        compiler_params=pltpu.CompilerParams(vmem_limit_bytes=VMEM),
        cost_estimate=pl.CostEstimate(
            flops=2_000_000_000, bytes_accessed=12_000_000, transcendentals=0
        ),
        name="finish",
    )(*args)


def bits_of(count):
    return count.bit_length() - 1


def on_device(
    layer_in,
    qkv_weight,
    out_weight,
    up_weight,
    down_weight,
    input_gain,
    input_bias,
    mixer_gain,
    mixer_bias,
    block_gain,
    block_bias,
    hidden_gain,
    hidden_bias,
    output_grad,
    seq_lengths,
):
    micro_count, tok, width = layer_in.shape
    reps = lax.axis_size("rep")
    seqs = lax.axis_size("seq")
    seq_bits = bits_of(seqs)
    hidden = up_weight.shape[1]
    xp, nt, got_qkv, got_pair, got_four, own_att, got_att, totals = forward_call(
        layer_in, qkv_weight, input_gain, input_bias, seq_lengths, reps
    )
    out, ng, nh, branch, mix, low, hid, dup, brl, cotp, da0, da1 = ffn_call(
        own_att,
        got_att,
        xp,
        output_grad,
        (out_weight, up_weight, down_weight),
        (mixer_gain, mixer_bias, block_gain, block_bias, hidden_gain, hidden_bias),
    )
    *grads, da1 = weight_grads((low, dup, hid, cotp, mix, brl), da1, width, hidden, seqs, reps)
    grads = [g.reshape((seqs // 4, 2, 2, reps // 2) + g.shape[1:]) for g in grads]
    token_grad, *totals = backward_call(
        (got_qkv, got_pair, got_four), (da0, da1), own_att, totals, seq_lengths, grads, seq_bits
    )
    input_grad, qkv_total, norm_total, hidden_total = tail_call(
        token_grad, qkv_weight, branch, xp, nt, input_gain, ng, nh, seq_bits
    )
    down_total, up_total, proj_total, qkv_total = (
        t.reshape(-1, t.shape[-1]) for t in (*totals, qkv_total)
    )
    *results, norm_total, hidden_total = finish_call(
        (out, input_grad), (qkv_total, proj_total, up_total, down_total, norm_total, hidden_total)
    )
    return (*results, norm_total.T, hidden_total.T)


def solution(mesh):
    tokens = P(None, ("seq", "rep"), None)
    rows = P("seq", None)
    return jax.shard_map(
        on_device,
        mesh=mesh,
        in_specs=(tokens,) + (P(),) * 12 + (tokens, P()),
        out_specs=(tokens, tokens) + (rows,) * 6,
        check_vma=False,
    )
```
